32 devices in a mesh: dp: 8 (over y, x, core), tensor: 4 (over z).
Axes of the slice: x: 2, y: 2, z: 4, core: 2. Of those that a mesh axis runs over, the one named last changes fastest.
Arguments:
- inputs: bfloat16 [2, 16384, 1024], P(None, ('dp', 'tensor')), may hold values from -6 to 6
- segment_ids: int32 [2, 8, 2048], P(None, 'dp'), may hold values from 0 to 3, never falling along the last dimension, each value on 1 to 1024 neighbouring positions
- token_valid: int32 [2, 8, 2048], P(None, 'dp'), may hold values from 0 to 1, as said below
- qkv_weight: bfloat16 [3, 1024, 1024], P(None, 'dp', 'tensor'), may hold values from -0.1875 to 0.1875
- qv_bias: float32 [2, 1024], P(None, 'tensor'), may hold values from -3 to 3
- out_weight: bfloat16 [1024, 1024], P('tensor', 'dp'), may hold values from -1.5 to 1.5
- norm_gains: float32 [2, 1024], replicated, may hold values from 0.25 to 1.75
- row_biases: float32 [4, 1024], replicated, may hold values from -3 to 3
- up_weight: bfloat16 [1024, 4096], P('dp', 'tensor'), may hold values from -0.1875 to 0.1875
- up_bias: float32 [4096], P('tensor'), may hold values from -3 to 3
- down_weight: bfloat16 [4096, 1024], P('tensor', 'dp'), may hold values from -0.09375 to 0.09375
- out_grad: bfloat16 [2, 16384, 1024], P(None, ('dp', 'tensor')), may hold values from -6 to 6
Outputs:
- layer_out: bfloat16 [2, 16384, 1024], P(None, ('dp', 'tensor'))
- input_grad: float32 [2, 16384, 1024], P(None, ('dp', 'tensor'))
- qkv_grad: float32 [3, 1024, 1024], P(None, 'dp', 'tensor')
- qv_bias_grad: float32 [2, 1024], P(None, 'tensor')
- out_weight_grad: float32 [1024, 1024], P('tensor', 'dp')
- gain_grad: float32 [2, 1024], replicated
- row_bias_grad: float32 [4, 1024], replicated
- up_weight_grad: float32 [1024, 4096], P('dp', 'tensor')
- up_bias_grad: float32 [4096], P('tensor')
- down_weight_grad: float32 [4096, 1024], P('tensor', 'dp')
The draws below stay inside these ranges and needn't reach their ends.
Inputs may be any that keep to these rules, and one draw needn't show every extreme that they name: `segment_ids`: segment numbers never fall along a sequence. `token_valid`: in each sequence the ones form a prefix of at least three quarters of it, and its last token is padding.
All inputs are finite; a program needn't handle non-finite values.
Results may differ from the reference program's by a relative error of at most 0.019.
Values may be sent and summed in bfloat16 or wider, within the bound.
A program may use at most 256 MiB of HBM per device.

```python
import math
import jax
import jax.numpy as jnp
import numpy as np
from jax import lax

D = 1024
HEADS = 16
HEAD = 64
FF = 4096
MB = 2
LEN = 2048
DOCS = 4
ROWS = 16384
N_DP = 8


def draw_token_valid(key, part):
    padding = jax.random.randint(key, (MB, N_DP, 1), 1, LEN // 4)
    position = lax.broadcasted_iota(jnp.int32, (MB, N_DP, LEN), 2)
    return (position < LEN - padding).astype(jnp.int32)


def raised(values, stream_key, source, target, parts, factor):
    def block_of(axis_at):
        return (jnp.arange(values.shape[axis_at]) // (values.shape[axis_at] // parts)).reshape((-1,) + (1,) * (values.ndim - 1 - axis_at))

    one_side = jax.random.permutation(stream_key, parts)[block_of(target)]
    other_side = (block_of(target) + parts // 2) % parts
    return jnp.where((block_of(source) == one_side) | (block_of(source) == other_side), factor * values, values)


def steps_of(rng, shape, split, low, high):
    def one(axis_at, parts):
        draws = jax.random.uniform(jax.random.fold_in(jax.random.fold_in(rng, 6), axis_at), (parts,), jnp.float32, low / len(split), high / len(split))
        return jnp.repeat(jnp.exp(draws), shape[axis_at] // parts).reshape((-1,) + (1,) * (len(shape) - axis_at - 1))

    level = one(*split[0])
    for cut in split[1:]:
        level = level * one(*cut)
    return level


def profile(amount, total, most, slope):
    weights = [(1 << 20) // math.isqrt(rank ** slope) + 1 for rank in range(2, amount + 1)]
    spare, holding = total - most - (amount - 1), [1] * (amount - 1)
    while spare > 0:
        movable = [i for i in range(amount - 1) if holding[i] < most]
        mass, remaining = sum([weights[i] for i in movable]), spare
        for i in movable:
            more = min(most - holding[i], max(1, remaining * weights[i] // mass), spare)
            holding[i] = holding[i] + more
            spare = spare - more
    return np.array([most] + holding)


def ragged_sizes(key, count, total, limit, slope):
    if count == 2:
        one = jax.random.randint(key, (), max(1, total - limit), min(limit, total - 1) + 1)
        return jnp.stack([one, total - one])
    lengths = jnp.asarray(profile(count, total, limit, slope), jnp.int32)
    twos = (count - 1) // 2
    donor, taker = lengths[1:1 + 2 * twos:2], lengths[2:2 + 2 * twos:2]
    slack = jnp.minimum(donor - 1, limit - taker)
    moved = jax.random.randint(jax.random.fold_in(key, 1), (twos,), 0, 1 << 20) % (slack + 1)
    lengths = lengths.at[1:1 + 2 * twos:2].set(donor - moved).at[2:2 + 2 * twos:2].set(taker + moved)
    return lengths[jax.random.permutation(jax.random.fold_in(key, 2), count)]


def gaussian(key, extent, deviation, most, cuts=(), kind=jnp.bfloat16):
    drawn = jax.random.normal(key, extent, jnp.float32) * deviation
    if len(cuts) > 0:
        drawn = steps_of(key, extent, cuts, -0.22, 0.18) * drawn
    return jnp.clip(drawn, min=-most, max=most).astype(kind)


def noise_with(rng, dims, scale, reach, cuts, heavy, kind=jnp.bfloat16):
    drawn = scale * jax.random.normal(rng, dims, jnp.float32)
    if cuts:
        drawn = drawn * steps_of(rng, dims, cuts, -0.22, 0.18)
    return jnp.clip(raised(drawn, jax.random.fold_in(rng, 3), *heavy), -reach, reach).astype(kind)


def setup_inputs(seed: int = 0) -> dict:
    splits = jax.random.split(jax.random.key(seed), 13)
    return {
        "inputs": gaussian(splits[0], (MB, ROWS, D), 1.0, 6.0, ((1, 32),)),
        "segment_ids": jax.vmap(lambda own: jnp.searchsorted(jnp.cumsum(ragged_sizes(own, DOCS, LEN, LEN // 2, 1)), jnp.arange(LEN), side="right"))(jax.random.split(splits[1], MB * N_DP)).reshape((MB, N_DP, LEN)).astype(jnp.int32),
        "token_valid": draw_token_valid(jax.random.fold_in(splits[12], 71), 0),
        "qkv_weight": gaussian(splits[3], (3, D, D), D ** -0.5, 0.1875, ((1, 8), (2, 4))),
        "qv_bias": gaussian(splits[4], (2, D), 0.5, 3.0, ((1, 4),), jnp.float32),
        "out_weight": gaussian(splits[5], (D, D), (D // 64) ** -0.5, 1.5, ((0, 4), (1, 8))),
        "norm_gains": jnp.clip(1.0 + 0.15 * jax.random.normal(splits[6], (2, D), jnp.float32), 0.25, 1.75),
        "row_biases": gaussian(splits[7], (4, D), 0.5, 3.0, (), jnp.float32),
        "up_weight": gaussian(splits[8], (D, FF), D ** -0.5, 0.1875, ((0, 8), (1, 4))),
        "up_bias": gaussian(splits[9], (FF,), 0.5, 3.0, ((0, 4),), jnp.float32),
        "down_weight": gaussian(splits[10], (FF, D), FF ** -0.5, 0.09375, ((0, 4), (1, 8))),
        "out_grad": noise_with(splits[11], (MB, ROWS, D), 1.0, 6.0, ((1, 32),), (1, 2, 32, 2.75)),
    }


@jax.custom_vjp
def low(v):
    return lax.optimization_barrier(v.astype(jnp.bfloat16)).astype(jnp.float32)

@jax.custom_vjp
def low_back(v):
    return v

def low_keep(v):
    return (low(v), None)

def low_pass(kept, grad):
    return (grad,)

def back_keep(v):
    return (v, None)

def back_low(kept, grad):
    return (low(grad),)
low.defvjp(low_keep, low_pass)
low_back.defvjp(back_keep, back_low)
HIGHEST = lax.Precision.HIGHEST

def product(first_factor, second_factor):
    return jnp.matmul(first_factor, second_factor, precision=HIGHEST)

def layer_norm(values, norm_gain, norm_shift):
    center = values - lax.optimization_barrier(jnp.mean(values, axis=-1, keepdims=True))
    spread = lax.optimization_barrier(jnp.mean(center * center, axis=-1, keepdims=True))
    return center * lax.rsqrt(spread + 1e-05) * norm_gain + norm_shift

def attend(queries, key_rows, value_rows, segment, valid_keys):
    length = queries.shape[0]
    block_rows = min(512, length)
    heads_q = queries.reshape(length // block_rows, block_rows, HEADS, HEAD)
    heads_k = key_rows.reshape(length, HEADS, HEAD)
    heads_v = value_rows.reshape(length, HEADS, HEAD)
    key_pos = jnp.arange(length, dtype=jnp.int32)
    query_pos = key_pos.reshape(length // block_rows, block_rows)
    query_seg = segment.reshape(length // block_rows, block_rows)

    def one_block(pieces):
        query_blk, pos_blk, seg_blk = pieces
        scores = jnp.einsum('qhe,khe->hqk', query_blk, heads_k, precision=HIGHEST) * HEAD ** (-0.5)
        scores = low_back(scores)
        allowed = (seg_blk[:, None] == segment[None, :]) & ((valid_keys[None, :] > 0) | (pos_blk[:, None] == key_pos[None, :]))
        attention = jax.nn.softmax(jnp.where(allowed[None], scores, -1e+30), axis=-1)
        context = jnp.einsum('hqk,khe->qhe', low(attention), heads_v, precision=HIGHEST)
        return context.reshape(block_rows, HEADS * HEAD)
    result = lax.map(jax.checkpoint(one_block), (heads_q, query_pos, query_seg))
    return result.reshape(length, HEADS * HEAD)

def one_sequence(tokens, segment, valid_keys, params):
    qkv_weight, qv_bias, out_weight, norm_gains, row_biases, up_weight, up_bias, down_weight = params
    queries = low_back(low(product(tokens, qkv_weight[0]) + qv_bias[0]))
    key_rows = low_back(low(product(tokens, qkv_weight[1])))
    value_rows = low_back(low(product(tokens, qkv_weight[2]) + qv_bias[1]))
    context = low_back(low(attend(queries, key_rows, value_rows, segment, valid_keys)))
    mixed_rows = tokens + low_back(product(context, out_weight)) + row_biases[0]
    hidden = layer_norm(mixed_rows, norm_gains[0], row_biases[1])
    pre_act = low_back(product(low(hidden), up_weight) + up_bias)
    active = low(jax.nn.gelu(pre_act, approximate=False))
    summed = hidden + low_back(product(active, down_weight)) + row_biases[2]
    return layer_norm(summed, norm_gains[1], row_biases[3])

def reference(inputs, segment_ids, token_valid, qkv_weight, qv_bias, out_weight, norm_gains, row_biases, up_weight, up_bias, down_weight, out_grad):
    count_seq = MB * N_DP
    sequences = inputs.astype(jnp.float32).reshape(count_seq, LEN, D)
    segments = segment_ids.reshape(count_seq, LEN)
    valid_all = token_valid.reshape(count_seq, LEN)
    params = (qkv_weight.astype(jnp.float32), qv_bias.astype(jnp.float32), out_weight.astype(jnp.float32), norm_gains.astype(jnp.float32), row_biases.astype(jnp.float32), up_weight.astype(jnp.float32), up_bias.astype(jnp.float32), down_weight.astype(jnp.float32))
    seq_step = jax.checkpoint(one_sequence)

    def forward(sequences, params):
        return lax.map(lambda pieces: seq_step(pieces[0], pieces[1], pieces[2], params), (sequences, segments, valid_all))
    result, pullback = jax.vjp(forward, sequences, params)
    seq_grad, param_grads = pullback(out_grad.astype(jnp.float32).reshape(count_seq, LEN, D))
    qkv_grad, qv_grad, out_grad_w, gain_grad, bias_grad, up_grad_w, up_bias_grad, down_grad_w = param_grads
    return (result.astype(jnp.bfloat16).reshape(MB, N_DP * LEN, D), seq_grad.reshape(MB, N_DP * LEN, D), qkv_grad, qv_grad, out_grad_w, gain_grad, bias_grad, up_grad_w, up_bias_grad, down_grad_w)
```

```python
import functools
import math
import jax
import jax.numpy as jnp
from jax import lax
from jax.sharding import PartitionSpec as P
from jax.experimental import pallas as pl
from jax.experimental.pallas import tpu as pltpu

HEAD = 64
PAIR = 2 * HEAD
NEG_FILL = -1e30
F32 = jnp.float32
BF16 = jnp.bfloat16
NT = (((1,), (1,)), ((), ()))
NN = (((1,), (0,)), ((), ()))
TN = (((0,), (0,)), ((), ()))


def dot(a, b, dims=NN, precision=None):
    return lax.dot_general(a, b, dims, preferred_element_type=F32, precision=precision)


def head_lanes(rows, which):
    lane = lax.broadcasted_iota(jnp.int32, (rows, PAIR), 1)
    return (lane < HEAD) if which == 0 else (lane >= HEAD)


def attend_fwd_kernel(bk, lo_ref, hi_ref, pad_ref, q_ref, k_ref, v_ref, qcode_ref, kcode_ref, o_ref, lse_ref):
    i = pl.program_id(1)
    bq = q_ref.shape[0]
    q = q_ref[...] * jnp.asarray(0.125, BF16)
    heads = [jnp.where(head_lanes(bq, w), q, jnp.zeros_like(q)) for w in (0, 1)]
    qcode = jnp.tile(qcode_ref[...], (1, bk // 128))
    first = i * bq

    def run(diagonal):
        def step(t, carry):
            at = pl.multiple_of(t * bk, bk)
            k = k_ref[pl.ds(at, bk), :]
            v = v_ref[pl.ds(at, bk), :]
            mask = qcode == kcode_ref[:, pl.ds(at, bk)]
            if diagonal:
                gap = lax.broadcasted_iota(jnp.int32, (bq, bk), 1) - lax.broadcasted_iota(jnp.int32, (bq, bk), 0)
                mask = mask | (gap == first - at)
            out = []
            for h in (0, 1):
                top, total, acc = carry[3 * h : 3 * h + 3]
                s = jnp.where(mask, dot(heads[h], k, NT), NEG_FILL)
                new = jnp.maximum(top, jnp.max(s, axis=1, keepdims=True))
                p = jnp.exp(s - new)
                old = jnp.exp(top - new)
                out += [
                    new,
                    total * old + jnp.sum(p, axis=1, keepdims=True),
                    acc * old + dot(p.astype(BF16), v),
                ]
            return tuple(out)

        one = (jnp.full((bq, 1), NEG_FILL, F32), jnp.zeros((bq, 1), F32), jnp.zeros((bq, PAIR), F32))
        ma, la, aa, mb, lb, ab = lax.fori_loop(lo_ref[i], hi_ref[i], step, one + one)
        o_ref[...] = jnp.where(head_lanes(bq, 0), aa / la, ab / lb).astype(BF16)
        lane = lax.broadcasted_iota(jnp.int32, (bq, PAIR), 1)
        wide = jnp.where(lane == 0, ma + jnp.log(la), mb + jnp.log(lb))
        lse_ref[...] = wide.T[0:8, :]

    pl.when(pad_ref[i] > 0)(lambda: run(True))
    pl.when(pad_ref[i] == 0)(lambda: run(False))


def attend_bwd_kernel(
    bq, lo_ref, hi_ref, pad_ref, q_ref, k_ref, v_ref, c_ref, dc_ref, lse_ref, qcode_ref, kcode_ref,
    dq_ref, dk_ref, dv_ref, dq_acc, delta,
):
    i = pl.program_id(1)
    bk = k_ref.shape[0]
    first = i * bk

    @pl.when(i == 0)
    def _():
        dq_acc[...] = jnp.zeros_like(dq_acc)
        row = lax.broadcasted_iota(jnp.int32, (8, PAIR), 0)
        lane = lax.broadcasted_iota(jnp.int32, (8, PAIR), 1)
        pick = jnp.where(lane // HEAD == row, 1.0, 0.0).astype(F32)
        prod = dc_ref[...].astype(F32) * c_ref[...].astype(F32)
        delta[...] = dot(pick, prod, NT, lax.Precision.HIGHEST)

    k = k_ref[...] * jnp.asarray(0.125, BF16)
    v = v_ref[...]
    kh = [jnp.where(head_lanes(bk, w), k, jnp.zeros_like(k)) for w in (0, 1)]
    vh = [jnp.where(head_lanes(bk, w), v, jnp.zeros_like(v)) for w in (0, 1)]
    kcode = jnp.tile(kcode_ref[...], (1, bq // 128))

    def run(diagonal):
        def step(t, carry):
            dk, dv = carry
            at = pl.multiple_of(t * bq, bq)
            rows = pl.ds(at, bq)
            q = q_ref[rows, :]
            dc = dc_ref[rows, :]
            mask = kcode == qcode_ref[:, rows]
            if diagonal:
                gap = lax.broadcasted_iota(jnp.int32, (bk, bq), 1) - lax.broadcasted_iota(jnp.int32, (bk, bq), 0)
                mask = mask | (gap == first - at)
            dq = jnp.zeros((bq, PAIR), F32)
            for h in (0, 1):
                s = dot(kh[h], q, NT)
                p = jnp.exp(jnp.where(mask, s - lse_ref[h : h + 1, rows], NEG_FILL))
                dp = dot(vh[h], dc, NT)
                ds = (p * (dp - delta[h : h + 1, rows])).astype(BF16)
                own = head_lanes(bq, h)
                dv = dv + dot(p.astype(BF16), jnp.where(own, dc, jnp.zeros_like(dc)))
                dk = dk + dot(ds, jnp.where(own, q, jnp.zeros_like(q)))
                dq = dq + dot(ds, kh[h], TN)
            dq_acc[rows, :] += dq
            return dk, dv

        zero = jnp.zeros((bk, PAIR), F32)
        dk, dv = lax.fori_loop(lo_ref[i], hi_ref[i], step, (zero, zero))
        dk_ref[...] = (dk * 0.125).astype(BF16)
        dv_ref[...] = dv.astype(BF16)

    pl.when(pad_ref[i] > 0)(lambda: run(True))
    pl.when(pad_ref[i] == 0)(lambda: run(False))

    @pl.when(i == pl.num_programs(1) - 1)
    def _():
        dq_ref[...] = dq_acc[...].astype(BF16)


def block_bounds(segment, valid, block, other):
    length = segment.shape[0]
    blocks = segment.reshape(length // block, block)
    lo = jnp.sum((segment[None, :] < blocks[:, :1]).astype(jnp.int32), axis=1) // other
    hi = (jnp.sum((segment[None, :] <= blocks[:, -1:]).astype(jnp.int32), axis=1) + other - 1) // other
    pad = jnp.sum((valid.reshape(length // block, block) == 0).astype(jnp.int32), axis=1)
    return lo, hi, pad


def attention_codes(segment, valid):
    kcode = jnp.where(valid > 0, segment, -1)
    qcode = segment
    wide = lambda a: jnp.broadcast_to(a[:, None], (a.shape[0], 128))
    return qcode, kcode, wide(qcode), wide(kcode)


def attend_fwd(qkv, segment, valid, bq=256, bk=256):
    length, width = qkv.shape
    pairs = width // 3 // PAIR
    lo, hi, pad = block_bounds(segment, valid, bq, bk)
    qcode, kcode, qwide, kwide = attention_codes(segment, valid)
    return pl.pallas_call(
        functools.partial(attend_fwd_kernel, bk),
        grid_spec=pltpu.PrefetchScalarGridSpec(
            num_scalar_prefetch=3,
            grid=(pairs, length // bq),
            in_specs=[
                pl.BlockSpec((bq, PAIR), lambda h, i, *_: (i, h)),
                pl.BlockSpec((length, PAIR), lambda h, i, *_: (0, pairs + h)),
                pl.BlockSpec((length, PAIR), lambda h, i, *_: (0, 2 * pairs + h)),
                pl.BlockSpec((bq, 128), lambda h, i, *_: (i, 0)),
                pl.BlockSpec((1, length), lambda h, i, *_: (0, 0)),
            ],
            out_specs=[
                pl.BlockSpec((bq, PAIR), lambda h, i, *_: (i, h)),
                pl.BlockSpec((8, bq), lambda h, i, *_: (h, i)),
            ],
        ),
        out_shape=[
            jax.ShapeDtypeStruct((length, pairs * PAIR), BF16),
            jax.ShapeDtypeStruct((pairs * 8, length), F32),
        ],
        compiler_params=pltpu.CompilerParams(dimension_semantics=("arbitrary", "arbitrary")),
        cost_estimate=pl.CostEstimate(flops=8 * 2 * length * length * PAIR, bytes_accessed=8 * length * width, transcendentals=4 * length * length),
    )(lo, hi, pad, qkv, qkv, qkv, qwide, kcode[None, :])


def attend_bwd(qkv, context, context_grad, lse, segment, valid, bq=256, bk=256):
    length, width = qkv.shape
    pairs = width // 3 // PAIR
    lo, hi, pad = block_bounds(segment, valid, bk, bq)
    qcode, kcode, qwide, kwide = attention_codes(segment, valid)
    whole = lambda at: pl.BlockSpec((length, PAIR), lambda h, i, *_: (0, at * pairs + h))
    part = lambda at: pl.BlockSpec((bk, PAIR), lambda h, i, *_: (i, at * pairs + h))
    shape = jax.ShapeDtypeStruct((length, pairs * PAIR), BF16)
    return pl.pallas_call(
        functools.partial(attend_bwd_kernel, bq),
        grid_spec=pltpu.PrefetchScalarGridSpec(
            num_scalar_prefetch=3,
            grid=(pairs, length // bk),
            in_specs=[
                whole(0), part(1), part(2), whole(0), whole(0),
                pl.BlockSpec((8, length), lambda h, i, *_: (h, 0)),
                pl.BlockSpec((1, length), lambda h, i, *_: (0, 0)),
                pl.BlockSpec((bk, 128), lambda h, i, *_: (i, 0)),
            ],
            out_specs=[whole(0), part(0), part(0)],
            scratch_shapes=[pltpu.VMEM((length, PAIR), F32), pltpu.VMEM((8, length), F32)],
        ),
        out_shape=[shape, shape, shape],
        compiler_params=pltpu.CompilerParams(dimension_semantics=("arbitrary", "arbitrary")),
        cost_estimate=pl.CostEstimate(flops=20 * 2 * length * length * PAIR, bytes_accessed=16 * length * width, transcendentals=4 * length * length),
    )(lo, hi, pad, qkv, qkv, qkv, context, context_grad, lse, qcode[None, :], kwide)


def norm_stats(values):
    center = values - jnp.mean(values, axis=1, keepdims=True)
    inverse = lax.rsqrt(jnp.mean(center * center, axis=1, keepdims=True) + 1e-05)
    return center * inverse, inverse


def norm_pull(incoming, normed, inverse, gain):
    scaled = incoming * gain
    return inverse * (
        scaled - jnp.mean(scaled, axis=1, keepdims=True) - normed * jnp.mean(scaled * normed, axis=1, keepdims=True)
    )


def col_sum(values):
    return jnp.sum(values, axis=0, keepdims=True)


def add_sums(ref, parts):
    @pl.when(pl.program_id(0) == 0)
    def _():
        ref[...] = jnp.zeros_like(ref)

    for at, part in enumerate(parts):
        ref[at : at + 1, :] += col_sum(part)


def mix_kernel(x_ref, c_ref, w_ref, bias_ref, gain_ref, hl_ref, n_ref, r_ref):
    mixed = x_ref[...].astype(F32) + dot(c_ref[...], w_ref[...]) + bias_ref[0:1, :]
    normed, inverse = norm_stats(mixed)
    hl_ref[...] = (normed * gain_ref[0:1, :] + bias_ref[1:2, :]).astype(BF16)
    n_ref[...] = normed
    r_ref[...] = jnp.broadcast_to(inverse, r_ref.shape)


def up_kernel(h_ref, w_ref, bias_ref, g_ref, slope_ref):
    u = dot(h_ref[...], w_ref[...]) + bias_ref[...]
    cdf = 0.5 + 0.5 * lax.erf(u * (1.0 / math.sqrt(2.0)))
    g_ref[...] = (u * cdf).astype(BF16)
    slope_ref[...] = (cdf + u * (jnp.exp(-0.5 * u * u) * (1.0 / math.sqrt(2.0 * math.pi)))).astype(BF16)


def down_kernel(g_ref, w_ref, n_ref, e_ref, bias_ref, gain_ref, out_ref, dr_ref, dz_ref, sum_ref):
    hidden = n_ref[...] * gain_ref[0:1, :] + bias_ref[1:2, :]
    normed, inverse = norm_stats(hidden + dot(g_ref[...], w_ref[...]) + bias_ref[2:3, :])
    out_ref[...] = (normed * gain_ref[1:2, :] + bias_ref[3:4, :]).astype(BF16)
    e = e_ref[...].astype(F32)
    dr = norm_pull(e, normed, inverse, gain_ref[1:2, :])
    dr_ref[...] = dr
    dz_ref[...] = dr.astype(BF16)
    add_sums(sum_ref, (e * normed, dr, e))


def slope_kernel(dz_ref, w_ref, slope_ref, du_ref, sum_ref):
    du = (dot(dz_ref[...], w_ref[...], NT) * slope_ref[...].astype(F32)).astype(BF16)
    du_ref[...] = du

    @pl.when(pl.program_id(1) == 0)
    def _():
        sum_ref[...] = jnp.zeros_like(sum_ref)

    sum_ref[0:1, :] += col_sum(du.astype(F32))


def mix_pull_kernel(du_ref, w_ref, dr_ref, n_ref, r_ref, gain_ref, dm_ref, da_ref, sum_ref):
    dh = dr_ref[...] + dot(du_ref[...], w_ref[...], NT)
    normed = n_ref[...]
    dm = norm_pull(dh, normed, r_ref[:, 0:1], gain_ref[0:1, :])
    dm_ref[...] = dm
    da_ref[...] = dm.astype(BF16)
    add_sums(sum_ref, (dh * normed, dm, dh))


def call(kernel, grid, ins, outs, flops, nbytes, *args):
    return pl.pallas_call(
        kernel,
        grid=grid,
        in_specs=ins,
        out_specs=outs[0],
        out_shape=outs[1],
        compiler_params=pltpu.CompilerParams(dimension_semantics=("arbitrary",) * len(grid)),
        cost_estimate=pl.CostEstimate(flops=flops, bytes_accessed=nbytes, transcendentals=0),
    )(*args)


def rows(block, width):
    return pl.BlockSpec((block, width), lambda i: (i, 0))


def held(shape):
    return pl.BlockSpec(shape, lambda i: (0, 0))


def once(shape):
    return pl.BlockSpec(shape, lambda i: (0, 0), pipeline_mode=pl.Buffered(1))


def sds(shape, dtype=BF16):
    return jax.ShapeDtypeStruct(shape, dtype)


def mix(x, c, w, biases, gains, block=256):
    n, d = x.shape
    r = functools.partial(rows, block)
    return call(
        mix_kernel, (n // block,),
        [r(d), r(c.shape[1]), once(w.shape), held(biases.shape), held(gains.shape)],
        ([r(d), r(d), r(128)], [sds((n, d)), sds((n, d), F32), sds((n, 128), F32)]),
        2 * n * d * d, 12 * n * d, x, c, w, biases, gains,
    )


def up(h, w, bias, block=256, cols=1024):
    n, d = h.shape
    f = w.shape[1]
    cols = min(cols, f)
    tile = pl.BlockSpec((block, cols), lambda j, i: (i, j))
    return call(
        up_kernel, (f // cols, n // block),
        [pl.BlockSpec((block, d), lambda j, i: (i, 0)), pl.BlockSpec((d, cols), lambda j, i: (0, j)), pl.BlockSpec((1, cols), lambda j, i: (0, j))],
        ([tile, tile], [sds((n, f)), sds((n, f))]),
        2 * n * d * f, 4 * n * f + 2 * d * f, h, w, bias,
    )


def down(g, w, normed, e, biases, gains, block=256):
    n, f = g.shape
    d = w.shape[1]
    r = functools.partial(rows, block)
    return call(
        down_kernel, (n // block,),
        [r(f), once(w.shape), r(d), r(d), held(biases.shape), held(gains.shape)],
        ([r(d), r(d), r(d), held((8, d))], [sds((n, d)), sds((n, d), F32), sds((n, d)), sds((8, d), F32)]),
        2 * n * d * f, 2 * n * f + 2 * d * f, g, w, normed, e, biases, gains,
    )


def slope_pull(dz, w, slope, block=256, cols=1024):
    n, d = dz.shape
    f = w.shape[0]
    tile = pl.BlockSpec((block, cols), lambda j, i: (i, j))
    return call(
        slope_kernel, (f // cols, n // block),
        [pl.BlockSpec((block, d), lambda j, i: (i, 0)), pl.BlockSpec((cols, d), lambda j, i: (j, 0)), tile],
        ([tile, pl.BlockSpec((8, cols), lambda j, i: (0, j))], [sds((n, f)), sds((8, f), F32)]),
        2 * n * d * f, 4 * n * f + 2 * d * f, dz, w, slope,
    )


def mix_pull(du, w, dr, normed, inverse, gains, block=256):
    n, f = du.shape
    d = w.shape[0]
    r = functools.partial(rows, block)
    return call(
        mix_pull_kernel, (n // block,),
        [r(f), once(w.shape), r(d), r(d), r(128), held(gains.shape)],
        ([r(d), r(d), held((8, d))], [sds((n, d), F32), sds((n, d)), sds((8, d), F32)]),
        2 * n * d * f, 2 * n * f + 2 * d * f, du, w, dr, normed, inverse, gains,
    )


def swap_cores(value):
    return lax.ppermute(value, "core", [(0, 1), (1, 0)])


def column_routes(tensor_size):
    first, second = [], []
    for core in range(2):
        for t in range(tensor_size):
            at = core * tensor_size + t
            first.append((at, (t >> 1) * tensor_size + 2 * core + (t & 1)))
            second.append((at, (t >> 1) * tensor_size + 2 * core + 1 - (t & 1)))
    return first, second


def back(route):
    return [(b, a) for a, b in route]


def by_core(core, mine, other, axis):
    return jnp.where(
        core == 0, jnp.concatenate([mine, other], axis=axis), jnp.concatenate([other, mine], axis=axis)
    )


def body(
    inputs, segment_ids, token_valid, qkv_weight, qv_bias, out_weight, norm_gains, row_biases,
    up_weight, up_bias, down_weight, out_grad,
):
    COL = ("core", "tensor")
    ALL = ("p", "core", "tensor")
    core, tensor = lax.axis_index("core"), lax.axis_index("tensor")
    n_p, n_t = lax.axis_size("p"), lax.axis_size("tensor")
    n_dp = 2 * n_p
    micro, held_rows, width = inputs.shape
    assert micro == 2 and n_t == 4
    odd = tensor & 1
    route_a, route_b = column_routes(n_t)

    def bring(value):
        a = lax.ppermute(value[odd], COL, route_a)
        b = lax.ppermute(value[1 - odd], COL, route_b)
        return jnp.where(odd == 0, jnp.concatenate([a, b]), jnp.concatenate([b, a]))

    def give(value):
        a = lax.ppermute(lax.dynamic_slice_in_dim(value, odd * held_rows, held_rows), COL, back(route_a))
        b = lax.ppermute(lax.dynamic_slice_in_dim(value, (1 - odd) * held_rows, held_rows), COL, back(route_b))
        return jnp.where(odd == 0, jnp.stack([a, b]), jnp.stack([b, a]))

    def gathered(weight):
        got = lax.all_gather(weight, ALL, axis=0, tiled=False)
        return got.reshape((n_dp, n_t) + weight.shape)

    x_own = bring(inputs)
    rows = x_own.shape[0]
    labels = jnp.stack([segment_ids[:, 0], token_valid[:, 0]], axis=1)[odd]
    labels = jnp.where((tensor >> 1) == core, labels, swap_cores(labels))
    segment, valid = labels[0], labels[1]

    bias_all = lax.all_gather(jnp.concatenate([qv_bias.reshape(-1), up_bias]), "tensor")
    n_qv = qv_bias.size
    qv_all = bias_all[:, :n_qv].reshape(n_t, 2, -1).transpose(1, 0, 2).reshape(2, -1)
    up_bias_all = bias_all[:, n_qv:].reshape(1, -1)

    w_qkv = gathered(qkv_weight)
    w_qkv = lax.dynamic_slice_in_dim(w_qkv, 2 * core, 2, 1)
    w_qkv = w_qkv.transpose(0, 3, 2, 1, 4).reshape(width, -1)
    own = w_qkv.shape[1] // 3
    w_out = gathered(out_weight).transpose(1, 2, 0, 3).reshape(-1, width)
    w_up = gathered(up_weight).transpose(0, 2, 1, 3).reshape(width, -1)
    w_down = gathered(down_weight).transpose(1, 2, 0, 3).reshape(-1, width)

    x_full = by_core(core, x_own, swap_cores(x_own), 0)
    qv_own = lax.dynamic_slice_in_dim(qv_all, core * own, own, 1)
    bias = jnp.concatenate([qv_own[0], jnp.zeros_like(qv_own[0]), qv_own[1]])
    qkv = (jnp.dot(x_full, w_qkv, preferred_element_type=F32) + bias).astype(BF16)
    context, lse = attend_fwd(qkv, segment, valid, 512, 512)
    mine = lax.dynamic_slice_in_dim(context, core * rows, rows)
    other = lax.dynamic_slice_in_dim(context, (1 - core) * rows, rows)
    c_own = by_core(core, mine, swap_cores(other), 1)
    hl, normed, inverse = mix(x_own, c_own, w_out, row_biases, norm_gains)
    active, slope = up(hl, w_up, up_bias_all)
    grad_own = bring(out_grad)
    layer, dr, dz, sums_two = down(active, w_down, normed, grad_own, row_biases, norm_gains)
    layer_out = give(layer)

    du, up_sum = slope_pull(dz, w_down, slope)
    dm, da, sums_one = mix_pull(du, w_up, dr, normed, inverse, norm_gains)
    g_down = dot(active, dz, TN).astype(BF16)
    g_up = dot(hl, du, TN).astype(BF16)
    g_out = dot(c_own, da, TN).astype(BF16)
    dc = dot(da, w_out, NT).astype(BF16)
    mine = lax.dynamic_slice_in_dim(dc, core * own, own, 1)
    other = lax.dynamic_slice_in_dim(dc, (1 - core) * own, own, 1)
    dc_full = by_core(core, mine, swap_cores(other), 0)
    dq, dk, dv = attend_bwd(qkv, context, dc_full, lse, segment, valid, 256, 512)
    dqkv = jnp.concatenate([dq, dk, dv], axis=1)
    g_qkv = dot(x_full, dqkv, TN).astype(BF16)
    qv_sum = jnp.stack([jnp.sum(dq.astype(F32), axis=0), jnp.sum(dv.astype(F32), axis=0)])
    dx = dot(dqkv, w_qkv, NT)
    mine = lax.dynamic_slice_in_dim(dx, core * rows, rows)
    other = lax.dynamic_slice_in_dim(dx, (1 - core) * rows, rows).astype(BF16)
    dx_own = mine + swap_cores(other).astype(F32) + dm
    input_grad = give(dx_own.astype(BF16)).astype(F32)

    def owner_sum(parts, join):
        keep = lax.dynamic_index_in_dim(parts, core, 1, keepdims=False)
        send = lax.dynamic_index_in_dim(parts, 1 - core, 1, keepdims=False)
        both = join(keep, swap_cores(send))
        some = lax.psum_scatter(both, "p", scatter_dimension=0, tiled=False)
        return lax.psum_scatter(some, "tensor", scatter_dimension=0, tiled=False).astype(F32)

    plus = lambda a, b: (a.astype(F32) + b.astype(F32)).astype(BF16)
    beside = lambda a, b: by_core(core, a, b, 1)
    down_total = owner_sum(g_down.reshape(n_t, -1, n_p, 2, down_weight.shape[1]).transpose(2, 3, 0, 1, 4), plus)
    up_total = owner_sum(g_up.reshape(n_p, 2, -1, n_t, up_weight.shape[1]).transpose(0, 1, 3, 2, 4), plus)
    out_total = owner_sum(g_out.reshape(n_t, -1, n_p, 2, out_weight.shape[1]).transpose(2, 3, 0, 1, 4), plus)
    qkv_total = owner_sum(
        g_qkv.reshape(n_p, 2, -1, 3, 2, qkv_weight.shape[2]).transpose(0, 1, 4, 3, 2, 5), beside
    )

    qv_pad = lax.dynamic_update_slice(jnp.zeros((2, width), F32), qv_sum, (0, core * own))
    small = jnp.concatenate(
        [
            jnp.stack([sums_one[0], sums_two[0], sums_one[1], sums_one[2], sums_two[1], sums_two[2]]).reshape(-1),
            qv_pad.reshape(-1),
            up_sum[0],
        ]
    )
    small = lax.psum(small, ALL)
    gain_sum = small[: 2 * width].reshape(2, width)
    bias_sum = small[2 * width : 6 * width].reshape(4, width)
    qv_total = lax.dynamic_slice_in_dim(small[6 * width : 8 * width].reshape(2, width), tensor * qv_bias.shape[1], qv_bias.shape[1], 1)
    up_bias_total = lax.dynamic_slice_in_dim(small[8 * width :], tensor * up_bias.shape[0], up_bias.shape[0])
    return (
        layer_out, input_grad, qkv_total, qv_total, out_total, gain_sum, bias_sum, up_total, up_bias_total, down_total,
    )


def solution(mesh):
    dp, tensor = mesh.devices.shape
    split = jax.sharding.Mesh(mesh.devices.reshape(dp // 2, 2, tensor), ("p", "core", "tensor"))
    pc = ("p", "core")
    tokens = P(None, ("p", "core", "tensor"), None)
    return jax.shard_map(
        body,
        mesh=split,
        in_specs=(
            tokens, P(None, pc, None), P(None, pc, None), P(None, pc, "tensor"), P(None, "tensor"), P("tensor", pc),
            P(), P(), P(pc, "tensor"), P("tensor"), P("tensor", pc), tokens,
        ),
        out_specs=(
            tokens, tokens, P(None, pc, "tensor"), P(None, "tensor"), P("tensor", pc), P(), P(), P(pc, "tensor"),
            P("tensor"), P("tensor", pc),
        ),
        check_vma=False,
    )
```

```python
import functools
import math
import jax
import jax.numpy as jnp
from jax import lax
from jax.sharding import PartitionSpec as P
from jax.experimental import pallas as pl
from jax.experimental.pallas import tpu as pltpu

HEAD = 64
PAIR = 2 * HEAD
NEG_FILL = -1e30
F32 = jnp.float32
BF16 = jnp.bfloat16
NT = (((1,), (1,)), ((), ()))
NN = (((1,), (0,)), ((), ()))
TN = (((0,), (0,)), ((), ()))


def dot(a, b, dims=NN, precision=None):
    return lax.dot_general(a, b, dims, preferred_element_type=F32, precision=precision)


def head_lanes(rows, which):
    lane = lax.broadcasted_iota(jnp.int32, (rows, PAIR), 1)
    return (lane < HEAD) if which == 0 else (lane >= HEAD)


def attend_fwd_kernel(bk, lo_ref, hi_ref, pad_ref, q_ref, k_ref, v_ref, qcode_ref, kcode_ref, o_ref, lse_ref):
    i = pl.program_id(1)
    bq = q_ref.shape[0]
    q = q_ref[...] * jnp.asarray(0.125, BF16)
    heads = [jnp.where(head_lanes(bq, w), q, jnp.zeros_like(q)) for w in (0, 1)]
    qcode = jnp.tile(qcode_ref[...], (1, bk // 128))
    first = i * bq

    def run(diagonal):
        def step(t, carry):
            at = pl.multiple_of(t * bk, bk)
            k = k_ref[pl.ds(at, bk), :]
            v = v_ref[pl.ds(at, bk), :]
            mask = qcode == kcode_ref[:, pl.ds(at, bk)]
            if diagonal:
                gap = lax.broadcasted_iota(jnp.int32, (bq, bk), 1) - lax.broadcasted_iota(jnp.int32, (bq, bk), 0)
                mask = mask | (gap == first - at)
            out = []
            for h in (0, 1):
                top, total, acc = carry[3 * h : 3 * h + 3]
                s = jnp.where(mask, dot(heads[h], k, NT), NEG_FILL)
                new = jnp.maximum(top, jnp.max(s, axis=1, keepdims=True))
                p = jnp.exp(s - new)
                old = jnp.exp(top - new)
                out += [
                    new,
                    total * old + jnp.sum(p, axis=1, keepdims=True),
                    acc * old + dot(p.astype(BF16), v),
                ]
            return tuple(out)

        one = (jnp.full((bq, 1), NEG_FILL, F32), jnp.zeros((bq, 1), F32), jnp.zeros((bq, PAIR), F32))
        ma, la, aa, mb, lb, ab = lax.fori_loop(lo_ref[i], hi_ref[i], step, one + one)
        o_ref[...] = jnp.where(head_lanes(bq, 0), aa / la, ab / lb).astype(BF16)
        lane = lax.broadcasted_iota(jnp.int32, (bq, PAIR), 1)
        wide = jnp.where(lane == 0, ma + jnp.log(la), mb + jnp.log(lb))
        lse_ref[...] = wide.T[0:8, :]

    pl.when(pad_ref[i] > 0)(lambda: run(True))
    pl.when(pad_ref[i] == 0)(lambda: run(False))


def attend_bwd_kernel(
    bq, lo_ref, hi_ref, pad_ref, q_ref, k_ref, v_ref, c_ref, dc_ref, lse_ref, qcode_ref, kcode_ref,
    dq_ref, dk_ref, dv_ref, dq_acc, delta,
):
    i = pl.program_id(1)
    bk = k_ref.shape[0]
    first = i * bk

    @pl.when(i == 0)
    def _():
        dq_acc[...] = jnp.zeros_like(dq_acc)
        row = lax.broadcasted_iota(jnp.int32, (8, PAIR), 0)
        lane = lax.broadcasted_iota(jnp.int32, (8, PAIR), 1)
        pick = jnp.where(lane // HEAD == row, 1.0, 0.0).astype(F32)
        prod = dc_ref[...].astype(F32) * c_ref[...].astype(F32)
        delta[...] = dot(pick, prod, NT, lax.Precision.HIGHEST)

    k = k_ref[...] * jnp.asarray(0.125, BF16)
    v = v_ref[...]
    kh = [jnp.where(head_lanes(bk, w), k, jnp.zeros_like(k)) for w in (0, 1)]
    vh = [jnp.where(head_lanes(bk, w), v, jnp.zeros_like(v)) for w in (0, 1)]
    kcode = jnp.tile(kcode_ref[...], (1, bq // 128))

    def run(diagonal):
        def step(t, carry):
            dk, dv = carry
            at = pl.multiple_of(t * bq, bq)
            rows = pl.ds(at, bq)
            q = q_ref[rows, :]
            dc = dc_ref[rows, :]
            mask = kcode == qcode_ref[:, rows]
            if diagonal:
                gap = lax.broadcasted_iota(jnp.int32, (bk, bq), 1) - lax.broadcasted_iota(jnp.int32, (bk, bq), 0)
                mask = mask | (gap == first - at)
            dq = jnp.zeros((bq, PAIR), F32)
            for h in (0, 1):
                s = dot(kh[h], q, NT)
                p = jnp.exp(jnp.where(mask, s - lse_ref[h : h + 1, rows], NEG_FILL))
                dp = dot(vh[h], dc, NT)
                ds = (p * (dp - delta[h : h + 1, rows])).astype(BF16)
                own = head_lanes(bq, h)
                dv = dv + dot(p.astype(BF16), jnp.where(own, dc, jnp.zeros_like(dc)))
                dk = dk + dot(ds, jnp.where(own, q, jnp.zeros_like(q)))
                dq = dq + dot(ds, kh[h], TN)
            dq_acc[rows, :] += dq
            return dk, dv

        zero = jnp.zeros((bk, PAIR), F32)
        dk, dv = lax.fori_loop(lo_ref[i], hi_ref[i], step, (zero, zero))
        dk_ref[...] = (dk * 0.125).astype(BF16)
        dv_ref[...] = dv.astype(BF16)

    pl.when(pad_ref[i] > 0)(lambda: run(True))
    pl.when(pad_ref[i] == 0)(lambda: run(False))

    @pl.when(i == pl.num_programs(1) - 1)
    def _():
        dq_ref[...] = dq_acc[...].astype(BF16)


def block_bounds(segment, valid, block, other):
    length = segment.shape[0]
    blocks = segment.reshape(length // block, block)
    lo = jnp.sum((segment[None, :] < blocks[:, :1]).astype(jnp.int32), axis=1) // other
    hi = (jnp.sum((segment[None, :] <= blocks[:, -1:]).astype(jnp.int32), axis=1) + other - 1) // other
    pad = jnp.sum((valid.reshape(length // block, block) == 0).astype(jnp.int32), axis=1)
    return lo, hi, pad


def attention_codes(segment, valid):
    kcode = jnp.where(valid > 0, segment, -1)
    qcode = segment
    wide = lambda a: jnp.broadcast_to(a[:, None], (a.shape[0], 128))
    return qcode, kcode, wide(qcode), wide(kcode)


def attend_fwd(qkv, segment, valid, bq=256, bk=256):
    length, width = qkv.shape
    pairs = width // 3 // PAIR
    lo, hi, pad = block_bounds(segment, valid, bq, bk)
    qcode, kcode, qwide, kwide = attention_codes(segment, valid)
    return pl.pallas_call(
        functools.partial(attend_fwd_kernel, bk),
        grid_spec=pltpu.PrefetchScalarGridSpec(
            num_scalar_prefetch=3,
            grid=(pairs, length // bq),
            in_specs=[
                pl.BlockSpec((bq, PAIR), lambda h, i, *_: (i, h)),
                pl.BlockSpec((length, PAIR), lambda h, i, *_: (0, pairs + h)),
                pl.BlockSpec((length, PAIR), lambda h, i, *_: (0, 2 * pairs + h)),
                pl.BlockSpec((bq, 128), lambda h, i, *_: (i, 0)),
                pl.BlockSpec((1, length), lambda h, i, *_: (0, 0)),
            ],
            out_specs=[
                pl.BlockSpec((bq, PAIR), lambda h, i, *_: (i, h)),
                pl.BlockSpec((8, bq), lambda h, i, *_: (h, i)),
            ],
        ),
        out_shape=[
            jax.ShapeDtypeStruct((length, pairs * PAIR), BF16),
            jax.ShapeDtypeStruct((pairs * 8, length), F32),
        ],
        compiler_params=pltpu.CompilerParams(dimension_semantics=("arbitrary", "arbitrary")),
        cost_estimate=pl.CostEstimate(flops=8 * 2 * length * length * PAIR, bytes_accessed=8 * length * width, transcendentals=4 * length * length),
    )(lo, hi, pad, qkv, qkv, qkv, qwide, kcode[None, :])


def attend_bwd(qkv, context, context_grad, lse, segment, valid, bq=256, bk=256):
    length, width = qkv.shape
    pairs = width // 3 // PAIR
    lo, hi, pad = block_bounds(segment, valid, bk, bq)
    qcode, kcode, qwide, kwide = attention_codes(segment, valid)
    whole = lambda at: pl.BlockSpec((length, PAIR), lambda h, i, *_: (0, at * pairs + h))
    part = lambda at: pl.BlockSpec((bk, PAIR), lambda h, i, *_: (i, at * pairs + h))
    shape = jax.ShapeDtypeStruct((length, pairs * PAIR), BF16)
    return pl.pallas_call(
        functools.partial(attend_bwd_kernel, bq),
        grid_spec=pltpu.PrefetchScalarGridSpec(
            num_scalar_prefetch=3,
            grid=(pairs, length // bk),
            in_specs=[
                whole(0), part(1), part(2), whole(0), whole(0),
                pl.BlockSpec((8, length), lambda h, i, *_: (h, 0)),
                pl.BlockSpec((1, length), lambda h, i, *_: (0, 0)),
                pl.BlockSpec((bk, 128), lambda h, i, *_: (i, 0)),
            ],
            out_specs=[whole(0), part(0), part(0)],
            scratch_shapes=[pltpu.VMEM((length, PAIR), F32), pltpu.VMEM((8, length), F32)],
        ),
        out_shape=[shape, shape, shape],
        compiler_params=pltpu.CompilerParams(dimension_semantics=("arbitrary", "arbitrary")),
        cost_estimate=pl.CostEstimate(flops=20 * 2 * length * length * PAIR, bytes_accessed=16 * length * width, transcendentals=4 * length * length),
    )(lo, hi, pad, qkv, qkv, qkv, context, context_grad, lse, qcode[None, :], kwide)


def norm_stats(values):
    center = values - jnp.mean(values, axis=1, keepdims=True)
    inverse = lax.rsqrt(jnp.mean(center * center, axis=1, keepdims=True) + 1e-05)
    return center * inverse, inverse


def norm_pull(incoming, normed, inverse, gain):
    scaled = incoming * gain
    return inverse * (
        scaled - jnp.mean(scaled, axis=1, keepdims=True) - normed * jnp.mean(scaled * normed, axis=1, keepdims=True)
    )


def col_sum(values):
    return jnp.sum(values, axis=0, keepdims=True)


def add_sums(ref, parts):
    @pl.when(pl.program_id(0) == 0)
    def _():
        ref[...] = jnp.zeros_like(ref)

    for at, part in enumerate(parts):
        ref[at : at + 1, :] += col_sum(part)


def mix_kernel(x_ref, c_ref, w_ref, bias_ref, gain_ref, hl_ref, n_ref, r_ref):
    mixed = x_ref[...].astype(F32) + dot(c_ref[...], w_ref[...]) + bias_ref[0:1, :]
    normed, inverse = norm_stats(mixed)
    hl_ref[...] = (normed * gain_ref[0:1, :] + bias_ref[1:2, :]).astype(BF16)
    n_ref[...] = normed
    r_ref[...] = jnp.broadcast_to(inverse, r_ref.shape)


def up_kernel(h_ref, w_ref, bias_ref, g_ref, slope_ref):
    u = dot(h_ref[...], w_ref[...]) + bias_ref[...]
    cdf = 0.5 + 0.5 * lax.erf(u * (1.0 / math.sqrt(2.0)))
    g_ref[...] = (u * cdf).astype(BF16)
    slope_ref[...] = (cdf + u * (jnp.exp(-0.5 * u * u) * (1.0 / math.sqrt(2.0 * math.pi)))).astype(BF16)


def down_kernel(g_ref, w_ref, n_ref, e_ref, bias_ref, gain_ref, out_ref, dr_ref, dz_ref, sum_ref):
    hidden = n_ref[...] * gain_ref[0:1, :] + bias_ref[1:2, :]
    normed, inverse = norm_stats(hidden + dot(g_ref[...], w_ref[...]) + bias_ref[2:3, :])
    out_ref[...] = (normed * gain_ref[1:2, :] + bias_ref[3:4, :]).astype(BF16)
    e = e_ref[...].astype(F32)
    dr = norm_pull(e, normed, inverse, gain_ref[1:2, :])
    dr_ref[...] = dr
    dz_ref[...] = dr.astype(BF16)
    add_sums(sum_ref, (e * normed, dr, e))


def slope_kernel(dz_ref, w_ref, slope_ref, du_ref, sum_ref):
    du = (dot(dz_ref[...], w_ref[...], NT) * slope_ref[...].astype(F32)).astype(BF16)
    du_ref[...] = du

    @pl.when(pl.program_id(1) == 0)
    def _():
        sum_ref[...] = jnp.zeros_like(sum_ref)

    sum_ref[0:1, :] += col_sum(du.astype(F32))


def mix_pull_kernel(du_ref, w_ref, dr_ref, n_ref, r_ref, gain_ref, dm_ref, da_ref, sum_ref):
    dh = dr_ref[...] + dot(du_ref[...], w_ref[...], NT)
    normed = n_ref[...]
    dm = norm_pull(dh, normed, r_ref[:, 0:1], gain_ref[0:1, :])
    dm_ref[...] = dm
    da_ref[...] = dm.astype(BF16)
    add_sums(sum_ref, (dh * normed, dm, dh))


def call(kernel, grid, ins, outs, flops, nbytes, *args):
    return pl.pallas_call(
        kernel,
        grid=grid,
        in_specs=ins,
        out_specs=outs[0],
        out_shape=outs[1],
        compiler_params=pltpu.CompilerParams(dimension_semantics=("arbitrary",) * len(grid)),
        cost_estimate=pl.CostEstimate(flops=flops, bytes_accessed=nbytes, transcendentals=0),
    )(*args)


def rows(block, width):
    return pl.BlockSpec((block, width), lambda i: (i, 0))


def held(shape):
    return pl.BlockSpec(shape, lambda i: (0, 0))


def once(shape):
    return pl.BlockSpec(shape, lambda i: (0, 0), pipeline_mode=pl.Buffered(1))


def sds(shape, dtype=BF16):
    return jax.ShapeDtypeStruct(shape, dtype)


def mix(x, c, w, biases, gains, block=256):
    n, d = x.shape
    r = functools.partial(rows, block)
    return call(
        mix_kernel, (n // block,),
        [r(d), r(c.shape[1]), once(w.shape), held(biases.shape), held(gains.shape)],
        ([r(d), r(d), r(128)], [sds((n, d)), sds((n, d), F32), sds((n, 128), F32)]),
        2 * n * d * d, 12 * n * d, x, c, w, biases, gains,
    )


def up(h, w, bias, block=256, cols=1024):
    n, d = h.shape
    f = w.shape[1]
    cols = min(cols, f)
    tile = pl.BlockSpec((block, cols), lambda j, i: (i, j))
    return call(
        up_kernel, (f // cols, n // block),
        [pl.BlockSpec((block, d), lambda j, i: (i, 0)), pl.BlockSpec((d, cols), lambda j, i: (0, j)), pl.BlockSpec((1, cols), lambda j, i: (0, j))],
        ([tile, tile], [sds((n, f)), sds((n, f))]),
        2 * n * d * f, 4 * n * f + 2 * d * f, h, w, bias,
    )


def down(g, w, normed, e, biases, gains, block=256):
    n, f = g.shape
    d = w.shape[1]
    r = functools.partial(rows, block)
    return call(
        down_kernel, (n // block,),
        [r(f), once(w.shape), r(d), r(d), held(biases.shape), held(gains.shape)],
        ([r(d), r(d), r(d), held((8, d))], [sds((n, d)), sds((n, d), F32), sds((n, d)), sds((8, d), F32)]),
        2 * n * d * f, 2 * n * f + 2 * d * f, g, w, normed, e, biases, gains,
    )


def slope_pull(dz, w, slope, block=256, cols=1024):
    n, d = dz.shape
    f = w.shape[0]
    tile = pl.BlockSpec((block, cols), lambda j, i: (i, j))
    return call(
        slope_kernel, (f // cols, n // block),
        [pl.BlockSpec((block, d), lambda j, i: (i, 0)), pl.BlockSpec((cols, d), lambda j, i: (j, 0)), tile],
        ([tile, pl.BlockSpec((8, cols), lambda j, i: (0, j))], [sds((n, f)), sds((8, f), F32)]),
        2 * n * d * f, 4 * n * f + 2 * d * f, dz, w, slope,
    )


def mix_pull(du, w, dr, normed, inverse, gains, block=256):
    n, f = du.shape
    d = w.shape[0]
    r = functools.partial(rows, block)
    return call(
        mix_pull_kernel, (n // block,),
        [r(f), once(w.shape), r(d), r(d), r(128), held(gains.shape)],
        ([r(d), r(d), held((8, d))], [sds((n, d), F32), sds((n, d)), sds((8, d), F32)]),
        2 * n * d * f, 2 * n * f + 2 * d * f, du, w, dr, normed, inverse, gains,
    )


def split_columns(acc, keep_ref, send_ref):
    n_p, c = keep_ref.shape[0], keep_ref.shape[3]
    for bit in (0, 1):

        @pl.when(lax.axis_index("core") == bit)
        def _():
            for p in range(n_p):
                at, to = (2 * p + bit) * c, (2 * p + 1 - bit) * c
                keep_ref[p, 0] = acc[:, at : at + c]
                send_ref[p, 0] = acc[:, to : to + c]


def split_rows(acc, place, keep_ref, send_ref):
    n_p, r = keep_ref.shape[0], keep_ref.shape[-2]
    for bit in (0, 1):

        @pl.when(lax.axis_index("core") == bit)
        def _():
            for p in range(n_p):
                at, to = (2 * p + bit) * r, (2 * p + 1 - bit) * r
                for cb in range(acc.shape[1] // 128):
                    keep_ref[(p, 0) + place + (cb,)] = acc[at : at + r, cb * 128 : cb * 128 + 128]
                    send_ref[(p, 0) + place + (cb,)] = acc[to : to + r, cb * 128 : cb * 128 + 128]


def col_grad_kernel(a_ref, b_ref, keep_ref, send_ref, acc):
    acc[...] = dot(a_ref[...], b_ref[...], TN).astype(BF16)
    split_columns(acc, keep_ref, send_ref)


def row_grad_kernel(a_ref, b_ref, keep_ref, send_ref, turned, acc):
    @pl.when(pl.program_id(0) == 0)
    def _():
        turned[...] = a_ref[...].T

    acc[...] = dot(turned[...], b_ref[...]).astype(BF16)
    split_rows(acc, (), keep_ref, send_ref)


def qkv_grad_kernel(x_ref, dq_ref, dk_ref, dv_ref, keep_ref, send_ref, sum_ref, turned, acc):
    @pl.when(pl.program_id(0) == 0)
    def _():
        turned[...] = x_ref[...].T

    for at, ref in enumerate((dq_ref, dk_ref, dv_ref)):
        acc[...] = dot(turned[...], ref[...]).astype(BF16)
        split_rows(acc, (at,), keep_ref, send_ref)
    sum_ref[0:1, :] = col_sum(dq_ref[...].astype(F32))
    sum_ref[1:2, :] = col_sum(dv_ref[...].astype(F32))


def grad_call(kernel, grid, ins, outs, scratch, flops, *args):
    return pl.pallas_call(
        kernel,
        grid=grid,
        in_specs=ins,
        out_specs=outs[0],
        out_shape=outs[1],
        scratch_shapes=scratch,
        compiler_params=pltpu.CompilerParams(dimension_semantics=("arbitrary",) * len(grid)),
        cost_estimate=pl.CostEstimate(flops=flops, bytes_accessed=flops // 512, transcendentals=0),
    )(*args)


def col_grad(a, b, n_p, n_t, block=512):
    n, f = a.shape
    d = b.shape[1]
    per_t, c = f // n_t, d // (2 * n_p)
    block = min(block, per_t)
    steps = per_t // block
    spec = pl.BlockSpec((n_p, 1, block, c), lambda i: (0, i // steps, i % steps, 0))
    shape = sds((n_p, n_t, per_t, c))
    return grad_call(
        col_grad_kernel, (f // block,),
        [pl.BlockSpec((n, block), lambda i: (0, i)), once((n, d))],
        ([spec, spec], [shape, shape]), [pltpu.VMEM((block, d), BF16)], 2 * n * f * d, a, b,
    )


def row_grad(a, b, n_p, n_t, block=512):
    n, d = a.shape
    f = b.shape[1]
    per_t, r = f // n_t, d // (2 * n_p)
    steps = per_t // block
    spec = pl.BlockSpec((n_p, 1, block // 128, r, 128), lambda i: (0, i // steps, i % steps, 0, 0))
    shape = sds((n_p, n_t, per_t // 128, r, 128))
    return grad_call(
        row_grad_kernel, (f // block,),
        [once((n, d)), pl.BlockSpec((n, block), lambda i: (0, i))],
        ([spec, spec], [shape, shape]),
        [pltpu.VMEM((d, n), BF16), pltpu.VMEM((d, block), BF16)], 2 * n * f * d, a, b,
    )


def qkv_grad(x, dq, dk, dv, n_p, n_t):
    n, d = x.shape
    f = dq.shape[1]
    half, r = f // (n_t // 2), d // (2 * n_p)
    spec = pl.BlockSpec((n_p, 1, 3, half // 128, r, 128), lambda i: (0, i, 0, 0, 0, 0))
    shape = sds((n_p, n_t // 2, 3, half // 128, r, 128))
    cols = pl.BlockSpec((n, half), lambda i: (0, i))
    return grad_call(
        qkv_grad_kernel, (n_t // 2,),
        [once((n, d)), cols, cols, cols],
        ([spec, spec, pl.BlockSpec((8, half), lambda i: (0, i))], [shape, shape, sds((8, f), F32)]),
        [pltpu.VMEM((d, n), BF16), pltpu.VMEM((d, half), BF16)], 6 * n * f * d, x, dq, dk, dv,
    )


def input_pull_kernel(core_ref, dq_ref, dk_ref, dv_ref, w_ref, *refs):
    f = dq_ref.shape[1]
    total = dot(dq_ref[...], w_ref[:, :f], NT)
    total = total + dot(dk_ref[...], w_ref[:, f : 2 * f], NT)
    total = total + dot(dv_ref[...], w_ref[:, 2 * f :], NT)
    if len(refs) == 2:
        total = total + refs[0][...]
    refs[-1][...] = total.astype(refs[-1].dtype)


def input_pull(part, dq, dk, dv, w, dm=None, block=256):
    n, f = dq.shape
    d = w.shape[0]
    steps = n // 2 // block
    cols = pl.BlockSpec((block, f), lambda i, at: (at[0] * steps + i, 0))
    own = pl.BlockSpec((block, d), lambda i, at: (i, 0))
    extra = [] if dm is None else [dm]
    return pl.pallas_call(
        input_pull_kernel,
        grid_spec=pltpu.PrefetchScalarGridSpec(
            num_scalar_prefetch=1,
            grid=(steps,),
            in_specs=[cols, cols, cols, pl.BlockSpec(w.shape, lambda i, at: (0, 0), pipeline_mode=pl.Buffered(1))]
            + [own] * len(extra),
            out_specs=own,
        ),
        out_shape=sds((n // 2, d), BF16 if dm is None else F32),
        compiler_params=pltpu.CompilerParams(dimension_semantics=("arbitrary",)),
        cost_estimate=pl.CostEstimate(flops=3 * n * f * d, bytes_accessed=8 * n * d, transcendentals=0),
    )(jnp.reshape(part, (1,)).astype(jnp.int32), dq, dk, dv, w, *extra)


def small_sum_kernel(n_p, n_t, in_ref, out_ref, pair, pair_sum, plane, plane_sum, column, send_sems, recv_sems):
    p, core, t = lax.axis_index("p"), lax.axis_index("core"), lax.axis_index("tensor")
    peers = [{"core": 1 - core}] + [{"p": lax.rem(p + r, n_p)} for r in range(1, n_p)]
    peers += [{"tensor": lax.rem(t + r, n_t)} for r in range(1, n_t)]
    barrier = pltpu.get_barrier_semaphore()
    for peer in peers:
        pl.semaphore_signal(barrier, inc=1, device_id=peer, device_id_type=pl.DeviceIdType.MESH)
    pl.semaphore_wait(barrier, len(peers))

    def exchange(first, count, source, slots, at):
        copies = []
        for j in range(count):
            copy = pltpu.make_async_remote_copy(
                src_ref=source, dst_ref=slots.at[at], send_sem=send_sems.at[first + j], recv_sem=recv_sems.at[first + j],
                device_id=peers[first + j], device_id_type=pl.DeviceIdType.MESH,
            )
            copy.start()
            copies.append(copy)
        for copy in copies:
            copy.wait()

    exchange(0, 1, in_ref, pair, 0)
    pair_sum[...] = in_ref[...] + pair[0]
    exchange(1, n_p - 1, pair_sum, plane, p)
    plane[p] = pair_sum[...]
    total = plane[0]
    for j in range(1, n_p):
        total = total + plane[j]
    plane_sum[...] = total
    exchange(n_p, n_t - 1, plane_sum, column, t)
    column[t] = plane_sum[...]
    total = column[0]
    for j in range(1, n_t):
        total = total + column[j]
    out_ref[...] = total


def small_sum(values, n_p, n_t):
    rows_ = values.shape[0]
    count = n_p + n_t - 1
    return pl.pallas_call(
        functools.partial(small_sum_kernel, n_p, n_t),
        out_shape=sds(values.shape, F32),
        in_specs=[pl.BlockSpec(memory_space=pltpu.VMEM)],
        out_specs=pl.BlockSpec(memory_space=pltpu.VMEM),
        scratch_shapes=[
            pltpu.VMEM((1, rows_, 128), F32), pltpu.VMEM((rows_, 128), F32), pltpu.VMEM((n_p, rows_, 128), F32),
            pltpu.VMEM((rows_, 128), F32), pltpu.VMEM((n_t, rows_, 128), F32),
            pltpu.SemaphoreType.DMA((count,)), pltpu.SemaphoreType.DMA((count,)),
        ],
        compiler_params=pltpu.CompilerParams(collective_id=0, has_side_effects=True),
    )(values)


def swap_cores(value):
    return lax.ppermute(value, "core", [(0, 1), (1, 0)])


def column_routes(tensor_size):
    first, second = [], []
    for core in range(2):
        for t in range(tensor_size):
            at = core * tensor_size + t
            first.append((at, (t >> 1) * tensor_size + 2 * core + (t & 1)))
            second.append((at, (t >> 1) * tensor_size + 2 * core + 1 - (t & 1)))
    return first, second


def back(route):
    return [(b, a) for a, b in route]


def by_core(core, mine, other, axis):
    return jnp.where(
        core == 0, jnp.concatenate([mine, other], axis=axis), jnp.concatenate([other, mine], axis=axis)
    )


def body(
    inputs, segment_ids, token_valid, qkv_weight, qv_bias, out_weight, norm_gains, row_biases,
    up_weight, up_bias, down_weight, out_grad,
):
    COL = ("core", "tensor")
    ALL = ("p", "core", "tensor")
    core, tensor = lax.axis_index("core"), lax.axis_index("tensor")
    n_p, n_t = lax.axis_size("p"), lax.axis_size("tensor")
    n_dp = 2 * n_p
    micro, held_rows, width = inputs.shape
    assert micro == 2 and n_t == 4
    odd = tensor & 1
    route_a, route_b = column_routes(n_t)

    def bring(value):
        a = lax.ppermute(value[odd], COL, route_a)
        b = lax.ppermute(value[1 - odd], COL, route_b)
        return jnp.where(odd == 0, jnp.concatenate([a, b]), jnp.concatenate([b, a]))

    def give(value):
        a = lax.ppermute(lax.dynamic_slice_in_dim(value, odd * held_rows, held_rows), COL, back(route_a))
        b = lax.ppermute(lax.dynamic_slice_in_dim(value, (1 - odd) * held_rows, held_rows), COL, back(route_b))
        return jnp.where(odd == 0, jnp.stack([a, b]), jnp.stack([b, a]))

    def gathered(weight):
        got = lax.all_gather(weight, ALL, axis=0, tiled=False)
        return got.reshape((n_dp, n_t) + weight.shape)

    x_own = bring(inputs)
    rows = x_own.shape[0]
    labels = jnp.stack([segment_ids[:, 0], token_valid[:, 0]], axis=1)[odd]
    labels = jnp.where((tensor >> 1) == core, labels, swap_cores(labels))
    segment, valid = labels[0], labels[1]

    bias_all = lax.all_gather(jnp.concatenate([qv_bias.reshape(-1), up_bias]), "tensor")
    n_qv = qv_bias.size
    qv_all = bias_all[:, :n_qv].reshape(n_t, 2, -1).transpose(1, 0, 2).reshape(2, -1)
    up_bias_all = bias_all[:, n_qv:].reshape(1, -1)

    w_qkv = gathered(qkv_weight)
    w_qkv = lax.dynamic_slice_in_dim(w_qkv, 2 * core, 2, 1)
    w_qkv = w_qkv.transpose(0, 3, 2, 1, 4).reshape(width, -1)
    own = w_qkv.shape[1] // 3
    w_out = gathered(out_weight).transpose(1, 2, 0, 3).reshape(-1, width)
    w_up = gathered(up_weight).transpose(0, 2, 1, 3).reshape(width, -1)
    w_down = gathered(down_weight).transpose(1, 2, 0, 3).reshape(-1, width)

    x_full = by_core(core, x_own, swap_cores(x_own), 0)
    qv_own = lax.dynamic_slice_in_dim(qv_all, core * own, own, 1)
    bias = jnp.concatenate([qv_own[0], jnp.zeros_like(qv_own[0]), qv_own[1]])
    qkv = (jnp.dot(x_full, w_qkv, preferred_element_type=F32) + bias).astype(BF16)
    context, lse = attend_fwd(qkv, segment, valid, 512, 512)
    mine = lax.dynamic_slice_in_dim(context, core * rows, rows)
    other = lax.dynamic_slice_in_dim(context, (1 - core) * rows, rows)
    c_own = by_core(core, mine, swap_cores(other), 1)
    hl, normed, inverse = mix(x_own, c_own, w_out, row_biases, norm_gains)
    active, slope = up(hl, w_up, up_bias_all)
    grad_own = bring(out_grad)
    layer, dr, dz, sums_two = down(active, w_down, normed, grad_own, row_biases, norm_gains)
    layer_out = give(layer)

    du, up_sum = slope_pull(dz, w_down, slope)
    dm, da, sums_one = mix_pull(du, w_up, dr, normed, inverse, norm_gains)
    down_keep, down_send = col_grad(active, dz, n_p, n_t)
    down_recv = swap_cores(down_send)
    up_keep, up_send = row_grad(hl, du, n_p, n_t)
    up_recv = swap_cores(up_send)
    out_keep, out_send = col_grad(c_own, da, n_p, n_t)
    out_recv = swap_cores(out_send)
    dc = dot(da, w_out, NT).astype(BF16)
    mine = lax.dynamic_slice_in_dim(dc, core * own, own, 1)
    other = lax.dynamic_slice_in_dim(dc, (1 - core) * own, own, 1)
    dc_full = by_core(core, mine, swap_cores(other), 0)

    def flat(values):
        return values.reshape(-1, values.shape[-1])

    def totals(axis, size, at, parts, dtype):
        widths = sorted({part.shape[-1] for part in parts})
        done = [None] * len(parts)
        for lanes in widths:
            index = [j for j, part in enumerate(parts) if part.shape[-1] == lanes]
            pick = lambda to: jnp.concatenate(
                [flat(lax.dynamic_index_in_dim(parts[j], to, 0, keepdims=False)) for j in index]
            )
            total = pick(at).astype(F32)
            for r in range(1, size):
                moved = lax.ppermute(pick((at + r) % size), axis, [(i, (i + r) % size) for i in range(size)])
                total = total + moved.astype(F32)
            total = total.astype(dtype)
            first = 0
            for j in index:
                shape = parts[j].shape[1:]
                count = math.prod(shape) // lanes
                done[j] = total[first : first + count].reshape(shape)
                first += count
        return done

    p_at = lax.axis_index("p")
    plus = lambda a, b: (a.astype(F32) + b.astype(F32)).astype(BF16)
    ffn_parts = [plus(down_keep, down_recv), plus(up_keep, up_recv), plus(out_keep, out_recv)]
    *ffn_parts, dc_full = lax.optimization_barrier((*ffn_parts, dc_full))
    ffn_parts = totals("p", n_p, p_at, ffn_parts, BF16)

    dq, dk, dv = attend_bwd(qkv, context, dc_full, lse, segment, valid, 256, 512)
    dx_other = swap_cores(input_pull(1 - core, dq, dk, dv, w_qkv))
    qkv_keep, qkv_send, qv_sum = qkv_grad(x_full, dq, dk, dv, n_p, n_t)
    qkv_recv = swap_cores(qkv_send)
    dx_mine = input_pull(core, dq, dk, dv, w_qkv, dm)
    input_grad = give((dx_mine + dx_other.astype(F32)).astype(BF16)).astype(F32)
    qkv_parts = totals("p", n_p, p_at, [by_core(core, qkv_keep, qkv_recv, 1)], BF16)
    down_total, up_total, out_total = totals("tensor", n_t, tensor, ffn_parts, F32)
    (qkv_total,) = totals("tensor", n_t, tensor, qkv_parts, F32)
    up_total = up_total.transpose(1, 0, 2).reshape(up_weight.shape)
    qkv_total = qkv_total.transpose(0, 2, 1, 3).reshape(qkv_weight.shape)

    qv_pad = lax.dynamic_update_slice(jnp.zeros((2, width), F32), qv_sum[0:2], (0, core * own))
    small = jnp.concatenate(
        [
            jnp.stack([sums_one[0], sums_two[0], sums_one[1], sums_one[2], sums_two[1], sums_two[2]]).reshape(-1),
            qv_pad.reshape(-1),
            up_sum[0],
        ]
    )
    small = small_sum(small.reshape(-1, 128), n_p, n_t).reshape(-1)
    gain_sum = small[: 2 * width].reshape(2, width)
    bias_sum = small[2 * width : 6 * width].reshape(4, width)
    qv_total = lax.dynamic_slice_in_dim(small[6 * width : 8 * width].reshape(2, width), tensor * qv_bias.shape[1], qv_bias.shape[1], 1)
    up_bias_total = lax.dynamic_slice_in_dim(small[8 * width :], tensor * up_bias.shape[0], up_bias.shape[0])
    return (
        layer_out, input_grad, qkv_total, qv_total, out_total, gain_sum, bias_sum, up_total, up_bias_total, down_total,
    )


def solution(mesh):
    dp, tensor = mesh.devices.shape
    split = jax.sharding.Mesh(mesh.devices.reshape(dp // 2, 2, tensor), ("p", "core", "tensor"))
    pc = ("p", "core")
    tokens = P(None, ("p", "core", "tensor"), None)
    return jax.shard_map(
        body,
        mesh=split,
        in_specs=(
            tokens, P(None, pc, None), P(None, pc, None), P(None, pc, "tensor"), P(None, "tensor"), P("tensor", pc),
            P(), P(), P(pc, "tensor"), P("tensor"), P("tensor", pc), tokens,
        ),
        out_specs=(
            tokens, tokens, P(None, pc, "tensor"), P(None, "tensor"), P("tensor", pc), P(), P(), P(pc, "tensor"),
            P("tensor"), P("tensor", pc),
        ),
        check_vma=False,
    )
```

```python
import functools
import math
import jax
import jax.numpy as jnp
from jax import lax
from jax.sharding import PartitionSpec as P
from jax.experimental import pallas as pl
from jax.experimental.pallas import tpu as pltpu

HEAD = 64
PAIR = 2 * HEAD
NEG_FILL = -1e30
F32 = jnp.float32
BF16 = jnp.bfloat16
NT = (((1,), (1,)), ((), ()))
NN = (((1,), (0,)), ((), ()))
TN = (((0,), (0,)), ((), ()))


def dot(a, b, dims=NN, precision=None):
    return lax.dot_general(a, b, dims, preferred_element_type=F32, precision=precision)


def head_lanes(rows, which):
    lane = lax.broadcasted_iota(jnp.int32, (rows, PAIR), 1)
    return (lane < HEAD) if which == 0 else (lane >= HEAD)


def attend_fwd_kernel(bk, lo_ref, hi_ref, pad_ref, q_ref, k_ref, v_ref, qcode_ref, kcode_ref, o_ref, lse_ref):
    i = pl.program_id(1)
    bq = q_ref.shape[0]
    q = q_ref[...] * jnp.asarray(0.125, BF16)
    heads = [jnp.where(head_lanes(bq, w), q, jnp.zeros_like(q)) for w in (0, 1)]
    qcode = jnp.tile(qcode_ref[...], (1, bk // 128))
    first = i * bq

    def run(diagonal):
        def step(t, carry):
            at = pl.multiple_of(t * bk, bk)
            k = k_ref[pl.ds(at, bk), :]
            v = v_ref[pl.ds(at, bk), :]
            mask = qcode == kcode_ref[:, pl.ds(at, bk)]
            if diagonal:
                gap = lax.broadcasted_iota(jnp.int32, (bq, bk), 1) - lax.broadcasted_iota(jnp.int32, (bq, bk), 0)
                mask = mask | (gap == first - at)
            out = []
            for h in (0, 1):
                top, total, acc = carry[3 * h : 3 * h + 3]
                s = jnp.where(mask, dot(heads[h], k, NT), NEG_FILL)
                new = jnp.maximum(top, jnp.max(s, axis=1, keepdims=True))
                p = jnp.exp(s - new)
                old = jnp.exp(top - new)
                out += [
                    new,
                    total * old + jnp.sum(p, axis=1, keepdims=True),
                    acc * old + dot(p.astype(BF16), v),
                ]
            return tuple(out)

        one = (jnp.full((bq, 1), NEG_FILL, F32), jnp.zeros((bq, 1), F32), jnp.zeros((bq, PAIR), F32))
        ma, la, aa, mb, lb, ab = lax.fori_loop(lo_ref[i], hi_ref[i], step, one + one)
        o_ref[...] = jnp.where(head_lanes(bq, 0), aa / la, ab / lb).astype(BF16)
        lane = lax.broadcasted_iota(jnp.int32, (bq, PAIR), 1)
        wide = jnp.where(lane == 0, ma + jnp.log(la), mb + jnp.log(lb))
        lse_ref[...] = wide.T[0:8, :]

    pl.when(pad_ref[i] > 0)(lambda: run(True))
    pl.when(pad_ref[i] == 0)(lambda: run(False))


def attend_bwd_kernel(
    bq, lo_ref, hi_ref, pad_ref, q_ref, k_ref, v_ref, c_ref, dc_ref, lse_ref, qcode_ref, kcode_ref,
    dq_ref, dk_ref, dv_ref, dq_acc, delta,
):
    i = pl.program_id(1)
    bk = k_ref.shape[0]
    first = i * bk

    @pl.when(i == 0)
    def _():
        dq_acc[...] = jnp.zeros_like(dq_acc)
        row = lax.broadcasted_iota(jnp.int32, (8, PAIR), 0)
        lane = lax.broadcasted_iota(jnp.int32, (8, PAIR), 1)
        pick = jnp.where(lane // HEAD == row, 1.0, 0.0).astype(F32)
        prod = dc_ref[...].astype(F32) * c_ref[...].astype(F32)
        delta[...] = dot(pick, prod, NT, lax.Precision.HIGHEST)

    k = k_ref[...] * jnp.asarray(0.125, BF16)
    v = v_ref[...]
    kh = [jnp.where(head_lanes(bk, w), k, jnp.zeros_like(k)) for w in (0, 1)]
    vh = [jnp.where(head_lanes(bk, w), v, jnp.zeros_like(v)) for w in (0, 1)]
    kcode = jnp.tile(kcode_ref[...], (1, bq // 128))

    def run(diagonal):
        def step(t, carry):
            dk, dv = carry
            at = pl.multiple_of(t * bq, bq)
            rows = pl.ds(at, bq)
            q = q_ref[rows, :]
            dc = dc_ref[rows, :]
            mask = kcode == qcode_ref[:, rows]
            if diagonal:
                gap = lax.broadcasted_iota(jnp.int32, (bk, bq), 1) - lax.broadcasted_iota(jnp.int32, (bk, bq), 0)
                mask = mask | (gap == first - at)
            dq = jnp.zeros((bq, PAIR), F32)
            for h in (0, 1):
                s = dot(kh[h], q, NT)
                p = jnp.exp(jnp.where(mask, s - lse_ref[h : h + 1, rows], NEG_FILL))
                dp = dot(vh[h], dc, NT)
                ds = (p * (dp - delta[h : h + 1, rows])).astype(BF16)
                own = head_lanes(bq, h)
                dv = dv + dot(p.astype(BF16), jnp.where(own, dc, jnp.zeros_like(dc)))
                dk = dk + dot(ds, jnp.where(own, q, jnp.zeros_like(q)))
                dq = dq + dot(ds, kh[h], TN)
            dq_acc[rows, :] += dq
            return dk, dv

        zero = jnp.zeros((bk, PAIR), F32)
        dk, dv = lax.fori_loop(lo_ref[i], hi_ref[i], step, (zero, zero))
        dk_ref[...] = (dk * 0.125).astype(BF16)
        dv_ref[...] = dv.astype(BF16)

    pl.when(pad_ref[i] > 0)(lambda: run(True))
    pl.when(pad_ref[i] == 0)(lambda: run(False))

    @pl.when(i == pl.num_programs(1) - 1)
    def _():
        dq_ref[...] = dq_acc[...].astype(BF16)


def block_bounds(segment, valid, block, other):
    length = segment.shape[0]
    blocks = segment.reshape(length // block, block)
    lo = jnp.sum((segment[None, :] < blocks[:, :1]).astype(jnp.int32), axis=1) // other
    hi = (jnp.sum((segment[None, :] <= blocks[:, -1:]).astype(jnp.int32), axis=1) + other - 1) // other
    pad = jnp.sum((valid.reshape(length // block, block) == 0).astype(jnp.int32), axis=1)
    return lo, hi, pad


def attention_codes(segment, valid):
    kcode = jnp.where(valid > 0, segment, -1)
    qcode = segment
    wide = lambda a: jnp.broadcast_to(a[:, None], (a.shape[0], 128))
    return qcode, kcode, wide(qcode), wide(kcode)


def qkv_at(pair, which):
    return pair // 2 * 6 + which * 2 + pair % 2


def attend_fwd(qkv, segment, valid, bq=256, bk=256):
    length, width = qkv.shape
    pairs = width // 3 // PAIR
    lo, hi, pad = block_bounds(segment, valid, bq, bk)
    qcode, kcode, qwide, kwide = attention_codes(segment, valid)
    return pl.pallas_call(
        functools.partial(attend_fwd_kernel, bk),
        grid_spec=pltpu.PrefetchScalarGridSpec(
            num_scalar_prefetch=3,
            grid=(pairs, length // bq),
            in_specs=[
                pl.BlockSpec((bq, PAIR), lambda h, i, *_: (i, qkv_at(h, 0))),
                pl.BlockSpec((length, PAIR), lambda h, i, *_: (0, qkv_at(h, 1))),
                pl.BlockSpec((length, PAIR), lambda h, i, *_: (0, qkv_at(h, 2))),
                pl.BlockSpec((bq, 128), lambda h, i, *_: (i, 0)),
                pl.BlockSpec((1, length), lambda h, i, *_: (0, 0)),
            ],
            out_specs=[
                pl.BlockSpec((bq, PAIR), lambda h, i, *_: (i, h)),
                pl.BlockSpec((8, bq), lambda h, i, *_: (h, i)),
            ],
        ),
        out_shape=[
            jax.ShapeDtypeStruct((length, pairs * PAIR), BF16),
            jax.ShapeDtypeStruct((pairs * 8, length), F32),
        ],
        compiler_params=pltpu.CompilerParams(dimension_semantics=("arbitrary", "arbitrary")),
        cost_estimate=pl.CostEstimate(flops=8 * 2 * length * length * PAIR, bytes_accessed=8 * length * width, transcendentals=4 * length * length),
    )(lo, hi, pad, qkv, qkv, qkv, qwide, kcode[None, :])


def attend_bwd(qkv, context, context_grad, lse, segment, valid, bq=256, bk=256):
    length, width = qkv.shape
    pairs = width // 3 // PAIR
    lo, hi, pad = block_bounds(segment, valid, bk, bq)
    qcode, kcode, qwide, kwide = attention_codes(segment, valid)
    whole = pl.BlockSpec((length, PAIR), lambda h, i, *_: (0, h))
    part = pl.BlockSpec((bk, PAIR), lambda h, i, *_: (i, h))
    cols = lambda at: pl.BlockSpec((bk, PAIR), lambda h, i, *_: (i, qkv_at(h, at)))
    shape = jax.ShapeDtypeStruct((length, pairs * PAIR), BF16)
    return pl.pallas_call(
        functools.partial(attend_bwd_kernel, bq),
        grid_spec=pltpu.PrefetchScalarGridSpec(
            num_scalar_prefetch=3,
            grid=(pairs, length // bk),
            in_specs=[
                pl.BlockSpec((length, PAIR), lambda h, i, *_: (0, qkv_at(h, 0))), cols(1), cols(2), whole, whole,
                pl.BlockSpec((8, length), lambda h, i, *_: (h, 0)),
                pl.BlockSpec((1, length), lambda h, i, *_: (0, 0)),
                pl.BlockSpec((bk, 128), lambda h, i, *_: (i, 0)),
            ],
            out_specs=[whole, part, part],
            scratch_shapes=[pltpu.VMEM((length, PAIR), F32), pltpu.VMEM((8, length), F32)],
        ),
        out_shape=[shape, shape, shape],
        compiler_params=pltpu.CompilerParams(dimension_semantics=("arbitrary", "arbitrary")),
        cost_estimate=pl.CostEstimate(flops=20 * 2 * length * length * PAIR, bytes_accessed=16 * length * width, transcendentals=4 * length * length),
    )(lo, hi, pad, qkv, qkv, qkv, context, context_grad, lse, qcode[None, :], kwide)


def norm_stats(values):
    center = values - jnp.mean(values, axis=1, keepdims=True)
    inverse = lax.rsqrt(jnp.mean(center * center, axis=1, keepdims=True) + 1e-05)
    return center * inverse, inverse


def norm_pull(incoming, normed, inverse, gain):
    scaled = incoming * gain
    return inverse * (
        scaled - jnp.mean(scaled, axis=1, keepdims=True) - normed * jnp.mean(scaled * normed, axis=1, keepdims=True)
    )


def col_sum(values):
    return jnp.sum(values, axis=0, keepdims=True)


def add_sums(ref, parts):
    @pl.when(pl.program_id(0) == 0)
    def _():
        ref[...] = jnp.zeros_like(ref)

    for at, part in enumerate(parts):
        ref[at : at + 1, :] += col_sum(part)


def mix_kernel(at_ref, x_ref, c_ref, w_ref, bias_ref, gain_ref, hl_ref, n_ref, r_ref):
    mixed = x_ref[...].astype(F32) + dot(c_ref[...], w_ref[...]) + bias_ref[0:1, :]
    normed, inverse = norm_stats(mixed)
    hl_ref[...] = (normed * gain_ref[0:1, :] + bias_ref[1:2, :]).astype(BF16)
    n_ref[...] = normed
    r_ref[...] = jnp.broadcast_to(inverse, r_ref.shape)


def up_kernel(h_ref, w_ref, bias_ref, g_ref, slope_ref):
    u = dot(h_ref[...], w_ref[...]) + bias_ref[...]
    cdf = 0.5 + 0.5 * lax.erf(u * (1.0 / math.sqrt(2.0)))
    g_ref[...] = (u * cdf).astype(BF16)
    slope_ref[...] = (cdf + u * (jnp.exp(-0.5 * u * u) * (1.0 / math.sqrt(2.0 * math.pi)))).astype(BF16)


def down_kernel(g_ref, w_ref, n_ref, e_ref, bias_ref, gain_ref, out_ref, dr_ref, dz_ref, sum_ref):
    hidden = n_ref[...] * gain_ref[0:1, :] + bias_ref[1:2, :]
    normed, inverse = norm_stats(hidden + dot(g_ref[...], w_ref[...]) + bias_ref[2:3, :])
    out_ref[...] = (normed * gain_ref[1:2, :] + bias_ref[3:4, :]).astype(BF16)
    e = e_ref[...].astype(F32)
    dr = norm_pull(e, normed, inverse, gain_ref[1:2, :])
    dr_ref[...] = dr
    dz_ref[...] = dr.astype(BF16)
    add_sums(sum_ref, (e * normed, dr, e))


def slope_kernel(dz_ref, w_ref, slope_ref, du_ref, sum_ref):
    du = (dot(dz_ref[...], w_ref[...], NT) * slope_ref[...].astype(F32)).astype(BF16)
    du_ref[...] = du

    @pl.when(pl.program_id(1) == 0)
    def _():
        sum_ref[...] = jnp.zeros_like(sum_ref)

    sum_ref[0:1, :] += col_sum(du.astype(F32))


def mix_pull_kernel(du_ref, w_ref, dr_ref, n_ref, r_ref, gain_ref, dm_ref, da_ref, sum_ref):
    dh = dr_ref[...] + dot(du_ref[...], w_ref[...], NT)
    normed = n_ref[...]
    dm = norm_pull(dh, normed, r_ref[:, 0:1], gain_ref[0:1, :])
    dm_ref[...] = dm
    da_ref[...] = dm.astype(BF16)
    add_sums(sum_ref, (dh * normed, dm, dh))


def call(kernel, grid, ins, outs, flops, nbytes, *args):
    return pl.pallas_call(
        kernel,
        grid=grid,
        in_specs=ins,
        out_specs=outs[0],
        out_shape=outs[1],
        compiler_params=pltpu.CompilerParams(dimension_semantics=("arbitrary",) * len(grid)),
        cost_estimate=pl.CostEstimate(flops=flops, bytes_accessed=nbytes, transcendentals=0),
    )(*args)


def rows(block, width):
    return pl.BlockSpec((block, width), lambda i: (i, 0))


def held(shape):
    return pl.BlockSpec(shape, lambda i: (0, 0))


def once(shape):
    return pl.BlockSpec(shape, lambda i: (0, 0), pipeline_mode=pl.Buffered(1))


def sds(shape, dtype=BF16):
    return jax.ShapeDtypeStruct(shape, dtype)


def mix(core_at, x, c, w, biases, gains, block=256):
    n, d = c.shape
    r = lambda width: pl.BlockSpec((block, width), lambda i, at: (i, 0))
    fixed = lambda value: pl.BlockSpec(value.shape, lambda i, at: (0, 0), pipeline_mode=pl.Buffered(1))
    steps = n // block
    return pl.pallas_call(
        mix_kernel,
        grid_spec=pltpu.PrefetchScalarGridSpec(
            num_scalar_prefetch=1,
            grid=(steps,),
            in_specs=[
                pl.BlockSpec((block, d), lambda i, at: (at[0] * steps + i, 0)), r(d), fixed(w), fixed(biases), fixed(gains),
            ],
            out_specs=[r(d), r(d), r(128)],
        ),
        out_shape=[sds((n, d)), sds((n, d), F32), sds((n, 128), F32)],
        compiler_params=pltpu.CompilerParams(dimension_semantics=("arbitrary",)),
        cost_estimate=pl.CostEstimate(flops=2 * n * d * d, bytes_accessed=12 * n * d, transcendentals=0),
    )(core_at, x, c, w, biases, gains)


def up(h, w, bias, block=256, cols=1024):
    n, d = h.shape
    f = w.shape[1]
    cols = min(cols, f)
    tile = pl.BlockSpec((block, cols), lambda j, i: (i, j))
    return call(
        up_kernel, (f // cols, n // block),
        [pl.BlockSpec((block, d), lambda j, i: (i, 0)), pl.BlockSpec((d, cols), lambda j, i: (0, j)), pl.BlockSpec((1, cols), lambda j, i: (0, j))],
        ([tile, tile], [sds((n, f)), sds((n, f))]),
        2 * n * d * f, 4 * n * f + 2 * d * f, h, w, bias,
    )


def down(g, w, normed, e, biases, gains, block=256):
    n, f = g.shape
    d = w.shape[1]
    r = functools.partial(rows, block)
    return call(
        down_kernel, (n // block,),
        [r(f), once(w.shape), r(d), r(d), held(biases.shape), held(gains.shape)],
        ([r(d), r(d), r(d), held((8, d))], [sds((n, d)), sds((n, d), F32), sds((n, d)), sds((8, d), F32)]),
        2 * n * d * f, 2 * n * f + 2 * d * f, g, w, normed, e, biases, gains,
    )


def slope_pull(dz, w, slope, block=256, cols=1024):
    n, d = dz.shape
    f = w.shape[0]
    tile = pl.BlockSpec((block, cols), lambda j, i: (i, j))
    return call(
        slope_kernel, (f // cols, n // block),
        [pl.BlockSpec((block, d), lambda j, i: (i, 0)), pl.BlockSpec((cols, d), lambda j, i: (j, 0)), tile],
        ([tile, pl.BlockSpec((8, cols), lambda j, i: (0, j))], [sds((n, f)), sds((8, f), F32)]),
        2 * n * d * f, 4 * n * f + 2 * d * f, dz, w, slope,
    )


def mix_pull(du, w, dr, normed, inverse, gains, block=256):
    n, f = du.shape
    d = w.shape[0]
    r = functools.partial(rows, block)
    return call(
        mix_pull_kernel, (n // block,),
        [r(f), once(w.shape), r(d), r(d), r(128), held(gains.shape)],
        ([r(d), r(d), held((8, d))], [sds((n, d), F32), sds((n, d)), sds((8, d), F32)]),
        2 * n * d * f, 2 * n * f + 2 * d * f, du, w, dr, normed, inverse, gains,
    )


def split_columns(acc, keep_ref, send_ref):
    n_p, c = keep_ref.shape[0], keep_ref.shape[3]
    for bit in (0, 1):

        @pl.when(lax.axis_index("core") == bit)
        def _():
            for p in range(n_p):
                at, to = (2 * p + bit) * c, (2 * p + 1 - bit) * c
                keep_ref[p, 0] = acc[:, at : at + c]
                send_ref[p, 0] = acc[:, to : to + c]


def split_rows(acc, place, keep_ref, send_ref):
    n_p, r = keep_ref.shape[0], keep_ref.shape[-2]
    for bit in (0, 1):

        @pl.when(lax.axis_index("core") == bit)
        def _():
            for p in range(n_p):
                at, to = (2 * p + bit) * r, (2 * p + 1 - bit) * r
                for cb in range(acc.shape[1] // 128):
                    keep_ref[(p, 0) + place + (cb,)] = acc[at : at + r, cb * 128 : cb * 128 + 128]
                    send_ref[(p, 0) + place + (cb,)] = acc[to : to + r, cb * 128 : cb * 128 + 128]


def col_grad_kernel(a_ref, b_ref, keep_ref, send_ref, acc):
    acc[...] = dot(a_ref[...], b_ref[...], TN).astype(BF16)
    split_columns(acc, keep_ref, send_ref)


def row_grad_kernel(a_ref, b_ref, keep_ref, send_ref, turned, acc):
    @pl.when(pl.program_id(0) == 0)
    def _():
        turned[...] = a_ref[...].T

    acc[...] = dot(turned[...], b_ref[...]).astype(BF16)
    split_rows(acc, (), keep_ref, send_ref)


def qkv_grad_kernel(x_ref, dq_ref, dk_ref, dv_ref, keep_ref, send_ref, sum_ref, turned, acc):
    @pl.when(pl.program_id(0) == 0)
    def _():
        turned[...] = x_ref[...].T

    for at, ref in enumerate((dq_ref, dk_ref, dv_ref)):
        acc[...] = dot(turned[...], ref[...]).astype(BF16)
        split_rows(acc, (at,), keep_ref, send_ref)
    sum_ref[0:1, :] = col_sum(dq_ref[...].astype(F32))
    sum_ref[1:2, :] = col_sum(dv_ref[...].astype(F32))


def grad_call(kernel, grid, ins, outs, scratch, flops, *args):
    return pl.pallas_call(
        kernel,
        grid=grid,
        in_specs=ins,
        out_specs=outs[0],
        out_shape=outs[1],
        scratch_shapes=scratch,
        compiler_params=pltpu.CompilerParams(dimension_semantics=("arbitrary",) * len(grid)),
        cost_estimate=pl.CostEstimate(flops=flops, bytes_accessed=flops // 512, transcendentals=0),
    )(*args)


def col_grad(a, b, n_p, n_t, block=512):
    n, f = a.shape
    d = b.shape[1]
    per_t, c = f // n_t, d // (2 * n_p)
    block = min(block, per_t)
    steps = per_t // block
    spec = pl.BlockSpec((n_p, 1, block, c), lambda i: (0, i // steps, i % steps, 0))
    shape = sds((n_p, n_t, per_t, c))
    return grad_call(
        col_grad_kernel, (f // block,),
        [pl.BlockSpec((n, block), lambda i: (0, i)), once((n, d))],
        ([spec, spec], [shape, shape]), [pltpu.VMEM((block, d), BF16)], 2 * n * f * d, a, b,
    )


def row_grad(a, b, n_p, n_t, block=512):
    n, d = a.shape
    f = b.shape[1]
    per_t, r = f // n_t, d // (2 * n_p)
    steps = per_t // block
    spec = pl.BlockSpec((n_p, 1, block // 128, r, 128), lambda i: (0, i // steps, i % steps, 0, 0))
    shape = sds((n_p, n_t, per_t // 128, r, 128))
    return grad_call(
        row_grad_kernel, (f // block,),
        [once((n, d)), pl.BlockSpec((n, block), lambda i: (0, i))],
        ([spec, spec], [shape, shape]),
        [pltpu.VMEM((d, n), BF16), pltpu.VMEM((d, block), BF16)], 2 * n * f * d, a, b,
    )


def qkv_grad(x, dq, dk, dv, n_p, n_t):
    n, d = x.shape
    f = dq.shape[1]
    half, r = f // (n_t // 2), d // (2 * n_p)
    spec = pl.BlockSpec((n_p, 1, 3, half // 128, r, 128), lambda i: (0, i, 0, 0, 0, 0))
    shape = sds((n_p, n_t // 2, 3, half // 128, r, 128))
    cols = pl.BlockSpec((n, half), lambda i: (0, i))
    return grad_call(
        qkv_grad_kernel, (n_t // 2,),
        [once((n, d)), cols, cols, cols],
        ([spec, spec, pl.BlockSpec((8, half), lambda i: (0, i))], [shape, shape, sds((8, f), F32)]),
        [pltpu.VMEM((d, n), BF16), pltpu.VMEM((d, half), BF16)], 6 * n * f * d, x, dq, dk, dv,
    )


def input_pull_kernel(at_ref, dq_ref, dk_ref, dv_ref, w_ref, *refs):
    c = w_ref.shape[1] // 6
    total = None
    for j in range(6):
        ref = (dq_ref, dk_ref, dv_ref)[j % 3]
        part = dot(ref[:, j // 3 * c : (j // 3 + 1) * c], w_ref[:, j * c : (j + 1) * c], NT)
        total = part if total is None else total + part
    if len(refs) == 2:
        total = total + refs[0][...]
    refs[-1][...] = total.astype(refs[-1].dtype)


def input_pull(part, core, dq, dk, dv, w, dm=None, block=256):
    n, f = dq.shape
    d = w.shape[0]
    steps = n // 2 // block
    cols = pl.BlockSpec((block, f), lambda i, at: (at[0] * steps + i, 0))
    own = pl.BlockSpec((block, d), lambda i, at: (i, 0))
    extra = [] if dm is None else [dm]
    held_w = pl.BlockSpec((d, w.shape[1] // 2), lambda i, at: (0, at[1]), pipeline_mode=pl.Buffered(1))
    return pl.pallas_call(
        input_pull_kernel,
        grid_spec=pltpu.PrefetchScalarGridSpec(
            num_scalar_prefetch=1,
            grid=(steps,),
            in_specs=[cols, cols, cols, held_w] + [own] * len(extra),
            out_specs=own,
        ),
        out_shape=sds((n // 2, d), BF16 if dm is None else F32),
        compiler_params=pltpu.CompilerParams(dimension_semantics=("arbitrary",)),
        cost_estimate=pl.CostEstimate(flops=3 * n * f * d, bytes_accessed=8 * n * d, transcendentals=0),
    )(jnp.stack([part, core]).astype(jnp.int32), dq, dk, dv, w, *extra)


def small_sum_kernel(n_p, n_t, in_ref, out_ref, pair, pair_sum, plane, plane_sum, column, send_sems, recv_sems):
    p, core, t = lax.axis_index("p"), lax.axis_index("core"), lax.axis_index("tensor")
    peers = [{"core": 1 - core}] + [{"p": lax.rem(p + r, n_p)} for r in range(1, n_p)]
    peers += [{"tensor": lax.rem(t + r, n_t)} for r in range(1, n_t)]
    barrier = pltpu.get_barrier_semaphore()
    for peer in peers:
        pl.semaphore_signal(barrier, inc=1, device_id=peer, device_id_type=pl.DeviceIdType.MESH)
    pl.semaphore_wait(barrier, len(peers))

    def exchange(first, count, source, slots, at):
        copies = []
        for j in range(count):
            copy = pltpu.make_async_remote_copy(
                src_ref=source, dst_ref=slots.at[at], send_sem=send_sems.at[first + j], recv_sem=recv_sems.at[first + j],
                device_id=peers[first + j], device_id_type=pl.DeviceIdType.MESH,
            )
            copy.start()
            copies.append(copy)
        for copy in copies:
            copy.wait()

    exchange(0, 1, in_ref, pair, 0)
    pair_sum[...] = in_ref[...] + pair[0]
    exchange(1, n_p - 1, pair_sum, plane, p)
    plane[p] = pair_sum[...]
    total = plane[0]
    for j in range(1, n_p):
        total = total + plane[j]
    plane_sum[...] = total
    exchange(n_p, n_t - 1, plane_sum, column, t)
    column[t] = plane_sum[...]
    total = column[0]
    for j in range(1, n_t):
        total = total + column[j]
    out_ref[...] = total


def small_sum(values, n_p, n_t):
    rows_ = values.shape[0]
    count = n_p + n_t - 1
    return pl.pallas_call(
        functools.partial(small_sum_kernel, n_p, n_t),
        out_shape=sds(values.shape, F32),
        in_specs=[pl.BlockSpec(memory_space=pltpu.VMEM)],
        out_specs=pl.BlockSpec(memory_space=pltpu.VMEM),
        scratch_shapes=[
            pltpu.VMEM((1, rows_, 128), F32), pltpu.VMEM((rows_, 128), F32), pltpu.VMEM((n_p, rows_, 128), F32),
            pltpu.VMEM((rows_, 128), F32), pltpu.VMEM((n_t, rows_, 128), F32),
            pltpu.SemaphoreType.DMA((count,)), pltpu.SemaphoreType.DMA((count,)),
        ],
        compiler_params=pltpu.CompilerParams(collective_id=0, has_side_effects=True),
    )(values)


MESH_ID = pl.DeviceIdType.MESH


def flip(value, bit):
    return value + bit - 2 * bit * ((value // bit) % 2)


def start_kernel(n_p, n_t, kinds, *refs):
    n = len(kinds)
    x_ref, bias_ref, *shards = refs[: n + 2]
    x_out, bias_out, *fulls = refs[n + 2 : 2 * n + 4]
    send_sems, recv_sems, own_sems = refs[2 * n + 4 :]
    p, core, t = lax.axis_index("p"), lax.axis_index("core"), lax.axis_index("tensor")
    me = 2 * p + core
    bits = [1 << s for s in range(n_p.bit_length() - 1)]
    column = [{"tensor": lax.rem(t + r, n_t)} for r in range(1, n_t)]
    across = [{"core": 1 - core, "tensor": lax.rem(t + r, n_t)} for r in range(n_t)]
    plane = [{"p": flip(p, bit)} for bit in bits]
    barrier = pltpu.get_barrier_semaphore()
    for peer in column + across + plane:
        pl.semaphore_signal(barrier, inc=1, device_id=peer, device_id_type=MESH_ID)
    pl.semaphore_wait(barrier, len(column + across + plane))

    used = [0, 0]

    def group():
        used[0] += 1
        return used[0] - 1

    def send(source, target, at, peer):
        pltpu.make_async_remote_copy(
            src_ref=source, dst_ref=target, send_sem=send_sems.at[at], recv_sem=recv_sems.at[at],
            device_id=peer, device_id_type=MESH_ID,
        ).start()

    def arrived(view, at):
        pltpu.make_async_copy(view, view, recv_sems.at[at]).wait()

    def left(view, at):
        pltpu.make_async_copy(view, view, send_sems.at[at]).wait()

    def keep(source, target):
        used[1] += 1
        copy = pltpu.make_async_copy(source, target, own_sems.at[used[1] - 1])
        copy.start()
        return copy

    def slab(i, d, half):
        full, kind = fulls[i], kinds[i]
        if kind == "rows":
            depth, wide = shards[i].shape[-2], full.shape[1] // 2
            return full.at[pl.ds(pl.multiple_of(d * depth, depth), depth), pl.ds(half * wide, wide)]
        depth, tall = shards[i].shape[-1], full.shape[0] // 2
        return full.at[pl.ds(half * tall, tall), pl.ds(pl.multiple_of(d * depth, depth), depth)]

    def slabs(i, count, half):
        full, kind = fulls[i], kinds[i]
        if kind == "rows":
            wide = full.shape[1] // 2
            return full.at[pl.ds(0, count * shards[i].shape[-2]), pl.ds(half * wide, wide)]
        tall = full.shape[0] // 2
        return full.at[pl.ds(half * tall, tall), pl.ds(0, count * shards[i].shape[-1])]

    def places(i):
        shard, full = shards[i], fulls[i]
        if kinds[i] == "columns":
            tall, depth = shard.shape
            return [(shard, full.at[pl.ds(pl.multiple_of(t * tall, tall), tall), pl.ds(pl.multiple_of(me * depth, depth), depth)])]
        depth, wide = shard.shape[-2:]
        rows_at = pl.ds(pl.multiple_of(me * depth, depth), depth)
        if len(shard.shape) == 2:
            return [(shard, full.at[rows_at, pl.ds(pl.multiple_of(t * wide, wide), wide)])]
        count = shard.shape[0]
        return [
            (shard.at[w], full.at[rows_at, pl.ds(pl.multiple_of((t * count + w) * wide, wide), wide)])
            for w in range(count)
        ]

    def shares(i, count):
        shard, full = shards[i], fulls[i]
        if kinds[i] == "columns":
            return full.at[pl.ds(0, count * shard.shape[0]), pl.ds(0, shard.shape[1])]
        wide = math.prod(shard.shape) // shard.shape[-2]
        return full.at[pl.ds(0, shard.shape[-2]), pl.ds(0, count * wide)]

    own, line = [], []
    for i in range(n):
        at = group()
        line.append(at)
        own.append([keep(source, target) for source, target in places(i)])
        for peer in column:
            for source, target in places(i):
                send(source, target, at, peer)
    bias_at = group()
    bias_own = keep(bias_ref, bias_out.at[t])
    for peer in column:
        send(bias_ref, bias_out.at[t], bias_at, peer)

    held = x_ref.shape[1]
    odd = t % 2
    x_rows = x_out.at[pl.ds(pl.multiple_of(t * held, held), held), :]
    x_at = [group(), group()]
    stays = core == t // 2
    peer_a = {"core": t // 2, "tensor": 2 * core + odd}
    peer_b = {"core": t // 2, "tensor": 2 * core + 1 - odd}

    pl.when(jnp.logical_not(stays))(lambda: send(x_ref.at[odd], x_rows, x_at[0], peer_a))
    x_own = pltpu.make_async_copy(x_ref.at[odd], x_rows, own_sems.at[used[1]])
    used[1] += 1
    pl.when(stays)(x_own.start)
    send(x_ref.at[1 - odd], x_rows, x_at[1], peer_b)

    partner = {"core": 1 - core}
    passes = []

    def forward(i, masks, half):
        at = group()
        guard = i == 0

        def go():
            for mask in masks:
                d = 2 * mask + core
                send(slab(i, d, half), slab(i, d, half), at, partner)

        if guard:
            pl.when(core == 1 - half)(go)
        else:
            go()
        passes.append((i, len(masks), half, at))

    states = {}

    def stage(i, s):
        if s == 0:
            for copy in own[i]:
                copy.wait()
            arrived(shares(i, n_t - 1), line[i])
            states[i] = {}
            for half in (0, 1):
                states[i][half] = ([p], None)
        else:
            for half in (0, 1):
                masks, at = states[i][half]
                arrived(slabs(i, len(masks), half), at)
                bit = bits[s - 1] if half == 0 else bits[-s]
                states[i][half] = (masks + [flip(m, bit) for m in masks], None)
        for half in (0, 1):
            masks, _ = states[i][half]
            if s < len(bits):
                at = group()
                bit = bits[s] if half == 0 else bits[-s - 1]
                for m in masks:
                    d = 2 * m + core
                    send(slab(i, d, half), slab(i, d, half), at, {"p": flip(p, bit)})
                states[i][half] = (masks, at)
                finish.append((i, len(masks), half, at))
            fresh = masks if s == 0 else masks[len(masks) // 2 :]
            forward(i, fresh, half)

    finish = []
    for step in range(n + len(bits)):
        for i in range(n):
            if 0 <= step - i <= len(bits):
                stage(i, step - i)

    pl.when(jnp.logical_not(stays))(lambda: arrived(x_rows, x_at[0]))
    pl.when(stays)(x_own.wait)
    arrived(x_rows, x_at[1])
    half_rows = x_out.at[pl.ds(pl.multiple_of(core * 2 * held, 2 * held), 2 * held), :]
    x_pass = group()
    send(half_rows, half_rows, x_pass, partner)
    bias_own.wait()
    arrived(bias_out.at[pl.ds(0, n_t - 1)], bias_at)
    for i, count, half, at in passes:
        if i == 0:
            pl.when(core == half)(functools.partial(arrived, slabs(i, count, half), at))
        else:
            arrived(slabs(i, count, half), at)
    arrived(half_rows, x_pass)
    left(half_rows, x_pass)
    for i, count, half, at in passes:
        if i == 0:
            pl.when(core == 1 - half)(functools.partial(left, slabs(i, count, half), at))
        else:
            left(slabs(i, count, half), at)
    for i, count, half, at in finish:
        left(slabs(i, count, half), at)
    for i in range(n):
        left(shares(i, n_t - 1), line[i])
    left(bias_out.at[pl.ds(0, n_t - 1)], bias_at)
    pl.when(jnp.logical_not(stays))(lambda: left(x_rows, x_at[0]))
    left(x_rows, x_at[1])


def start_gather(x, bias, shards, kinds, n_p, n_t):
    n_dp = 2 * n_p
    fulls = []
    for shard, kind in zip(shards, kinds):
        if kind == "columns":
            fulls.append(sds((shard.shape[0] * n_t, shard.shape[1] * n_dp)))
        else:
            fulls.append(sds((shard.shape[-2] * n_dp, math.prod(shard.shape) // shard.shape[-2] * n_t)))
    bits = n_p.bit_length() - 1
    count = len(shards) * (1 + 2 * bits + 2 * (bits + 1)) + 4
    vmem, away = pl.BlockSpec(memory_space=pltpu.VMEM), pl.BlockSpec(memory_space=pl.ANY)
    return pl.pallas_call(
        functools.partial(start_kernel, n_p, n_t, kinds),
        out_shape=[sds((n_t * x.shape[1], x.shape[2])), sds((n_t,) + bias.shape, F32)] + fulls,
        in_specs=[vmem] * (2 + len(shards)),
        out_specs=[away] * (2 + len(shards)),
        scratch_shapes=[
            pltpu.SemaphoreType.DMA((count,)), pltpu.SemaphoreType.DMA((count,)), pltpu.SemaphoreType.DMA((10,)),
        ],
        compiler_params=pltpu.CompilerParams(collective_id=1, has_side_effects=True),
    )(x, bias, *shards)


def project_kernel(core_ref, x_ref, w_ref, bias_ref, out_ref):
    out_ref[...] = (dot(x_ref[...], w_ref[...]) + bias_ref[...]).astype(BF16)


def project(core_at, x, w, bias, block=256):
    n, d = x.shape
    f = w.shape[1] // 2
    return pl.pallas_call(
        project_kernel,
        grid_spec=pltpu.PrefetchScalarGridSpec(
            num_scalar_prefetch=1,
            grid=(n // block,),
            in_specs=[
                pl.BlockSpec((block, d), lambda i, at: (i, 0)),
                pl.BlockSpec((d, f), lambda i, at: (0, at[0]), pipeline_mode=pl.Buffered(1)),
                pl.BlockSpec((1, f), lambda i, at: (0, 0)),
            ],
            out_specs=pl.BlockSpec((block, f), lambda i, at: (i, 0)),
        ),
        out_shape=sds((n, f)),
        compiler_params=pltpu.CompilerParams(dimension_semantics=("arbitrary",)),
        cost_estimate=pl.CostEstimate(flops=2 * n * d * f, bytes_accessed=4 * n * d + 2 * n * f, transcendentals=0),
    )(core_at, x, w, bias)


def swap_cores(value):
    return lax.ppermute(value, "core", [(0, 1), (1, 0)])


def column_routes(tensor_size):
    first, second = [], []
    for core in range(2):
        for t in range(tensor_size):
            at = core * tensor_size + t
            first.append((at, (t >> 1) * tensor_size + 2 * core + (t & 1)))
            second.append((at, (t >> 1) * tensor_size + 2 * core + 1 - (t & 1)))
    return first, second


def back(route):
    return [(b, a) for a, b in route]


def by_core(core, mine, other, axis):
    return jnp.where(
        core == 0, jnp.concatenate([mine, other], axis=axis), jnp.concatenate([other, mine], axis=axis)
    )


def body(
    inputs, segment_ids, token_valid, qkv_weight, qv_bias, out_weight, norm_gains, row_biases,
    up_weight, up_bias, down_weight, out_grad,
):
    COL = ("core", "tensor")
    ALL = ("p", "core", "tensor")
    core, tensor = lax.axis_index("core"), lax.axis_index("tensor")
    n_p, n_t = lax.axis_size("p"), lax.axis_size("tensor")
    n_dp = 2 * n_p
    micro, held_rows, width = inputs.shape
    assert micro == 2 and n_t == 4
    odd = tensor & 1
    route_a, route_b = column_routes(n_t)

    def bring(value):
        a = lax.ppermute(value[odd], COL, route_a)
        b = lax.ppermute(value[1 - odd], COL, route_b)
        return jnp.where(odd == 0, jnp.concatenate([a, b]), jnp.concatenate([b, a]))

    def give(value):
        a = lax.ppermute(lax.dynamic_slice_in_dim(value, odd * held_rows, held_rows), COL, back(route_a))
        b = lax.ppermute(lax.dynamic_slice_in_dim(value, (1 - odd) * held_rows, held_rows), COL, back(route_b))
        return jnp.where(odd == 0, jnp.stack([a, b]), jnp.stack([b, a]))

    def gathered(weight):
        got = lax.all_gather(weight, ALL, axis=0, tiled=False)
        return got.reshape((n_dp, n_t) + weight.shape)

    labels = jnp.stack([segment_ids[:, 0], token_valid[:, 0]], axis=1)[odd]
    labels = jnp.where((tensor >> 1) == core, labels, swap_cores(labels))
    segment, valid = labels[0], labels[1]

    shards, kinds = [qkv_weight, up_weight], ["rows", "rows"]
    wide = out_weight.shape[1] % 128 == 0
    if wide:
        shards, kinds = [qkv_weight, out_weight, up_weight, down_weight], ["rows", "columns", "rows", "columns"]
    local_bias = jnp.concatenate([qv_bias.reshape(-1), up_bias]).reshape(-1, 128)
    x_full, bias_all, *fulls = start_gather(inputs, local_bias, shards, kinds, n_p, n_t)
    if wide:
        w_qkv, w_out, w_up, w_down = fulls
    else:
        w_qkv, w_up = fulls
        w_out = gathered(out_weight).transpose(1, 2, 0, 3).reshape(-1, width)
        w_down = gathered(down_weight).transpose(1, 2, 0, 3).reshape(-1, width)
    out_grad, x_full = lax.optimization_barrier((out_grad, x_full))
    rows = x_full.shape[0] // 2
    own = w_qkv.shape[1] // 6
    bias_all = bias_all.reshape(n_t, -1)
    n_qv = qv_bias.size
    up_bias_all = bias_all[:, n_qv:].reshape(1, -1)
    qv_own = lax.dynamic_slice_in_dim(bias_all[:, :n_qv], 2 * core, 2).reshape(2, 2, -1)
    bias = jnp.stack([qv_own[:, 0], jnp.zeros_like(qv_own[:, 0]), qv_own[:, 1]], axis=1).reshape(1, -1)
    core_at = jnp.reshape(core, (1,)).astype(jnp.int32)
    qkv = project(core_at, x_full, w_qkv, bias)
    context, lse = attend_fwd(qkv, segment, valid, 512, 512)
    mine = lax.dynamic_slice_in_dim(context, core * rows, rows)
    other = lax.dynamic_slice_in_dim(context, (1 - core) * rows, rows)
    c_own = by_core(core, mine, swap_cores(other), 1)
    hl, normed, inverse = mix(core_at, x_full, c_own, w_out, row_biases, norm_gains)
    active, slope = up(hl, w_up, up_bias_all)
    grad_own = bring(out_grad)
    layer, dr, dz, sums_two = down(active, w_down, normed, grad_own, row_biases, norm_gains)
    layer_out = give(layer)

    du, up_sum = slope_pull(dz, w_down, slope)
    dm, da, sums_one = mix_pull(du, w_up, dr, normed, inverse, norm_gains)
    down_keep, down_send = col_grad(active, dz, n_p, n_t)
    down_recv = swap_cores(down_send)
    up_keep, up_send = row_grad(hl, du, n_p, n_t)
    up_recv = swap_cores(up_send)
    out_keep, out_send = col_grad(c_own, da, n_p, n_t)
    out_recv = swap_cores(out_send)
    dc = dot(da, w_out, NT).astype(BF16)
    mine = lax.dynamic_slice_in_dim(dc, core * own, own, 1)
    other = lax.dynamic_slice_in_dim(dc, (1 - core) * own, own, 1)
    dc_full = by_core(core, mine, swap_cores(other), 0)

    def pieces(size, at, *parts):
        pick = lambda part, to: lax.dynamic_index_in_dim(part, to, 0, keepdims=False)
        out = []
        for r in range(size):
            to = (at + r) % size
            total = pick(parts[0], to)
            for part in parts[1:]:
                total = (total.astype(F32) + pick(part, to).astype(F32)).astype(BF16)
            out.append(total)
        return out

    def collect(axis, size, own_piece, *others):
        total = own_piece.astype(F32)
        for r, piece in enumerate(others, 1):
            total = total + lax.ppermute(piece, axis, [(i, (i + r) % size) for i in range(size)]).astype(F32)
        return total

    p_at = lax.axis_index("p")
    ffn_parts = [
        pieces(n_p, p_at, down_keep, down_recv), pieces(n_p, p_at, up_keep, up_recv), pieces(n_p, p_at, out_keep, out_recv),
    ]
    ffn_parts, dc_full = lax.optimization_barrier((ffn_parts, dc_full))
    ffn_sums = [collect("p", n_p, *part).astype(BF16) for part in ffn_parts]

    dq, dk, dv = attend_bwd(qkv, context, dc_full, lse, segment, valid, 256, 512)
    dx_other = swap_cores(input_pull(1 - core, core, dq, dk, dv, w_qkv))
    qkv_keep, qkv_send, qv_sum = qkv_grad(x_full, dq, dk, dv, n_p, n_t)
    qkv_recv = swap_cores(qkv_send)
    dx_mine = input_pull(core, core, dq, dk, dv, w_qkv, dm)
    input_grad = give((dx_mine + dx_other.astype(F32)).astype(BF16)).astype(F32)
    qkv_sum = collect("p", n_p, *pieces(n_p, p_at, by_core(core, qkv_keep, qkv_recv, 1))).astype(BF16)
    down_total, up_total, out_total, qkv_total = [
        collect("tensor", n_t, *pieces(n_t, tensor, part)) for part in (*ffn_sums, qkv_sum)
    ]
    up_total = up_total.transpose(1, 0, 2).reshape(up_weight.shape)
    qkv_total = qkv_total.transpose(0, 2, 1, 3).reshape(qkv_weight.shape)

    qv_pad = lax.dynamic_update_slice(jnp.zeros((2, width), F32), qv_sum[0:2], (0, core * own))
    small = jnp.concatenate(
        [
            jnp.stack([sums_one[0], sums_two[0], sums_one[1], sums_one[2], sums_two[1], sums_two[2]]).reshape(-1),
            qv_pad.reshape(-1),
            up_sum[0],
        ]
    )
    small = small_sum(small.reshape(-1, 128), n_p, n_t).reshape(-1)
    gain_sum = small[: 2 * width].reshape(2, width)
    bias_sum = small[2 * width : 6 * width].reshape(4, width)
    qv_total = lax.dynamic_slice_in_dim(small[6 * width : 8 * width].reshape(2, width), tensor * qv_bias.shape[1], qv_bias.shape[1], 1)
    up_bias_total = lax.dynamic_slice_in_dim(small[8 * width :], tensor * up_bias.shape[0], up_bias.shape[0])
    return (
        layer_out, input_grad, qkv_total, qv_total, out_total, gain_sum, bias_sum, up_total, up_bias_total, down_total,
    )


def solution(mesh):
    dp, tensor = mesh.devices.shape
    split = jax.sharding.Mesh(mesh.devices.reshape(dp // 2, 2, tensor), ("p", "core", "tensor"))
    pc = ("p", "core")
    tokens = P(None, ("p", "core", "tensor"), None)
    return jax.shard_map(
        body,
        mesh=split,
        in_specs=(
            tokens, P(None, pc, None), P(None, pc, None), P(None, pc, "tensor"), P(None, "tensor"), P("tensor", pc),
            P(), P(), P(pc, "tensor"), P("tensor"), P("tensor", pc), tokens,
        ),
        out_specs=(
            tokens, tokens, P(None, pc, "tensor"), P(None, "tensor"), P("tensor", pc), P(), P(), P(pc, "tensor"),
            P("tensor"), P("tensor", pc),
        ),
        check_vma=False,
    )
```

```python
import functools
import math
import jax
import jax.numpy as jnp
from jax import lax
from jax.sharding import PartitionSpec as P
from jax.experimental import pallas as pl
from jax.experimental.pallas import tpu as pltpu

HEAD = 64
PAIR = 2 * HEAD
NEG_FILL = -1e30
F32 = jnp.float32
BF16 = jnp.bfloat16
NT = (((1,), (1,)), ((), ()))
NN = (((1,), (0,)), ((), ()))
TN = (((0,), (0,)), ((), ()))


def dot(a, b, dims=NN, precision=None):
    return lax.dot_general(a, b, dims, preferred_element_type=F32, precision=precision)


def head_lanes(rows, which):
    lane = lax.broadcasted_iota(jnp.int32, (rows, PAIR), 1)
    return (lane < HEAD) if which == 0 else (lane >= HEAD)


def attend_fwd_kernel(bk, lo_ref, hi_ref, pad_ref, q_ref, k_ref, v_ref, qcode_ref, kcode_ref, o_ref, lse_ref, v_turned):
    i = pl.program_id(1)
    bq = q_ref.shape[0]

    @pl.when(i == 0)
    def _():
        v_turned[...] = v_ref[...].T

    q = q_ref[...] * jnp.asarray(0.125, BF16)
    heads = [jnp.where(head_lanes(bq, w), q, jnp.zeros_like(q)) for w in (0, 1)]
    qcode = qcode_ref[...]
    first = i * bq

    def run(diagonal):
        def step(t, carry):
            at = pl.multiple_of(t * bk, bk)
            keys = pl.ds(at, bk)
            k = k_ref[keys, :]
            mask = jnp.tile(kcode_ref[keys, :], (1, bq // 128)) == qcode
            if diagonal:
                gap = lax.broadcasted_iota(jnp.int32, (bk, bq), 0) - lax.broadcasted_iota(jnp.int32, (bk, bq), 1)
                mask = mask | (gap == first - at)
            out = []
            for h in (0, 1):
                top, total, acc = carry[3 * h : 3 * h + 3]
                s = jnp.where(mask, dot(k, heads[h], NT), NEG_FILL)
                new = jnp.maximum(top, jnp.max(s, axis=0, keepdims=True))
                p = jnp.exp(s - new)
                old = jnp.exp(top - new)
                v = v_turned[h * HEAD : (h + 1) * HEAD, keys]
                out += [
                    new,
                    total * old + jnp.sum(p, axis=0, keepdims=True),
                    acc * old + dot(v, p.astype(BF16)),
                ]
            return tuple(out)

        one = (jnp.full((1, bq), NEG_FILL, F32), jnp.zeros((1, bq), F32), jnp.zeros((HEAD, bq), F32))
        ma, la, aa, mb, lb, ab = lax.fori_loop(lo_ref[i], hi_ref[i], step, one + one)
        o_ref[...] = jnp.concatenate([aa / la, ab / lb], axis=0).T.astype(BF16)
        lse_ref[0:1, :] = ma + jnp.log(la)
        lse_ref[1:2, :] = mb + jnp.log(lb)

    pl.when(pad_ref[i] > 0)(lambda: run(True))
    pl.when(pad_ref[i] == 0)(lambda: run(False))


def attend_bwd_kernel(
    bq, lo_ref, hi_ref, pad_ref, q_ref, k_ref, v_ref, c_ref, dc_ref, lse_ref, qcode_ref, kcode_ref,
    dq_ref, dk_ref, dv_ref, dq_acc, delta,
):
    i = pl.program_id(1)
    bk = k_ref.shape[0]
    first = i * bk

    @pl.when(i == 0)
    def _():
        dq_acc[...] = jnp.zeros_like(dq_acc)
        row = lax.broadcasted_iota(jnp.int32, (8, PAIR), 0)
        lane = lax.broadcasted_iota(jnp.int32, (8, PAIR), 1)
        pick = jnp.where(lane // HEAD == row, 1.0, 0.0).astype(F32)
        prod = dc_ref[...].astype(F32) * c_ref[...].astype(F32)
        delta[...] = dot(pick, prod, NT, lax.Precision.HIGHEST)

    k = k_ref[...] * jnp.asarray(0.125, BF16)
    v = v_ref[...]
    k_turned = k.T
    kh = [jnp.where(head_lanes(bk, w), k, jnp.zeros_like(k)) for w in (0, 1)]
    vh = [jnp.where(head_lanes(bk, w), v, jnp.zeros_like(v)) for w in (0, 1)]
    kcode = jnp.tile(kcode_ref[...], (1, bq // 128))

    def run(diagonal):
        def step(t, carry):
            dk, dv = carry
            at = pl.multiple_of(t * bq, bq)
            rows = pl.ds(at, bq)
            q = q_ref[rows, :]
            dc = dc_ref[rows, :]
            mask = kcode == qcode_ref[:, rows]
            if diagonal:
                gap = lax.broadcasted_iota(jnp.int32, (bk, bq), 1) - lax.broadcasted_iota(jnp.int32, (bk, bq), 0)
                mask = mask | (gap == first - at)
            for h in (0, 1):
                s = dot(kh[h], q, NT)
                p = jnp.exp(jnp.where(mask, s - lse_ref[h : h + 1, rows], NEG_FILL))
                dp = dot(vh[h], dc, NT)
                ds = (p * (dp - delta[h : h + 1, rows])).astype(BF16)
                own = head_lanes(bq, h)
                dv = dv + dot(p.astype(BF16), jnp.where(own, dc, jnp.zeros_like(dc)))
                dk = dk + dot(ds, jnp.where(own, q, jnp.zeros_like(q)))
                dq_acc[h * HEAD : (h + 1) * HEAD, rows] += dot(k_turned[h * HEAD : (h + 1) * HEAD, :], ds)
            return dk, dv

        zero = jnp.zeros((bk, PAIR), F32)
        dk, dv = lax.fori_loop(lo_ref[i], hi_ref[i], step, (zero, zero))
        dk_ref[...] = (dk * 0.125).astype(BF16)
        dv_ref[...] = dv.astype(BF16)

    pl.when(pad_ref[i] > 0)(lambda: run(True))
    pl.when(pad_ref[i] == 0)(lambda: run(False))

    @pl.when(i == pl.num_programs(1) - 1)
    def _():
        dq_ref[...] = dq_acc[...].T.astype(BF16)


def block_bounds(segment, valid, block, other):
    length = segment.shape[0]
    blocks = segment.reshape(length // block, block)
    lo = jnp.sum((segment[None, :] < blocks[:, :1]).astype(jnp.int32), axis=1) // other
    hi = (jnp.sum((segment[None, :] <= blocks[:, -1:]).astype(jnp.int32), axis=1) + other - 1) // other
    pad = jnp.sum((valid.reshape(length // block, block) == 0).astype(jnp.int32), axis=1)
    return lo, hi, pad


def attention_codes(segment, valid):
    kcode = jnp.where(valid > 0, segment, -1)
    qcode = segment
    wide = lambda a: jnp.broadcast_to(a[:, None], (a.shape[0], 128))
    return qcode, kcode, wide(qcode), wide(kcode)


def qkv_at(pair, which):
    return pair // 2 * 6 + which * 2 + pair % 2


def attend_fwd(qkv, segment, valid, bq=256, bk=256):
    length, width = qkv.shape
    pairs = width // 3 // PAIR
    lo, hi, pad = block_bounds(segment, valid, bq, bk)
    qcode, kcode, qwide, kwide = attention_codes(segment, valid)
    return pl.pallas_call(
        functools.partial(attend_fwd_kernel, bk),
        grid_spec=pltpu.PrefetchScalarGridSpec(
            num_scalar_prefetch=3,
            grid=(pairs, length // bq),
            in_specs=[
                pl.BlockSpec((bq, PAIR), lambda h, i, *_: (i, qkv_at(h, 0))),
                pl.BlockSpec((length, PAIR), lambda h, i, *_: (0, qkv_at(h, 1))),
                pl.BlockSpec((length, PAIR), lambda h, i, *_: (0, qkv_at(h, 2))),
                pl.BlockSpec((1, bq), lambda h, i, *_: (0, i)),
                pl.BlockSpec((length, 128), lambda h, i, *_: (0, 0)),
            ],
            out_specs=[
                pl.BlockSpec((bq, PAIR), lambda h, i, *_: (i, h)),
                pl.BlockSpec((8, bq), lambda h, i, *_: (h, i)),
            ],
            scratch_shapes=[pltpu.VMEM((PAIR, length), BF16)],
        ),
        out_shape=[
            jax.ShapeDtypeStruct((length, pairs * PAIR), BF16),
            jax.ShapeDtypeStruct((pairs * 8, length), F32),
        ],
        compiler_params=pltpu.CompilerParams(dimension_semantics=("arbitrary", "arbitrary")),
        cost_estimate=pl.CostEstimate(flops=8 * 2 * length * length * PAIR, bytes_accessed=8 * length * width, transcendentals=4 * length * length),
    )(lo, hi, pad, qkv, qkv, qkv, qcode[None, :], kwide)


def attend_bwd(part, qkv, context, context_grad, lse, segment, valid, bq=256, bk=256):
    length, width = qkv.shape
    pairs = width // 6 // PAIR
    base = part * pairs
    lo, hi, pad = block_bounds(segment, valid, bk, bq)
    qcode, kcode, qwide, kwide = attention_codes(segment, valid)
    whole = pl.BlockSpec((length, PAIR), lambda h, i, *_: (0, h))
    piece = pl.BlockSpec((bk, PAIR), lambda h, i, *_: (i, h))
    source = pl.BlockSpec((length, PAIR), lambda h, i, *_: (0, base + h))
    cols = lambda at: pl.BlockSpec((bk, PAIR), lambda h, i, *_: (i, qkv_at(base + h, at)))
    shape = jax.ShapeDtypeStruct((length, pairs * PAIR), BF16)
    return pl.pallas_call(
        functools.partial(attend_bwd_kernel, bq),
        grid_spec=pltpu.PrefetchScalarGridSpec(
            num_scalar_prefetch=3,
            grid=(pairs, length // bk),
            in_specs=[
                pl.BlockSpec((length, PAIR), lambda h, i, *_: (0, qkv_at(base + h, 0))), cols(1), cols(2), source, source,
                pl.BlockSpec((8, length), lambda h, i, *_: (base + h, 0)),
                pl.BlockSpec((1, length), lambda h, i, *_: (0, 0)),
                pl.BlockSpec((bk, 128), lambda h, i, *_: (i, 0)),
            ],
            out_specs=[whole, piece, piece],
            scratch_shapes=[pltpu.VMEM((PAIR, length), F32), pltpu.VMEM((8, length), F32)],
        ),
        out_shape=[shape, shape, shape],
        compiler_params=pltpu.CompilerParams(dimension_semantics=("arbitrary", "arbitrary")),
        cost_estimate=pl.CostEstimate(flops=20 * 2 * length * length * PAIR, bytes_accessed=16 * length * width, transcendentals=4 * length * length),
    )(lo, hi, pad, qkv, qkv, qkv, context, context_grad, lse, qcode[None, :], kwide)


def norm_stats(values):
    center = values - jnp.mean(values, axis=1, keepdims=True)
    inverse = lax.rsqrt(jnp.mean(center * center, axis=1, keepdims=True) + 1e-05)
    return center * inverse, inverse


def norm_pull(incoming, normed, inverse, gain):
    scaled = incoming * gain
    return inverse * (
        scaled - jnp.mean(scaled, axis=1, keepdims=True) - normed * jnp.mean(scaled * normed, axis=1, keepdims=True)
    )


def col_sum(values):
    return jnp.sum(values, axis=0, keepdims=True)


def add_sums(ref, parts):
    @pl.when(pl.program_id(0) == 0)
    def _():
        ref[...] = jnp.zeros_like(ref)

    for at, part in enumerate(parts):
        ref[at : at + 1, :] += col_sum(part)


def mix_kernel(at_ref, x_ref, c_ref, w_ref, bias_ref, gain_ref, hl_ref, turned_ref, n_ref, r_ref):
    mixed = x_ref[...].astype(F32) + dot(c_ref[...], w_ref[...]) + bias_ref[0:1, :]
    normed, inverse = norm_stats(mixed)
    hl = (normed * gain_ref[0:1, :] + bias_ref[1:2, :]).astype(BF16)
    hl_ref[...] = hl
    turned_ref[...] = hl.T
    n_ref[...] = normed
    r_ref[...] = jnp.broadcast_to(inverse, r_ref.shape)


def up_kernel(h_ref, w_ref, bias_ref, g_ref, slope_ref):
    u = dot(h_ref[...], w_ref[...]) + bias_ref[...]
    cdf = 0.5 + 0.5 * lax.erf(u * (1.0 / math.sqrt(2.0)))
    g_ref[...] = (u * cdf).astype(BF16)
    slope_ref[...] = (cdf + u * (jnp.exp(-0.5 * u * u) * (1.0 / math.sqrt(2.0 * math.pi)))).astype(BF16)


def down_kernel(g_ref, w_ref, n_ref, e_ref, bias_ref, gain_ref, out_ref, dr_ref, dz_ref, sum_ref):
    hidden = n_ref[...] * gain_ref[0:1, :] + bias_ref[1:2, :]
    normed, inverse = norm_stats(hidden + dot(g_ref[...], w_ref[...]) + bias_ref[2:3, :])
    out_ref[...] = (normed * gain_ref[1:2, :] + bias_ref[3:4, :]).astype(BF16)
    e = e_ref[...].astype(F32)
    dr = norm_pull(e, normed, inverse, gain_ref[1:2, :])
    dr_ref[...] = dr
    dz_ref[...] = dr.astype(BF16)
    add_sums(sum_ref, (e * normed, dr, e))


def slope_kernel(dz_ref, w_ref, slope_ref, du_ref, sum_ref):
    du = (dot(dz_ref[...], w_ref[...], NT) * slope_ref[...].astype(F32)).astype(BF16)
    du_ref[...] = du

    @pl.when(pl.program_id(1) == 0)
    def _():
        sum_ref[...] = jnp.zeros_like(sum_ref)

    sum_ref[0:1, :] += col_sum(du.astype(F32))


def mix_pull_kernel(du_ref, w_ref, dr_ref, n_ref, r_ref, gain_ref, dm_ref, da_ref, sum_ref):
    dh = dr_ref[...] + dot(du_ref[...], w_ref[...], NT)
    normed = n_ref[...]
    dm = norm_pull(dh, normed, r_ref[:, 0:1], gain_ref[0:1, :])
    dm_ref[...] = dm
    da_ref[...] = dm.astype(BF16)
    add_sums(sum_ref, (dh * normed, dm, dh))


def call(kernel, grid, ins, outs, flops, nbytes, *args):
    return pl.pallas_call(
        kernel,
        grid=grid,
        in_specs=ins,
        out_specs=outs[0],
        out_shape=outs[1],
        compiler_params=pltpu.CompilerParams(dimension_semantics=("arbitrary",) * len(grid)),
        cost_estimate=pl.CostEstimate(flops=flops, bytes_accessed=nbytes, transcendentals=0),
    )(*args)


def rows(block, width):
    return pl.BlockSpec((block, width), lambda i: (i, 0))


def held(shape):
    return pl.BlockSpec(shape, lambda i: (0, 0))


def once(shape):
    return pl.BlockSpec(shape, lambda i: (0, 0), pipeline_mode=pl.Buffered(1))


def sds(shape, dtype=BF16):
    return jax.ShapeDtypeStruct(shape, dtype)


def mix(core_at, x, c, w, biases, gains, block=256):
    n, d = c.shape
    r = lambda width: pl.BlockSpec((block, width), lambda i, at: (i, 0))
    fixed = lambda value: pl.BlockSpec(value.shape, lambda i, at: (0, 0), pipeline_mode=pl.Buffered(1))
    steps = n // block
    return pl.pallas_call(
        mix_kernel,
        grid_spec=pltpu.PrefetchScalarGridSpec(
            num_scalar_prefetch=1,
            grid=(steps,),
            in_specs=[
                pl.BlockSpec((block, d), lambda i, at: (at[0] * steps + i, 0)), r(d), fixed(w), fixed(biases), fixed(gains),
            ],
            out_specs=[r(d), pl.BlockSpec((d, block), lambda i, at: (0, i)), r(d), r(128)],
        ),
        out_shape=[sds((n, d)), sds((d, n)), sds((n, d), F32), sds((n, 128), F32)],
        compiler_params=pltpu.CompilerParams(dimension_semantics=("arbitrary",)),
        cost_estimate=pl.CostEstimate(flops=2 * n * d * d, bytes_accessed=12 * n * d, transcendentals=0),
    )(core_at, x, c, w, biases, gains)


def up(h, w, bias, block=256, cols=1024):
    n, d = h.shape
    f = w.shape[1]
    cols = min(cols, f)
    tile = pl.BlockSpec((block, cols), lambda j, i: (i, j))
    return call(
        up_kernel, (f // cols, n // block),
        [pl.BlockSpec((block, d), lambda j, i: (i, 0)), pl.BlockSpec((d, cols), lambda j, i: (0, j)), pl.BlockSpec((1, cols), lambda j, i: (0, j))],
        ([tile, tile], [sds((n, f)), sds((n, f))]),
        2 * n * d * f, 4 * n * f + 2 * d * f, h, w, bias,
    )


def down(g, w, normed, e, biases, gains, block=256):
    n, f = g.shape
    d = w.shape[1]
    r = functools.partial(rows, block)
    return call(
        down_kernel, (n // block,),
        [r(f), once(w.shape), r(d), r(d), held(biases.shape), held(gains.shape)],
        ([r(d), r(d), r(d), held((8, d))], [sds((n, d)), sds((n, d), F32), sds((n, d)), sds((8, d), F32)]),
        2 * n * d * f, 2 * n * f + 2 * d * f, g, w, normed, e, biases, gains,
    )


def slope_pull(dz, w, slope, block=256, cols=1024):
    n, d = dz.shape
    f = w.shape[0]
    tile = pl.BlockSpec((block, cols), lambda j, i: (i, j))
    return call(
        slope_kernel, (f // cols, n // block),
        [pl.BlockSpec((block, d), lambda j, i: (i, 0)), pl.BlockSpec((cols, d), lambda j, i: (j, 0)), tile],
        ([tile, pl.BlockSpec((8, cols), lambda j, i: (0, j))], [sds((n, f)), sds((8, f), F32)]),
        2 * n * d * f, 4 * n * f + 2 * d * f, dz, w, slope,
    )


def mix_pull(du, w, dr, normed, inverse, gains, block=256):
    n, f = du.shape
    d = w.shape[0]
    r = functools.partial(rows, block)
    return call(
        mix_pull_kernel, (n // block,),
        [r(f), once(w.shape), r(d), r(d), r(128), held(gains.shape)],
        ([r(d), r(d), held((8, d))], [sds((n, d), F32), sds((n, d)), sds((8, d), F32)]),
        2 * n * d * f, 2 * n * f + 2 * d * f, du, w, dr, normed, inverse, gains,
    )


def split_columns(acc, keep_ref, send_ref):
    n_p, c = keep_ref.shape[0], keep_ref.shape[3]
    for bit in (0, 1):

        @pl.when(lax.axis_index("core") == bit)
        def _():
            for p in range(n_p):
                at, to = (2 * p + bit) * c, (2 * p + 1 - bit) * c
                keep_ref[p, 0] = acc[:, at : at + c]
                send_ref[p, 0] = acc[:, to : to + c]


def split_rows(acc, place, keep_ref, send_ref):
    n_p, r = keep_ref.shape[0], keep_ref.shape[-2]
    for bit in (0, 1):

        @pl.when(lax.axis_index("core") == bit)
        def _():
            for p in range(n_p):
                at, to = (2 * p + bit) * r, (2 * p + 1 - bit) * r
                for cb in range(acc.shape[1] // 128):
                    keep_ref[(p, 0) + place + (cb,)] = acc[at : at + r, cb * 128 : cb * 128 + 128]
                    send_ref[(p, 0) + place + (cb,)] = acc[to : to + r, cb * 128 : cb * 128 + 128]


def col_grad_kernel(a_ref, b_ref, keep_ref, send_ref, acc):
    acc[...] = dot(a_ref[...], b_ref[...], TN).astype(BF16)
    split_columns(acc, keep_ref, send_ref)


def row_grad_kernel(a_ref, b_ref, keep_ref, send_ref, acc):
    acc[...] = dot(a_ref[...], b_ref[...]).astype(BF16)
    split_rows(acc, (), keep_ref, send_ref)


def qkv_grad_kernel(x_ref, dq_ref, dk_ref, dv_ref, keep_ref, send_ref, sum_ref, acc):
    for at, ref in enumerate((dq_ref, dk_ref, dv_ref)):
        acc[...] = dot(x_ref[...], ref[...]).astype(BF16)
        split_rows(acc, (at,), keep_ref, send_ref)
    sum_ref[0:1, :] = col_sum(dq_ref[...].astype(F32))
    sum_ref[1:2, :] = col_sum(dv_ref[...].astype(F32))


def grad_call(kernel, grid, ins, outs, scratch, flops, *args):
    return pl.pallas_call(
        kernel,
        grid=grid,
        in_specs=ins,
        out_specs=outs[0],
        out_shape=outs[1],
        scratch_shapes=scratch,
        compiler_params=pltpu.CompilerParams(dimension_semantics=("arbitrary",) * len(grid)),
        cost_estimate=pl.CostEstimate(flops=flops, bytes_accessed=flops // 512, transcendentals=0),
    )(*args)


def col_grad(a, b, n_p, n_t, block=512):
    n, f = a.shape
    d = b.shape[1]
    per_t, c = f // n_t, d // (2 * n_p)
    block = min(block, per_t)
    steps = per_t // block
    spec = pl.BlockSpec((n_p, 1, block, c), lambda i: (0, i // steps, i % steps, 0))
    shape = sds((n_p, n_t, per_t, c))
    return grad_call(
        col_grad_kernel, (f // block,),
        [pl.BlockSpec((n, block), lambda i: (0, i)), once((n, d))],
        ([spec, spec], [shape, shape]), [pltpu.VMEM((block, d), BF16)], 2 * n * f * d, a, b,
    )


def row_grad(a, b, n_p, n_t, block=512):
    d, n = a.shape
    f = b.shape[1]
    per_t, r = f // n_t, d // (2 * n_p)
    steps = per_t // block
    spec = pl.BlockSpec((n_p, 1, block // 128, r, 128), lambda i: (0, i // steps, i % steps, 0, 0))
    shape = sds((n_p, n_t, per_t // 128, r, 128))
    return grad_call(
        row_grad_kernel, (f // block,),
        [once((d, n)), pl.BlockSpec((n, block), lambda i: (0, i))],
        ([spec, spec], [shape, shape]), [pltpu.VMEM((d, block), BF16)], 2 * n * f * d, a, b,
    )


def qkv_grad(x, dq, dk, dv, n_p):
    d, n = x.shape
    f = dq.shape[1]
    r = d // (2 * n_p)
    spec = pl.BlockSpec((n_p, 1, 3, f // 128, r, 128), lambda i: (0, 0, 0, 0, 0, 0))
    shape = sds((n_p, 1, 3, f // 128, r, 128))
    return grad_call(
        qkv_grad_kernel, (1,),
        [held((d, n)), held((n, f)), held((n, f)), held((n, f))],
        ([spec, spec, held((8, f))], [shape, shape, sds((8, f), F32)]),
        [pltpu.VMEM((d, f), BF16)], 6 * n * f * d, x, dq, dk, dv,
    )


def input_pull_kernel(extra, at_ref, *refs):
    parts, w_ref = refs[:6], refs[6]
    c = w_ref.shape[1] // 6
    total = dot(parts[0][...], w_ref[:, :c], NT)
    for j in range(1, 6):
        total = total + dot(parts[j][...], w_ref[:, j * c : (j + 1) * c], NT)
    if extra:
        total = total + refs[7][...]
    refs[-1][...] = total.astype(refs[-1].dtype)


def input_pull(half, core, parts, w, dm=None, block=256):
    n, f = parts[0].shape
    d = w.shape[0]
    steps = n // 2 // block
    cols = pl.BlockSpec((block, f), lambda i, at: (at[0] * steps + i, 0))
    own = pl.BlockSpec((block, d), lambda i, at: (i, 0))
    extra = [] if dm is None else [dm]
    held_w = pl.BlockSpec((d, w.shape[1] // 2), lambda i, at: (0, at[1]), pipeline_mode=pl.Buffered(1))
    return pl.pallas_call(
        functools.partial(input_pull_kernel, len(extra)),
        grid_spec=pltpu.PrefetchScalarGridSpec(
            num_scalar_prefetch=1,
            grid=(steps,),
            in_specs=[cols] * 6 + [held_w] + [own] * len(extra),
            out_specs=own,
        ),
        out_shape=sds((n // 2, d), BF16 if dm is None else F32),
        compiler_params=pltpu.CompilerParams(dimension_semantics=("arbitrary",)),
        cost_estimate=pl.CostEstimate(flops=6 * n * f * d, bytes_accessed=8 * n * d, transcendentals=0),
    )(jnp.stack([half, core]).astype(jnp.int32), *parts, w, *extra)


def small_sum_kernel(n_p, n_t, in_ref, out_ref, pair, pair_sum, plane, plane_sum, column, send_sems, recv_sems):
    p, core, t = lax.axis_index("p"), lax.axis_index("core"), lax.axis_index("tensor")
    peers = [{"core": 1 - core}] + [{"p": lax.rem(p + r, n_p)} for r in range(1, n_p)]
    peers += [{"tensor": lax.rem(t + r, n_t)} for r in range(1, n_t)]
    barrier = pltpu.get_barrier_semaphore()
    for peer in peers:
        pl.semaphore_signal(barrier, inc=1, device_id=peer, device_id_type=pl.DeviceIdType.MESH)
    pl.semaphore_wait(barrier, len(peers))

    def exchange(first, count, source, slots, at):
        copies = []
        for j in range(count):
            copy = pltpu.make_async_remote_copy(
                src_ref=source, dst_ref=slots.at[at], send_sem=send_sems.at[first + j], recv_sem=recv_sems.at[first + j],
                device_id=peers[first + j], device_id_type=pl.DeviceIdType.MESH,
            )
            copy.start()
            copies.append(copy)
        for copy in copies:
            copy.wait()

    exchange(0, 1, in_ref, pair, 0)
    pair_sum[...] = in_ref[...] + pair[0]
    exchange(1, n_p - 1, pair_sum, plane, p)
    plane[p] = pair_sum[...]
    total = plane[0]
    for j in range(1, n_p):
        total = total + plane[j]
    plane_sum[...] = total
    exchange(n_p, n_t - 1, plane_sum, column, t)
    column[t] = plane_sum[...]
    total = column[0]
    for j in range(1, n_t):
        total = total + column[j]
    out_ref[...] = total


def small_sum(values, n_p, n_t):
    rows_ = values.shape[0]
    count = n_p + n_t - 1
    return pl.pallas_call(
        functools.partial(small_sum_kernel, n_p, n_t),
        out_shape=sds(values.shape, F32),
        in_specs=[pl.BlockSpec(memory_space=pltpu.VMEM)],
        out_specs=pl.BlockSpec(memory_space=pltpu.VMEM),
        scratch_shapes=[
            pltpu.VMEM((1, rows_, 128), F32), pltpu.VMEM((rows_, 128), F32), pltpu.VMEM((n_p, rows_, 128), F32),
            pltpu.VMEM((rows_, 128), F32), pltpu.VMEM((n_t, rows_, 128), F32),
            pltpu.SemaphoreType.DMA((count,)), pltpu.SemaphoreType.DMA((count,)),
        ],
        compiler_params=pltpu.CompilerParams(collective_id=0, has_side_effects=True),
    )(values)


MESH_ID = pl.DeviceIdType.MESH


def flip(value, bit):
    return value + bit - 2 * bit * ((value // bit) % 2)


def start_kernel(n_p, n_t, kinds, *refs):
    n = len(kinds)
    x_ref, bias_ref, *shards = refs[: n + 2]
    x_out, bias_out, *fulls = refs[n + 2 : 2 * n + 4]
    send_sems, recv_sems, own_sems = refs[2 * n + 4 :]
    p, core, t = lax.axis_index("p"), lax.axis_index("core"), lax.axis_index("tensor")
    me = 2 * p + core
    bits = [1 << s for s in range(n_p.bit_length() - 1)]
    column = [{"tensor": lax.rem(t + r, n_t)} for r in range(1, n_t)]
    across = [{"core": 1 - core, "tensor": lax.rem(t + r, n_t)} for r in range(n_t)]
    plane = [{"p": flip(p, bit)} for bit in bits]
    barrier = pltpu.get_barrier_semaphore()
    for peer in column + across + plane:
        pl.semaphore_signal(barrier, inc=1, device_id=peer, device_id_type=MESH_ID)
    pl.semaphore_wait(barrier, len(column + across + plane))

    used = [0, 0]

    def group():
        used[0] += 1
        return used[0] - 1

    def send(source, target, at, peer):
        pltpu.make_async_remote_copy(
            src_ref=source, dst_ref=target, send_sem=send_sems.at[at], recv_sem=recv_sems.at[at],
            device_id=peer, device_id_type=MESH_ID,
        ).start()

    def arrived(view, at):
        pltpu.make_async_copy(view, view, recv_sems.at[at]).wait()

    def left(view, at):
        pltpu.make_async_copy(view, view, send_sems.at[at]).wait()

    def keep(source, target):
        used[1] += 1
        copy = pltpu.make_async_copy(source, target, own_sems.at[used[1] - 1])
        copy.start()
        return copy

    def slab(i, d, half):
        full, kind = fulls[i], kinds[i]
        if kind == "rows":
            depth, wide = shards[i].shape[-2], full.shape[1] // 2
            return full.at[pl.ds(pl.multiple_of(d * depth, depth), depth), pl.ds(half * wide, wide)]
        depth, tall = shards[i].shape[-1], full.shape[0] // 2
        return full.at[pl.ds(half * tall, tall), pl.ds(pl.multiple_of(d * depth, depth), depth)]

    def slabs(i, count, half):
        full, kind = fulls[i], kinds[i]
        if kind == "rows":
            wide = full.shape[1] // 2
            return full.at[pl.ds(0, count * shards[i].shape[-2]), pl.ds(half * wide, wide)]
        tall = full.shape[0] // 2
        return full.at[pl.ds(half * tall, tall), pl.ds(0, count * shards[i].shape[-1])]

    def places(i):
        shard, full = shards[i], fulls[i]
        if kinds[i] == "columns":
            tall, depth = shard.shape
            return [(shard, full.at[pl.ds(pl.multiple_of(t * tall, tall), tall), pl.ds(pl.multiple_of(me * depth, depth), depth)])]
        depth, wide = shard.shape[-2:]
        rows_at = pl.ds(pl.multiple_of(me * depth, depth), depth)
        if len(shard.shape) == 2:
            return [(shard, full.at[rows_at, pl.ds(pl.multiple_of(t * wide, wide), wide)])]
        count = shard.shape[0]
        return [
            (shard.at[w], full.at[rows_at, pl.ds(pl.multiple_of((t * count + w) * wide, wide), wide)])
            for w in range(count)
        ]

    def shares(i, count):
        shard, full = shards[i], fulls[i]
        if kinds[i] == "columns":
            return full.at[pl.ds(0, count * shard.shape[0]), pl.ds(0, shard.shape[1])]
        wide = math.prod(shard.shape) // shard.shape[-2]
        return full.at[pl.ds(0, shard.shape[-2]), pl.ds(0, count * wide)]

    own, line = [], []
    for i in range(n):
        at = group()
        line.append(at)
        own.append([keep(source, target) for source, target in places(i)])
        for peer in column:
            for source, target in places(i):
                send(source, target, at, peer)
    bias_at = group()
    bias_own = keep(bias_ref, bias_out.at[t])
    for peer in column:
        send(bias_ref, bias_out.at[t], bias_at, peer)

    held = x_ref.shape[1]
    odd = t % 2
    x_rows = x_out.at[pl.ds(pl.multiple_of(t * held, held), held), :]
    x_at = [group(), group()]
    stays = core == t // 2
    peer_a = {"core": t // 2, "tensor": 2 * core + odd}
    peer_b = {"core": t // 2, "tensor": 2 * core + 1 - odd}

    pl.when(jnp.logical_not(stays))(lambda: send(x_ref.at[odd], x_rows, x_at[0], peer_a))
    x_own = pltpu.make_async_copy(x_ref.at[odd], x_rows, own_sems.at[used[1]])
    used[1] += 1
    pl.when(stays)(x_own.start)
    send(x_ref.at[1 - odd], x_rows, x_at[1], peer_b)

    partner = {"core": 1 - core}
    passes = []

    def forward(i, masks, half):
        at = group()
        guard = i == 0

        def go():
            for mask in masks:
                d = 2 * mask + core
                send(slab(i, d, half), slab(i, d, half), at, partner)

        if guard:
            pl.when(core == 1 - half)(go)
        else:
            go()
        passes.append((i, len(masks), half, at))

    states = {}

    def stage(i, s):
        if s == 0:
            for copy in own[i]:
                copy.wait()
            arrived(shares(i, n_t - 1), line[i])
            states[i] = {}
            for half in (0, 1):
                states[i][half] = ([p], None)
        else:
            for half in (0, 1):
                masks, at = states[i][half]
                arrived(slabs(i, len(masks), half), at)
                bit = bits[s - 1] if half == 0 else bits[-s]
                states[i][half] = (masks + [flip(m, bit) for m in masks], None)
        for half in (0, 1):
            masks, _ = states[i][half]
            if s < len(bits):
                at = group()
                bit = bits[s] if half == 0 else bits[-s - 1]
                for m in masks:
                    d = 2 * m + core
                    send(slab(i, d, half), slab(i, d, half), at, {"p": flip(p, bit)})
                states[i][half] = (masks, at)
                finish.append((i, len(masks), half, at))
            fresh = masks if s == 0 else masks[len(masks) // 2 :]
            forward(i, fresh, half)

    finish = []
    for step in range(n + len(bits)):
        for i in range(n):
            if 0 <= step - i <= len(bits):
                stage(i, step - i)

    pl.when(jnp.logical_not(stays))(lambda: arrived(x_rows, x_at[0]))
    pl.when(stays)(x_own.wait)
    arrived(x_rows, x_at[1])
    half_rows = x_out.at[pl.ds(pl.multiple_of(core * 2 * held, 2 * held), 2 * held), :]
    x_pass = group()
    send(half_rows, half_rows, x_pass, partner)
    bias_own.wait()
    arrived(bias_out.at[pl.ds(0, n_t - 1)], bias_at)
    for i, count, half, at in passes:
        if i == 0:
            pl.when(core == half)(functools.partial(arrived, slabs(i, count, half), at))
        else:
            arrived(slabs(i, count, half), at)
    arrived(half_rows, x_pass)
    left(half_rows, x_pass)
    for i, count, half, at in passes:
        if i == 0:
            pl.when(core == 1 - half)(functools.partial(left, slabs(i, count, half), at))
        else:
            left(slabs(i, count, half), at)
    for i, count, half, at in finish:
        left(slabs(i, count, half), at)
    for i in range(n):
        left(shares(i, n_t - 1), line[i])
    left(bias_out.at[pl.ds(0, n_t - 1)], bias_at)
    pl.when(jnp.logical_not(stays))(lambda: left(x_rows, x_at[0]))
    left(x_rows, x_at[1])


def start_gather(x, bias, shards, kinds, n_p, n_t):
    n_dp = 2 * n_p
    fulls = []
    for shard, kind in zip(shards, kinds):
        if kind == "columns":
            fulls.append(sds((shard.shape[0] * n_t, shard.shape[1] * n_dp)))
        else:
            fulls.append(sds((shard.shape[-2] * n_dp, math.prod(shard.shape) // shard.shape[-2] * n_t)))
    bits = n_p.bit_length() - 1
    count = len(shards) * (1 + 2 * bits + 2 * (bits + 1)) + 4
    vmem, away = pl.BlockSpec(memory_space=pltpu.VMEM), pl.BlockSpec(memory_space=pl.ANY)
    return pl.pallas_call(
        functools.partial(start_kernel, n_p, n_t, kinds),
        out_shape=[sds((n_t * x.shape[1], x.shape[2])), sds((n_t,) + bias.shape, F32)] + fulls,
        in_specs=[vmem] * (2 + len(shards)),
        out_specs=[away] * (2 + len(shards)),
        scratch_shapes=[
            pltpu.SemaphoreType.DMA((count,)), pltpu.SemaphoreType.DMA((count,)), pltpu.SemaphoreType.DMA((10,)),
        ],
        compiler_params=pltpu.CompilerParams(collective_id=1, has_side_effects=True),
    )(x, bias, *shards)


def project_kernel(core_ref, x_ref, w_ref, bias_ref, out_ref, turned_ref):
    turned_ref[...] = x_ref[...].T
    out_ref[...] = (dot(x_ref[...], w_ref[...]) + bias_ref[...]).astype(BF16)


def project(core_at, x, w, bias, block=256):
    n, d = x.shape
    f = w.shape[1] // 2
    return pl.pallas_call(
        project_kernel,
        grid_spec=pltpu.PrefetchScalarGridSpec(
            num_scalar_prefetch=1,
            grid=(n // block,),
            in_specs=[
                pl.BlockSpec((block, d), lambda i, at: (i, 0)),
                pl.BlockSpec((d, f), lambda i, at: (0, at[0]), pipeline_mode=pl.Buffered(1)),
                pl.BlockSpec((1, f), lambda i, at: (0, 0)),
            ],
            out_specs=[pl.BlockSpec((block, f), lambda i, at: (i, 0)), pl.BlockSpec((d, block), lambda i, at: (0, i))],
        ),
        out_shape=[sds((n, f)), sds((d, n))],
        compiler_params=pltpu.CompilerParams(dimension_semantics=("arbitrary",)),
        cost_estimate=pl.CostEstimate(flops=2 * n * d * f, bytes_accessed=4 * n * d + 2 * n * f, transcendentals=0),
    )(core_at, x, w, bias)


def swap_cores(value):
    return lax.ppermute(value, "core", [(0, 1), (1, 0)])


def column_routes(tensor_size):
    first, second = [], []
    for core in range(2):
        for t in range(tensor_size):
            at = core * tensor_size + t
            first.append((at, (t >> 1) * tensor_size + 2 * core + (t & 1)))
            second.append((at, (t >> 1) * tensor_size + 2 * core + 1 - (t & 1)))
    return first, second


def back(route):
    return [(b, a) for a, b in route]


def by_core(core, mine, other, axis):
    return jnp.where(
        core == 0, jnp.concatenate([mine, other], axis=axis), jnp.concatenate([other, mine], axis=axis)
    )


def body(
    inputs, segment_ids, token_valid, qkv_weight, qv_bias, out_weight, norm_gains, row_biases,
    up_weight, up_bias, down_weight, out_grad,
):
    COL = ("core", "tensor")
    ALL = ("p", "core", "tensor")
    core, tensor = lax.axis_index("core"), lax.axis_index("tensor")
    n_p, n_t = lax.axis_size("p"), lax.axis_size("tensor")
    n_dp = 2 * n_p
    micro, held_rows, width = inputs.shape
    assert micro == 2 and n_t == 4
    odd = tensor & 1
    route_a, route_b = column_routes(n_t)

    def bring(value):
        a = lax.ppermute(value[odd], COL, route_a)
        b = lax.ppermute(value[1 - odd], COL, route_b)
        return jnp.where(odd == 0, jnp.concatenate([a, b]), jnp.concatenate([b, a]))

    def blocks(value):
        return [lax.dynamic_slice_in_dim(value, at * held_rows, held_rows) for at in (odd, 1 - odd)]

    def give(a, b):
        a, b = lax.ppermute(a, COL, back(route_a)), lax.ppermute(b, COL, back(route_b))
        return jnp.where(odd == 0, jnp.stack([a, b]), jnp.stack([b, a]))

    def gathered(weight):
        got = lax.all_gather(weight, ALL, axis=0, tiled=False)
        return got.reshape((n_dp, n_t) + weight.shape)

    labels = jnp.stack([segment_ids[:, 0], token_valid[:, 0]], axis=1)[odd]
    labels = jnp.where((tensor >> 1) == core, labels, swap_cores(labels))
    segment, valid = labels[0], labels[1]

    shards, kinds = [qkv_weight, up_weight], ["rows", "rows"]
    wide = out_weight.shape[1] % 128 == 0
    if wide:
        shards, kinds = [qkv_weight, out_weight, up_weight, down_weight], ["rows", "columns", "rows", "columns"]
    local_bias = jnp.concatenate([qv_bias.reshape(-1), up_bias]).reshape(-1, 128)
    x_full, bias_all, *fulls = start_gather(inputs, local_bias, shards, kinds, n_p, n_t)
    if wide:
        w_qkv, w_out, w_up, w_down = fulls
    else:
        w_qkv, w_up = fulls
        w_out = gathered(out_weight).transpose(1, 2, 0, 3).reshape(-1, width)
        w_down = gathered(down_weight).transpose(1, 2, 0, 3).reshape(-1, width)
    out_grad, x_full = lax.optimization_barrier((out_grad, x_full))
    rows = x_full.shape[0] // 2
    own = w_qkv.shape[1] // 6
    bias_all = bias_all.reshape(n_t, -1)
    n_qv = qv_bias.size
    up_bias_all = bias_all[:, n_qv:].reshape(1, -1)
    qv_own = lax.dynamic_slice_in_dim(bias_all[:, :n_qv], 2 * core, 2).reshape(2, 2, -1)
    bias = jnp.stack([qv_own[:, 0], jnp.zeros_like(qv_own[:, 0]), qv_own[:, 1]], axis=1).reshape(1, -1)
    core_at = jnp.reshape(core, (1,)).astype(jnp.int32)
    qkv, x_turned = project(core_at, x_full, w_qkv, bias)
    context, lse = attend_fwd(qkv, segment, valid, 512, 512)
    mine = lax.dynamic_slice_in_dim(context, core * rows, rows)
    other = lax.dynamic_slice_in_dim(context, (1 - core) * rows, rows)
    c_own = by_core(core, mine, swap_cores(other), 1)
    hl, hl_turned, normed, inverse = mix(core_at, x_full, c_own, w_out, row_biases, norm_gains)
    active, slope = up(hl, w_up, up_bias_all)
    grad_own = bring(out_grad)
    layer, dr, dz, sums_two = down(active, w_down, normed, grad_own, row_biases, norm_gains)
    layer_out = give(*blocks(layer))

    p_bits = [1 << s for s in range(n_p.bit_length() - 1)]
    t_bits = [2, 1]

    class Total:
        def __init__(self, parts, downward):
            lead = [("p", n_p, bit) for bit in reversed(p_bits)] + [("tensor", n_t, bit) for bit in t_bits]
            lead = lead[: len(lead) - (parts[0].shape[1] == 2)]
            self.rest = parts[0].shape[2:]
            self.dims = lead
            self.parts = [part.reshape((2,) * len(lead) + self.rest) for part in parts]
            order = list(reversed(p_bits)) if downward else p_bits
            self.groups = [order[:1], order[1:], t_bits[:1], t_bits[1:]]

        def sum_of(self, pick):
            total = pick(self.parts[0]).astype(F32)
            for part in self.parts[1:]:
                total = total + pick(part).astype(F32)
            return total

        def cut_one(self, axis, bit):
            at = [d[0] + str(d[2]) for d in self.dims].index(axis + str(bit))
            size = self.dims[at][1]
            self.dims = self.dims[:at] + self.dims[at + 1 :]
            mine = (lax.axis_index(axis) // bit) % 2
            side = lambda which: self.sum_of(lambda part: lax.dynamic_index_in_dim(part, which, at, keepdims=False)).astype(BF16)
            self.live = [side(mine), side(1 - mine)]
            self.route = (axis, [(i, i ^ bit) for i in range(size)])

        def move(self):
            self.parts = [self.live[0], lax.ppermute(self.live[1], *self.route)]
            return self

        def cut(self, group):
            axis = "p" if group < 2 else "tensor"
            for j, bit in enumerate(self.groups[group]):
                if j:
                    self.move()
                self.cut_one(axis, bit)
            return self

    def together(sums, *others):
        lives, others = lax.optimization_barrier(([s.live for s in sums], others))
        for s, live in zip(sums, lives):
            s.live = live
            s.move()
        return others

    du, up_sum = slope_pull(dz, w_down, slope)
    active, du = lax.optimization_barrier((active, du))
    down_keep, down_send = col_grad(active, dz, n_p, n_t)
    down_send, du = lax.optimization_barrier((down_send, du))
    down_recv = swap_cores(down_send)
    up_keep, up_send = row_grad(hl_turned, du, n_p, n_t)
    up_recv = swap_cores(up_send)
    down_sum = Total([down_keep, down_recv], False).cut(0)
    (du,) = together([down_sum], du)
    dm, da, sums_one = mix_pull(du, w_up, dr, normed, inverse, norm_gains)
    dc = dot(da, w_out, NT).astype(BF16)
    mine = lax.dynamic_slice_in_dim(dc, core * own, own, 1)
    other = lax.dynamic_slice_in_dim(dc, (1 - core) * own, own, 1)
    dc_recv = swap_cores(other)
    up_sums = Total([up_keep, up_recv], True).cut(0)
    out_keep, out_send = col_grad(c_own, da, n_p, n_t)
    out_recv = swap_cores(out_send)
    dc_full = by_core(core, mine, dc_recv, 0)
    down_sum.cut(1)
    dc_full, layer_out = together([down_sum, up_sums], dc_full, layer_out)

    first = attend_bwd(0, qkv, context, dc_full, lse, segment, valid, 512, 256)
    out_sum = Total([out_keep, out_recv], False)
    keep, send, sum_first = qkv_grad(x_turned, *first, n_p)
    first_sum = Total([by_core(core, keep, swap_cores(send), 1)], True)
    (dc_full,) = together([down_sum.cut(2), up_sums.cut(1), out_sum.cut(0), first_sum.cut(0)], dc_full)
    second = attend_bwd(1, qkv, context, dc_full, lse, segment, valid, 512, 256)
    (second,) = together([down_sum.cut(3), up_sums.cut(2), out_sum.cut(1), first_sum.cut(1)], second)

    dx_other = swap_cores(input_pull(1 - core, core, (*first, *second), w_qkv))
    dx_mine = input_pull(core, core, (*first, *second), w_qkv, dm)
    dx = (dx_mine + dx_other.astype(F32)).astype(BF16)
    dx, second = lax.optimization_barrier((blocks(dx), second))
    input_grad = give(*dx).astype(F32)
    keep, send, sum_second = qkv_grad(x_turned, *second, n_p)
    second_sum = Total([by_core(core, keep, swap_cores(send), 1)], True).cut(0).move()
    first_sum.cut(2).move()
    up_sums.cut(3).move()
    out_sum.cut(2).move().cut(3).move()
    second_sum.cut(1).move().cut(2).move()
    qv_sum = jnp.concatenate([sum_first, sum_second], axis=1)
    same = lambda part: part
    down_total, up_total, out_total = down_sum.sum_of(same), up_sums.sum_of(same), out_sum.sum_of(same)
    pair = [first_sum.sum_of(same), second_sum.sum_of(same)]
    moved = lax.ppermute(jnp.where(odd == 0, pair[1], pair[0]).astype(BF16), "tensor", [(i, i ^ 1) for i in range(n_t)])
    qkv_total = jnp.where(odd == 0, pair[0], pair[1]) + moved.astype(F32)
    up_total = up_total.transpose(1, 0, 2).reshape(up_weight.shape)
    qkv_total = qkv_total.transpose(0, 2, 1, 3).reshape(qkv_weight.shape)

    qv_pad = lax.dynamic_update_slice(jnp.zeros((2, width), F32), qv_sum[0:2], (0, core * own))
    small = jnp.concatenate(
        [
            jnp.stack([sums_one[0], sums_two[0], sums_one[1], sums_one[2], sums_two[1], sums_two[2]]).reshape(-1),
            qv_pad.reshape(-1),
            up_sum[0],
        ]
    )
    small = small_sum(small.reshape(-1, 128), n_p, n_t).reshape(-1)
    gain_sum = small[: 2 * width].reshape(2, width)
    bias_sum = small[2 * width : 6 * width].reshape(4, width)
    qv_total = lax.dynamic_slice_in_dim(small[6 * width : 8 * width].reshape(2, width), tensor * qv_bias.shape[1], qv_bias.shape[1], 1)
    up_bias_total = lax.dynamic_slice_in_dim(small[8 * width :], tensor * up_bias.shape[0], up_bias.shape[0])
    return (
        layer_out, input_grad, qkv_total, qv_total, out_total, gain_sum, bias_sum, up_total, up_bias_total, down_total,
    )


def solution(mesh):
    dp, tensor = mesh.devices.shape
    split = jax.sharding.Mesh(mesh.devices.reshape(dp // 2, 2, tensor), ("p", "core", "tensor"))
    pc = ("p", "core")
    tokens = P(None, ("p", "core", "tensor"), None)
    return jax.shard_map(
        body,
        mesh=split,
        in_specs=(
            tokens, P(None, pc, None), P(None, pc, None), P(None, pc, "tensor"), P(None, "tensor"), P("tensor", pc),
            P(), P(), P(pc, "tensor"), P("tensor"), P("tensor", pc), tokens,
        ),
        out_specs=(
            tokens, tokens, P(None, pc, "tensor"), P(None, "tensor"), P("tensor", pc), P(), P(), P(pc, "tensor"),
            P("tensor"), P("tensor", pc),
        ),
        check_vma=False,
    )
```

```python
import functools
import math
import jax
import jax.numpy as jnp
from jax import lax
from jax.sharding import PartitionSpec as P
from jax.experimental import pallas as pl
from jax.experimental.pallas import tpu as pltpu

HEAD = 64
PAIR = 2 * HEAD
NEG_FILL = -1e30
F32 = jnp.float32
BF16 = jnp.bfloat16
NT = (((1,), (1,)), ((), ()))
NN = (((1,), (0,)), ((), ()))
TN = (((0,), (0,)), ((), ()))


def dot(a, b, dims=NN, precision=None):
    return lax.dot_general(a, b, dims, preferred_element_type=F32, precision=precision)


def head_lanes(rows, which):
    lane = lax.broadcasted_iota(jnp.int32, (rows, PAIR), 1)
    return (lane < HEAD) if which == 0 else (lane >= HEAD)


def attend_fwd_kernel(bk, lo_ref, hi_ref, pad_ref, q_ref, k_ref, v_ref, qcode_ref, kcode_ref, o_ref, lse_ref, v_turned):
    i = pl.program_id(1)
    bq = q_ref.shape[0]

    @pl.when(i == 0)
    def _():
        v_turned[...] = v_ref[...].T

    q = q_ref[...] * jnp.asarray(0.125, BF16)
    heads = [jnp.where(head_lanes(bq, w), q, jnp.zeros_like(q)) for w in (0, 1)]
    qcode = qcode_ref[...]
    first = i * bq

    def run(diagonal):
        def step(t, carry):
            at = pl.multiple_of(t * bk, bk)
            keys = pl.ds(at, bk)
            k = k_ref[keys, :]
            mask = jnp.tile(kcode_ref[keys, :], (1, bq // 128)) == qcode
            if diagonal:
                gap = lax.broadcasted_iota(jnp.int32, (bk, bq), 0) - lax.broadcasted_iota(jnp.int32, (bk, bq), 1)
                mask = mask | (gap == first - at)
            out = []
            for h in (0, 1):
                top, total, acc = carry[3 * h : 3 * h + 3]
                s = jnp.where(mask, dot(k, heads[h], NT), NEG_FILL)
                new = jnp.maximum(top, jnp.max(s, axis=0, keepdims=True))
                p = jnp.exp(s - new)
                old = jnp.exp(top - new)
                v = v_turned[h * HEAD : (h + 1) * HEAD, keys]
                out += [
                    new,
                    total * old + jnp.sum(p, axis=0, keepdims=True),
                    acc * old + dot(v, p.astype(BF16)),
                ]
            return tuple(out)

        one = (jnp.full((1, bq), NEG_FILL, F32), jnp.zeros((1, bq), F32), jnp.zeros((HEAD, bq), F32))
        ma, la, aa, mb, lb, ab = lax.fori_loop(lo_ref[i], hi_ref[i], step, one + one)
        o_ref[...] = jnp.concatenate([aa / la, ab / lb], axis=0).T.astype(BF16)
        lse_ref[0:1, :] = ma + jnp.log(la)
        lse_ref[1:2, :] = mb + jnp.log(lb)

    pl.when(pad_ref[i] > 0)(lambda: run(True))
    pl.when(pad_ref[i] == 0)(lambda: run(False))


def attend_bwd_kernel(
    bq, lo_ref, hi_ref, pad_ref, q_ref, k_ref, v_ref, c_ref, dc_ref, lse_ref, qcode_ref, kcode_ref,
    dq_ref, dk_ref, dv_ref, dq_acc, delta,
):
    i = pl.program_id(1)
    bk = k_ref.shape[0]
    first = i * bk

    @pl.when(i == 0)
    def _():
        dq_acc[...] = jnp.zeros_like(dq_acc)
        row = lax.broadcasted_iota(jnp.int32, (8, PAIR), 0)
        lane = lax.broadcasted_iota(jnp.int32, (8, PAIR), 1)
        pick = jnp.where(lane // HEAD == row, 1.0, 0.0).astype(F32)
        prod = dc_ref[...].astype(F32) * c_ref[...].astype(F32)
        delta[...] = dot(pick, prod, NT, lax.Precision.HIGHEST)

    k = k_ref[...] * jnp.asarray(0.125, BF16)
    v = v_ref[...]
    k_turned = k.T
    kh = [jnp.where(head_lanes(bk, w), k, jnp.zeros_like(k)) for w in (0, 1)]
    vh = [jnp.where(head_lanes(bk, w), v, jnp.zeros_like(v)) for w in (0, 1)]
    kcode = jnp.tile(kcode_ref[...], (1, bq // 128))

    def run(diagonal):
        def step(t, carry):
            dk, dv = carry
            at = pl.multiple_of(t * bq, bq)
            rows = pl.ds(at, bq)
            q = q_ref[rows, :]
            dc = dc_ref[rows, :]
            mask = kcode == qcode_ref[:, rows]
            if diagonal:
                gap = lax.broadcasted_iota(jnp.int32, (bk, bq), 1) - lax.broadcasted_iota(jnp.int32, (bk, bq), 0)
                mask = mask | (gap == first - at)
            for h in (0, 1):
                s = dot(kh[h], q, NT)
                p = jnp.exp(jnp.where(mask, s - lse_ref[h : h + 1, rows], NEG_FILL))
                dp = dot(vh[h], dc, NT)
                ds = (p * (dp - delta[h : h + 1, rows])).astype(BF16)
                own = head_lanes(bq, h)
                dv = dv + dot(p.astype(BF16), jnp.where(own, dc, jnp.zeros_like(dc)))
                dk = dk + dot(ds, jnp.where(own, q, jnp.zeros_like(q)))
                dq_acc[h * HEAD : (h + 1) * HEAD, rows] += dot(k_turned[h * HEAD : (h + 1) * HEAD, :], ds)
            return dk, dv

        zero = jnp.zeros((bk, PAIR), F32)
        dk, dv = lax.fori_loop(lo_ref[i], hi_ref[i], step, (zero, zero))
        dk_ref[...] = (dk * 0.125).astype(BF16)
        dv_ref[...] = dv.astype(BF16)

    pl.when(pad_ref[i] > 0)(lambda: run(True))
    pl.when(pad_ref[i] == 0)(lambda: run(False))

    @pl.when(i == pl.num_programs(1) - 1)
    def _():
        dq_ref[...] = dq_acc[...].T.astype(BF16)


def block_bounds(segment, valid, block, other):
    length = segment.shape[0]
    blocks = segment.reshape(length // block, block)
    lo = jnp.sum((segment[None, :] < blocks[:, :1]).astype(jnp.int32), axis=1) // other
    hi = (jnp.sum((segment[None, :] <= blocks[:, -1:]).astype(jnp.int32), axis=1) + other - 1) // other
    pad = jnp.sum((valid.reshape(length // block, block) == 0).astype(jnp.int32), axis=1)
    return lo, hi, pad


def attention_codes(segment, valid):
    kcode = jnp.where(valid > 0, segment, -1)
    qcode = segment
    wide = lambda a: jnp.broadcast_to(a[:, None], (a.shape[0], 128))
    return qcode, kcode, wide(qcode), wide(kcode)


def qkv_at(pair, which):
    return pair // 2 * 6 + which * 2 + pair % 2


def attend_fwd(qkv, segment, valid, bq=256, bk=256):
    length, width = qkv.shape
    pairs = width // 3 // PAIR
    lo, hi, pad = block_bounds(segment, valid, bq, bk)
    qcode, kcode, qwide, kwide = attention_codes(segment, valid)
    return pl.pallas_call(
        functools.partial(attend_fwd_kernel, bk),
        grid_spec=pltpu.PrefetchScalarGridSpec(
            num_scalar_prefetch=3,
            grid=(pairs, length // bq),
            in_specs=[
                pl.BlockSpec((bq, PAIR), lambda h, i, *_: (i, qkv_at(h, 0))),
                pl.BlockSpec((length, PAIR), lambda h, i, *_: (0, qkv_at(h, 1))),
                pl.BlockSpec((length, PAIR), lambda h, i, *_: (0, qkv_at(h, 2))),
                pl.BlockSpec((1, bq), lambda h, i, *_: (0, i)),
                pl.BlockSpec((length, 128), lambda h, i, *_: (0, 0)),
            ],
            out_specs=[
                pl.BlockSpec((bq, PAIR), lambda h, i, *_: (i, h)),
                pl.BlockSpec((8, bq), lambda h, i, *_: (h, i)),
            ],
            scratch_shapes=[pltpu.VMEM((PAIR, length), BF16)],
        ),
        out_shape=[
            jax.ShapeDtypeStruct((length, pairs * PAIR), BF16),
            jax.ShapeDtypeStruct((pairs * 8, length), F32),
        ],
        compiler_params=pltpu.CompilerParams(dimension_semantics=("arbitrary", "arbitrary")),
        cost_estimate=pl.CostEstimate(flops=8 * 2 * length * length * PAIR, bytes_accessed=8 * length * width, transcendentals=4 * length * length),
    )(lo, hi, pad, qkv, qkv, qkv, qcode[None, :], kwide)


def attend_bwd(part, qkv, context, context_grad, lse, segment, valid, bq=256, bk=256):
    length, width = qkv.shape
    pairs = width // 6 // PAIR
    base = part * pairs
    lo, hi, pad = block_bounds(segment, valid, bk, bq)
    qcode, kcode, qwide, kwide = attention_codes(segment, valid)
    whole = pl.BlockSpec((length, PAIR), lambda h, i, *_: (0, h))
    piece = pl.BlockSpec((bk, PAIR), lambda h, i, *_: (i, h))
    source = pl.BlockSpec((length, PAIR), lambda h, i, *_: (0, base + h))
    cols = lambda at: pl.BlockSpec((bk, PAIR), lambda h, i, *_: (i, qkv_at(base + h, at)))
    shape = jax.ShapeDtypeStruct((length, pairs * PAIR), BF16)
    return pl.pallas_call(
        functools.partial(attend_bwd_kernel, bq),
        grid_spec=pltpu.PrefetchScalarGridSpec(
            num_scalar_prefetch=3,
            grid=(pairs, length // bk),
            in_specs=[
                pl.BlockSpec((length, PAIR), lambda h, i, *_: (0, qkv_at(base + h, 0))), cols(1), cols(2), source, source,
                pl.BlockSpec((8, length), lambda h, i, *_: (base + h, 0)),
                pl.BlockSpec((1, length), lambda h, i, *_: (0, 0)),
                pl.BlockSpec((bk, 128), lambda h, i, *_: (i, 0)),
            ],
            out_specs=[whole, piece, piece],
            scratch_shapes=[pltpu.VMEM((PAIR, length), F32), pltpu.VMEM((8, length), F32)],
        ),
        out_shape=[shape, shape, shape],
        compiler_params=pltpu.CompilerParams(dimension_semantics=("arbitrary", "arbitrary")),
        cost_estimate=pl.CostEstimate(flops=20 * 2 * length * length * PAIR, bytes_accessed=16 * length * width, transcendentals=4 * length * length),
    )(lo, hi, pad, qkv, qkv, qkv, context, context_grad, lse, qcode[None, :], kwide)


def norm_stats(values):
    center = values - jnp.mean(values, axis=1, keepdims=True)
    inverse = lax.rsqrt(jnp.mean(center * center, axis=1, keepdims=True) + 1e-05)
    return center * inverse, inverse


def norm_pull(incoming, normed, inverse, gain):
    scaled = incoming * gain
    return inverse * (
        scaled - jnp.mean(scaled, axis=1, keepdims=True) - normed * jnp.mean(scaled * normed, axis=1, keepdims=True)
    )


def col_sum(values):
    return jnp.sum(values, axis=0, keepdims=True)


def add_sums(ref, parts):
    @pl.when(pl.program_id(0) == 0)
    def _():
        ref[...] = jnp.zeros_like(ref)

    for at, part in enumerate(parts):
        ref[at : at + 1, :] += col_sum(part)


def mix_kernel(at_ref, x_ref, c_ref, w_ref, bias_ref, gain_ref, hl_ref, turned_ref, n_ref, r_ref):
    mixed = x_ref[...].astype(F32) + dot(c_ref[...], w_ref[...]) + bias_ref[0:1, :]
    normed, inverse = norm_stats(mixed)
    hl = (normed * gain_ref[0:1, :] + bias_ref[1:2, :]).astype(BF16)
    hl_ref[...] = hl
    turned_ref[...] = hl.T
    n_ref[...] = normed
    r_ref[...] = jnp.broadcast_to(inverse, r_ref.shape)


def up_kernel(h_ref, w_ref, bias_ref, g_ref, slope_ref):
    u = dot(h_ref[...], w_ref[...]) + bias_ref[...]
    cdf = 0.5 + 0.5 * lax.erf(u * (1.0 / math.sqrt(2.0)))
    g_ref[...] = (u * cdf).astype(BF16)
    slope_ref[...] = (cdf + u * (jnp.exp(-0.5 * u * u) * (1.0 / math.sqrt(2.0 * math.pi)))).astype(BF16)


def down_kernel(g_ref, w_ref, n_ref, e_ref, bias_ref, gain_ref, out_ref, dr_ref, dz_ref, sum_ref):
    hidden = n_ref[...] * gain_ref[0:1, :] + bias_ref[1:2, :]
    normed, inverse = norm_stats(hidden + dot(g_ref[...], w_ref[...]) + bias_ref[2:3, :])
    out_ref[...] = (normed * gain_ref[1:2, :] + bias_ref[3:4, :]).astype(BF16)
    e = e_ref[...].astype(F32)
    dr = norm_pull(e, normed, inverse, gain_ref[1:2, :])
    dr_ref[...] = dr
    dz_ref[...] = dr.astype(BF16)
    add_sums(sum_ref, (e * normed, dr, e))


def slope_kernel(dz_ref, w_ref, slope_ref, du_ref, sum_ref):
    du = (dot(dz_ref[...], w_ref[...], NT) * slope_ref[...].astype(F32)).astype(BF16)
    du_ref[...] = du

    @pl.when(pl.program_id(1) == 0)
    def _():
        sum_ref[...] = jnp.zeros_like(sum_ref)

    sum_ref[0:1, :] += col_sum(du.astype(F32))


def mix_pull_kernel(du_ref, w_ref, dr_ref, n_ref, r_ref, gain_ref, dm_ref, da_ref, sum_ref):
    dh = dr_ref[...] + dot(du_ref[...], w_ref[...], NT)
    normed = n_ref[...]
    dm = norm_pull(dh, normed, r_ref[:, 0:1], gain_ref[0:1, :])
    dm_ref[...] = dm
    da_ref[...] = dm.astype(BF16)
    add_sums(sum_ref, (dh * normed, dm, dh))


def call(kernel, grid, ins, outs, flops, nbytes, *args):
    return pl.pallas_call(
        kernel,
        grid=grid,
        in_specs=ins,
        out_specs=outs[0],
        out_shape=outs[1],
        compiler_params=pltpu.CompilerParams(dimension_semantics=("arbitrary",) * len(grid)),
        cost_estimate=pl.CostEstimate(flops=flops, bytes_accessed=nbytes, transcendentals=0),
    )(*args)


def rows(block, width):
    return pl.BlockSpec((block, width), lambda i: (i, 0))


def held(shape):
    return pl.BlockSpec(shape, lambda i: (0, 0))


def once(shape):
    return pl.BlockSpec(shape, lambda i: (0, 0), pipeline_mode=pl.Buffered(1))


def sds(shape, dtype=BF16):
    return jax.ShapeDtypeStruct(shape, dtype)


def mix(core_at, x, c, w, biases, gains, block=256):
    n, d = c.shape
    r = lambda width: pl.BlockSpec((block, width), lambda i, at: (i, 0))
    fixed = lambda value: pl.BlockSpec(value.shape, lambda i, at: (0, 0), pipeline_mode=pl.Buffered(1))
    steps = n // block
    return pl.pallas_call(
        mix_kernel,
        grid_spec=pltpu.PrefetchScalarGridSpec(
            num_scalar_prefetch=1,
            grid=(steps,),
            in_specs=[
                pl.BlockSpec((block, d), lambda i, at: (at[0] * steps + i, 0)), r(d), fixed(w), fixed(biases), fixed(gains),
            ],
            out_specs=[r(d), pl.BlockSpec((d, block), lambda i, at: (0, i)), r(d), r(128)],
        ),
        out_shape=[sds((n, d)), sds((d, n)), sds((n, d), F32), sds((n, 128), F32)],
        compiler_params=pltpu.CompilerParams(dimension_semantics=("arbitrary",)),
        cost_estimate=pl.CostEstimate(flops=2 * n * d * d, bytes_accessed=12 * n * d, transcendentals=0),
    )(core_at, x, c, w, biases, gains)


def up(h, w, bias, block=256, cols=1024):
    n, d = h.shape
    f = w.shape[1]
    cols = min(cols, f)
    tile = pl.BlockSpec((block, cols), lambda j, i: (i, j))
    return call(
        up_kernel, (f // cols, n // block),
        [pl.BlockSpec((block, d), lambda j, i: (i, 0)), pl.BlockSpec((d, cols), lambda j, i: (0, j)), pl.BlockSpec((1, cols), lambda j, i: (0, j))],
        ([tile, tile], [sds((n, f)), sds((n, f))]),
        2 * n * d * f, 4 * n * f + 2 * d * f, h, w, bias,
    )


def down(g, w, normed, e, biases, gains, block=256):
    n, f = g.shape
    d = w.shape[1]
    r = functools.partial(rows, block)
    return call(
        down_kernel, (n // block,),
        [r(f), once(w.shape), r(d), r(d), held(biases.shape), held(gains.shape)],
        ([r(d), r(d), r(d), held((8, d))], [sds((n, d)), sds((n, d), F32), sds((n, d)), sds((8, d), F32)]),
        2 * n * d * f, 2 * n * f + 2 * d * f, g, w, normed, e, biases, gains,
    )


def slope_pull(dz, w, slope, block=256, cols=1024):
    n, d = dz.shape
    f = w.shape[0]
    tile = pl.BlockSpec((block, cols), lambda j, i: (i, j))
    return call(
        slope_kernel, (f // cols, n // block),
        [pl.BlockSpec((block, d), lambda j, i: (i, 0)), pl.BlockSpec((cols, d), lambda j, i: (j, 0)), tile],
        ([tile, pl.BlockSpec((8, cols), lambda j, i: (0, j))], [sds((n, f)), sds((8, f), F32)]),
        2 * n * d * f, 4 * n * f + 2 * d * f, dz, w, slope,
    )


def mix_pull(du, w, dr, normed, inverse, gains, block=256):
    n, f = du.shape
    d = w.shape[0]
    r = functools.partial(rows, block)
    return call(
        mix_pull_kernel, (n // block,),
        [r(f), once(w.shape), r(d), r(d), r(128), held(gains.shape)],
        ([r(d), r(d), held((8, d))], [sds((n, d), F32), sds((n, d)), sds((8, d), F32)]),
        2 * n * d * f, 2 * n * f + 2 * d * f, du, w, dr, normed, inverse, gains,
    )


def split_columns(acc, keep_ref, send_ref):
    n_p, c = keep_ref.shape[0], keep_ref.shape[3]
    for bit in (0, 1):

        @pl.when(lax.axis_index("core") == bit)
        def _():
            for p in range(n_p):
                at, to = (2 * p + bit) * c, (2 * p + 1 - bit) * c
                keep_ref[p, 0] = acc[:, at : at + c]
                send_ref[p, 0] = acc[:, to : to + c]


def split_rows(acc, place, keep_ref, send_ref):
    n_p, r = keep_ref.shape[0], keep_ref.shape[-2]
    for bit in (0, 1):

        @pl.when(lax.axis_index("core") == bit)
        def _():
            for p in range(n_p):
                at, to = (2 * p + bit) * r, (2 * p + 1 - bit) * r
                for cb in range(acc.shape[1] // 128):
                    keep_ref[(p, 0) + place + (cb,)] = acc[at : at + r, cb * 128 : cb * 128 + 128]
                    send_ref[(p, 0) + place + (cb,)] = acc[to : to + r, cb * 128 : cb * 128 + 128]


def col_grad_kernel(a_ref, b_ref, keep_ref, send_ref, acc):
    acc[...] = dot(a_ref[...], b_ref[...], TN).astype(BF16)
    split_columns(acc, keep_ref, send_ref)


def row_grad_kernel(a_ref, b_ref, keep_ref, send_ref, acc):
    acc[...] = dot(a_ref[...], b_ref[...]).astype(BF16)
    split_rows(acc, (), keep_ref, send_ref)


def qkv_grad_kernel(x_ref, dq_ref, dk_ref, dv_ref, keep_ref, send_ref, sum_ref, acc):
    for at, ref in enumerate((dq_ref, dk_ref, dv_ref)):
        acc[...] = dot(x_ref[...], ref[...]).astype(BF16)
        split_rows(acc, (at,), keep_ref, send_ref)
    sum_ref[0:1, :] = col_sum(dq_ref[...].astype(F32))
    sum_ref[1:2, :] = col_sum(dv_ref[...].astype(F32))


def grad_call(kernel, grid, ins, outs, scratch, flops, *args):
    return pl.pallas_call(
        kernel,
        grid=grid,
        in_specs=ins,
        out_specs=outs[0],
        out_shape=outs[1],
        scratch_shapes=scratch,
        compiler_params=pltpu.CompilerParams(dimension_semantics=("arbitrary",) * len(grid)),
        cost_estimate=pl.CostEstimate(flops=flops, bytes_accessed=flops // 512, transcendentals=0),
    )(*args)


def col_grad(a, b, n_p, n_t, block=512):
    n, f = a.shape
    d = b.shape[1]
    per_t, c = f // n_t, d // (2 * n_p)
    block = min(block, per_t)
    steps = per_t // block
    spec = pl.BlockSpec((n_p, 1, block, c), lambda i: (0, i // steps, i % steps, 0))
    shape = sds((n_p, n_t, per_t, c))
    return grad_call(
        col_grad_kernel, (f // block,),
        [pl.BlockSpec((n, block), lambda i: (0, i)), once((n, d))],
        ([spec, spec], [shape, shape]), [pltpu.VMEM((block, d), BF16)], 2 * n * f * d, a, b,
    )


def row_grad(a, b, n_p, n_t, block=512):
    d, n = a.shape
    f = b.shape[1]
    per_t, r = f // n_t, d // (2 * n_p)
    steps = per_t // block
    spec = pl.BlockSpec((n_p, 1, block // 128, r, 128), lambda i: (0, i // steps, i % steps, 0, 0))
    shape = sds((n_p, n_t, per_t // 128, r, 128))
    return grad_call(
        row_grad_kernel, (f // block,),
        [once((d, n)), pl.BlockSpec((n, block), lambda i: (0, i))],
        ([spec, spec], [shape, shape]), [pltpu.VMEM((d, block), BF16)], 2 * n * f * d, a, b,
    )


def qkv_grad(x, dq, dk, dv, n_p):
    d, n = x.shape
    f = dq.shape[1]
    r = d // (2 * n_p)
    spec = pl.BlockSpec((n_p, 1, 3, f // 128, r, 128), lambda i: (0, 0, 0, 0, 0, 0))
    shape = sds((n_p, 1, 3, f // 128, r, 128))
    return grad_call(
        qkv_grad_kernel, (1,),
        [held((d, n)), held((n, f)), held((n, f)), held((n, f))],
        ([spec, spec, held((8, f))], [shape, shape, sds((8, f), F32)]),
        [pltpu.VMEM((d, f), BF16)], 6 * n * f * d, x, dq, dk, dv,
    )


def input_pull_kernel(extra, at_ref, *refs):
    parts, w_ref = refs[:6], refs[6]
    c = w_ref.shape[1] // 6
    total = dot(parts[0][...], w_ref[:, :c], NT)
    for j in range(1, 6):
        total = total + dot(parts[j][...], w_ref[:, j * c : (j + 1) * c], NT)
    if extra:
        total = total + refs[7][...]
    refs[-1][...] = total.astype(refs[-1].dtype)


def input_pull(half, core, parts, w, dm=None, block=256):
    n, f = parts[0].shape
    d = w.shape[0]
    steps = n // 2 // block
    cols = pl.BlockSpec((block, f), lambda i, at: (at[0] * steps + i, 0))
    own = pl.BlockSpec((block, d), lambda i, at: (i, 0))
    extra = [] if dm is None else [dm]
    held_w = pl.BlockSpec((d, w.shape[1] // 2), lambda i, at: (0, at[1]), pipeline_mode=pl.Buffered(1))
    return pl.pallas_call(
        functools.partial(input_pull_kernel, len(extra)),
        grid_spec=pltpu.PrefetchScalarGridSpec(
            num_scalar_prefetch=1,
            grid=(steps,),
            in_specs=[cols] * 6 + [held_w] + [own] * len(extra),
            out_specs=own,
        ),
        out_shape=sds((n // 2, d), BF16 if dm is None else F32),
        compiler_params=pltpu.CompilerParams(dimension_semantics=("arbitrary",)),
        cost_estimate=pl.CostEstimate(flops=6 * n * f * d, bytes_accessed=8 * n * d, transcendentals=0),
    )(jnp.stack([half, core]).astype(jnp.int32), *parts, w, *extra)


MESH_ID = pl.DeviceIdType.MESH


def flip(value, bit):
    return value + bit - 2 * bit * ((value // bit) % 2)


def start_kernel(n_p, n_t, kinds, *refs):
    n = len(kinds)
    x_ref, bias_ref, *shards = refs[: n + 2]
    x_out, bias_out, *fulls = refs[n + 2 : 2 * n + 4]
    send_sems, recv_sems, own_sems = refs[2 * n + 4 :]
    p, core, t = lax.axis_index("p"), lax.axis_index("core"), lax.axis_index("tensor")
    me = 2 * p + core
    bits = [1 << s for s in range(n_p.bit_length() - 1)]
    column = [{"tensor": lax.rem(t + r, n_t)} for r in range(1, n_t)]
    across = [{"core": 1 - core, "tensor": lax.rem(t + r, n_t)} for r in range(n_t)]
    plane = [{"p": flip(p, bit)} for bit in bits]
    barrier = pltpu.get_barrier_semaphore()
    for peer in column + across + plane:
        pl.semaphore_signal(barrier, inc=1, device_id=peer, device_id_type=MESH_ID)
    pl.semaphore_wait(barrier, len(column + across + plane))

    used = [0, 0]

    def group():
        used[0] += 1
        return used[0] - 1

    def send(source, target, at, peer):
        pltpu.make_async_remote_copy(
            src_ref=source, dst_ref=target, send_sem=send_sems.at[at], recv_sem=recv_sems.at[at],
            device_id=peer, device_id_type=MESH_ID,
        ).start()

    def arrived(view, at):
        pltpu.make_async_copy(view, view, recv_sems.at[at]).wait()

    def left(view, at):
        pltpu.make_async_copy(view, view, send_sems.at[at]).wait()

    def keep(source, target):
        used[1] += 1
        copy = pltpu.make_async_copy(source, target, own_sems.at[used[1] - 1])
        copy.start()
        return copy

    def slab(i, d, half):
        full, kind = fulls[i], kinds[i]
        if kind == "rows":
            depth, wide = shards[i].shape[-2], full.shape[1] // 2
            return full.at[pl.ds(pl.multiple_of(d * depth, depth), depth), pl.ds(half * wide, wide)]
        depth, tall = shards[i].shape[-1], full.shape[0] // 2
        return full.at[pl.ds(half * tall, tall), pl.ds(pl.multiple_of(d * depth, depth), depth)]

    def slabs(i, count, half):
        full, kind = fulls[i], kinds[i]
        if kind == "rows":
            wide = full.shape[1] // 2
            return full.at[pl.ds(0, count * shards[i].shape[-2]), pl.ds(half * wide, wide)]
        tall = full.shape[0] // 2
        return full.at[pl.ds(half * tall, tall), pl.ds(0, count * shards[i].shape[-1])]

    def places(i, t):
        shard, full = shards[i], fulls[i]
        if kinds[i] == "columns":
            tall, depth = shard.shape
            return [(shard, full.at[pl.ds(pl.multiple_of(t * tall, tall), tall), pl.ds(pl.multiple_of(me * depth, depth), depth)])]
        depth, wide = shard.shape[-2:]
        rows_at = pl.ds(pl.multiple_of(me * depth, depth), depth)
        if len(shard.shape) == 2:
            return [(shard, full.at[rows_at, pl.ds(pl.multiple_of(t * wide, wide), wide)])]
        count = shard.shape[0]
        return [
            (shard.at[w], full.at[rows_at, pl.ds(pl.multiple_of((t * count + w) * wide, wide), wide)])
            for w in range(count)
        ]

    def shares(i, count):
        shard, full = shards[i], fulls[i]
        if kinds[i] == "columns":
            return full.at[pl.ds(0, count * shard.shape[0]), pl.ds(0, shard.shape[1])]
        wide = math.prod(shard.shape) // shard.shape[-2]
        return full.at[pl.ds(0, shard.shape[-2]), pl.ds(0, count * wide)]

    hops = n_t - 1
    own = [[keep(source, target) for source, target in places(i, t)] for i in range(n)]
    right, left_to = {"tensor": lax.rem(t + 1, n_t)}, {"tensor": lax.rem(t + n_t - 1, n_t)}
    line = [[(group(), group()) for _ in range(hops)] for _ in range(n)]

    def hop(i, s):
        to_right, to_left = line[i][s]

        @pl.when(jnp.logical_and(t + 1 < n_t, t >= s))
        def _():
            for source, target in places(i, t - s):
                send(source if s == 0 else target, target, to_right, right)

        @pl.when(jnp.logical_and(t >= 1, t + s < n_t))
        def _():
            for source, target in places(i, t + s):
                send(source if s == 0 else target, target, to_left, left_to)

    def hop_arrived(i, s):
        to_right, to_left = line[i][s]
        pl.when(t >= s + 1)(lambda: arrived(shares(i, 1), to_right))
        pl.when(t + s + 1 < n_t)(lambda: arrived(shares(i, 1), to_left))

    def hop_left(i, s):
        to_right, to_left = line[i][s]
        pl.when(jnp.logical_and(t + 1 < n_t, t >= s))(lambda: left(shares(i, 1), to_right))
        pl.when(jnp.logical_and(t >= 1, t + s < n_t))(lambda: left(shares(i, 1), to_left))

    for i in range(n):
        hop(i, 0)
    bias_at = group()
    bias_own = keep(bias_ref, bias_out.at[t])
    for peer in column:
        send(bias_ref, bias_out.at[t], bias_at, peer)

    held = x_ref.shape[1]
    odd = t % 2
    x_rows = x_out.at[pl.ds(pl.multiple_of(t * held, held), held), :]
    x_at = [group(), group()]
    stays = core == t // 2
    peer_a = {"core": t // 2, "tensor": 2 * core + odd}
    peer_b = {"core": t // 2, "tensor": 2 * core + 1 - odd}

    pl.when(jnp.logical_not(stays))(lambda: send(x_ref.at[odd], x_rows, x_at[0], peer_a))
    x_own = pltpu.make_async_copy(x_ref.at[odd], x_rows, own_sems.at[used[1]])
    used[1] += 1
    pl.when(stays)(x_own.start)
    send(x_ref.at[1 - odd], x_rows, x_at[1], peer_b)

    partner = {"core": 1 - core}
    passes = []

    def forward(i, masks, half):
        at = group()
        guard = i == 0

        def go():
            for mask in masks:
                d = 2 * mask + core
                send(slab(i, d, half), slab(i, d, half), at, partner)

        if guard:
            pl.when(core == 1 - half)(go)
        else:
            go()
        passes.append((i, len(masks), half, at))

    states = {}

    def stage(i, s):
        if s == 0:
            hop_arrived(i, hops - 1)
            states[i] = {}
            for half in (0, 1):
                states[i][half] = ([p], None)
        else:
            for half in (0, 1):
                masks, at = states[i][half]
                arrived(slabs(i, len(masks), half), at)
                bit = bits[s - 1] if half == 0 else bits[-s]
                states[i][half] = (masks + [flip(m, bit) for m in masks], None)
        for half in (0, 1):
            masks, _ = states[i][half]
            if s < len(bits):
                at = group()
                bit = bits[s] if half == 0 else bits[-s - 1]
                for m in masks:
                    d = 2 * m + core
                    send(slab(i, d, half), slab(i, d, half), at, {"p": flip(p, bit)})
                states[i][half] = (masks, at)
                finish.append((i, len(masks), half, at))
            fresh = masks if s == 0 else masks[len(masks) // 2 :]
            forward(i, fresh, half)

    finish = []
    for step in range(n + hops - 1 + len(bits)):
        for i in range(n):
            at = step - i
            if 0 <= at < hops - 1:
                if at == 0:
                    for copy in own[i]:
                        copy.wait()
                hop_arrived(i, at)
                hop(i, at + 1)
            elif 0 <= at - (hops - 1) <= len(bits):
                stage(i, at - (hops - 1))

    pl.when(jnp.logical_not(stays))(lambda: arrived(x_rows, x_at[0]))
    pl.when(stays)(x_own.wait)
    arrived(x_rows, x_at[1])
    half_rows = x_out.at[pl.ds(pl.multiple_of(core * 2 * held, 2 * held), 2 * held), :]
    x_pass = group()
    send(half_rows, half_rows, x_pass, partner)
    bias_own.wait()
    arrived(bias_out.at[pl.ds(0, n_t - 1)], bias_at)
    for i, count, half, at in passes:
        if i == 0:
            pl.when(core == half)(functools.partial(arrived, slabs(i, count, half), at))
        else:
            arrived(slabs(i, count, half), at)
    arrived(half_rows, x_pass)
    left(half_rows, x_pass)
    for i, count, half, at in passes:
        if i == 0:
            pl.when(core == 1 - half)(functools.partial(left, slabs(i, count, half), at))
        else:
            left(slabs(i, count, half), at)
    for i, count, half, at in finish:
        left(slabs(i, count, half), at)
    for i in range(n):
        for s in range(hops):
            hop_left(i, s)
    left(bias_out.at[pl.ds(0, n_t - 1)], bias_at)
    pl.when(jnp.logical_not(stays))(lambda: left(x_rows, x_at[0]))
    left(x_rows, x_at[1])


def start_gather(x, bias, shards, kinds, n_p, n_t):
    n_dp = 2 * n_p
    fulls = []
    for shard, kind in zip(shards, kinds):
        if kind == "columns":
            fulls.append(sds((shard.shape[0] * n_t, shard.shape[1] * n_dp)))
        else:
            fulls.append(sds((shard.shape[-2] * n_dp, math.prod(shard.shape) // shard.shape[-2] * n_t)))
    bits = n_p.bit_length() - 1
    count = len(shards) * (2 * (n_t - 1) + 2 * bits + 2 * (bits + 1)) + 4
    vmem, away = pl.BlockSpec(memory_space=pltpu.VMEM), pl.BlockSpec(memory_space=pl.ANY)
    return pl.pallas_call(
        functools.partial(start_kernel, n_p, n_t, kinds),
        out_shape=[sds((n_t * x.shape[1], x.shape[2])), sds((n_t,) + bias.shape, F32)] + fulls,
        in_specs=[vmem] * (2 + len(shards)),
        out_specs=[away] * (2 + len(shards)),
        scratch_shapes=[
            pltpu.SemaphoreType.DMA((count,)), pltpu.SemaphoreType.DMA((count,)), pltpu.SemaphoreType.DMA((10,)),
        ],
        compiler_params=pltpu.CompilerParams(collective_id=1, has_side_effects=True),
    )(x, bias, *shards)


def project_kernel(core_ref, x_ref, w_ref, bias_ref, out_ref, turned_ref):
    turned_ref[...] = x_ref[...].T
    out_ref[...] = (dot(x_ref[...], w_ref[...]) + bias_ref[...]).astype(BF16)


def project(core_at, x, w, bias, block=256):
    n, d = x.shape
    f = w.shape[1] // 2
    return pl.pallas_call(
        project_kernel,
        grid_spec=pltpu.PrefetchScalarGridSpec(
            num_scalar_prefetch=1,
            grid=(n // block,),
            in_specs=[
                pl.BlockSpec((block, d), lambda i, at: (i, 0)),
                pl.BlockSpec((d, f), lambda i, at: (0, at[0]), pipeline_mode=pl.Buffered(1)),
                pl.BlockSpec((1, f), lambda i, at: (0, 0)),
            ],
            out_specs=[pl.BlockSpec((block, f), lambda i, at: (i, 0)), pl.BlockSpec((d, block), lambda i, at: (0, i))],
        ),
        out_shape=[sds((n, f)), sds((d, n))],
        compiler_params=pltpu.CompilerParams(dimension_semantics=("arbitrary",)),
        cost_estimate=pl.CostEstimate(flops=2 * n * d * f, bytes_accessed=4 * n * d + 2 * n * f, transcendentals=0),
    )(core_at, x, w, bias)


def finish_kernel(n_p, n_t, *refs):
    dx, keep2, send2, first_a, first_b, up_a, up_b, out_a, out_b, small = refs[:10]
    given, qkv_out, up_out, out_out, small_out = refs[10:15]
    recv2, pair1, pair2, slot1, slot2, last, last_slot, up_cur, up_slot, out_cur, out_slot = refs[15:26]
    out_next, out_last, small_cur, small_slot = refs[26:30]
    bits = [n_p >> (s + 1) for s in range(n_p.bit_length() - 1)]
    curs, slots = refs[30 : 30 + len(bits)], refs[30 + len(bits) : 30 + 2 * len(bits)]
    send_sems, recv_sems = refs[-2:]
    p, core, t = lax.axis_index("p"), lax.axis_index("core"), lax.axis_index("tensor")
    partner = {"core": 1 - core}
    column = [{"tensor": lax.rem(t + r, n_t)} for r in range(1, n_t)]
    column += [{"core": 1 - core, "tensor": lax.rem(t + r, n_t)} for r in range(n_t)]
    plane = [{"p": flip(p, bit)} for bit in bits]
    line = {bit: {"tensor": flip(t, bit)} for bit in (2, 1)}
    barrier = pltpu.get_barrier_semaphore()
    for peer in column + plane:
        pl.semaphore_signal(barrier, inc=1, device_id=peer, device_id_type=MESH_ID)
    pl.semaphore_wait(barrier, len(column + plane))

    used = [0]

    def send(source, target, peer):
        at = used[0]
        used[0] += 1
        copy = pltpu.make_async_remote_copy(
            src_ref=source, dst_ref=target, send_sem=send_sems.at[at], recv_sem=recv_sems.at[at],
            device_id=peer, device_id_type=MESH_ID,
        )
        return copy

    def go(source, target, peer):
        copy = send(source, target, peer)
        copy.start()
        return copy

    def plus(a, b):
        return (a.astype(F32) + b.astype(F32)).astype(BF16)

    u, odd = t // 2, t % 2
    swap = go(send2, recv2, partner)
    for at in (0, 1):
        pair1[at] = plus(first_a[at], first_b[at])
    first_move = go(pair1.at[1 - u], slot1, line[2])
    for at in range(4):
        out_cur[at] = plus(out_a[at], out_b[at])
    out_move = go(out_cur.at[pl.ds(2 * (1 - u), 2)], out_slot, line[2])
    for at in (0, 1):
        up_cur[at] = plus(up_a[at], up_b[at])
    up_move = go(up_cur.at[1 - odd], up_slot, line[1])

    held = given.shape[1]
    stays = core == u
    rows_a = dx.at[pl.ds(pl.multiple_of(odd * held, held), held), :]
    rows_b = dx.at[pl.ds(pl.multiple_of((1 - odd) * held, held), held), :]
    give_a = send(rows_a, given.at[odd], {"core": u, "tensor": 2 * core + odd})
    pl.when(jnp.logical_not(stays))(give_a.start)

    @pl.when(stays)
    def _():
        given[odd] = dx[pl.ds(pl.multiple_of(odd * held, held), held), :]

    moves = []
    small_cur[0] = small[...]
    peers = [partner] + plane
    for at, peer in enumerate(peers):
        copy = go(small_cur.at[at], small_slot.at[at], peer)
        copy.wait()
        small_cur[at + 1] = small_cur[at] + small_slot[at]

    swap.wait()
    source = [keep2, recv2]
    for s, bit in enumerate(bits):
        mine = (p // bit) % 2
        copies = [
            go(source[j].at[pl.ds((1 - mine) * bit, bit)], slots[s].at[j], plane[s]) for j in (0, 1)
        ]
        for j, copy in enumerate(copies):
            copy.wait()
            if bit == 1:
                pair2[core if j == 0 else 1 - core] = plus(source[j][mine], slots[s][j, 0])
            else:
                for at in range(bit):
                    curs[s][j, at] = plus(source[j][mine * bit + at], slots[s][j, at])
        source = [curs[s].at[0], curs[s].at[1]]
    second_move = go(pair2.at[1 - u], slot2, line[2])
    give_b = go(rows_b, given.at[odd], {"core": u, "tensor": 2 * core + 1 - odd})

    up_move.wait()
    up_out[...] = up_cur[odd].astype(F32) + up_slot[...].astype(F32)
    out_move.wait()
    for at in (0, 1):
        out_next[at] = plus(out_cur[2 * u + at], out_slot[at])
    out_move = go(out_next.at[1 - odd], out_last, line[1])
    first_move.wait()
    last[0] = plus(pair1[u], slot1[...])
    second_move.wait()
    last[1] = plus(pair2[u], slot2[...])
    last_move = go(last.at[1 - odd], last_slot, line[1])
    for bit in (2, 1):
        at = len(peers)
        copy = go(small_cur.at[at], small_slot.at[at], line[bit])
        copy.wait()
        peers.append(None)
        if bit == 1:
            small_out[...] = small_cur[at] + small_slot[at]
        else:
            small_cur[at + 1] = small_cur[at] + small_slot[at]
    out_move.wait()
    out_out[...] = out_next[odd].astype(F32) + out_last[...].astype(F32)
    last_move.wait()
    qkv_out[...] = last[odd].astype(F32) + last_slot[...].astype(F32)
    pl.when(jnp.logical_not(stays))(give_a.wait)
    give_b.wait()


def finish(n_p, n_t, dx, keep2, send2, first, up_, out_, small):
    rows_, lanes = keep2.shape[1:]
    bits = n_p.bit_length() - 1
    steps = 1 + bits + 2
    block = lambda count, like: pltpu.VMEM((count,) + like.shape[1:], BF16)
    one = lambda like: pltpu.VMEM(like.shape[1:], BF16)
    sizes = [n_p >> (s + 1) for s in range(bits)]
    halves = [pltpu.VMEM((2, size, rows_, lanes), BF16) for size in sizes]
    vmem = pl.BlockSpec(memory_space=pltpu.VMEM)
    count = 9 + steps + 2 * bits
    return pl.pallas_call(
        functools.partial(finish_kernel, n_p, n_t),
        out_shape=[
            sds((2, dx.shape[0] // 2, dx.shape[1])), sds((rows_, lanes), F32), sds(up_[0].shape[1:], F32),
            sds(out_[0].shape[1:], F32), sds(small.shape, F32),
        ],
        in_specs=[vmem] * 10,
        out_specs=[vmem] * 5,
        scratch_shapes=[
            block(n_p, keep2), block(2, keep2), block(2, keep2), one(keep2), one(keep2), block(2, keep2), one(keep2),
            block(2, up_[0]), one(up_[0]), block(4, out_[0]), block(2, out_[0]), block(2, out_[0]), one(out_[0]),
            pltpu.VMEM((steps,) + small.shape, F32), pltpu.VMEM((steps,) + small.shape, F32),
            *halves, *halves,
            pltpu.SemaphoreType.DMA((count,)), pltpu.SemaphoreType.DMA((count,)),
        ],
        compiler_params=pltpu.CompilerParams(collective_id=0, has_side_effects=True),
    )(dx, keep2, send2, *first, *up_, *out_, small)


def swap_cores(value):
    return lax.ppermute(value, "core", [(0, 1), (1, 0)])


def column_routes(tensor_size):
    first, second = [], []
    for core in range(2):
        for t in range(tensor_size):
            at = core * tensor_size + t
            first.append((at, (t >> 1) * tensor_size + 2 * core + (t & 1)))
            second.append((at, (t >> 1) * tensor_size + 2 * core + 1 - (t & 1)))
    return first, second


def back(route):
    return [(b, a) for a, b in route]


def by_core(core, mine, other, axis):
    return jnp.where(
        core == 0, jnp.concatenate([mine, other], axis=axis), jnp.concatenate([other, mine], axis=axis)
    )


def body(
    inputs, segment_ids, token_valid, qkv_weight, qv_bias, out_weight, norm_gains, row_biases,
    up_weight, up_bias, down_weight, out_grad,
):
    COL = ("core", "tensor")
    ALL = ("p", "core", "tensor")
    core, tensor = lax.axis_index("core"), lax.axis_index("tensor")
    n_p, n_t = lax.axis_size("p"), lax.axis_size("tensor")
    n_dp = 2 * n_p
    micro, held_rows, width = inputs.shape
    assert micro == 2 and n_t == 4
    odd = tensor & 1
    route_a, route_b = column_routes(n_t)

    def bring(value):
        a = lax.ppermute(value[odd], COL, route_a)
        b = lax.ppermute(value[1 - odd], COL, route_b)
        return jnp.where(odd == 0, jnp.concatenate([a, b]), jnp.concatenate([b, a]))

    def blocks(value):
        return [lax.dynamic_slice_in_dim(value, at * held_rows, held_rows) for at in (odd, 1 - odd)]

    def give(a, b):
        a, b = lax.ppermute(a, COL, back(route_a)), lax.ppermute(b, COL, back(route_b))
        return jnp.where(odd == 0, jnp.stack([a, b]), jnp.stack([b, a]))

    def gathered(weight):
        got = lax.all_gather(weight, ALL, axis=0, tiled=False)
        return got.reshape((n_dp, n_t) + weight.shape)

    labels = jnp.stack([segment_ids[:, 0], token_valid[:, 0]], axis=1)[odd]
    labels = jnp.where((tensor >> 1) == core, labels, swap_cores(labels))
    segment, valid = labels[0], labels[1]

    shards, kinds = [qkv_weight, up_weight], ["rows", "rows"]
    wide = out_weight.shape[1] % 128 == 0
    if wide:
        shards, kinds = [qkv_weight, out_weight, up_weight, down_weight], ["rows", "columns", "rows", "columns"]
    local_bias = jnp.concatenate([qv_bias.reshape(-1), up_bias]).reshape(-1, 128)
    x_full, bias_all, *fulls = start_gather(inputs, local_bias, shards, kinds, n_p, n_t)
    if wide:
        w_qkv, w_out, w_up, w_down = fulls
    else:
        w_qkv, w_up = fulls
        w_out = gathered(out_weight).transpose(1, 2, 0, 3).reshape(-1, width)
        w_down = gathered(down_weight).transpose(1, 2, 0, 3).reshape(-1, width)
    out_grad, x_full = lax.optimization_barrier((out_grad, x_full))
    rows = x_full.shape[0] // 2
    own = w_qkv.shape[1] // 6
    bias_all = bias_all.reshape(n_t, -1)
    n_qv = qv_bias.size
    up_bias_all = bias_all[:, n_qv:].reshape(1, -1)
    qv_own = lax.dynamic_slice_in_dim(bias_all[:, :n_qv], 2 * core, 2).reshape(2, 2, -1)
    bias = jnp.stack([qv_own[:, 0], jnp.zeros_like(qv_own[:, 0]), qv_own[:, 1]], axis=1).reshape(1, -1)
    core_at = jnp.reshape(core, (1,)).astype(jnp.int32)
    qkv, x_turned = project(core_at, x_full, w_qkv, bias)
    context, lse = attend_fwd(qkv, segment, valid, 512, 512)
    mine = lax.dynamic_slice_in_dim(context, core * rows, rows)
    other = lax.dynamic_slice_in_dim(context, (1 - core) * rows, rows)
    c_own = by_core(core, mine, swap_cores(other), 1)
    hl, hl_turned, normed, inverse = mix(core_at, x_full, c_own, w_out, row_biases, norm_gains)
    active, slope = up(hl, w_up, up_bias_all)
    grad_own = bring(out_grad)
    layer, dr, dz, sums_two = down(active, w_down, normed, grad_own, row_biases, norm_gains)
    layer_out = give(*blocks(layer))

    p_bits = [1 << s for s in range(n_p.bit_length() - 1)]
    t_bits = [2, 1]

    class Total:
        def __init__(self, parts, downward):
            lead = [("p", n_p, bit) for bit in reversed(p_bits)] + [("tensor", n_t, bit) for bit in t_bits]
            lead = lead[: len(lead) - (parts[0].shape[1] == 2)]
            self.rest = parts[0].shape[2:]
            self.dims = lead
            self.parts = [part.reshape((2,) * len(lead) + self.rest) for part in parts]
            order = list(reversed(p_bits)) if downward else p_bits
            self.groups = [order[:1], order[1:], t_bits[:1], t_bits[1:]]

        def sum_of(self, pick):
            total = pick(self.parts[0]).astype(F32)
            for part in self.parts[1:]:
                total = total + pick(part).astype(F32)
            return total

        def cut_one(self, axis, bit):
            at = [d[0] + str(d[2]) for d in self.dims].index(axis + str(bit))
            size = self.dims[at][1]
            self.dims = self.dims[:at] + self.dims[at + 1 :]
            mine = (lax.axis_index(axis) // bit) % 2
            side = lambda which: self.sum_of(lambda part: lax.dynamic_index_in_dim(part, which, at, keepdims=False)).astype(BF16)
            self.live = [side(mine), side(1 - mine)]
            self.route = (axis, [(i, i ^ bit) for i in range(size)])

        def move(self):
            self.parts = [self.live[0], lax.ppermute(self.live[1], *self.route)]
            return self

        def cut(self, group):
            axis = "p" if group < 2 else "tensor"
            for j, bit in enumerate(self.groups[group]):
                if j:
                    self.move()
                self.cut_one(axis, bit)
            return self

    def together(sums, *others):
        lives, others = lax.optimization_barrier(([s.live for s in sums], others))
        for s, live in zip(sums, lives):
            s.live = live
            s.move()
        return others

    du, up_sum = slope_pull(dz, w_down, slope)
    active, du = lax.optimization_barrier((active, du))
    down_keep, down_send = col_grad(active, dz, n_p, n_t)
    down_send, du = lax.optimization_barrier((down_send, du))
    down_recv = swap_cores(down_send)
    up_keep, up_send = row_grad(hl_turned, du, n_p, n_t)
    up_recv = swap_cores(up_send)
    down_sum = Total([down_keep, down_recv], False).cut(0)
    (du,) = together([down_sum], du)
    dm, da, sums_one = mix_pull(du, w_up, dr, normed, inverse, norm_gains)
    dc = dot(da, w_out, NT).astype(BF16)
    mine = lax.dynamic_slice_in_dim(dc, core * own, own, 1)
    other = lax.dynamic_slice_in_dim(dc, (1 - core) * own, own, 1)
    dc_recv = swap_cores(other)
    up_sums = Total([up_keep, up_recv], True).cut(0)
    out_keep, out_send = col_grad(c_own, da, n_p, n_t)
    out_recv = swap_cores(out_send)
    dc_full = by_core(core, mine, dc_recv, 0)
    down_sum.cut(1)
    dc_full, layer_out = together([down_sum, up_sums], dc_full, layer_out)

    first = attend_bwd(0, qkv, context, dc_full, lse, segment, valid, 512, 256)
    out_sum = Total([out_keep, out_recv], False)
    keep, send, sum_first = qkv_grad(x_turned, *first, n_p)
    first_sum = Total([by_core(core, keep, swap_cores(send), 1)], True)
    (dc_full,) = together([down_sum.cut(2), up_sums.cut(1), out_sum.cut(0), first_sum.cut(0)], dc_full)
    second = attend_bwd(1, qkv, context, dc_full, lse, segment, valid, 512, 256)
    (second,) = together([down_sum.cut(3), up_sums.cut(2), out_sum.cut(1), first_sum.cut(1)], second)

    dx_other = swap_cores(input_pull(1 - core, core, (*first, *second), w_qkv))
    dx_mine = input_pull(core, core, (*first, *second), w_qkv, dm)
    dx = (dx_mine + dx_other.astype(F32)).astype(BF16)
    keep, send, sum_second = qkv_grad(x_turned, *second, n_p)
    qv_sum = jnp.concatenate([sum_first, sum_second], axis=1)
    down_total = down_sum.sum_of(lambda part: part)
    qv_pad = lax.dynamic_update_slice(jnp.zeros((2, width), F32), qv_sum[0:2], (0, core * own))
    small = jnp.concatenate(
        [
            jnp.stack([sums_one[0], sums_two[0], sums_one[1], sums_one[2], sums_two[1], sums_two[2]]).reshape(-1),
            qv_pad.reshape(-1),
            up_sum[0],
        ]
    )
    rows_of = lambda part, count: part.reshape(count, -1, part.shape[-1])
    given, qkv_total, up_total, out_total, small = finish(
        n_p, n_t, dx, rows_of(keep, n_p), rows_of(send, n_p), [rows_of(part, 2) for part in first_sum.parts],
        [rows_of(part, 2) for part in up_sums.parts], [rows_of(part, 4) for part in out_sum.parts], small.reshape(-1, 128),
    )
    input_grad = given.astype(F32)
    small = small.reshape(-1)
    up_total = up_total.reshape(up_sums.rest).transpose(1, 0, 2).reshape(up_weight.shape)
    qkv_total = qkv_total.reshape(first_sum.rest).transpose(0, 2, 1, 3).reshape(qkv_weight.shape)
    gain_sum = small[: 2 * width].reshape(2, width)
    bias_sum = small[2 * width : 6 * width].reshape(4, width)
    qv_total = lax.dynamic_slice_in_dim(small[6 * width : 8 * width].reshape(2, width), tensor * qv_bias.shape[1], qv_bias.shape[1], 1)
    up_bias_total = lax.dynamic_slice_in_dim(small[8 * width :], tensor * up_bias.shape[0], up_bias.shape[0])
    return (
        layer_out, input_grad, qkv_total, qv_total, out_total, gain_sum, bias_sum, up_total, up_bias_total, down_total,
    )


def solution(mesh):
    dp, tensor = mesh.devices.shape
    split = jax.sharding.Mesh(mesh.devices.reshape(dp // 2, 2, tensor), ("p", "core", "tensor"))
    pc = ("p", "core")
    tokens = P(None, ("p", "core", "tensor"), None)
    return jax.shard_map(
        body,
        mesh=split,
        in_specs=(
            tokens, P(None, pc, None), P(None, pc, None), P(None, pc, "tensor"), P(None, "tensor"), P("tensor", pc),
            P(), P(), P(pc, "tensor"), P("tensor"), P("tensor", pc), tokens,
        ),
        out_specs=(
            tokens, tokens, P(None, pc, "tensor"), P(None, "tensor"), P("tensor", pc), P(), P(), P(pc, "tensor"),
            P("tensor"), P("tensor", pc),
        ),
        check_vma=False,
    )
```

```python
import functools
import math
import jax
import jax.numpy as jnp
from jax import lax
from jax.sharding import PartitionSpec as P
from jax.experimental import pallas as pl
from jax.experimental.pallas import tpu as pltpu

HEAD = 64
PAIR = 2 * HEAD
NEG_FILL = -1e30
F32 = jnp.float32
BF16 = jnp.bfloat16
NT = (((1,), (1,)), ((), ()))
NN = (((1,), (0,)), ((), ()))
TN = (((0,), (0,)), ((), ()))


def dot(a, b, dims=NN, precision=None):
    return lax.dot_general(a, b, dims, preferred_element_type=F32, precision=precision)


def head_lanes(rows, which):
    lane = lax.broadcasted_iota(jnp.int32, (rows, PAIR), 1)
    return (lane < HEAD) if which == 0 else (lane >= HEAD)


def attend_fwd_kernel(bk, lo_ref, hi_ref, pad_ref, q_ref, k_ref, v_ref, qcode_ref, kcode_ref, o_ref, lse_ref, v_turned):
    i = pl.program_id(1)
    bq = q_ref.shape[0]

    @pl.when(i == 0)
    def _():
        v_turned[...] = v_ref[...].T

    q = q_ref[...] * jnp.asarray(0.125, BF16)
    heads = [jnp.where(head_lanes(bq, w), q, jnp.zeros_like(q)) for w in (0, 1)]
    qcode = qcode_ref[...]
    first = i * bq

    def run(diagonal):
        def step(t, carry):
            at = pl.multiple_of(t * bk, bk)
            keys = pl.ds(at, bk)
            k = k_ref[keys, :]
            mask = jnp.tile(kcode_ref[keys, :], (1, bq // 128)) == qcode
            if diagonal:
                gap = lax.broadcasted_iota(jnp.int32, (bk, bq), 0) - lax.broadcasted_iota(jnp.int32, (bk, bq), 1)
                mask = mask | (gap == first - at)
            out = []
            for h in (0, 1):
                top, total, acc = carry[3 * h : 3 * h + 3]
                s = jnp.where(mask, dot(k, heads[h], NT), NEG_FILL)
                new = jnp.maximum(top, jnp.max(s, axis=0, keepdims=True))
                p = jnp.exp(s - new)
                old = jnp.exp(top - new)
                v = v_turned[h * HEAD : (h + 1) * HEAD, keys]
                out += [
                    new,
                    total * old + jnp.sum(p, axis=0, keepdims=True),
                    acc * old + dot(v, p.astype(BF16)),
                ]
            return tuple(out)

        one = (jnp.full((1, bq), NEG_FILL, F32), jnp.zeros((1, bq), F32), jnp.zeros((HEAD, bq), F32))
        ma, la, aa, mb, lb, ab = lax.fori_loop(lo_ref[i], hi_ref[i], step, one + one)
        o_ref[...] = jnp.concatenate([aa / la, ab / lb], axis=0).T.astype(BF16)
        lse_ref[0:1, :] = ma + jnp.log(la)
        lse_ref[1:2, :] = mb + jnp.log(lb)

    pl.when(pad_ref[i] > 0)(lambda: run(True))
    pl.when(pad_ref[i] == 0)(lambda: run(False))


def attend_bwd_kernel(
    bq, lo_ref, hi_ref, pad_ref, q_ref, k_ref, v_ref, c_ref, dc_ref, lse_ref, qcode_ref, kcode_ref,
    dq_ref, dk_ref, dv_ref, dq_acc, delta,
):
    i = pl.program_id(1)
    bk = k_ref.shape[0]
    first = i * bk

    @pl.when(i == 0)
    def _():
        dq_acc[...] = jnp.zeros_like(dq_acc)
        row = lax.broadcasted_iota(jnp.int32, (8, PAIR), 0)
        lane = lax.broadcasted_iota(jnp.int32, (8, PAIR), 1)
        pick = jnp.where(lane // HEAD == row, 1.0, 0.0).astype(F32)
        prod = dc_ref[...].astype(F32) * c_ref[...].astype(F32)
        delta[...] = dot(pick, prod, NT, lax.Precision.HIGHEST)

    k = k_ref[...] * jnp.asarray(0.125, BF16)
    v = v_ref[...]
    k_turned = k.T
    kh = [jnp.where(head_lanes(bk, w), k, jnp.zeros_like(k)) for w in (0, 1)]
    vh = [jnp.where(head_lanes(bk, w), v, jnp.zeros_like(v)) for w in (0, 1)]
    kcode = jnp.tile(kcode_ref[...], (1, bq // 128))

    def run(diagonal):
        def step(t, carry):
            dk, dv = carry
            at = pl.multiple_of(t * bq, bq)
            rows = pl.ds(at, bq)
            q = q_ref[rows, :]
            dc = dc_ref[rows, :]
            mask = kcode == qcode_ref[:, rows]
            if diagonal:
                gap = lax.broadcasted_iota(jnp.int32, (bk, bq), 1) - lax.broadcasted_iota(jnp.int32, (bk, bq), 0)
                mask = mask | (gap == first - at)
            for h in (0, 1):
                s = dot(kh[h], q, NT)
                p = jnp.exp(jnp.where(mask, s - lse_ref[h : h + 1, rows], NEG_FILL))
                dp = dot(vh[h], dc, NT)
                ds = (p * (dp - delta[h : h + 1, rows])).astype(BF16)
                own = head_lanes(bq, h)
                dv = dv + dot(p.astype(BF16), jnp.where(own, dc, jnp.zeros_like(dc)))
                dk = dk + dot(ds, jnp.where(own, q, jnp.zeros_like(q)))
                dq_acc[h * HEAD : (h + 1) * HEAD, rows] += dot(k_turned[h * HEAD : (h + 1) * HEAD, :], ds)
            return dk, dv

        zero = jnp.zeros((bk, PAIR), F32)
        dk, dv = lax.fori_loop(lo_ref[i], hi_ref[i], step, (zero, zero))
        dk_ref[...] = (dk * 0.125).astype(BF16)
        dv_ref[...] = dv.astype(BF16)

    pl.when(pad_ref[i] > 0)(lambda: run(True))
    pl.when(pad_ref[i] == 0)(lambda: run(False))

    @pl.when(i == pl.num_programs(1) - 1)
    def _():
        dq_ref[...] = dq_acc[...].T.astype(BF16)


def block_bounds(segment, valid, block, other):
    length = segment.shape[0]
    blocks = segment.reshape(length // block, block)
    lo = jnp.sum((segment[None, :] < blocks[:, :1]).astype(jnp.int32), axis=1) // other
    hi = (jnp.sum((segment[None, :] <= blocks[:, -1:]).astype(jnp.int32), axis=1) + other - 1) // other
    pad = jnp.sum((valid.reshape(length // block, block) == 0).astype(jnp.int32), axis=1)
    return lo, hi, pad


def attention_codes(segment, valid):
    kcode = jnp.where(valid > 0, segment, -1)
    qcode = segment
    wide = lambda a: jnp.broadcast_to(a[:, None], (a.shape[0], 128))
    return qcode, kcode, wide(qcode), wide(kcode)


def qkv_at(pair, which):
    return pair // 2 * 6 + which * 2 + pair % 2


def attend_fwd(qkv, segment, valid, bq=256, bk=256):
    length, width = qkv.shape
    pairs = width // 3 // PAIR
    lo, hi, pad = block_bounds(segment, valid, bq, bk)
    qcode, kcode, qwide, kwide = attention_codes(segment, valid)
    return pl.pallas_call(
        functools.partial(attend_fwd_kernel, bk),
        grid_spec=pltpu.PrefetchScalarGridSpec(
            num_scalar_prefetch=3,
            grid=(pairs, length // bq),
            in_specs=[
                pl.BlockSpec((bq, PAIR), lambda h, i, *_: (i, qkv_at(h, 0))),
                pl.BlockSpec((length, PAIR), lambda h, i, *_: (0, qkv_at(h, 1))),
                pl.BlockSpec((length, PAIR), lambda h, i, *_: (0, qkv_at(h, 2))),
                pl.BlockSpec((1, bq), lambda h, i, *_: (0, i)),
                pl.BlockSpec((length, 128), lambda h, i, *_: (0, 0)),
            ],
            out_specs=[
                pl.BlockSpec((bq, PAIR), lambda h, i, *_: (i, h)),
                pl.BlockSpec((8, bq), lambda h, i, *_: (h, i)),
            ],
            scratch_shapes=[pltpu.VMEM((PAIR, length), BF16)],
        ),
        out_shape=[
            jax.ShapeDtypeStruct((length, pairs * PAIR), BF16),
            jax.ShapeDtypeStruct((pairs * 8, length), F32),
        ],
        compiler_params=pltpu.CompilerParams(dimension_semantics=("arbitrary", "arbitrary")),
        cost_estimate=pl.CostEstimate(flops=8 * 2 * length * length * PAIR, bytes_accessed=8 * length * width, transcendentals=4 * length * length),
    )(lo, hi, pad, qkv, qkv, qkv, qcode[None, :], kwide)


def attend_bwd(part, qkv, context, context_grad, lse, segment, valid, bq=256, bk=256):
    length, width = qkv.shape
    pairs = width // 6 // PAIR
    base = part * pairs
    lo, hi, pad = block_bounds(segment, valid, bk, bq)
    qcode, kcode, qwide, kwide = attention_codes(segment, valid)
    whole = pl.BlockSpec((length, PAIR), lambda h, i, *_: (0, h))
    piece = pl.BlockSpec((bk, PAIR), lambda h, i, *_: (i, h))
    source = pl.BlockSpec((length, PAIR), lambda h, i, *_: (0, base + h))
    cols = lambda at: pl.BlockSpec((bk, PAIR), lambda h, i, *_: (i, qkv_at(base + h, at)))
    shape = jax.ShapeDtypeStruct((length, pairs * PAIR), BF16)
    return pl.pallas_call(
        functools.partial(attend_bwd_kernel, bq),
        grid_spec=pltpu.PrefetchScalarGridSpec(
            num_scalar_prefetch=3,
            grid=(pairs, length // bk),
            in_specs=[
                pl.BlockSpec((length, PAIR), lambda h, i, *_: (0, qkv_at(base + h, 0))), cols(1), cols(2), source, source,
                pl.BlockSpec((8, length), lambda h, i, *_: (base + h, 0)),
                pl.BlockSpec((1, length), lambda h, i, *_: (0, 0)),
                pl.BlockSpec((bk, 128), lambda h, i, *_: (i, 0)),
            ],
            out_specs=[whole, piece, piece],
            scratch_shapes=[pltpu.VMEM((PAIR, length), F32), pltpu.VMEM((8, length), F32)],
        ),
        out_shape=[shape, shape, shape],
        compiler_params=pltpu.CompilerParams(dimension_semantics=("arbitrary", "arbitrary")),
        cost_estimate=pl.CostEstimate(flops=20 * 2 * length * length * PAIR, bytes_accessed=16 * length * width, transcendentals=4 * length * length),
    )(lo, hi, pad, qkv, qkv, qkv, context, context_grad, lse, qcode[None, :], kwide)


def norm_stats(values):
    center = values - jnp.mean(values, axis=1, keepdims=True)
    inverse = lax.rsqrt(jnp.mean(center * center, axis=1, keepdims=True) + 1e-05)
    return center * inverse, inverse


def norm_pull(incoming, normed, inverse, gain):
    scaled = incoming * gain
    return inverse * (
        scaled - jnp.mean(scaled, axis=1, keepdims=True) - normed * jnp.mean(scaled * normed, axis=1, keepdims=True)
    )


def col_sum(values):
    return jnp.sum(values, axis=0, keepdims=True)


def add_sums(ref, parts):
    @pl.when(pl.program_id(0) == 0)
    def _():
        ref[...] = jnp.zeros_like(ref)

    for at, part in enumerate(parts):
        ref[at : at + 1, :] += col_sum(part)


def mix_kernel(at_ref, x_ref, c_ref, w_ref, bias_ref, gain_ref, hl_ref, turned_ref, n_ref, r_ref):
    mixed = x_ref[...].astype(F32) + dot(c_ref[...], w_ref[...]) + bias_ref[0:1, :]
    normed, inverse = norm_stats(mixed)
    hl = (normed * gain_ref[0:1, :] + bias_ref[1:2, :]).astype(BF16)
    hl_ref[...] = hl
    turned_ref[...] = hl.T
    n_ref[...] = normed
    r_ref[...] = jnp.broadcast_to(inverse, r_ref.shape)


def up_kernel(h_ref, w_ref, bias_ref, g_ref, slope_ref):
    u = dot(h_ref[...], w_ref[...]) + bias_ref[...]
    cdf = 0.5 + 0.5 * lax.erf(u * (1.0 / math.sqrt(2.0)))
    g_ref[...] = (u * cdf).astype(BF16)
    slope_ref[...] = (cdf + u * (jnp.exp(-0.5 * u * u) * (1.0 / math.sqrt(2.0 * math.pi)))).astype(BF16)


def down_kernel(g_ref, w_ref, n_ref, e_ref, bias_ref, gain_ref, out_ref, dr_ref, dz_ref, sum_ref):
    hidden = n_ref[...] * gain_ref[0:1, :] + bias_ref[1:2, :]
    normed, inverse = norm_stats(hidden + dot(g_ref[...], w_ref[...]) + bias_ref[2:3, :])
    out_ref[...] = (normed * gain_ref[1:2, :] + bias_ref[3:4, :]).astype(BF16)
    e = e_ref[...].astype(F32)
    dr = norm_pull(e, normed, inverse, gain_ref[1:2, :])
    dr_ref[...] = dr
    dz_ref[...] = dr.astype(BF16)
    add_sums(sum_ref, (e * normed, dr, e))


def slope_kernel(dz_ref, w_ref, slope_ref, du_ref, sum_ref):
    du = (dot(dz_ref[...], w_ref[...], NT) * slope_ref[...].astype(F32)).astype(BF16)
    du_ref[...] = du

    @pl.when(pl.program_id(1) == 0)
    def _():
        sum_ref[...] = jnp.zeros_like(sum_ref)

    sum_ref[0:1, :] += col_sum(du.astype(F32))


def mix_pull_kernel(du_ref, w_ref, dr_ref, n_ref, r_ref, gain_ref, dm_ref, da_ref, sum_ref):
    dh = dr_ref[...] + dot(du_ref[...], w_ref[...], NT)
    normed = n_ref[...]
    dm = norm_pull(dh, normed, r_ref[:, 0:1], gain_ref[0:1, :])
    dm_ref[...] = dm
    da_ref[...] = dm.astype(BF16)
    add_sums(sum_ref, (dh * normed, dm, dh))


def call(kernel, grid, ins, outs, flops, nbytes, *args):
    return pl.pallas_call(
        kernel,
        grid=grid,
        in_specs=ins,
        out_specs=outs[0],
        out_shape=outs[1],
        compiler_params=pltpu.CompilerParams(dimension_semantics=("arbitrary",) * len(grid)),
        cost_estimate=pl.CostEstimate(flops=flops, bytes_accessed=nbytes, transcendentals=0),
    )(*args)


def rows(block, width):
    return pl.BlockSpec((block, width), lambda i: (i, 0))


def held(shape):
    return pl.BlockSpec(shape, lambda i: (0, 0))


def once(shape):
    return pl.BlockSpec(shape, lambda i: (0, 0), pipeline_mode=pl.Buffered(1))


def sds(shape, dtype=BF16):
    return jax.ShapeDtypeStruct(shape, dtype)


def mix(core_at, x, c, w, biases, gains, block=256):
    n, d = c.shape
    r = lambda width: pl.BlockSpec((block, width), lambda i, at: (i, 0))
    fixed = lambda value: pl.BlockSpec(value.shape, lambda i, at: (0, 0), pipeline_mode=pl.Buffered(1))
    steps = n // block
    return pl.pallas_call(
        mix_kernel,
        grid_spec=pltpu.PrefetchScalarGridSpec(
            num_scalar_prefetch=1,
            grid=(steps,),
            in_specs=[
                pl.BlockSpec((block, d), lambda i, at: (at[0] * steps + i, 0)), r(d), fixed(w), fixed(biases), fixed(gains),
            ],
            out_specs=[r(d), pl.BlockSpec((d, block), lambda i, at: (0, i)), r(d), r(128)],
        ),
        out_shape=[sds((n, d)), sds((d, n)), sds((n, d), F32), sds((n, 128), F32)],
        compiler_params=pltpu.CompilerParams(dimension_semantics=("arbitrary",)),
        cost_estimate=pl.CostEstimate(flops=2 * n * d * d, bytes_accessed=12 * n * d, transcendentals=0),
    )(core_at, x, c, w, biases, gains)


def up(h, w, bias, block=256, cols=1024):
    n, d = h.shape
    f = w.shape[1]
    cols = min(cols, f)
    tile = pl.BlockSpec((block, cols), lambda j, i: (i, j))
    return call(
        up_kernel, (f // cols, n // block),
        [pl.BlockSpec((block, d), lambda j, i: (i, 0)), pl.BlockSpec((d, cols), lambda j, i: (0, j)), pl.BlockSpec((1, cols), lambda j, i: (0, j))],
        ([tile, tile], [sds((n, f)), sds((n, f))]),
        2 * n * d * f, 4 * n * f + 2 * d * f, h, w, bias,
    )


def down(g, w, normed, e, biases, gains, block=256):
    n, f = g.shape
    d = w.shape[1]
    r = functools.partial(rows, block)
    return call(
        down_kernel, (n // block,),
        [r(f), once(w.shape), r(d), r(d), held(biases.shape), held(gains.shape)],
        ([r(d), r(d), r(d), held((8, d))], [sds((n, d)), sds((n, d), F32), sds((n, d)), sds((8, d), F32)]),
        2 * n * d * f, 2 * n * f + 2 * d * f, g, w, normed, e, biases, gains,
    )


def slope_pull(dz, w, slope, block=256, cols=1024):
    n, d = dz.shape
    f = w.shape[0]
    tile = pl.BlockSpec((block, cols), lambda j, i: (i, j))
    return call(
        slope_kernel, (f // cols, n // block),
        [pl.BlockSpec((block, d), lambda j, i: (i, 0)), pl.BlockSpec((cols, d), lambda j, i: (j, 0)), tile],
        ([tile, pl.BlockSpec((8, cols), lambda j, i: (0, j))], [sds((n, f)), sds((8, f), F32)]),
        2 * n * d * f, 4 * n * f + 2 * d * f, dz, w, slope,
    )


def mix_pull(du, w, dr, normed, inverse, gains, block=256):
    n, f = du.shape
    d = w.shape[0]
    r = functools.partial(rows, block)
    return call(
        mix_pull_kernel, (n // block,),
        [r(f), once(w.shape), r(d), r(d), r(128), held(gains.shape)],
        ([r(d), r(d), held((8, d))], [sds((n, d), F32), sds((n, d)), sds((8, d), F32)]),
        2 * n * d * f, 2 * n * f + 2 * d * f, du, w, dr, normed, inverse, gains,
    )


def split_columns(acc, keep_ref, send_ref):
    n_p, c = keep_ref.shape[0], keep_ref.shape[3]
    for bit in (0, 1):

        @pl.when(lax.axis_index("core") == bit)
        def _():
            for p in range(n_p):
                at, to = (2 * p + bit) * c, (2 * p + 1 - bit) * c
                keep_ref[p, 0] = acc[:, at : at + c]
                send_ref[p, 0] = acc[:, to : to + c]


def split_rows(acc, place, keep_ref, send_ref):
    n_p, r = keep_ref.shape[0], keep_ref.shape[-2]
    for bit in (0, 1):

        @pl.when(lax.axis_index("core") == bit)
        def _():
            for p in range(n_p):
                at, to = (2 * p + bit) * r, (2 * p + 1 - bit) * r
                for cb in range(acc.shape[1] // 128):
                    keep_ref[(p, 0) + place + (cb,)] = acc[at : at + r, cb * 128 : cb * 128 + 128]
                    send_ref[(p, 0) + place + (cb,)] = acc[to : to + r, cb * 128 : cb * 128 + 128]


def col_grad_kernel(a_ref, b_ref, keep_ref, send_ref, acc):
    acc[...] = dot(a_ref[...], b_ref[...], TN).astype(BF16)
    split_columns(acc, keep_ref, send_ref)


def row_grad_kernel(a_ref, b_ref, keep_ref, send_ref, acc):
    acc[...] = dot(a_ref[...], b_ref[...]).astype(BF16)
    split_rows(acc, (), keep_ref, send_ref)


def qkv_grad_kernel(x_ref, dq_ref, dk_ref, dv_ref, keep_ref, send_ref, sum_ref, acc):
    for at, ref in enumerate((dq_ref, dk_ref, dv_ref)):
        acc[...] = dot(x_ref[...], ref[...]).astype(BF16)
        split_rows(acc, (at,), keep_ref, send_ref)
    sum_ref[0:1, :] = col_sum(dq_ref[...].astype(F32))
    sum_ref[1:2, :] = col_sum(dv_ref[...].astype(F32))


def grad_call(kernel, grid, ins, outs, scratch, flops, *args):
    return pl.pallas_call(
        kernel,
        grid=grid,
        in_specs=ins,
        out_specs=outs[0],
        out_shape=outs[1],
        scratch_shapes=scratch,
        compiler_params=pltpu.CompilerParams(dimension_semantics=("arbitrary",) * len(grid)),
        cost_estimate=pl.CostEstimate(flops=flops, bytes_accessed=flops // 512, transcendentals=0),
    )(*args)


def col_grad(a, b, n_p, n_t, block=512):
    n, f = a.shape
    d = b.shape[1]
    per_t, c = f // n_t, d // (2 * n_p)
    block = min(block, per_t)
    steps = per_t // block
    spec = pl.BlockSpec((n_p, 1, block, c), lambda i: (0, i // steps, i % steps, 0))
    shape = sds((n_p, n_t, per_t, c))
    return grad_call(
        col_grad_kernel, (f // block,),
        [pl.BlockSpec((n, block), lambda i: (0, i)), once((n, d))],
        ([spec, spec], [shape, shape]), [pltpu.VMEM((block, d), BF16)], 2 * n * f * d, a, b,
    )


def row_grad(a, b, n_p, n_t, block=512):
    d, n = a.shape
    f = b.shape[1]
    per_t, r = f // n_t, d // (2 * n_p)
    steps = per_t // block
    spec = pl.BlockSpec((n_p, 1, block // 128, r, 128), lambda i: (0, i // steps, i % steps, 0, 0))
    shape = sds((n_p, n_t, per_t // 128, r, 128))
    return grad_call(
        row_grad_kernel, (f // block,),
        [once((d, n)), pl.BlockSpec((n, block), lambda i: (0, i))],
        ([spec, spec], [shape, shape]), [pltpu.VMEM((d, block), BF16)], 2 * n * f * d, a, b,
    )


def qkv_grad(x, dq, dk, dv, n_p):
    d, n = x.shape
    f = dq.shape[1]
    r = d // (2 * n_p)
    spec = pl.BlockSpec((n_p, 1, 3, f // 128, r, 128), lambda i: (0, 0, 0, 0, 0, 0))
    shape = sds((n_p, 1, 3, f // 128, r, 128))
    return grad_call(
        qkv_grad_kernel, (1,),
        [held((d, n)), held((n, f)), held((n, f)), held((n, f))],
        ([spec, spec, held((8, f))], [shape, shape, sds((8, f), F32)]),
        [pltpu.VMEM((d, f), BF16)], n * f * d // 64, x, dq, dk, dv,
    )


def input_pull_kernel(extra, at_ref, *refs):
    parts, w_ref = refs[:6], refs[6]
    c = w_ref.shape[1] // 6
    total = dot(parts[0][...], w_ref[:, :c], NT)
    for j in range(1, 6):
        total = total + dot(parts[j][...], w_ref[:, j * c : (j + 1) * c], NT)
    if extra:
        total = total + refs[7][...]
    refs[-1][...] = total.astype(refs[-1].dtype)


def input_pull(half, core, parts, w, dm=None, block=256):
    n, f = parts[0].shape
    d = w.shape[0]
    steps = n // 2 // block
    cols = pl.BlockSpec((block, f), lambda i, at: (at[0] * steps + i, 0))
    own = pl.BlockSpec((block, d), lambda i, at: (i, 0))
    extra = [] if dm is None else [dm]
    held_w = pl.BlockSpec((d, w.shape[1] // 2), lambda i, at: (0, at[1]), pipeline_mode=pl.Buffered(1))
    return pl.pallas_call(
        functools.partial(input_pull_kernel, len(extra)),
        grid_spec=pltpu.PrefetchScalarGridSpec(
            num_scalar_prefetch=1,
            grid=(steps,),
            in_specs=[cols] * 6 + [held_w] + [own] * len(extra),
            out_specs=own,
        ),
        out_shape=sds((n // 2, d), BF16 if dm is None else F32),
        compiler_params=pltpu.CompilerParams(dimension_semantics=("arbitrary",)),
        cost_estimate=pl.CostEstimate(flops=6 * n * f * d, bytes_accessed=8 * n * d, transcendentals=0),
    )(jnp.stack([half, core]).astype(jnp.int32), *parts, w, *extra)


MESH_ID = pl.DeviceIdType.MESH


def flip(value, bit):
    return value + bit - 2 * bit * ((value // bit) % 2)


def start_kernel(n_p, n_t, kinds, *refs):
    n = len(kinds)
    x_ref, bias_ref, *shards = refs[: n + 2]
    x_out, bias_out, *fulls = refs[n + 2 : 2 * n + 4]
    send_sems, recv_sems, own_sems = refs[2 * n + 4 :]
    p, core, t = lax.axis_index("p"), lax.axis_index("core"), lax.axis_index("tensor")
    me = 2 * p + core
    bits = [1 << s for s in range(n_p.bit_length() - 1)]
    column = [{"tensor": lax.rem(t + r, n_t)} for r in range(1, n_t)]
    across = [{"core": 1 - core, "tensor": lax.rem(t + r, n_t)} for r in range(n_t)]
    plane = [{"p": flip(p, bit)} for bit in bits]
    barrier = pltpu.get_barrier_semaphore()
    for peer in column + across + plane:
        pl.semaphore_signal(barrier, inc=1, device_id=peer, device_id_type=MESH_ID)
    pl.semaphore_wait(barrier, len(column + across + plane))

    used = [0, 0]

    def group():
        used[0] += 1
        return used[0] - 1

    def send(source, target, at, peer):
        pltpu.make_async_remote_copy(
            src_ref=source, dst_ref=target, send_sem=send_sems.at[at], recv_sem=recv_sems.at[at],
            device_id=peer, device_id_type=MESH_ID,
        ).start()

    def arrived(view, at):
        pltpu.make_async_copy(view, view, recv_sems.at[at]).wait()

    def left(view, at):
        pltpu.make_async_copy(view, view, send_sems.at[at]).wait()

    def keep(source, target):
        used[1] += 1
        copy = pltpu.make_async_copy(source, target, own_sems.at[used[1] - 1])
        copy.start()
        return copy

    def slab(i, d, half):
        full, kind = fulls[i], kinds[i]
        if kind == "rows":
            depth, wide = shards[i].shape[-2], full.shape[1] // 2
            return full.at[pl.ds(pl.multiple_of(d * depth, depth), depth), pl.ds(half * wide, wide)]
        depth, tall = shards[i].shape[-1], full.shape[0] // 2
        return full.at[pl.ds(half * tall, tall), pl.ds(pl.multiple_of(d * depth, depth), depth)]

    def slabs(i, count, half):
        full, kind = fulls[i], kinds[i]
        if kind == "rows":
            wide = full.shape[1] // 2
            return full.at[pl.ds(0, count * shards[i].shape[-2]), pl.ds(half * wide, wide)]
        tall = full.shape[0] // 2
        return full.at[pl.ds(half * tall, tall), pl.ds(0, count * shards[i].shape[-1])]

    def places(i, t):
        shard, full = shards[i], fulls[i]
        if kinds[i] == "columns":
            tall, depth = shard.shape
            return [(shard, full.at[pl.ds(pl.multiple_of(t * tall, tall), tall), pl.ds(pl.multiple_of(me * depth, depth), depth)])]
        depth, wide = shard.shape[-2:]
        rows_at = pl.ds(pl.multiple_of(me * depth, depth), depth)
        if len(shard.shape) == 2:
            return [(shard, full.at[rows_at, pl.ds(pl.multiple_of(t * wide, wide), wide)])]
        count = shard.shape[0]
        return [
            (shard.at[w], full.at[rows_at, pl.ds(pl.multiple_of((t * count + w) * wide, wide), wide)])
            for w in range(count)
        ]

    def shares(i, count):
        shard, full = shards[i], fulls[i]
        if kinds[i] == "columns":
            return full.at[pl.ds(0, count * shard.shape[0]), pl.ds(0, shard.shape[1])]
        wide = math.prod(shard.shape) // shard.shape[-2]
        return full.at[pl.ds(0, shard.shape[-2]), pl.ds(0, count * wide)]

    hops = n_t - 1
    own = [[keep(source, target) for source, target in places(i, t)] for i in range(n)]
    right, left_to = {"tensor": lax.rem(t + 1, n_t)}, {"tensor": lax.rem(t + n_t - 1, n_t)}
    line = [[(group(), group()) for _ in range(hops)] for _ in range(n)]

    def hop(i, s):
        to_right, to_left = line[i][s]

        @pl.when(jnp.logical_and(t + 1 < n_t, t >= s))
        def _():
            for source, target in places(i, t - s):
                send(source if s == 0 else target, target, to_right, right)

        @pl.when(jnp.logical_and(t >= 1, t + s < n_t))
        def _():
            for source, target in places(i, t + s):
                send(source if s == 0 else target, target, to_left, left_to)

    def hop_arrived(i, s):
        to_right, to_left = line[i][s]
        pl.when(t >= s + 1)(lambda: arrived(shares(i, 1), to_right))
        pl.when(t + s + 1 < n_t)(lambda: arrived(shares(i, 1), to_left))

    def hop_left(i, s):
        to_right, to_left = line[i][s]
        pl.when(jnp.logical_and(t + 1 < n_t, t >= s))(lambda: left(shares(i, 1), to_right))
        pl.when(jnp.logical_and(t >= 1, t + s < n_t))(lambda: left(shares(i, 1), to_left))

    for i in range(n):
        hop(i, 0)
    bias_at = group()
    bias_own = keep(bias_ref, bias_out.at[t])
    for peer in column:
        send(bias_ref, bias_out.at[t], bias_at, peer)

    held = x_ref.shape[1]
    odd = t % 2
    x_rows = x_out.at[pl.ds(pl.multiple_of(t * held, held), held), :]
    x_at = [group(), group()]
    stays = core == t // 2
    peer_a = {"core": t // 2, "tensor": 2 * core + odd}
    peer_b = {"core": t // 2, "tensor": 2 * core + 1 - odd}

    x_own = pltpu.make_async_copy(x_ref.at[odd], x_rows, own_sems.at[used[1]])
    used[1] += 1
    pl.when(stays)(x_own.start)

    def send_tokens():
        pl.when(jnp.logical_not(stays))(lambda: send(x_ref.at[odd], x_rows, x_at[0], peer_a))
        send(x_ref.at[1 - odd], x_rows, x_at[1], peer_b)

    partner = {"core": 1 - core}
    passes = []

    def forward(i, masks, half):
        at = group()
        guard = i == 0

        def go():
            for mask in masks:
                d = 2 * mask + core
                send(slab(i, d, half), slab(i, d, half), at, partner)

        if guard:
            pl.when(core == 1 - half)(go)
        else:
            go()
        passes.append((i, len(masks), half, at))

    states = {}

    def stage(i, s):
        if s == 0:
            hop_arrived(i, hops - 1)
            states[i] = {}
            for half in (0, 1):
                states[i][half] = ([p], None)
        else:
            for half in (0, 1):
                masks, at = states[i][half]
                arrived(slabs(i, len(masks), half), at)
                bit = bits[s - 1] if half == 0 else bits[-s]
                states[i][half] = (masks + [flip(m, bit) for m in masks], None)
        for half in (0, 1):
            masks, _ = states[i][half]
            if s < len(bits):
                at = group()
                bit = bits[s] if half == 0 else bits[-s - 1]
                for m in masks:
                    d = 2 * m + core
                    send(slab(i, d, half), slab(i, d, half), at, {"p": flip(p, bit)})
                states[i][half] = (masks, at)
                finish.append((i, len(masks), half, at))
            fresh = masks if s == 0 else masks[len(masks) // 2 :]
            forward(i, fresh, half)

    finish = []
    for step in range(n + hops - 1 + len(bits)):
        for i in range(n):
            at = step - i
            if 0 <= at < hops - 1:
                if at == 0:
                    for copy in own[i]:
                        copy.wait()
                hop_arrived(i, at)
                hop(i, at + 1)
                if i == n - 1 and at == hops - 2:
                    send_tokens()
            elif 0 <= at - (hops - 1) <= len(bits):
                stage(i, at - (hops - 1))

    pl.when(jnp.logical_not(stays))(lambda: arrived(x_rows, x_at[0]))
    pl.when(stays)(x_own.wait)
    arrived(x_rows, x_at[1])
    half_rows = x_out.at[pl.ds(pl.multiple_of(core * 2 * held, 2 * held), 2 * held), :]
    x_pass = group()
    send(half_rows, half_rows, x_pass, partner)
    bias_own.wait()
    arrived(bias_out.at[pl.ds(0, n_t - 1)], bias_at)
    for i, count, half, at in passes:
        if i == 0:
            pl.when(core == half)(functools.partial(arrived, slabs(i, count, half), at))
        else:
            arrived(slabs(i, count, half), at)
    arrived(half_rows, x_pass)
    left(half_rows, x_pass)
    for i, count, half, at in passes:
        if i == 0:
            pl.when(core == 1 - half)(functools.partial(left, slabs(i, count, half), at))
        else:
            left(slabs(i, count, half), at)
    for i, count, half, at in finish:
        left(slabs(i, count, half), at)
    for i in range(n):
        for s in range(hops):
            hop_left(i, s)
    left(bias_out.at[pl.ds(0, n_t - 1)], bias_at)
    pl.when(jnp.logical_not(stays))(lambda: left(x_rows, x_at[0]))
    left(x_rows, x_at[1])


def start_gather(x, bias, shards, kinds, n_p, n_t):
    n_dp = 2 * n_p
    fulls = []
    for shard, kind in zip(shards, kinds):
        if kind == "columns":
            fulls.append(sds((shard.shape[0] * n_t, shard.shape[1] * n_dp)))
        else:
            fulls.append(sds((shard.shape[-2] * n_dp, math.prod(shard.shape) // shard.shape[-2] * n_t)))
    bits = n_p.bit_length() - 1
    count = len(shards) * (2 * (n_t - 1) + 2 * bits + 2 * (bits + 1)) + 4
    vmem, away = pl.BlockSpec(memory_space=pltpu.VMEM), pl.BlockSpec(memory_space=pl.ANY)
    return pl.pallas_call(
        functools.partial(start_kernel, n_p, n_t, kinds),
        out_shape=[sds((n_t * x.shape[1], x.shape[2])), sds((n_t,) + bias.shape, F32)] + fulls,
        in_specs=[vmem] * (2 + len(shards)),
        out_specs=[away] * (2 + len(shards)),
        scratch_shapes=[
            pltpu.SemaphoreType.DMA((count,)), pltpu.SemaphoreType.DMA((count,)), pltpu.SemaphoreType.DMA((10,)),
        ],
        compiler_params=pltpu.CompilerParams(collective_id=1, has_side_effects=True),
    )(x, bias, *shards)


def project_kernel(core_ref, x_ref, w_ref, bias_ref, out_ref, turned_ref):
    turned_ref[...] = x_ref[...].T
    out_ref[...] = (dot(x_ref[...], w_ref[...]) + bias_ref[...]).astype(BF16)


def project(core_at, x, w, bias, block=256):
    n, d = x.shape
    f = w.shape[1] // 2
    return pl.pallas_call(
        project_kernel,
        grid_spec=pltpu.PrefetchScalarGridSpec(
            num_scalar_prefetch=1,
            grid=(n // block,),
            in_specs=[
                pl.BlockSpec((block, d), lambda i, at: (i, 0)),
                pl.BlockSpec((d, f), lambda i, at: (0, at[0]), pipeline_mode=pl.Buffered(1)),
                pl.BlockSpec((1, f), lambda i, at: (0, 0)),
            ],
            out_specs=[pl.BlockSpec((block, f), lambda i, at: (i, 0)), pl.BlockSpec((d, block), lambda i, at: (0, i))],
        ),
        out_shape=[sds((n, f)), sds((d, n))],
        compiler_params=pltpu.CompilerParams(dimension_semantics=("arbitrary",)),
        cost_estimate=pl.CostEstimate(flops=2 * n * d * f, bytes_accessed=4 * n * d + 2 * n * f, transcendentals=0),
    )(core_at, x, w, bias)


def finish_kernel(n_p, n_t, *refs):
    dx, keep2, send2, first_a, first_b, up_a, up_b, out_a, out_b, small = refs[:10]
    given, qkv_out, up_out, out_out, small_out = refs[10:15]
    recv2, pair1, pair2, slot1, slot2, last, last_slot, up_cur, up_slot, out_cur, out_slot = refs[15:26]
    out_next, out_last, small_cur, small_slot = refs[26:30]
    bits = [n_p >> (s + 1) for s in range(n_p.bit_length() - 1)]
    curs, slots = refs[30 : 30 + len(bits)], refs[30 + len(bits) : 30 + 2 * len(bits)]
    send_sems, recv_sems = refs[-2:]
    p, core, t = lax.axis_index("p"), lax.axis_index("core"), lax.axis_index("tensor")
    partner = {"core": 1 - core}
    column = [{"tensor": lax.rem(t + r, n_t)} for r in range(1, n_t)]
    column += [{"core": 1 - core, "tensor": lax.rem(t + r, n_t)} for r in range(n_t)]
    plane = [{"p": flip(p, bit)} for bit in bits]
    line = {bit: {"tensor": flip(t, bit)} for bit in (2, 1)}
    barrier = pltpu.get_barrier_semaphore()
    for peer in column + plane:
        pl.semaphore_signal(barrier, inc=1, device_id=peer, device_id_type=MESH_ID)
    pl.semaphore_wait(barrier, len(column + plane))

    used = [0]

    def send(source, target, peer):
        at = used[0]
        used[0] += 1
        copy = pltpu.make_async_remote_copy(
            src_ref=source, dst_ref=target, send_sem=send_sems.at[at], recv_sem=recv_sems.at[at],
            device_id=peer, device_id_type=MESH_ID,
        )
        return copy

    def go(source, target, peer):
        copy = send(source, target, peer)
        copy.start()
        return copy

    def plus(a, b):
        return (a.astype(F32) + b.astype(F32)).astype(BF16)

    u, odd = t // 2, t % 2
    swap = go(send2, recv2, partner)
    for at in (0, 1):
        pair1[at] = plus(first_a[at], first_b[at])
    first_move = go(pair1.at[1 - u], slot1, line[2])
    for at in range(4):
        out_cur[at] = plus(out_a[at], out_b[at])
    out_move = go(out_cur.at[pl.ds(2 * (1 - u), 2)], out_slot, line[2])
    for at in (0, 1):
        up_cur[at] = plus(up_a[at], up_b[at])
    up_move = go(up_cur.at[1 - odd], up_slot, line[1])

    held = given.shape[1]
    stays = core == u
    rows_a = dx.at[pl.ds(pl.multiple_of(odd * held, held), held), :]
    rows_b = dx.at[pl.ds(pl.multiple_of((1 - odd) * held, held), held), :]
    give_a = send(rows_a, given.at[odd], {"core": u, "tensor": 2 * core + odd})
    pl.when(jnp.logical_not(stays))(give_a.start)

    @pl.when(stays)
    def _():
        given[odd] = dx[pl.ds(pl.multiple_of(odd * held, held), held), :]

    moves = []
    small_cur[0] = small[...]
    peers = [partner] + plane
    for at, peer in enumerate(peers):
        copy = go(small_cur.at[at], small_slot.at[at], peer)
        copy.wait()
        small_cur[at + 1] = small_cur[at] + small_slot[at]

    swap.wait()
    source = [keep2, recv2]
    for s, bit in enumerate(bits):
        mine = (p // bit) % 2
        copies = [
            go(source[j].at[pl.ds((1 - mine) * bit, bit)], slots[s].at[j], plane[s]) for j in (0, 1)
        ]
        for j, copy in enumerate(copies):
            copy.wait()
            if bit == 1:
                pair2[core if j == 0 else 1 - core] = plus(source[j][mine], slots[s][j, 0])
            else:
                for at in range(bit):
                    curs[s][j, at] = plus(source[j][mine * bit + at], slots[s][j, at])
        source = [curs[s].at[0], curs[s].at[1]]
    second_move = go(pair2.at[1 - u], slot2, line[2])
    give_b = go(rows_b, given.at[odd], {"core": u, "tensor": 2 * core + 1 - odd})

    up_move.wait()
    up_out[...] = up_cur[odd].astype(F32) + up_slot[...].astype(F32)
    out_move.wait()
    for at in (0, 1):
        out_next[at] = plus(out_cur[2 * u + at], out_slot[at])
    out_move = go(out_next.at[1 - odd], out_last, line[1])
    first_move.wait()
    last[0] = plus(pair1[u], slot1[...])
    second_move.wait()
    last[1] = plus(pair2[u], slot2[...])
    last_move = go(last.at[1 - odd], last_slot, line[1])
    for bit in (2, 1):
        at = len(peers)
        copy = go(small_cur.at[at], small_slot.at[at], line[bit])
        copy.wait()
        peers.append(None)
        if bit == 1:
            small_out[...] = small_cur[at] + small_slot[at]
        else:
            small_cur[at + 1] = small_cur[at] + small_slot[at]
    out_move.wait()
    out_out[...] = out_next[odd].astype(F32) + out_last[...].astype(F32)
    last_move.wait()
    qkv_out[...] = last[odd].astype(F32) + last_slot[...].astype(F32)
    pl.when(jnp.logical_not(stays))(give_a.wait)
    give_b.wait()


def finish(n_p, n_t, dx, keep2, send2, first, up_, out_, small):
    rows_, lanes = keep2.shape[1:]
    bits = n_p.bit_length() - 1
    steps = 1 + bits + 2
    block = lambda count, like: pltpu.VMEM((count,) + like.shape[1:], BF16)
    one = lambda like: pltpu.VMEM(like.shape[1:], BF16)
    sizes = [n_p >> (s + 1) for s in range(bits)]
    halves = [pltpu.VMEM((2, size, rows_, lanes), BF16) for size in sizes]
    vmem = pl.BlockSpec(memory_space=pltpu.VMEM)
    count = 9 + steps + 2 * bits
    return pl.pallas_call(
        functools.partial(finish_kernel, n_p, n_t),
        out_shape=[
            sds((2, dx.shape[0] // 2, dx.shape[1])), sds((rows_, lanes), F32), sds(up_[0].shape[1:], F32),
            sds(out_[0].shape[1:], F32), sds(small.shape, F32),
        ],
        in_specs=[vmem] * 10,
        out_specs=[vmem] * 5,
        scratch_shapes=[
            block(n_p, keep2), block(2, keep2), block(2, keep2), one(keep2), one(keep2), block(2, keep2), one(keep2),
            block(2, up_[0]), one(up_[0]), block(4, out_[0]), block(2, out_[0]), block(2, out_[0]), one(out_[0]),
            pltpu.VMEM((steps,) + small.shape, F32), pltpu.VMEM((steps,) + small.shape, F32),
            *halves, *halves,
            pltpu.SemaphoreType.DMA((count,)), pltpu.SemaphoreType.DMA((count,)),
        ],
        compiler_params=pltpu.CompilerParams(collective_id=0, has_side_effects=True),
    )(dx, keep2, send2, *first, *up_, *out_, small)


def swap_cores(value):
    return lax.ppermute(value, "core", [(0, 1), (1, 0)])


def column_routes(tensor_size):
    first, second = [], []
    for core in range(2):
        for t in range(tensor_size):
            at = core * tensor_size + t
            first.append((at, (t >> 1) * tensor_size + 2 * core + (t & 1)))
            second.append((at, (t >> 1) * tensor_size + 2 * core + 1 - (t & 1)))
    return first, second


def back(route):
    return [(b, a) for a, b in route]


def by_core(core, mine, other, axis):
    return jnp.where(
        core == 0, jnp.concatenate([mine, other], axis=axis), jnp.concatenate([other, mine], axis=axis)
    )


def body(
    inputs, segment_ids, token_valid, qkv_weight, qv_bias, out_weight, norm_gains, row_biases,
    up_weight, up_bias, down_weight, out_grad,
):
    COL = ("core", "tensor")
    ALL = ("p", "core", "tensor")
    core, tensor = lax.axis_index("core"), lax.axis_index("tensor")
    n_p, n_t = lax.axis_size("p"), lax.axis_size("tensor")
    n_dp = 2 * n_p
    micro, held_rows, width = inputs.shape
    assert micro == 2 and n_t == 4
    odd = tensor & 1
    route_a, route_b = column_routes(n_t)

    def bring(value):
        a = lax.ppermute(value[odd], COL, route_a)
        b = lax.ppermute(value[1 - odd], COL, route_b)
        return jnp.where(odd == 0, jnp.concatenate([a, b]), jnp.concatenate([b, a]))

    def blocks(value):
        return [lax.dynamic_slice_in_dim(value, at * held_rows, held_rows) for at in (odd, 1 - odd)]

    def give(a, b):
        a, b = lax.ppermute(a, COL, back(route_a)), lax.ppermute(b, COL, back(route_b))
        return jnp.where(odd == 0, jnp.stack([a, b]), jnp.stack([b, a]))

    def gathered(weight):
        got = lax.all_gather(weight, ALL, axis=0, tiled=False)
        return got.reshape((n_dp, n_t) + weight.shape)

    labels = jnp.stack([segment_ids[:, 0], token_valid[:, 0]], axis=1)[odd]
    labels = jnp.where((tensor >> 1) == core, labels, swap_cores(labels))
    segment, valid = labels[0], labels[1]

    shards, kinds = [qkv_weight, up_weight], ["rows", "rows"]
    wide = out_weight.shape[1] % 128 == 0
    if wide:
        shards, kinds = [qkv_weight, out_weight, up_weight, down_weight], ["rows", "columns", "rows", "columns"]
    local_bias = jnp.concatenate([qv_bias.reshape(-1), up_bias]).reshape(-1, 128)
    x_full, bias_all, *fulls = start_gather(inputs, local_bias, shards, kinds, n_p, n_t)
    if wide:
        w_qkv, w_out, w_up, w_down = fulls
    else:
        w_qkv, w_up = fulls
        w_out = gathered(out_weight).transpose(1, 2, 0, 3).reshape(-1, width)
        w_down = gathered(down_weight).transpose(1, 2, 0, 3).reshape(-1, width)
    out_grad, x_full = lax.optimization_barrier((out_grad, x_full))
    rows = x_full.shape[0] // 2
    own = w_qkv.shape[1] // 6
    bias_all = bias_all.reshape(n_t, -1)
    n_qv = qv_bias.size
    up_bias_all = bias_all[:, n_qv:].reshape(1, -1)
    qv_own = lax.dynamic_slice_in_dim(bias_all[:, :n_qv], 2 * core, 2).reshape(2, 2, -1)
    bias = jnp.stack([qv_own[:, 0], jnp.zeros_like(qv_own[:, 0]), qv_own[:, 1]], axis=1).reshape(1, -1)
    core_at = jnp.reshape(core, (1,)).astype(jnp.int32)
    qkv, x_turned = project(core_at, x_full, w_qkv, bias)
    context, lse = attend_fwd(qkv, segment, valid, 512, 512)
    mine = lax.dynamic_slice_in_dim(context, core * rows, rows)
    other = lax.dynamic_slice_in_dim(context, (1 - core) * rows, rows)
    c_own = by_core(core, mine, swap_cores(other), 1)
    hl, hl_turned, normed, inverse = mix(core_at, x_full, c_own, w_out, row_biases, norm_gains)
    active, slope = up(hl, w_up, up_bias_all)
    grad_own = bring(out_grad)
    layer, dr, dz, sums_two = down(active, w_down, normed, grad_own, row_biases, norm_gains)
    layer_out = give(*blocks(layer))

    p_bits = [1 << s for s in range(n_p.bit_length() - 1)]
    t_bits = [2, 1]

    class Total:
        def __init__(self, parts, downward):
            lead = [("p", n_p, bit) for bit in reversed(p_bits)] + [("tensor", n_t, bit) for bit in t_bits]
            lead = lead[: len(lead) - (parts[0].shape[1] == 2)]
            self.rest = parts[0].shape[2:]
            self.dims = lead
            self.parts = [part.reshape((2,) * len(lead) + self.rest) for part in parts]
            order = list(reversed(p_bits)) if downward else p_bits
            self.groups = [order[:1], order[1:], t_bits[:1], t_bits[1:]]

        def sum_of(self, pick):
            total = pick(self.parts[0]).astype(F32)
            for part in self.parts[1:]:
                total = total + pick(part).astype(F32)
            return total

        def cut_one(self, axis, bit):
            at = [d[0] + str(d[2]) for d in self.dims].index(axis + str(bit))
            size = self.dims[at][1]
            self.dims = self.dims[:at] + self.dims[at + 1 :]
            mine = (lax.axis_index(axis) // bit) % 2
            side = lambda which: self.sum_of(lambda part: lax.dynamic_index_in_dim(part, which, at, keepdims=False)).astype(BF16)
            self.live = [side(mine), side(1 - mine)]
            self.route = (axis, [(i, i ^ bit) for i in range(size)])

        def move(self):
            self.parts = [self.live[0], lax.ppermute(self.live[1], *self.route)]
            return self

        def cut(self, group):
            axis = "p" if group < 2 else "tensor"
            for j, bit in enumerate(self.groups[group]):
                if j:
                    self.move()
                self.cut_one(axis, bit)
            return self

    def together(sums, *others):
        lives, others = lax.optimization_barrier(([s.live for s in sums], others))
        for s, live in zip(sums, lives):
            s.live = live
            s.move()
        return others

    du, up_sum = slope_pull(dz, w_down, slope)
    active, du = lax.optimization_barrier((active, du))
    down_keep, down_send = col_grad(active, dz, n_p, n_t)
    down_send, du = lax.optimization_barrier((down_send, du))
    down_recv = swap_cores(down_send)
    up_keep, up_send = row_grad(hl_turned, du, n_p, n_t)
    up_recv = swap_cores(up_send)
    down_sum = Total([down_keep, down_recv], False).cut(0)
    (du,) = together([down_sum], du)
    dm, da, sums_one = mix_pull(du, w_up, dr, normed, inverse, norm_gains)
    dc = dot(da, w_out, NT).astype(BF16)
    mine = lax.dynamic_slice_in_dim(dc, core * own, own, 1)
    other = lax.dynamic_slice_in_dim(dc, (1 - core) * own, own, 1)
    dc_recv = swap_cores(other)
    up_sums = Total([up_keep, up_recv], True).cut(0)
    out_keep, out_send = col_grad(c_own, da, n_p, n_t)
    out_recv = swap_cores(out_send)
    dc_full = by_core(core, mine, dc_recv, 0)
    down_sum.cut(1)
    dc_full, layer_out = together([down_sum, up_sums], dc_full, layer_out)

    first = attend_bwd(0, qkv, context, dc_full, lse, segment, valid, 512, 256)
    out_sum = Total([out_keep, out_recv], False)
    keep, send, sum_first = qkv_grad(x_turned, *first, n_p)
    first_sum = Total([by_core(core, keep, swap_cores(send), 1)], True)
    (dc_full,) = together([down_sum.cut(2), up_sums.cut(1), out_sum.cut(0), first_sum.cut(0)], dc_full)
    second = attend_bwd(1, qkv, context, dc_full, lse, segment, valid, 512, 256)
    (second,) = together([down_sum.cut(3), up_sums.cut(2), out_sum.cut(1), first_sum.cut(1)], second)

    dx_other = swap_cores(input_pull(1 - core, core, (*first, *second), w_qkv))
    dx_mine = input_pull(core, core, (*first, *second), w_qkv, dm)
    dx = (dx_mine + dx_other.astype(F32)).astype(BF16)
    keep, send, sum_second = qkv_grad(x_turned, *second, n_p)
    qv_sum = jnp.concatenate([sum_first, sum_second], axis=1)
    down_total = down_sum.sum_of(lambda part: part)
    qv_pad = lax.dynamic_update_slice(jnp.zeros((2, width), F32), qv_sum[0:2], (0, core * own))
    small = jnp.concatenate(
        [
            jnp.stack([sums_one[0], sums_two[0], sums_one[1], sums_one[2], sums_two[1], sums_two[2]]).reshape(-1),
            qv_pad.reshape(-1),
            up_sum[0],
        ]
    )
    rows_of = lambda part, count: part.reshape(count, -1, part.shape[-1])
    given, qkv_total, up_total, out_total, small = finish(
        n_p, n_t, dx, rows_of(keep, n_p), rows_of(send, n_p), [rows_of(part, 2) for part in first_sum.parts],
        [rows_of(part, 2) for part in up_sums.parts], [rows_of(part, 4) for part in out_sum.parts], small.reshape(-1, 128),
    )
    input_grad = given.astype(F32)
    small = small.reshape(-1)
    up_total = up_total.reshape(up_sums.rest).transpose(1, 0, 2).reshape(up_weight.shape)
    qkv_total = qkv_total.reshape(first_sum.rest).transpose(0, 2, 1, 3).reshape(qkv_weight.shape)
    gain_sum = small[: 2 * width].reshape(2, width)
    bias_sum = small[2 * width : 6 * width].reshape(4, width)
    qv_total = lax.dynamic_slice_in_dim(small[6 * width : 8 * width].reshape(2, width), tensor * qv_bias.shape[1], qv_bias.shape[1], 1)
    up_bias_total = lax.dynamic_slice_in_dim(small[8 * width :], tensor * up_bias.shape[0], up_bias.shape[0])
    return (
        layer_out, input_grad, qkv_total, qv_total, out_total, gain_sum, bias_sum, up_total, up_bias_total, down_total,
    )


def solution(mesh):
    dp, tensor = mesh.devices.shape
    split = jax.sharding.Mesh(mesh.devices.reshape(dp // 2, 2, tensor), ("p", "core", "tensor"))
    pc = ("p", "core")
    tokens = P(None, ("p", "core", "tensor"), None)
    return jax.shard_map(
        body,
        mesh=split,
        in_specs=(
            tokens, P(None, pc, None), P(None, pc, None), P(None, pc, "tensor"), P(None, "tensor"), P("tensor", pc),
            P(), P(), P(pc, "tensor"), P("tensor"), P("tensor", pc), tokens,
        ),
        out_specs=(
            tokens, tokens, P(None, pc, "tensor"), P(None, "tensor"), P("tensor", pc), P(), P(), P(pc, "tensor"),
            P("tensor"), P("tensor", pc),
        ),
        check_vma=False,
    )
```

```python
import functools
import math
import jax
import jax.numpy as jnp
from jax import lax
from jax.sharding import PartitionSpec as P
from jax.experimental import pallas as pl
from jax.experimental.pallas import tpu as pltpu

HEAD = 64
PAIR = 2 * HEAD
NEG_FILL = -1e30
F32 = jnp.float32
BF16 = jnp.bfloat16
NT = (((1,), (1,)), ((), ()))
NN = (((1,), (0,)), ((), ()))
TN = (((0,), (0,)), ((), ()))


def dot(a, b, dims=NN, precision=None):
    return lax.dot_general(a, b, dims, preferred_element_type=F32, precision=precision)


def head_lanes(rows, which):
    lane = lax.broadcasted_iota(jnp.int32, (rows, PAIR), 1)
    return (lane < HEAD) if which == 0 else (lane >= HEAD)


def attend_fwd_kernel(bk, lo_ref, hi_ref, pad_ref, q_ref, k_ref, v_ref, qcode_ref, kcode_ref, o_ref, lse_ref, v_turned):
    i = pl.program_id(1)
    bq = q_ref.shape[0]

    @pl.when(i == 0)
    def _():
        v_turned[...] = v_ref[...].T

    q = q_ref[...] * jnp.asarray(0.125, BF16)
    heads = [jnp.where(head_lanes(bq, w), q, jnp.zeros_like(q)) for w in (0, 1)]
    qcode = qcode_ref[...]
    first = i * bq

    def run(diagonal):
        def step(t, carry):
            at = pl.multiple_of(t * bk, bk)
            keys = pl.ds(at, bk)
            k = k_ref[keys, :]
            mask = jnp.tile(kcode_ref[keys, :], (1, bq // 128)) == qcode
            if diagonal:
                gap = lax.broadcasted_iota(jnp.int32, (bk, bq), 0) - lax.broadcasted_iota(jnp.int32, (bk, bq), 1)
                mask = mask | (gap == first - at)
            out = []
            for h in (0, 1):
                top, total, acc = carry[3 * h : 3 * h + 3]
                s = jnp.where(mask, dot(k, heads[h], NT), NEG_FILL)
                new = jnp.maximum(top, jnp.max(s, axis=0, keepdims=True))
                p = jnp.exp(s - new)
                old = jnp.exp(top - new)
                v = v_turned[h * HEAD : (h + 1) * HEAD, keys]
                out += [
                    new,
                    total * old + jnp.sum(p, axis=0, keepdims=True),
                    acc * old + dot(v, p.astype(BF16)),
                ]
            return tuple(out)

        one = (jnp.full((1, bq), NEG_FILL, F32), jnp.zeros((1, bq), F32), jnp.zeros((HEAD, bq), F32))
        ma, la, aa, mb, lb, ab = lax.fori_loop(lo_ref[i], hi_ref[i], step, one + one)
        o_ref[...] = jnp.concatenate([aa / la, ab / lb], axis=0).T.astype(BF16)
        lse_ref[0:1, :] = ma + jnp.log(la)
        lse_ref[1:2, :] = mb + jnp.log(lb)

    pl.when(pad_ref[i] > 0)(lambda: run(True))
    pl.when(pad_ref[i] == 0)(lambda: run(False))


def attend_bwd_kernel(
    bq, lo_ref, hi_ref, pad_ref, q_ref, k_ref, v_ref, c_ref, dc_ref, lse_ref, qcode_ref, kcode_ref,
    dq_ref, dk_ref, dv_ref, dq_acc, delta,
):
    i = pl.program_id(1)
    bk = k_ref.shape[0]
    first = i * bk

    @pl.when(i == 0)
    def _():
        dq_acc[...] = jnp.zeros_like(dq_acc)
        row = lax.broadcasted_iota(jnp.int32, (8, PAIR), 0)
        lane = lax.broadcasted_iota(jnp.int32, (8, PAIR), 1)
        pick = jnp.where(lane // HEAD == row, 1.0, 0.0).astype(F32)
        prod = dc_ref[...].astype(F32) * c_ref[...].astype(F32)
        delta[...] = dot(pick, prod, NT, lax.Precision.HIGHEST)

    k = k_ref[...] * jnp.asarray(0.125, BF16)
    v = v_ref[...]
    k_turned = k.T
    kh = [jnp.where(head_lanes(bk, w), k, jnp.zeros_like(k)) for w in (0, 1)]
    vh = [jnp.where(head_lanes(bk, w), v, jnp.zeros_like(v)) for w in (0, 1)]
    kcode = jnp.tile(kcode_ref[...], (1, bq // 128))

    def run(diagonal):
        def step(t, carry):
            dk, dv = carry
            at = pl.multiple_of(t * bq, bq)
            rows = pl.ds(at, bq)
            q = q_ref[rows, :]
            dc = dc_ref[rows, :]
            mask = kcode == qcode_ref[:, rows]
            if diagonal:
                gap = lax.broadcasted_iota(jnp.int32, (bk, bq), 1) - lax.broadcasted_iota(jnp.int32, (bk, bq), 0)
                mask = mask | (gap == first - at)
            for h in (0, 1):
                s = dot(kh[h], q, NT)
                p = jnp.exp(jnp.where(mask, s - lse_ref[h : h + 1, rows], NEG_FILL))
                dp = dot(vh[h], dc, NT)
                ds = (p * (dp - delta[h : h + 1, rows])).astype(BF16)
                own = head_lanes(bq, h)
                dv = dv + dot(p.astype(BF16), jnp.where(own, dc, jnp.zeros_like(dc)))
                dk = dk + dot(ds, jnp.where(own, q, jnp.zeros_like(q)))
                dq_acc[h * HEAD : (h + 1) * HEAD, rows] += dot(k_turned[h * HEAD : (h + 1) * HEAD, :], ds)
            return dk, dv

        zero = jnp.zeros((bk, PAIR), F32)
        dk, dv = lax.fori_loop(lo_ref[i], hi_ref[i], step, (zero, zero))
        dk_ref[...] = (dk * 0.125).astype(BF16)
        dv_ref[...] = dv.astype(BF16)

    pl.when(pad_ref[i] > 0)(lambda: run(True))
    pl.when(pad_ref[i] == 0)(lambda: run(False))

    @pl.when(i == pl.num_programs(1) - 1)
    def _():
        dq_ref[...] = dq_acc[...].T.astype(BF16)


def block_bounds(segment, valid, block, other):
    length = segment.shape[0]
    blocks = segment.reshape(length // block, block)
    lo = jnp.sum((segment[None, :] < blocks[:, :1]).astype(jnp.int32), axis=1) // other
    hi = (jnp.sum((segment[None, :] <= blocks[:, -1:]).astype(jnp.int32), axis=1) + other - 1) // other
    pad = jnp.sum((valid.reshape(length // block, block) == 0).astype(jnp.int32), axis=1)
    return lo, hi, pad


def attention_codes(segment, valid):
    kcode = jnp.where(valid > 0, segment, -1)
    qcode = segment
    wide = lambda a: jnp.broadcast_to(a[:, None], (a.shape[0], 128))
    return qcode, kcode, wide(qcode), wide(kcode)


def qkv_at(pair, which):
    return pair // 2 * 6 + which * 2 + pair % 2


def attend_fwd(qkv, segment, valid, bq=256, bk=256):
    length, width = qkv.shape
    pairs = width // 3 // PAIR
    lo, hi, pad = block_bounds(segment, valid, bq, bk)
    qcode, kcode, qwide, kwide = attention_codes(segment, valid)
    return pl.pallas_call(
        functools.partial(attend_fwd_kernel, bk),
        grid_spec=pltpu.PrefetchScalarGridSpec(
            num_scalar_prefetch=3,
            grid=(pairs, length // bq),
            in_specs=[
                pl.BlockSpec((bq, PAIR), lambda h, i, *_: (i, qkv_at(h, 0))),
                pl.BlockSpec((length, PAIR), lambda h, i, *_: (0, qkv_at(h, 1))),
                pl.BlockSpec((length, PAIR), lambda h, i, *_: (0, qkv_at(h, 2))),
                pl.BlockSpec((1, bq), lambda h, i, *_: (0, i)),
                pl.BlockSpec((length, 128), lambda h, i, *_: (0, 0)),
            ],
            out_specs=[
                pl.BlockSpec((bq, PAIR), lambda h, i, *_: (i, h)),
                pl.BlockSpec((8, bq), lambda h, i, *_: (h, i)),
            ],
            scratch_shapes=[pltpu.VMEM((PAIR, length), BF16)],
        ),
        out_shape=[
            jax.ShapeDtypeStruct((length, pairs * PAIR), BF16),
            jax.ShapeDtypeStruct((pairs * 8, length), F32),
        ],
        compiler_params=pltpu.CompilerParams(dimension_semantics=("arbitrary", "arbitrary")),
        cost_estimate=pl.CostEstimate(flops=8 * 2 * length * length * PAIR, bytes_accessed=8 * length * width, transcendentals=4 * length * length),
    )(lo, hi, pad, qkv, qkv, qkv, qcode[None, :], kwide)


def attend_bwd(part, qkv, context, context_grad, lse, segment, valid, bq=256, bk=256):
    length, width = qkv.shape
    pairs = width // 6 // PAIR
    base = part * pairs
    lo, hi, pad = block_bounds(segment, valid, bk, bq)
    qcode, kcode, qwide, kwide = attention_codes(segment, valid)
    whole = pl.BlockSpec((length, PAIR), lambda h, i, *_: (0, h))
    piece = pl.BlockSpec((bk, PAIR), lambda h, i, *_: (i, h))
    source = pl.BlockSpec((length, PAIR), lambda h, i, *_: (0, base + h))
    cols = lambda at: pl.BlockSpec((bk, PAIR), lambda h, i, *_: (i, qkv_at(base + h, at)))
    shape = jax.ShapeDtypeStruct((length, pairs * PAIR), BF16)
    return pl.pallas_call(
        functools.partial(attend_bwd_kernel, bq),
        grid_spec=pltpu.PrefetchScalarGridSpec(
            num_scalar_prefetch=3,
            grid=(pairs, length // bk),
            in_specs=[
                pl.BlockSpec((length, PAIR), lambda h, i, *_: (0, qkv_at(base + h, 0))), cols(1), cols(2), source, source,
                pl.BlockSpec((8, length), lambda h, i, *_: (base + h, 0)),
                pl.BlockSpec((1, length), lambda h, i, *_: (0, 0)),
                pl.BlockSpec((bk, 128), lambda h, i, *_: (i, 0)),
            ],
            out_specs=[whole, piece, piece],
            scratch_shapes=[pltpu.VMEM((PAIR, length), F32), pltpu.VMEM((8, length), F32)],
        ),
        out_shape=[shape, shape, shape],
        compiler_params=pltpu.CompilerParams(dimension_semantics=("arbitrary", "arbitrary")),
        cost_estimate=pl.CostEstimate(flops=20 * 2 * length * length * PAIR, bytes_accessed=16 * length * width, transcendentals=4 * length * length),
    )(lo, hi, pad, qkv, qkv, qkv, context, context_grad, lse, qcode[None, :], kwide)


def norm_stats(values):
    center = values - jnp.mean(values, axis=1, keepdims=True)
    inverse = lax.rsqrt(jnp.mean(center * center, axis=1, keepdims=True) + 1e-05)
    return center * inverse, inverse


def norm_pull(incoming, normed, inverse, gain):
    scaled = incoming * gain
    return inverse * (
        scaled - jnp.mean(scaled, axis=1, keepdims=True) - normed * jnp.mean(scaled * normed, axis=1, keepdims=True)
    )


def col_sum(values):
    return jnp.sum(values, axis=0, keepdims=True)


def add_sums(ref, parts):
    @pl.when(pl.program_id(0) == 0)
    def _():
        ref[...] = jnp.zeros_like(ref)

    for at, part in enumerate(parts):
        ref[at : at + 1, :] += col_sum(part)


def mix_kernel(at_ref, x_ref, c_ref, w_ref, bias_ref, gain_ref, hl_ref, turned_ref, n_ref, r_ref):
    mixed = x_ref[...].astype(F32) + dot(c_ref[...], w_ref[...]) + bias_ref[0:1, :]
    normed, inverse = norm_stats(mixed)
    hl = (normed * gain_ref[0:1, :] + bias_ref[1:2, :]).astype(BF16)
    hl_ref[...] = hl
    turned_ref[...] = hl.T
    n_ref[...] = normed
    r_ref[...] = jnp.broadcast_to(inverse, r_ref.shape)


def up_kernel(h_ref, w_ref, bias_ref, g_ref, slope_ref):
    u = dot(h_ref[...], w_ref[...]) + bias_ref[...]
    cdf = 0.5 + 0.5 * lax.erf(u * (1.0 / math.sqrt(2.0)))
    g_ref[...] = (u * cdf).astype(BF16)
    slope_ref[...] = (cdf + u * (jnp.exp(-0.5 * u * u) * (1.0 / math.sqrt(2.0 * math.pi)))).astype(BF16)


def down_kernel(g_ref, w_ref, n_ref, e_ref, bias_ref, gain_ref, out_ref, dr_ref, dz_ref, sum_ref):
    hidden = n_ref[...] * gain_ref[0:1, :] + bias_ref[1:2, :]
    normed, inverse = norm_stats(hidden + dot(g_ref[...], w_ref[...]) + bias_ref[2:3, :])
    out_ref[...] = (normed * gain_ref[1:2, :] + bias_ref[3:4, :]).astype(BF16)
    e = e_ref[...].astype(F32)
    dr = norm_pull(e, normed, inverse, gain_ref[1:2, :])
    dr_ref[...] = dr
    dz_ref[...] = dr.astype(BF16)
    add_sums(sum_ref, (e * normed, dr, e))


def slope_kernel(dz_ref, w_ref, slope_ref, du_ref, sum_ref):
    du = (dot(dz_ref[...], w_ref[...], NT) * slope_ref[...].astype(F32)).astype(BF16)
    du_ref[...] = du

    @pl.when(pl.program_id(1) == 0)
    def _():
        sum_ref[...] = jnp.zeros_like(sum_ref)

    sum_ref[0:1, :] += col_sum(du.astype(F32))


def mix_pull_kernel(du_ref, w_ref, dr_ref, n_ref, r_ref, gain_ref, dm_ref, da_ref, sum_ref):
    dh = dr_ref[...] + dot(du_ref[...], w_ref[...], NT)
    normed = n_ref[...]
    dm = norm_pull(dh, normed, r_ref[:, 0:1], gain_ref[0:1, :])
    dm_ref[...] = dm
    da_ref[...] = dm.astype(BF16)
    add_sums(sum_ref, (dh * normed, dm, dh))


def call(kernel, grid, ins, outs, flops, nbytes, *args):
    return pl.pallas_call(
        kernel,
        grid=grid,
        in_specs=ins,
        out_specs=outs[0],
        out_shape=outs[1],
        compiler_params=pltpu.CompilerParams(dimension_semantics=("arbitrary",) * len(grid)),
        cost_estimate=pl.CostEstimate(flops=flops, bytes_accessed=nbytes, transcendentals=0),
    )(*args)


def rows(block, width):
    return pl.BlockSpec((block, width), lambda i: (i, 0))


def held(shape):
    return pl.BlockSpec(shape, lambda i: (0, 0))


def once(shape):
    return pl.BlockSpec(shape, lambda i: (0, 0), pipeline_mode=pl.Buffered(1))


def sds(shape, dtype=BF16):
    return jax.ShapeDtypeStruct(shape, dtype)


def mix(core_at, x, c, w, biases, gains, block=256):
    n, d = c.shape
    r = lambda width: pl.BlockSpec((block, width), lambda i, at: (i, 0))
    fixed = lambda value: pl.BlockSpec(value.shape, lambda i, at: (0, 0), pipeline_mode=pl.Buffered(1))
    steps = n // block
    return pl.pallas_call(
        mix_kernel,
        grid_spec=pltpu.PrefetchScalarGridSpec(
            num_scalar_prefetch=1,
            grid=(steps,),
            in_specs=[
                pl.BlockSpec((block, d), lambda i, at: (at[0] * steps + i, 0)), r(d), fixed(w), fixed(biases), fixed(gains),
            ],
            out_specs=[r(d), pl.BlockSpec((d, block), lambda i, at: (0, i)), r(d), r(128)],
        ),
        out_shape=[sds((n, d)), sds((d, n)), sds((n, d), F32), sds((n, 128), F32)],
        compiler_params=pltpu.CompilerParams(dimension_semantics=("arbitrary",)),
        cost_estimate=pl.CostEstimate(flops=2 * n * d * d, bytes_accessed=12 * n * d, transcendentals=0),
    )(core_at, x, c, w, biases, gains)


def up(h, w, bias, block=256, cols=1024):
    n, d = h.shape
    f = w.shape[1]
    cols = min(cols, f)
    tile = pl.BlockSpec((block, cols), lambda j, i: (i, j))
    return call(
        up_kernel, (f // cols, n // block),
        [pl.BlockSpec((block, d), lambda j, i: (i, 0)), pl.BlockSpec((d, cols), lambda j, i: (0, j)), pl.BlockSpec((1, cols), lambda j, i: (0, j))],
        ([tile, tile], [sds((n, f)), sds((n, f))]),
        2 * n * d * f, 4 * n * f + 2 * d * f, h, w, bias,
    )


def down(g, w, normed, e, biases, gains, block=256):
    n, f = g.shape
    d = w.shape[1]
    r = functools.partial(rows, block)
    return call(
        down_kernel, (n // block,),
        [r(f), once(w.shape), r(d), r(d), held(biases.shape), held(gains.shape)],
        ([r(d), r(d), r(d), held((8, d))], [sds((n, d)), sds((n, d), F32), sds((n, d)), sds((8, d), F32)]),
        2 * n * d * f, 2 * n * f + 2 * d * f, g, w, normed, e, biases, gains,
    )


def slope_pull(dz, w, slope, block=256, cols=1024):
    n, d = dz.shape
    f = w.shape[0]
    tile = pl.BlockSpec((block, cols), lambda j, i: (i, j))
    return call(
        slope_kernel, (f // cols, n // block),
        [pl.BlockSpec((block, d), lambda j, i: (i, 0)), pl.BlockSpec((cols, d), lambda j, i: (j, 0)), tile],
        ([tile, pl.BlockSpec((8, cols), lambda j, i: (0, j))], [sds((n, f)), sds((8, f), F32)]),
        2 * n * d * f, 4 * n * f + 2 * d * f, dz, w, slope,
    )


def mix_pull(du, w, dr, normed, inverse, gains, block=256):
    n, f = du.shape
    d = w.shape[0]
    r = functools.partial(rows, block)
    return call(
        mix_pull_kernel, (n // block,),
        [r(f), once(w.shape), r(d), r(d), r(128), held(gains.shape)],
        ([r(d), r(d), held((8, d))], [sds((n, d), F32), sds((n, d)), sds((8, d), F32)]),
        2 * n * d * f, 2 * n * f + 2 * d * f, du, w, dr, normed, inverse, gains,
    )


def split_columns(acc, keep_ref, send_ref):
    n_p, c = keep_ref.shape[0], keep_ref.shape[3]
    for bit in (0, 1):

        @pl.when(lax.axis_index("core") == bit)
        def _():
            for p in range(n_p):
                at, to = (2 * p + bit) * c, (2 * p + 1 - bit) * c
                keep_ref[p, 0] = acc[:, at : at + c]
                send_ref[p, 0] = acc[:, to : to + c]


def split_rows(acc, place, keep_ref, send_ref):
    n_p, r = keep_ref.shape[0], keep_ref.shape[-2]
    for bit in (0, 1):

        @pl.when(lax.axis_index("core") == bit)
        def _():
            for p in range(n_p):
                at, to = (2 * p + bit) * r, (2 * p + 1 - bit) * r
                for cb in range(acc.shape[1] // 128):
                    keep_ref[(p, 0) + place + (cb,)] = acc[at : at + r, cb * 128 : cb * 128 + 128]
                    send_ref[(p, 0) + place + (cb,)] = acc[to : to + r, cb * 128 : cb * 128 + 128]


def col_grad_kernel(a_ref, b_ref, keep_ref, send_ref, acc):
    acc[...] = dot(a_ref[...], b_ref[...], TN).astype(BF16)
    split_columns(acc, keep_ref, send_ref)


def row_grad_kernel(a_ref, b_ref, keep_ref, send_ref, acc):
    acc[...] = dot(a_ref[...], b_ref[...]).astype(BF16)
    split_rows(acc, (), keep_ref, send_ref)


def grad_call(kernel, grid, ins, outs, scratch, flops, *args):
    return pl.pallas_call(
        kernel,
        grid=grid,
        in_specs=ins,
        out_specs=outs[0],
        out_shape=outs[1],
        scratch_shapes=scratch,
        compiler_params=pltpu.CompilerParams(dimension_semantics=("arbitrary",) * len(grid)),
        cost_estimate=pl.CostEstimate(flops=flops, bytes_accessed=flops // 512, transcendentals=0),
    )(*args)


def col_grad(a, b, n_p, n_t, block=512):
    n, f = a.shape
    d = b.shape[1]
    per_t, c = f // n_t, d // (2 * n_p)
    block = min(block, per_t)
    steps = per_t // block
    spec = pl.BlockSpec((n_p, 1, block, c), lambda i: (0, i // steps, i % steps, 0))
    shape = sds((n_p, n_t, per_t, c))
    return grad_call(
        col_grad_kernel, (f // block,),
        [pl.BlockSpec((n, block), lambda i: (0, i)), once((n, d))],
        ([spec, spec], [shape, shape]), [pltpu.VMEM((block, d), BF16)], 2 * n * f * d, a, b,
    )


def row_grad(a, b, n_p, n_t, block=512):
    d, n = a.shape
    f = b.shape[1]
    per_t, r = f // n_t, d // (2 * n_p)
    steps = per_t // block
    spec = pl.BlockSpec((n_p, 1, block // 128, r, 128), lambda i: (0, i // steps, i % steps, 0, 0))
    shape = sds((n_p, n_t, per_t // 128, r, 128))
    return grad_call(
        row_grad_kernel, (f // block,),
        [once((d, n)), pl.BlockSpec((n, block), lambda i: (0, i))],
        ([spec, spec], [shape, shape]), [pltpu.VMEM((d, block), BF16)], 2 * n * f * d, a, b,
    )


def input_pull_kernel(extra, at_ref, *refs):
    parts, w_ref = refs[:6], refs[6]
    c = w_ref.shape[1] // 6
    total = dot(parts[0][...], w_ref[:, :c], NT)
    for j in range(1, 6):
        total = total + dot(parts[j][...], w_ref[:, j * c : (j + 1) * c], NT)
    if extra:
        total = total + refs[7][...]
    refs[-1][...] = total.astype(refs[-1].dtype)


def input_pull(half, core, parts, w, dm=None, block=256):
    n, f = parts[0].shape
    d = w.shape[0]
    steps = n // 2 // block
    cols = pl.BlockSpec((block, f), lambda i, at: (at[0] * steps + i, 0))
    own = pl.BlockSpec((block, d), lambda i, at: (i, 0))
    extra = [] if dm is None else [dm]
    held_w = pl.BlockSpec((d, w.shape[1] // 2), lambda i, at: (0, at[1]), pipeline_mode=pl.Buffered(1))
    return pl.pallas_call(
        functools.partial(input_pull_kernel, len(extra)),
        grid_spec=pltpu.PrefetchScalarGridSpec(
            num_scalar_prefetch=1,
            grid=(steps,),
            in_specs=[cols] * 6 + [held_w] + [own] * len(extra),
            out_specs=own,
        ),
        out_shape=sds((n // 2, d), BF16 if dm is None else F32),
        compiler_params=pltpu.CompilerParams(dimension_semantics=("arbitrary",)),
        cost_estimate=pl.CostEstimate(flops=6 * n * f * d, bytes_accessed=8 * n * d, transcendentals=0),
    )(jnp.stack([half, core]).astype(jnp.int32), *parts, w, *extra)


MESH_ID = pl.DeviceIdType.MESH


def flip(value, bit):
    return value + bit - 2 * bit * ((value // bit) % 2)


def start_kernel(n_p, n_t, kinds, *refs):
    n = len(kinds)
    x_ref, bias_ref, *shards = refs[: n + 2]
    x_out, bias_out, *fulls = refs[n + 2 : 2 * n + 4]
    send_sems, recv_sems, own_sems = refs[2 * n + 4 :]
    p, core, t = lax.axis_index("p"), lax.axis_index("core"), lax.axis_index("tensor")
    me = 2 * p + core
    bits = [1 << s for s in range(n_p.bit_length() - 1)]
    column = [{"tensor": lax.rem(t + r, n_t)} for r in range(1, n_t)]
    across = [{"core": 1 - core, "tensor": lax.rem(t + r, n_t)} for r in range(n_t)]
    plane = [{"p": flip(p, bit)} for bit in bits]
    barrier = pltpu.get_barrier_semaphore()
    for peer in column + across + plane:
        pl.semaphore_signal(barrier, inc=1, device_id=peer, device_id_type=MESH_ID)
    pl.semaphore_wait(barrier, len(column + across + plane))

    used = [0, 0]

    def group():
        used[0] += 1
        return used[0] - 1

    def send(source, target, at, peer):
        pltpu.make_async_remote_copy(
            src_ref=source, dst_ref=target, send_sem=send_sems.at[at], recv_sem=recv_sems.at[at],
            device_id=peer, device_id_type=MESH_ID,
        ).start()

    def arrived(view, at):
        pltpu.make_async_copy(view, view, recv_sems.at[at]).wait()

    def left(view, at):
        pltpu.make_async_copy(view, view, send_sems.at[at]).wait()

    def keep(source, target):
        used[1] += 1
        copy = pltpu.make_async_copy(source, target, own_sems.at[used[1] - 1])
        copy.start()
        return copy

    def slab(i, d, half):
        full, kind = fulls[i], kinds[i]
        if kind == "rows":
            depth, wide = shards[i].shape[-2], full.shape[1] // 2
            return full.at[pl.ds(pl.multiple_of(d * depth, depth), depth), pl.ds(half * wide, wide)]
        depth, tall = shards[i].shape[-1], full.shape[0] // 2
        return full.at[pl.ds(half * tall, tall), pl.ds(pl.multiple_of(d * depth, depth), depth)]

    def slabs(i, count, half):
        full, kind = fulls[i], kinds[i]
        if kind == "rows":
            wide = full.shape[1] // 2
            return full.at[pl.ds(0, count * shards[i].shape[-2]), pl.ds(half * wide, wide)]
        tall = full.shape[0] // 2
        return full.at[pl.ds(half * tall, tall), pl.ds(0, count * shards[i].shape[-1])]

    def places(i, t):
        shard, full = shards[i], fulls[i]
        if kinds[i] == "columns":
            tall, depth = shard.shape
            return [(shard, full.at[pl.ds(pl.multiple_of(t * tall, tall), tall), pl.ds(pl.multiple_of(me * depth, depth), depth)])]
        depth, wide = shard.shape[-2:]
        rows_at = pl.ds(pl.multiple_of(me * depth, depth), depth)
        if len(shard.shape) == 2:
            return [(shard, full.at[rows_at, pl.ds(pl.multiple_of(t * wide, wide), wide)])]
        count = shard.shape[0]
        return [
            (shard.at[w], full.at[rows_at, pl.ds(pl.multiple_of((t * count + w) * wide, wide), wide)])
            for w in range(count)
        ]

    def shares(i, count):
        shard, full = shards[i], fulls[i]
        if kinds[i] == "columns":
            return full.at[pl.ds(0, count * shard.shape[0]), pl.ds(0, shard.shape[1])]
        wide = math.prod(shard.shape) // shard.shape[-2]
        return full.at[pl.ds(0, shard.shape[-2]), pl.ds(0, count * wide)]

    hops = n_t - 1
    own = [[keep(source, target) for source, target in places(i, t)] for i in range(n)]
    right, left_to = {"tensor": lax.rem(t + 1, n_t)}, {"tensor": lax.rem(t + n_t - 1, n_t)}
    line = [[(group(), group()) for _ in range(hops)] for _ in range(n)]

    def hop(i, s):
        to_right, to_left = line[i][s]

        @pl.when(jnp.logical_and(t + 1 < n_t, t >= s))
        def _():
            for source, target in places(i, t - s):
                send(source if s == 0 else target, target, to_right, right)

        @pl.when(jnp.logical_and(t >= 1, t + s < n_t))
        def _():
            for source, target in places(i, t + s):
                send(source if s == 0 else target, target, to_left, left_to)

    def hop_arrived(i, s):
        to_right, to_left = line[i][s]
        pl.when(t >= s + 1)(lambda: arrived(shares(i, 1), to_right))
        pl.when(t + s + 1 < n_t)(lambda: arrived(shares(i, 1), to_left))

    def hop_left(i, s):
        to_right, to_left = line[i][s]
        pl.when(jnp.logical_and(t + 1 < n_t, t >= s))(lambda: left(shares(i, 1), to_right))
        pl.when(jnp.logical_and(t >= 1, t + s < n_t))(lambda: left(shares(i, 1), to_left))

    for i in range(n):
        hop(i, 0)
    bias_at = group()
    bias_own = keep(bias_ref, bias_out.at[t])
    for peer in column:
        send(bias_ref, bias_out.at[t], bias_at, peer)

    held = x_ref.shape[1]
    odd = t % 2
    x_rows = x_out.at[pl.ds(pl.multiple_of(t * held, held), held), :]
    x_at = [group(), group()]
    stays = core == t // 2
    peer_a = {"core": t // 2, "tensor": 2 * core + odd}
    peer_b = {"core": t // 2, "tensor": 2 * core + 1 - odd}

    x_own = pltpu.make_async_copy(x_ref.at[odd], x_rows, own_sems.at[used[1]])
    used[1] += 1
    pl.when(stays)(x_own.start)

    def send_tokens():
        pl.when(jnp.logical_not(stays))(lambda: send(x_ref.at[odd], x_rows, x_at[0], peer_a))
        send(x_ref.at[1 - odd], x_rows, x_at[1], peer_b)

    partner = {"core": 1 - core}
    passes = []

    def forward(i, masks, half):
        at = group()
        guard = i == 0

        def go():
            for mask in masks:
                d = 2 * mask + core
                send(slab(i, d, half), slab(i, d, half), at, partner)

        if guard:
            pl.when(core == 1 - half)(go)
        else:
            go()
        passes.append((i, len(masks), half, at))

    states = {}

    def stage(i, s):
        if s == 0:
            hop_arrived(i, hops - 1)
            states[i] = {}
            for half in (0, 1):
                states[i][half] = ([p], None)
        else:
            for half in (0, 1):
                masks, at = states[i][half]
                arrived(slabs(i, len(masks), half), at)
                bit = bits[s - 1] if half == 0 else bits[-s]
                states[i][half] = (masks + [flip(m, bit) for m in masks], None)
        for half in (0, 1):
            masks, _ = states[i][half]
            if s < len(bits):
                at = group()
                bit = bits[s] if half == 0 else bits[-s - 1]
                for m in masks:
                    d = 2 * m + core
                    send(slab(i, d, half), slab(i, d, half), at, {"p": flip(p, bit)})
                states[i][half] = (masks, at)
                finish.append((i, len(masks), half, at))
            fresh = masks if s == 0 else masks[len(masks) // 2 :]
            forward(i, fresh, half)

    finish = []
    for step in range(n + hops - 1 + len(bits)):
        for i in range(n):
            at = step - i
            if 0 <= at < hops - 1:
                if at == 0:
                    for copy in own[i]:
                        copy.wait()
                hop_arrived(i, at)
                hop(i, at + 1)
                if i == n - 1 and at == hops - 2:
                    send_tokens()
            elif 0 <= at - (hops - 1) <= len(bits):
                stage(i, at - (hops - 1))

    pl.when(jnp.logical_not(stays))(lambda: arrived(x_rows, x_at[0]))
    pl.when(stays)(x_own.wait)
    arrived(x_rows, x_at[1])
    half_rows = x_out.at[pl.ds(pl.multiple_of(core * 2 * held, 2 * held), 2 * held), :]
    x_pass = group()
    send(half_rows, half_rows, x_pass, partner)
    bias_own.wait()
    arrived(bias_out.at[pl.ds(0, n_t - 1)], bias_at)
    for i, count, half, at in passes:
        if i == 0:
            pl.when(core == half)(functools.partial(arrived, slabs(i, count, half), at))
        else:
            arrived(slabs(i, count, half), at)
    arrived(half_rows, x_pass)
    left(half_rows, x_pass)
    for i, count, half, at in passes:
        if i == 0:
            pl.when(core == 1 - half)(functools.partial(left, slabs(i, count, half), at))
        else:
            left(slabs(i, count, half), at)
    for i, count, half, at in finish:
        left(slabs(i, count, half), at)
    for i in range(n):
        for s in range(hops):
            hop_left(i, s)
    left(bias_out.at[pl.ds(0, n_t - 1)], bias_at)
    pl.when(jnp.logical_not(stays))(lambda: left(x_rows, x_at[0]))
    left(x_rows, x_at[1])


def start_gather(x, bias, shards, kinds, n_p, n_t):
    n_dp = 2 * n_p
    fulls = []
    for shard, kind in zip(shards, kinds):
        if kind == "columns":
            fulls.append(sds((shard.shape[0] * n_t, shard.shape[1] * n_dp)))
        else:
            fulls.append(sds((shard.shape[-2] * n_dp, math.prod(shard.shape) // shard.shape[-2] * n_t)))
    bits = n_p.bit_length() - 1
    count = len(shards) * (2 * (n_t - 1) + 2 * bits + 2 * (bits + 1)) + 4
    vmem, away = pl.BlockSpec(memory_space=pltpu.VMEM), pl.BlockSpec(memory_space=pl.ANY)
    return pl.pallas_call(
        functools.partial(start_kernel, n_p, n_t, kinds),
        out_shape=[sds((n_t * x.shape[1], x.shape[2])), sds((n_t,) + bias.shape, F32)] + fulls,
        in_specs=[vmem] * (2 + len(shards)),
        out_specs=[away] * (2 + len(shards)),
        scratch_shapes=[
            pltpu.SemaphoreType.DMA((count,)), pltpu.SemaphoreType.DMA((count,)), pltpu.SemaphoreType.DMA((10,)),
        ],
        compiler_params=pltpu.CompilerParams(collective_id=1, has_side_effects=True),
    )(x, bias, *shards)


def project_kernel(core_ref, x_ref, w_ref, bias_ref, out_ref, turned_ref):
    turned_ref[...] = x_ref[...].T
    out_ref[...] = (dot(x_ref[...], w_ref[...]) + bias_ref[...]).astype(BF16)


def project(core_at, x, w, bias, block=256):
    n, d = x.shape
    f = w.shape[1] // 2
    return pl.pallas_call(
        project_kernel,
        grid_spec=pltpu.PrefetchScalarGridSpec(
            num_scalar_prefetch=1,
            grid=(n // block,),
            in_specs=[
                pl.BlockSpec((block, d), lambda i, at: (i, 0)),
                pl.BlockSpec((d, f), lambda i, at: (0, at[0]), pipeline_mode=pl.Buffered(1)),
                pl.BlockSpec((1, f), lambda i, at: (0, 0)),
            ],
            out_specs=[pl.BlockSpec((block, f), lambda i, at: (i, 0)), pl.BlockSpec((d, block), lambda i, at: (0, i))],
        ),
        out_shape=[sds((n, f)), sds((d, n))],
        compiler_params=pltpu.CompilerParams(dimension_semantics=("arbitrary",)),
        cost_estimate=pl.CostEstimate(flops=2 * n * d * f, bytes_accessed=4 * n * d + 2 * n * f, transcendentals=0),
    )(core_at, x, w, bias)


def finish_kernel(n_p, n_t, *refs):
    dx, x_turned, *grads, up_a, up_b, out_a, out_b, small = refs[:13]
    given, qkv_out, up_out, out_out, small_out = refs[13:18]
    keep2, send2, acc, recv2, pairs, slots1, last, last_slot, up_cur, up_slot, out_cur, out_slot = refs[18:30]
    out_next, out_last, small_cur, small_slot = refs[30:34]
    bits = [n_p >> (s + 1) for s in range(n_p.bit_length() - 1)]
    curs, slots = refs[34 : 34 + len(bits)], refs[34 + len(bits) : 34 + 2 * len(bits)]
    send_sems, recv_sems = refs[-2:]
    p, core, t = lax.axis_index("p"), lax.axis_index("core"), lax.axis_index("tensor")
    partner = {"core": 1 - core}
    column = [{"tensor": lax.rem(t + r, n_t)} for r in range(1, n_t)]
    column += [{"core": 1 - core, "tensor": lax.rem(t + r, n_t)} for r in range(n_t)]
    plane = [{"p": flip(p, bit)} for bit in bits]
    line = {bit: {"tensor": flip(t, bit)} for bit in (2, 1)}
    barrier = pltpu.get_barrier_semaphore()
    for peer in column + plane:
        pl.semaphore_signal(barrier, inc=1, device_id=peer, device_id_type=MESH_ID)
    pl.semaphore_wait(barrier, len(column + plane))

    used = [0]

    def send(source, target, peer):
        at = used[0]
        used[0] += 1
        copy = pltpu.make_async_remote_copy(
            src_ref=source, dst_ref=target, send_sem=send_sems.at[at], recv_sem=recv_sems.at[at],
            device_id=peer, device_id_type=MESH_ID,
        )
        return copy

    def go(source, target, peer):
        copy = send(source, target, peer)
        copy.start()
        return copy

    def plus(a, b):
        return (a.astype(F32) + b.astype(F32)).astype(BF16)

    u, odd = t // 2, t % 2
    for at in range(4):
        out_cur[at % 2, at // 2] = plus(out_a[at], out_b[at])
    out_move = go(out_cur.at[1 - odd], out_slot, line[1])
    for at in (0, 1):
        up_cur[at] = plus(up_a[at], up_b[at])
    up_move = go(up_cur.at[1 - u], up_slot, line[2])

    held = given.shape[1]
    stays = core == u
    rows_a = dx.at[pl.ds(pl.multiple_of(odd * held, held), held), :]
    rows_b = dx.at[pl.ds(pl.multiple_of((1 - odd) * held, held), held), :]
    give_a = send(rows_a, given.at[odd], {"core": u, "tensor": 2 * core + odd})
    pl.when(jnp.logical_not(stays))(give_a.start)
    give_b = go(rows_b, given.at[odd], {"core": u, "tensor": 2 * core + 1 - odd})

    @pl.when(stays)
    def _():
        given[odd] = dx[pl.ds(pl.multiple_of(odd * held, held), held), :]

    orders = [bits, bits[::-1]]

    def spot(part, j):
        return sum(n_p >> (s + 1) for s, bit in enumerate(orders[part]) if j // bit % 2)

    r = keep2.shape[2] // 6
    swaps = []
    for part in (0, 1):
        for which in range(3):
            acc[...] = dot(x_turned[...], grads[3 * part + which][...]).astype(BF16)
            for bit in (0, 1):

                @pl.when(core == bit)
                def _():
                    for j in range(n_p):
                        at, to = (2 * j + bit) * r, (2 * j + 1 - bit) * r
                        for cb in (0, 1):
                            place = pl.ds((2 * which + cb) * r, r)
                            keep2[part, spot(part, j), place, :] = acc[at : at + r, cb * 128 : cb * 128 + 128]
                            send2[part, spot(part, j), place, :] = acc[to : to + r, cb * 128 : cb * 128 + 128]
        swaps.append(go(send2.at[part], recv2.at[part], partner))
    small_cur[0] = small[...]
    per_row = dx.shape[1] // 128
    for part in (0, 1):
        for which in (0, 1):
            total = jnp.sum(grads[3 * part + 2 * which][...].astype(F32), axis=0, keepdims=True)
            for bit in (0, 1):

                @pl.when(core == bit)
                def _():
                    at = (6 + which) * per_row + bit * (per_row // 2) + part * (per_row // 4)
                    for cb in (0, 1):
                        small_cur[0, at + cb : at + cb + 1, :] = total[:, cb * 128 : cb * 128 + 128]

    peers = [partner] + plane
    for at, peer in enumerate(peers):
        copy = go(small_cur.at[at], small_slot.at[at], peer)
        copy.wait()
        small_cur[at + 1] = small_cur[at] + small_slot[at]

    sources = []
    for part in (0, 1):
        swaps[part].wait()
        sources.append([keep2.at[part], recv2.at[part]])
    for s in range(len(bits)):
        size = n_p >> (s + 1)
        copies = []
        for part in (0, 1):
            bit = orders[part][s]
            mine = (p // bit) % 2
            peer = {"p": flip(p, bit)}
            copies.append(
                [go(sources[part][j].at[pl.ds((1 - mine) * size, size)], slots[s].at[part, j], peer) for j in (0, 1)]
            )
        for part in (0, 1):
            mine = (p // orders[part][s]) % 2
            for j in (0, 1):
                copies[part][j].wait()
                if size == 1:
                    pairs[part, core if j == 0 else 1 - core] = plus(sources[part][j][mine], slots[s][part, j, 0])
                else:
                    for at in range(size):
                        curs[s][part, j, at] = plus(sources[part][j][mine * size + at], slots[s][part, j, at])
            sources[part] = [curs[s].at[part, 0], curs[s].at[part, 1]]
    pair_move = go(pairs.at[1 - odd], slots1, line[1])
    out_move.wait()
    for at in (0, 1):
        out_next[at] = plus(out_cur[odd, at], out_slot[at])
    out_move = go(out_next.at[1 - u], out_last, line[2])
    pair_move.wait()
    for at in (0, 1):
        last[at] = plus(pairs[odd, at], slots1[at])
    last_move = go(last.at[1 - u], last_slot, line[2])
    for bit in (1, 2):
        at = len(peers)
        copy = go(small_cur.at[at], small_slot.at[at], line[bit])
        copy.wait()
        peers.append(None)
        if bit == 2:
            small_out[...] = small_cur[at] + small_slot[at]
        else:
            small_cur[at + 1] = small_cur[at] + small_slot[at]
    up_move.wait()
    up_out[...] = up_cur[u].astype(F32) + up_slot[...].astype(F32)
    out_move.wait()
    out_out[...] = out_next[u].astype(F32) + out_last[...].astype(F32)
    last_move.wait()
    qkv_out[...] = last[u].astype(F32) + last_slot[...].astype(F32)
    pl.when(jnp.logical_not(stays))(give_a.wait)
    give_b.wait()


def finish(n_p, n_t, dx, x_turned, first, second, up_, out_, small):
    d, wide = x_turned.shape[0], first[0].shape[1]
    rows_ = 3 * wide * d // (2 * n_p) // 128
    bits = n_p.bit_length() - 1
    steps = 1 + bits + 2
    box = lambda *lead: pltpu.VMEM(lead + (rows_, 128), BF16)
    like = lambda lead, value: pltpu.VMEM(lead + value.shape[1:], BF16)
    halves = [box(2, 2, n_p >> (s + 1)) for s in range(bits)]
    vmem = pl.BlockSpec(memory_space=pltpu.VMEM)
    count = 9 + steps + 4 * bits
    return pl.pallas_call(
        functools.partial(finish_kernel, n_p, n_t),
        out_shape=[
            sds((2, dx.shape[0] // 2, dx.shape[1])), sds((rows_, 128), F32), sds(up_[0].shape[1:], F32),
            sds(out_[0].shape[1:], F32), sds(small.shape, F32),
        ],
        in_specs=[vmem] * 13,
        out_specs=[vmem] * 5,
        scratch_shapes=[
            box(2, n_p), box(2, n_p), pltpu.VMEM((d, wide), BF16), box(2, n_p), box(2, 2), box(2), box(2), box(),
            like((2,), up_[0]), like((), up_[0]), like((2, 2), out_[0]), like((2,), out_[0]), like((2,), out_[0]),
            like((), out_[0]), pltpu.VMEM((steps,) + small.shape, F32), pltpu.VMEM((steps,) + small.shape, F32),
            *halves, *halves,
            pltpu.SemaphoreType.DMA((count,)), pltpu.SemaphoreType.DMA((count,)),
        ],
        compiler_params=pltpu.CompilerParams(collective_id=0, has_side_effects=True),
    )(dx, x_turned, *first, *second, *up_, *out_, small)


def swap_cores(value):
    return lax.ppermute(value, "core", [(0, 1), (1, 0)])


def column_routes(tensor_size):
    first, second = [], []
    for core in range(2):
        for t in range(tensor_size):
            at = core * tensor_size + t
            first.append((at, (t >> 1) * tensor_size + 2 * core + (t & 1)))
            second.append((at, (t >> 1) * tensor_size + 2 * core + 1 - (t & 1)))
    return first, second


def back(route):
    return [(b, a) for a, b in route]


def by_core(core, mine, other, axis):
    return jnp.where(
        core == 0, jnp.concatenate([mine, other], axis=axis), jnp.concatenate([other, mine], axis=axis)
    )


def body(
    inputs, segment_ids, token_valid, qkv_weight, qv_bias, out_weight, norm_gains, row_biases,
    up_weight, up_bias, down_weight, out_grad,
):
    COL = ("core", "tensor")
    ALL = ("p", "core", "tensor")
    core, tensor = lax.axis_index("core"), lax.axis_index("tensor")
    n_p, n_t = lax.axis_size("p"), lax.axis_size("tensor")
    n_dp = 2 * n_p
    micro, held_rows, width = inputs.shape
    assert micro == 2 and n_t == 4
    odd = tensor & 1
    route_a, route_b = column_routes(n_t)

    def bring(value):
        a = lax.ppermute(value[odd], COL, route_a)
        b = lax.ppermute(value[1 - odd], COL, route_b)
        return jnp.where(odd == 0, jnp.concatenate([a, b]), jnp.concatenate([b, a]))

    def blocks(value):
        return [lax.dynamic_slice_in_dim(value, at * held_rows, held_rows) for at in (odd, 1 - odd)]

    def give(a, b):
        a, b = lax.ppermute(a, COL, back(route_a)), lax.ppermute(b, COL, back(route_b))
        return jnp.where(odd == 0, jnp.stack([a, b]), jnp.stack([b, a]))

    def gathered(weight):
        got = lax.all_gather(weight, ALL, axis=0, tiled=False)
        return got.reshape((n_dp, n_t) + weight.shape)

    labels = jnp.stack([segment_ids[:, 0], token_valid[:, 0]], axis=1)[odd]
    labels = jnp.where((tensor >> 1) == core, labels, swap_cores(labels))
    segment, valid = labels[0], labels[1]

    shards, kinds = [qkv_weight, up_weight], ["rows", "rows"]
    wide = out_weight.shape[1] % 128 == 0
    if wide:
        shards, kinds = [qkv_weight, out_weight, up_weight, down_weight], ["rows", "columns", "rows", "columns"]
    local_bias = jnp.concatenate([qv_bias.reshape(-1), up_bias]).reshape(-1, 128)
    x_full, bias_all, *fulls = start_gather(inputs, local_bias, shards, kinds, n_p, n_t)
    if wide:
        w_qkv, w_out, w_up, w_down = fulls
    else:
        w_qkv, w_up = fulls
        w_out = gathered(out_weight).transpose(1, 2, 0, 3).reshape(-1, width)
        w_down = gathered(down_weight).transpose(1, 2, 0, 3).reshape(-1, width)
    out_grad, x_full = lax.optimization_barrier((out_grad, x_full))
    rows = x_full.shape[0] // 2
    own = w_qkv.shape[1] // 6
    bias_all = bias_all.reshape(n_t, -1)
    n_qv = qv_bias.size
    up_bias_all = bias_all[:, n_qv:].reshape(1, -1)
    qv_own = lax.dynamic_slice_in_dim(bias_all[:, :n_qv], 2 * core, 2).reshape(2, 2, -1)
    bias = jnp.stack([qv_own[:, 0], jnp.zeros_like(qv_own[:, 0]), qv_own[:, 1]], axis=1).reshape(1, -1)
    core_at = jnp.reshape(core, (1,)).astype(jnp.int32)
    qkv, x_turned = project(core_at, x_full, w_qkv, bias)
    context, lse = attend_fwd(qkv, segment, valid, 512, 512)
    mine = lax.dynamic_slice_in_dim(context, core * rows, rows)
    other = lax.dynamic_slice_in_dim(context, (1 - core) * rows, rows)
    c_own = by_core(core, mine, swap_cores(other), 1)
    hl, hl_turned, normed, inverse = mix(core_at, x_full, c_own, w_out, row_biases, norm_gains)
    active, slope = up(hl, w_up, up_bias_all)
    grad_own = bring(out_grad)
    layer, dr, dz, sums_two = down(active, w_down, normed, grad_own, row_biases, norm_gains)
    layer_out = give(*blocks(layer))

    p_bits = [1 << s for s in range(n_p.bit_length() - 1)]
    t_bits = [1, 2]

    class Total:
        def __init__(self, parts, downward):
            lead = [("p", n_p, bit) for bit in reversed(p_bits)] + [("tensor", n_t, bit) for bit in (2, 1)]
            self.rest = parts[0].shape[2:]
            self.dims = lead
            self.parts = [part.reshape((2,) * len(lead) + self.rest) for part in parts]
            order = list(reversed(p_bits)) if downward else p_bits
            self.groups = [order[:1], order[1:], t_bits[:1], t_bits[1:]]

        def sum_of(self, pick):
            total = pick(self.parts[0]).astype(F32)
            for part in self.parts[1:]:
                total = total + pick(part).astype(F32)
            return total

        def cut_one(self, axis, bit):
            at = [d[0] + str(d[2]) for d in self.dims].index(axis + str(bit))
            size = self.dims[at][1]
            self.dims = self.dims[:at] + self.dims[at + 1 :]
            mine = (lax.axis_index(axis) // bit) % 2
            side = lambda which: self.sum_of(lambda part: lax.dynamic_index_in_dim(part, which, at, keepdims=False)).astype(BF16)
            self.live = [side(mine), side(1 - mine)]
            self.route = (axis, [(i, i ^ bit) for i in range(size)])

        def move(self):
            self.parts = [self.live[0], lax.ppermute(self.live[1], *self.route)]
            return self

        def cut(self, group):
            axis = "p" if group < 2 else "tensor"
            for j, bit in enumerate(self.groups[group]):
                if j:
                    self.move()
                self.cut_one(axis, bit)
            return self

    def together(sums, *others):
        lives, others = lax.optimization_barrier(([s.live for s in sums], others))
        for s, live in zip(sums, lives):
            s.live = live
            s.move()
        return others

    du, up_sum = slope_pull(dz, w_down, slope)
    active, du = lax.optimization_barrier((active, du))
    down_keep, down_send = col_grad(active, dz, n_p, n_t)
    down_send, du = lax.optimization_barrier((down_send, du))
    down_recv = swap_cores(down_send)
    up_keep, up_send = row_grad(hl_turned, du, n_p, n_t)
    up_recv = swap_cores(up_send)
    down_sum = Total([down_keep, down_recv], False).cut(0)
    (du,) = together([down_sum], du)
    dm, da, sums_one = mix_pull(du, w_up, dr, normed, inverse, norm_gains)
    dc = dot(da, w_out, NT).astype(BF16)
    mine = lax.dynamic_slice_in_dim(dc, core * own, own, 1)
    other = lax.dynamic_slice_in_dim(dc, (1 - core) * own, own, 1)
    dc_recv = swap_cores(other)
    up_sums = Total([up_keep, up_recv], True).cut(0)
    out_keep, out_send = col_grad(c_own, da, n_p, n_t)
    out_recv = swap_cores(out_send)
    dc_full = by_core(core, mine, dc_recv, 0)
    down_sum.cut(1)
    dc_full, layer_out = together([down_sum, up_sums], dc_full, layer_out)

    first = attend_bwd(0, qkv, context, dc_full, lse, segment, valid, 512, 256)
    out_sum = Total([out_keep, out_recv], False)
    (dc_full,) = together([down_sum.cut(2), up_sums.cut(1), out_sum.cut(0)], dc_full)
    second = attend_bwd(1, qkv, context, dc_full, lse, segment, valid, 512, 256)
    (second,) = together([down_sum.cut(3), up_sums.cut(2), out_sum.cut(1)], second)

    dx_other = swap_cores(input_pull(1 - core, core, (*first, *second), w_qkv))
    dx_mine = input_pull(core, core, (*first, *second), w_qkv, dm)
    dx = (dx_mine + dx_other.astype(F32)).astype(BF16)
    down_total = down_sum.sum_of(lambda part: part)
    small = jnp.concatenate(
        [
            jnp.stack([sums_one[0], sums_two[0], sums_one[1], sums_one[2], sums_two[1], sums_two[2]]).reshape(-1),
            jnp.zeros((2 * width,), F32),
            up_sum[0],
        ]
    )
    rows_of = lambda part, count: part.reshape(count, -1, part.shape[-1])
    given, qkv_total, up_total, out_total, small = finish(
        n_p, n_t, dx, x_turned, first, second, [rows_of(part, 2) for part in up_sums.parts],
        [rows_of(part, 4) for part in out_sum.parts], small.reshape(-1, 128),
    )
    input_grad = given.astype(F32)
    small = small.reshape(-1)
    up_total = up_total.reshape(up_sums.rest).transpose(1, 0, 2).reshape(up_weight.shape)
    qkv_total = qkv_total.reshape(3, own // 256, -1, 128).transpose(0, 2, 1, 3).reshape(qkv_weight.shape)
    gain_sum = small[: 2 * width].reshape(2, width)
    bias_sum = small[2 * width : 6 * width].reshape(4, width)
    qv_total = lax.dynamic_slice_in_dim(small[6 * width : 8 * width].reshape(2, width), tensor * qv_bias.shape[1], qv_bias.shape[1], 1)
    up_bias_total = lax.dynamic_slice_in_dim(small[8 * width :], tensor * up_bias.shape[0], up_bias.shape[0])
    return (
        layer_out, input_grad, qkv_total, qv_total, out_total, gain_sum, bias_sum, up_total, up_bias_total, down_total,
    )


def solution(mesh):
    dp, tensor = mesh.devices.shape
    split = jax.sharding.Mesh(mesh.devices.reshape(dp // 2, 2, tensor), ("p", "core", "tensor"))
    pc = ("p", "core")
    tokens = P(None, ("p", "core", "tensor"), None)
    return jax.shard_map(
        body,
        mesh=split,
        in_specs=(
            tokens, P(None, pc, None), P(None, pc, None), P(None, pc, "tensor"), P(None, "tensor"), P("tensor", pc),
            P(), P(), P(pc, "tensor"), P("tensor"), P("tensor", pc), tokens,
        ),
        out_specs=(
            tokens, tokens, P(None, pc, "tensor"), P(None, "tensor"), P("tensor", pc), P(), P(), P(pc, "tensor"),
            P("tensor"), P("tensor", pc),
        ),
        check_vma=False,
    )
```

```python
import functools
import math
import jax
import jax.numpy as jnp
from jax import lax
from jax.sharding import PartitionSpec as P
from jax.experimental import pallas as pl
from jax.experimental.pallas import tpu as pltpu

HEAD = 64
PAIR = 2 * HEAD
NEG_FILL = -1e30
F32 = jnp.float32
BF16 = jnp.bfloat16
NT = (((1,), (1,)), ((), ()))
NN = (((1,), (0,)), ((), ()))
TN = (((0,), (0,)), ((), ()))


def dot(a, b, dims=NN, precision=None):
    return lax.dot_general(a, b, dims, preferred_element_type=F32, precision=precision)


def head_lanes(rows, which):
    lane = lax.broadcasted_iota(jnp.int32, (rows, PAIR), 1)
    return (lane < HEAD) if which == 0 else (lane >= HEAD)


def attend_fwd_kernel(bk, lo_ref, hi_ref, pad_ref, q_ref, k_ref, v_ref, qcode_ref, kcode_ref, o_ref, lse_ref, v_turned):
    i = pl.program_id(1)
    bq = q_ref.shape[0]

    @pl.when(i == 0)
    def _():
        v_turned[...] = v_ref[...].T

    q = q_ref[...] * jnp.asarray(0.125, BF16)
    heads = [jnp.where(head_lanes(bq, w), q, jnp.zeros_like(q)) for w in (0, 1)]
    qcode = qcode_ref[...]
    first = i * bq

    def run(diagonal):
        def step(t, carry):
            at = pl.multiple_of(t * bk, bk)
            keys = pl.ds(at, bk)
            k = k_ref[keys, :]
            mask = jnp.tile(kcode_ref[keys, :], (1, bq // 128)) == qcode
            if diagonal:
                gap = lax.broadcasted_iota(jnp.int32, (bk, bq), 0) - lax.broadcasted_iota(jnp.int32, (bk, bq), 1)
                mask = mask | (gap == first - at)
            out = []
            for h in (0, 1):
                top, total, acc = carry[3 * h : 3 * h + 3]
                s = jnp.where(mask, dot(k, heads[h], NT), NEG_FILL)
                new = jnp.maximum(top, jnp.max(s, axis=0, keepdims=True))
                p = jnp.exp(s - new)
                old = jnp.exp(top - new)
                v = v_turned[h * HEAD : (h + 1) * HEAD, keys]
                out += [
                    new,
                    total * old + jnp.sum(p, axis=0, keepdims=True),
                    acc * old + dot(v, p.astype(BF16)),
                ]
            return tuple(out)

        one = (jnp.full((1, bq), NEG_FILL, F32), jnp.zeros((1, bq), F32), jnp.zeros((HEAD, bq), F32))
        ma, la, aa, mb, lb, ab = lax.fori_loop(lo_ref[i], hi_ref[i], step, one + one)
        o_ref[...] = jnp.concatenate([aa / la, ab / lb], axis=0).T.astype(BF16)
        lse_ref[0:1, :] = ma + jnp.log(la)
        lse_ref[1:2, :] = mb + jnp.log(lb)

    pl.when(pad_ref[i] > 0)(lambda: run(True))
    pl.when(pad_ref[i] == 0)(lambda: run(False))


def attend_bwd_kernel(
    bq, lo_ref, hi_ref, pad_ref, q_ref, k_ref, v_ref, c_ref, dc_ref, lse_ref, qcode_ref, kcode_ref,
    dq_ref, dk_ref, dv_ref, dq_acc, delta,
):
    i = pl.program_id(1)
    bk = k_ref.shape[0]
    first = i * bk

    @pl.when(i == 0)
    def _():
        dq_acc[...] = jnp.zeros_like(dq_acc)
        row = lax.broadcasted_iota(jnp.int32, (8, PAIR), 0)
        lane = lax.broadcasted_iota(jnp.int32, (8, PAIR), 1)
        pick = jnp.where(lane // HEAD == row, 1.0, 0.0).astype(F32)
        prod = dc_ref[...].astype(F32) * c_ref[...].astype(F32)
        delta[...] = dot(pick, prod, NT, lax.Precision.HIGHEST)

    k = k_ref[...] * jnp.asarray(0.125, BF16)
    v = v_ref[...]
    k_turned = k.T
    kh = [jnp.where(head_lanes(bk, w), k, jnp.zeros_like(k)) for w in (0, 1)]
    vh = [jnp.where(head_lanes(bk, w), v, jnp.zeros_like(v)) for w in (0, 1)]
    kcode = jnp.tile(kcode_ref[...], (1, bq // 128))

    def run(diagonal):
        def step(t, carry):
            dk, dv = carry
            at = pl.multiple_of(t * bq, bq)
            rows = pl.ds(at, bq)
            q = q_ref[rows, :]
            dc = dc_ref[rows, :]
            mask = kcode == qcode_ref[:, rows]
            if diagonal:
                gap = lax.broadcasted_iota(jnp.int32, (bk, bq), 1) - lax.broadcasted_iota(jnp.int32, (bk, bq), 0)
                mask = mask | (gap == first - at)
            for h in (0, 1):
                s = dot(kh[h], q, NT)
                p = jnp.exp(jnp.where(mask, s - lse_ref[h : h + 1, rows], NEG_FILL))
                dp = dot(vh[h], dc, NT)
                ds = (p * (dp - delta[h : h + 1, rows])).astype(BF16)
                own = head_lanes(bq, h)
                dv = dv + dot(p.astype(BF16), jnp.where(own, dc, jnp.zeros_like(dc)))
                dk = dk + dot(ds, jnp.where(own, q, jnp.zeros_like(q)))
                dq_acc[h * HEAD : (h + 1) * HEAD, rows] += dot(k_turned[h * HEAD : (h + 1) * HEAD, :], ds)
            return dk, dv

        zero = jnp.zeros((bk, PAIR), F32)
        dk, dv = lax.fori_loop(lo_ref[i], hi_ref[i], step, (zero, zero))
        dk_ref[...] = (dk * 0.125).astype(BF16)
        dv_ref[...] = dv.astype(BF16)

    pl.when(pad_ref[i] > 0)(lambda: run(True))
    pl.when(pad_ref[i] == 0)(lambda: run(False))

    @pl.when(i == pl.num_programs(1) - 1)
    def _():
        dq_ref[...] = dq_acc[...].T.astype(BF16)


def block_bounds(segment, valid, block, other):
    length = segment.shape[0]
    blocks = segment.reshape(length // block, block)
    lo = jnp.sum((segment[None, :] < blocks[:, :1]).astype(jnp.int32), axis=1) // other
    hi = (jnp.sum((segment[None, :] <= blocks[:, -1:]).astype(jnp.int32), axis=1) + other - 1) // other
    pad = jnp.sum((valid.reshape(length // block, block) == 0).astype(jnp.int32), axis=1)
    return lo, hi, pad


def attention_codes(segment, valid):
    kcode = jnp.where(valid > 0, segment, -1)
    qcode = segment
    wide = lambda a: jnp.broadcast_to(a[:, None], (a.shape[0], 128))
    return qcode, kcode, wide(qcode), wide(kcode)


def qkv_at(pair, which):
    return pair // 2 * 6 + which * 2 + pair % 2


def attend_fwd(qkv, segment, valid, bq=256, bk=256):
    length, width = qkv.shape
    pairs = width // 3 // PAIR
    lo, hi, pad = block_bounds(segment, valid, bq, bk)
    qcode, kcode, qwide, kwide = attention_codes(segment, valid)
    return pl.pallas_call(
        functools.partial(attend_fwd_kernel, bk),
        grid_spec=pltpu.PrefetchScalarGridSpec(
            num_scalar_prefetch=3,
            grid=(pairs, length // bq),
            in_specs=[
                pl.BlockSpec((bq, PAIR), lambda h, i, *_: (i, qkv_at(h, 0))),
                pl.BlockSpec((length, PAIR), lambda h, i, *_: (0, qkv_at(h, 1))),
                pl.BlockSpec((length, PAIR), lambda h, i, *_: (0, qkv_at(h, 2))),
                pl.BlockSpec((1, bq), lambda h, i, *_: (0, i)),
                pl.BlockSpec((length, 128), lambda h, i, *_: (0, 0)),
            ],
            out_specs=[
                pl.BlockSpec((bq, PAIR), lambda h, i, *_: (i, h)),
                pl.BlockSpec((8, bq), lambda h, i, *_: (h, i)),
            ],
            scratch_shapes=[pltpu.VMEM((PAIR, length), BF16)],
        ),
        out_shape=[
            jax.ShapeDtypeStruct((length, pairs * PAIR), BF16),
            jax.ShapeDtypeStruct((pairs * 8, length), F32),
        ],
        compiler_params=pltpu.CompilerParams(dimension_semantics=("arbitrary", "arbitrary")),
        cost_estimate=pl.CostEstimate(flops=8 * 2 * length * length * PAIR, bytes_accessed=8 * length * width, transcendentals=4 * length * length),
    )(lo, hi, pad, qkv, qkv, qkv, qcode[None, :], kwide)


def attend_bwd(part, qkv, context, context_grad, lse, segment, valid, bq=256, bk=256):
    length, width = qkv.shape
    pairs = width // 6 // PAIR
    base = part * pairs
    lo, hi, pad = block_bounds(segment, valid, bk, bq)
    qcode, kcode, qwide, kwide = attention_codes(segment, valid)
    whole = pl.BlockSpec((length, PAIR), lambda h, i, *_: (0, h))
    piece = pl.BlockSpec((bk, PAIR), lambda h, i, *_: (i, h))
    source = pl.BlockSpec((length, PAIR), lambda h, i, *_: (0, base + h))
    cols = lambda at: pl.BlockSpec((bk, PAIR), lambda h, i, *_: (i, qkv_at(base + h, at)))
    shape = jax.ShapeDtypeStruct((length, pairs * PAIR), BF16)
    return pl.pallas_call(
        functools.partial(attend_bwd_kernel, bq),
        grid_spec=pltpu.PrefetchScalarGridSpec(
            num_scalar_prefetch=3,
            grid=(pairs, length // bk),
            in_specs=[
                pl.BlockSpec((length, PAIR), lambda h, i, *_: (0, qkv_at(base + h, 0))), cols(1), cols(2), source, source,
                pl.BlockSpec((8, length), lambda h, i, *_: (base + h, 0)),
                pl.BlockSpec((1, length), lambda h, i, *_: (0, 0)),
                pl.BlockSpec((bk, 128), lambda h, i, *_: (i, 0)),
            ],
            out_specs=[whole, piece, piece],
            scratch_shapes=[pltpu.VMEM((PAIR, length), F32), pltpu.VMEM((8, length), F32)],
        ),
        out_shape=[shape, shape, shape],
        compiler_params=pltpu.CompilerParams(dimension_semantics=("arbitrary", "arbitrary")),
        cost_estimate=pl.CostEstimate(flops=20 * 2 * length * length * PAIR, bytes_accessed=16 * length * width, transcendentals=4 * length * length),
    )(lo, hi, pad, qkv, qkv, qkv, context, context_grad, lse, qcode[None, :], kwide)


def norm_stats(values):
    center = values - jnp.mean(values, axis=1, keepdims=True)
    inverse = lax.rsqrt(jnp.mean(center * center, axis=1, keepdims=True) + 1e-05)
    return center * inverse, inverse


def norm_pull(incoming, normed, inverse, gain):
    scaled = incoming * gain
    return inverse * (
        scaled - jnp.mean(scaled, axis=1, keepdims=True) - normed * jnp.mean(scaled * normed, axis=1, keepdims=True)
    )


def col_sum(values):
    return jnp.sum(values, axis=0, keepdims=True)


def add_sums(ref, parts):
    @pl.when(pl.program_id(0) == 0)
    def _():
        ref[...] = jnp.zeros_like(ref)

    for at, part in enumerate(parts):
        ref[at : at + 1, :] += col_sum(part)


def mix_kernel(at_ref, x_ref, c_ref, w_ref, bias_ref, gain_ref, hl_ref, turned_ref, n_ref, r_ref):
    mixed = x_ref[...].astype(F32) + dot(c_ref[...], w_ref[...]) + bias_ref[0:1, :]
    normed, inverse = norm_stats(mixed)
    hl = (normed * gain_ref[0:1, :] + bias_ref[1:2, :]).astype(BF16)
    hl_ref[...] = hl
    turned_ref[...] = hl.T
    n_ref[...] = normed
    r_ref[...] = jnp.broadcast_to(inverse, r_ref.shape)


def up_kernel(h_ref, w_ref, bias_ref, g_ref, slope_ref):
    u = dot(h_ref[...], w_ref[...]) + bias_ref[...]
    cdf = 0.5 + 0.5 * lax.erf(u * (1.0 / math.sqrt(2.0)))
    g_ref[...] = (u * cdf).astype(BF16)
    slope_ref[...] = (cdf + u * (jnp.exp(-0.5 * u * u) * (1.0 / math.sqrt(2.0 * math.pi)))).astype(BF16)


def down_kernel(g_ref, w_ref, n_ref, e_ref, bias_ref, gain_ref, out_ref, dr_ref, dz_ref, sum_ref):
    hidden = n_ref[...] * gain_ref[0:1, :] + bias_ref[1:2, :]
    normed, inverse = norm_stats(hidden + dot(g_ref[...], w_ref[...]) + bias_ref[2:3, :])
    out_ref[...] = (normed * gain_ref[1:2, :] + bias_ref[3:4, :]).astype(BF16)
    e = e_ref[...].astype(F32)
    dr = norm_pull(e, normed, inverse, gain_ref[1:2, :])
    dr_ref[...] = dr
    dz_ref[...] = dr.astype(BF16)
    add_sums(sum_ref, (e * normed, dr, e))


def slope_kernel(dz_ref, w_ref, slope_ref, du_ref, sum_ref):
    du = (dot(dz_ref[...], w_ref[...], NT) * slope_ref[...].astype(F32)).astype(BF16)
    du_ref[...] = du

    @pl.when(pl.program_id(1) == 0)
    def _():
        sum_ref[...] = jnp.zeros_like(sum_ref)

    sum_ref[0:1, :] += col_sum(du.astype(F32))


def mix_pull_kernel(du_ref, w_ref, dr_ref, n_ref, r_ref, gain_ref, dm_ref, da_ref, sum_ref):
    dh = dr_ref[...] + dot(du_ref[...], w_ref[...], NT)
    normed = n_ref[...]
    dm = norm_pull(dh, normed, r_ref[:, 0:1], gain_ref[0:1, :])
    dm_ref[...] = dm
    da_ref[...] = dm.astype(BF16)
    add_sums(sum_ref, (dh * normed, dm, dh))


def call(kernel, grid, ins, outs, flops, nbytes, *args):
    return pl.pallas_call(
        kernel,
        grid=grid,
        in_specs=ins,
        out_specs=outs[0],
        out_shape=outs[1],
        compiler_params=pltpu.CompilerParams(dimension_semantics=("arbitrary",) * len(grid)),
        cost_estimate=pl.CostEstimate(flops=flops, bytes_accessed=nbytes, transcendentals=0),
    )(*args)


def rows(block, width):
    return pl.BlockSpec((block, width), lambda i: (i, 0))


def held(shape):
    return pl.BlockSpec(shape, lambda i: (0, 0))


def once(shape):
    return pl.BlockSpec(shape, lambda i: (0, 0), pipeline_mode=pl.Buffered(1))


def sds(shape, dtype=BF16):
    return jax.ShapeDtypeStruct(shape, dtype)


def mix(core_at, x, c, w, biases, gains, block=256):
    n, d = c.shape
    r = lambda width: pl.BlockSpec((block, width), lambda i, at: (i, 0))
    fixed = lambda value: pl.BlockSpec(value.shape, lambda i, at: (0, 0), pipeline_mode=pl.Buffered(1))
    steps = n // block
    return pl.pallas_call(
        mix_kernel,
        grid_spec=pltpu.PrefetchScalarGridSpec(
            num_scalar_prefetch=1,
            grid=(steps,),
            in_specs=[
                pl.BlockSpec((block, d), lambda i, at: (at[0] * steps + i, 0)), r(d), fixed(w), fixed(biases), fixed(gains),
            ],
            out_specs=[r(d), pl.BlockSpec((d, block), lambda i, at: (0, i)), r(d), r(128)],
        ),
        out_shape=[sds((n, d)), sds((d, n)), sds((n, d), F32), sds((n, 128), F32)],
        compiler_params=pltpu.CompilerParams(dimension_semantics=("arbitrary",)),
        cost_estimate=pl.CostEstimate(flops=2 * n * d * d, bytes_accessed=12 * n * d, transcendentals=0),
    )(core_at, x, c, w, biases, gains)


def up(h, w, bias, block=256, cols=1024):
    n, d = h.shape
    f = w.shape[1]
    cols = min(cols, f)
    tile = pl.BlockSpec((block, cols), lambda j, i: (i, j))
    return call(
        up_kernel, (f // cols, n // block),
        [pl.BlockSpec((block, d), lambda j, i: (i, 0)), pl.BlockSpec((d, cols), lambda j, i: (0, j)), pl.BlockSpec((1, cols), lambda j, i: (0, j))],
        ([tile, tile], [sds((n, f)), sds((n, f))]),
        2 * n * d * f, 4 * n * f + 2 * d * f, h, w, bias,
    )


def down(g, w, normed, e, biases, gains, block=256):
    n, f = g.shape
    d = w.shape[1]
    r = functools.partial(rows, block)
    return call(
        down_kernel, (n // block,),
        [r(f), once(w.shape), r(d), r(d), held(biases.shape), held(gains.shape)],
        ([r(d), r(d), r(d), held((8, d))], [sds((n, d)), sds((n, d), F32), sds((n, d)), sds((8, d), F32)]),
        2 * n * d * f, 2 * n * f + 2 * d * f, g, w, normed, e, biases, gains,
    )


def slope_pull(dz, w, slope, block=256, cols=1024):
    n, d = dz.shape
    f = w.shape[0]
    tile = pl.BlockSpec((block, cols), lambda j, i: (i, j))
    return call(
        slope_kernel, (f // cols, n // block),
        [pl.BlockSpec((block, d), lambda j, i: (i, 0)), pl.BlockSpec((cols, d), lambda j, i: (j, 0)), tile],
        ([tile, pl.BlockSpec((8, cols), lambda j, i: (0, j))], [sds((n, f)), sds((8, f), F32)]),
        2 * n * d * f, 4 * n * f + 2 * d * f, dz, w, slope,
    )


def mix_pull(du, w, dr, normed, inverse, gains, block=256):
    n, f = du.shape
    d = w.shape[0]
    r = functools.partial(rows, block)
    return call(
        mix_pull_kernel, (n // block,),
        [r(f), once(w.shape), r(d), r(d), r(128), held(gains.shape)],
        ([r(d), r(d), held((8, d))], [sds((n, d), F32), sds((n, d)), sds((8, d), F32)]),
        2 * n * d * f, 2 * n * f + 2 * d * f, du, w, dr, normed, inverse, gains,
    )


def split_columns(acc, keep_ref, send_ref):
    n_p, c = keep_ref.shape[0], keep_ref.shape[3]
    for bit in (0, 1):

        @pl.when(lax.axis_index("core") == bit)
        def _():
            for p in range(n_p):
                at, to = (2 * p + bit) * c, (2 * p + 1 - bit) * c
                keep_ref[p, 0] = acc[:, at : at + c]
                send_ref[p, 0] = acc[:, to : to + c]


def split_rows(acc, place, keep_ref, send_ref):
    n_p, r = keep_ref.shape[0], keep_ref.shape[-2]
    for bit in (0, 1):

        @pl.when(lax.axis_index("core") == bit)
        def _():
            for p in range(n_p):
                at, to = (2 * p + bit) * r, (2 * p + 1 - bit) * r
                for cb in range(acc.shape[1] // 128):
                    keep_ref[(p, 0) + place + (cb,)] = acc[at : at + r, cb * 128 : cb * 128 + 128]
                    send_ref[(p, 0) + place + (cb,)] = acc[to : to + r, cb * 128 : cb * 128 + 128]


def col_grad_kernel(a_ref, b_ref, keep_ref, send_ref, acc):
    acc[...] = dot(a_ref[...], b_ref[...], TN).astype(BF16)
    split_columns(acc, keep_ref, send_ref)


def row_grad_kernel(a_ref, b_ref, keep_ref, send_ref, acc):
    acc[...] = dot(a_ref[...], b_ref[...]).astype(BF16)
    split_rows(acc, (), keep_ref, send_ref)


def grad_call(kernel, grid, ins, outs, scratch, flops, *args):
    return pl.pallas_call(
        kernel,
        grid=grid,
        in_specs=ins,
        out_specs=outs[0],
        out_shape=outs[1],
        scratch_shapes=scratch,
        compiler_params=pltpu.CompilerParams(dimension_semantics=("arbitrary",) * len(grid)),
        cost_estimate=pl.CostEstimate(flops=flops, bytes_accessed=flops // 512, transcendentals=0),
    )(*args)


def col_grad(a, b, n_p, n_t, block=512):
    n, f = a.shape
    d = b.shape[1]
    per_t, c = f // n_t, d // (2 * n_p)
    block = min(block, per_t)
    steps = per_t // block
    spec = pl.BlockSpec((n_p, 1, block, c), lambda i: (0, i // steps, i % steps, 0))
    shape = sds((n_p, n_t, per_t, c))
    return grad_call(
        col_grad_kernel, (f // block,),
        [pl.BlockSpec((n, block), lambda i: (0, i)), once((n, d))],
        ([spec, spec], [shape, shape]), [pltpu.VMEM((block, d), BF16)], 2 * n * f * d, a, b,
    )


def row_grad(a, b, n_p, n_t, block=512):
    d, n = a.shape
    f = b.shape[1]
    per_t, r = f // n_t, d // (2 * n_p)
    steps = per_t // block
    spec = pl.BlockSpec((n_p, 1, block // 128, r, 128), lambda i: (0, i // steps, i % steps, 0, 0))
    shape = sds((n_p, n_t, per_t // 128, r, 128))
    return grad_call(
        row_grad_kernel, (f // block,),
        [once((d, n)), pl.BlockSpec((n, block), lambda i: (0, i))],
        ([spec, spec], [shape, shape]), [pltpu.VMEM((d, block), BF16)], 2 * n * f * d, a, b,
    )


def input_pull_kernel(extra, at_ref, *refs):
    parts, w_ref = refs[:6], refs[6]
    c = w_ref.shape[1] // 6
    total = dot(parts[0][...], w_ref[:, :c], NT)
    for j in range(1, 6):
        total = total + dot(parts[j][...], w_ref[:, j * c : (j + 1) * c], NT)
    if extra:
        total = total + refs[7][...]
    refs[-1][...] = total.astype(refs[-1].dtype)


def input_pull(half, core, parts, w, dm=None, block=256):
    n, f = parts[0].shape
    d = w.shape[0]
    steps = n // 2 // block
    cols = pl.BlockSpec((block, f), lambda i, at: (at[0] * steps + i, 0))
    own = pl.BlockSpec((block, d), lambda i, at: (i, 0))
    extra = [] if dm is None else [dm]
    held_w = pl.BlockSpec((d, w.shape[1] // 2), lambda i, at: (0, at[1]), pipeline_mode=pl.Buffered(1))
    return pl.pallas_call(
        functools.partial(input_pull_kernel, len(extra)),
        grid_spec=pltpu.PrefetchScalarGridSpec(
            num_scalar_prefetch=1,
            grid=(steps,),
            in_specs=[cols] * 6 + [held_w] + [own] * len(extra),
            out_specs=own,
        ),
        out_shape=sds((n // 2, d), BF16 if dm is None else F32),
        compiler_params=pltpu.CompilerParams(dimension_semantics=("arbitrary",)),
        cost_estimate=pl.CostEstimate(flops=6 * n * f * d, bytes_accessed=8 * n * d, transcendentals=0),
    )(jnp.stack([half, core]).astype(jnp.int32), *parts, w, *extra)


MESH_ID = pl.DeviceIdType.MESH


def flip(value, bit):
    return value + bit - 2 * bit * ((value // bit) % 2)


def start_kernel(n_p, n_t, kinds, *refs):
    n = len(kinds)
    x_ref, bias_ref, *shards = refs[: n + 2]
    x_out, bias_out, *fulls = refs[n + 2 : 2 * n + 4]
    send_sems, recv_sems, own_sems = refs[2 * n + 4 :]
    p, core, t = lax.axis_index("p"), lax.axis_index("core"), lax.axis_index("tensor")
    me = 2 * p + core
    bits = [1 << s for s in range(n_p.bit_length() - 1)]
    column = [{"tensor": lax.rem(t + r, n_t)} for r in range(1, n_t)]
    across = [{"core": 1 - core, "tensor": lax.rem(t + r, n_t)} for r in range(n_t)]
    plane = [{"p": flip(p, bit)} for bit in bits]
    barrier = pltpu.get_barrier_semaphore()
    for peer in column + across + plane:
        pl.semaphore_signal(barrier, inc=1, device_id=peer, device_id_type=MESH_ID)
    pl.semaphore_wait(barrier, len(column + across + plane))

    used = [0, 0]

    def group():
        used[0] += 1
        return used[0] - 1

    def send(source, target, at, peer):
        pltpu.make_async_remote_copy(
            src_ref=source, dst_ref=target, send_sem=send_sems.at[at], recv_sem=recv_sems.at[at],
            device_id=peer, device_id_type=MESH_ID,
        ).start()

    def arrived(view, at):
        pltpu.make_async_copy(view, view, recv_sems.at[at]).wait()

    def left(view, at):
        pltpu.make_async_copy(view, view, send_sems.at[at]).wait()

    def keep(source, target):
        used[1] += 1
        copy = pltpu.make_async_copy(source, target, own_sems.at[used[1] - 1])
        copy.start()
        return copy

    def slab(i, d, half):
        full, kind = fulls[i], kinds[i]
        if kind == "rows":
            depth, wide = shards[i].shape[-2], full.shape[1] // 2
            return full.at[pl.ds(pl.multiple_of(d * depth, depth), depth), pl.ds(half * wide, wide)]
        depth, tall = shards[i].shape[-1], full.shape[0] // 2
        return full.at[pl.ds(half * tall, tall), pl.ds(pl.multiple_of(d * depth, depth), depth)]

    def slabs(i, count, half):
        full, kind = fulls[i], kinds[i]
        if kind == "rows":
            wide = full.shape[1] // 2
            return full.at[pl.ds(0, count * shards[i].shape[-2]), pl.ds(half * wide, wide)]
        tall = full.shape[0] // 2
        return full.at[pl.ds(half * tall, tall), pl.ds(0, count * shards[i].shape[-1])]

    def places(i, t):
        shard, full = shards[i], fulls[i]
        if kinds[i] == "columns":
            tall, depth = shard.shape
            return [(shard, full.at[pl.ds(pl.multiple_of(t * tall, tall), tall), pl.ds(pl.multiple_of(me * depth, depth), depth)])]
        depth, wide = shard.shape[-2:]
        rows_at = pl.ds(pl.multiple_of(me * depth, depth), depth)
        if len(shard.shape) == 2:
            return [(shard, full.at[rows_at, pl.ds(pl.multiple_of(t * wide, wide), wide)])]
        count = shard.shape[0]
        return [
            (shard.at[w], full.at[rows_at, pl.ds(pl.multiple_of((t * count + w) * wide, wide), wide)])
            for w in range(count)
        ]

    def shares(i, count):
        shard, full = shards[i], fulls[i]
        if kinds[i] == "columns":
            return full.at[pl.ds(0, count * shard.shape[0]), pl.ds(0, shard.shape[1])]
        wide = math.prod(shard.shape) // shard.shape[-2]
        return full.at[pl.ds(0, shard.shape[-2]), pl.ds(0, count * wide)]

    hops = n_t - 1
    own = [[keep(source, target) for source, target in places(i, t)] for i in range(n)]
    right, left_to = {"tensor": lax.rem(t + 1, n_t)}, {"tensor": lax.rem(t + n_t - 1, n_t)}
    line = [[(group(), group()) for _ in range(hops)] for _ in range(n)]

    def hop(i, s):
        to_right, to_left = line[i][s]

        @pl.when(jnp.logical_and(t + 1 < n_t, t >= s))
        def _():
            for source, target in places(i, t - s):
                send(source if s == 0 else target, target, to_right, right)

        @pl.when(jnp.logical_and(t >= 1, t + s < n_t))
        def _():
            for source, target in places(i, t + s):
                send(source if s == 0 else target, target, to_left, left_to)

    def hop_arrived(i, s):
        to_right, to_left = line[i][s]
        pl.when(t >= s + 1)(lambda: arrived(shares(i, 1), to_right))
        pl.when(t + s + 1 < n_t)(lambda: arrived(shares(i, 1), to_left))

    def hop_left(i, s):
        to_right, to_left = line[i][s]
        pl.when(jnp.logical_and(t + 1 < n_t, t >= s))(lambda: left(shares(i, 1), to_right))
        pl.when(jnp.logical_and(t >= 1, t + s < n_t))(lambda: left(shares(i, 1), to_left))

    for i in range(n):
        hop(i, 0)
    bias_at = group()
    bias_own = keep(bias_ref, bias_out.at[t])
    for peer in column:
        send(bias_ref, bias_out.at[t], bias_at, peer)

    held = x_ref.shape[1]
    odd = t % 2
    x_rows = x_out.at[pl.ds(pl.multiple_of(t * held, held), held), :]
    x_at = [group(), group()]
    stays = core == t // 2
    peer_a = {"core": t // 2, "tensor": 2 * core + odd}
    peer_b = {"core": t // 2, "tensor": 2 * core + 1 - odd}

    x_own = pltpu.make_async_copy(x_ref.at[odd], x_rows, own_sems.at[used[1]])
    used[1] += 1
    pl.when(stays)(x_own.start)

    def send_tokens():
        pl.when(jnp.logical_not(stays))(lambda: send(x_ref.at[odd], x_rows, x_at[0], peer_a))
        send(x_ref.at[1 - odd], x_rows, x_at[1], peer_b)

    partner = {"core": 1 - core}
    passes = []

    def forward(i, masks, half):
        at = group()
        guard = i == 0

        def go():
            for mask in masks:
                d = 2 * mask + core
                send(slab(i, d, half), slab(i, d, half), at, partner)

        if guard:
            pl.when(core == 1 - half)(go)
        else:
            go()
        passes.append((i, len(masks), half, at))

    states = {}

    def stage(i, s):
        if s == 0:
            hop_arrived(i, hops - 1)
            states[i] = {}
            for half in (0, 1):
                states[i][half] = ([p], None)
        else:
            for half in (0, 1):
                masks, at = states[i][half]
                arrived(slabs(i, len(masks), half), at)
                bit = bits[s - 1] if half == 0 else bits[-s]
                states[i][half] = (masks + [flip(m, bit) for m in masks], None)
        for half in (0, 1):
            masks, _ = states[i][half]
            if s < len(bits):
                at = group()
                bit = bits[s] if half == 0 else bits[-s - 1]
                for m in masks:
                    d = 2 * m + core
                    send(slab(i, d, half), slab(i, d, half), at, {"p": flip(p, bit)})
                states[i][half] = (masks, at)
                finish.append((i, len(masks), half, at))
            fresh = masks if s == 0 else masks[len(masks) // 2 :]
            forward(i, fresh, half)

    finish = []
    for step in range(n + hops - 1 + len(bits)):
        for i in range(n):
            at = step - i
            if 0 <= at < hops - 1:
                if at == 0:
                    for copy in own[i]:
                        copy.wait()
                hop_arrived(i, at)
                hop(i, at + 1)
                if i == n - 1 and at == hops - 2:
                    send_tokens()
            elif 0 <= at - (hops - 1) <= len(bits):
                stage(i, at - (hops - 1))

    pl.when(jnp.logical_not(stays))(lambda: arrived(x_rows, x_at[0]))
    pl.when(stays)(x_own.wait)
    arrived(x_rows, x_at[1])
    half_rows = x_out.at[pl.ds(pl.multiple_of(core * 2 * held, 2 * held), 2 * held), :]
    x_pass = group()
    send(half_rows, half_rows, x_pass, partner)
    bias_own.wait()
    arrived(bias_out.at[pl.ds(0, n_t - 1)], bias_at)
    for i, count, half, at in passes:
        if i == 0:
            pl.when(core == half)(functools.partial(arrived, slabs(i, count, half), at))
        else:
            arrived(slabs(i, count, half), at)
    arrived(half_rows, x_pass)
    left(half_rows, x_pass)
    for i, count, half, at in passes:
        if i == 0:
            pl.when(core == 1 - half)(functools.partial(left, slabs(i, count, half), at))
        else:
            left(slabs(i, count, half), at)
    for i, count, half, at in finish:
        left(slabs(i, count, half), at)
    for i in range(n):
        for s in range(hops):
            hop_left(i, s)
    left(bias_out.at[pl.ds(0, n_t - 1)], bias_at)
    pl.when(jnp.logical_not(stays))(lambda: left(x_rows, x_at[0]))
    left(x_rows, x_at[1])


def start_gather(x, bias, shards, kinds, n_p, n_t):
    n_dp = 2 * n_p
    fulls = []
    for shard, kind in zip(shards, kinds):
        if kind == "columns":
            fulls.append(sds((shard.shape[0] * n_t, shard.shape[1] * n_dp)))
        else:
            fulls.append(sds((shard.shape[-2] * n_dp, math.prod(shard.shape) // shard.shape[-2] * n_t)))
    bits = n_p.bit_length() - 1
    count = len(shards) * (2 * (n_t - 1) + 2 * bits + 2 * (bits + 1)) + 4
    vmem, away = pl.BlockSpec(memory_space=pltpu.VMEM), pl.BlockSpec(memory_space=pl.ANY)
    return pl.pallas_call(
        functools.partial(start_kernel, n_p, n_t, kinds),
        out_shape=[sds((n_t * x.shape[1], x.shape[2])), sds((n_t,) + bias.shape, F32)] + fulls,
        in_specs=[vmem] * (2 + len(shards)),
        out_specs=[away] * (2 + len(shards)),
        scratch_shapes=[
            pltpu.SemaphoreType.DMA((count,)), pltpu.SemaphoreType.DMA((count,)), pltpu.SemaphoreType.DMA((10,)),
        ],
        compiler_params=pltpu.CompilerParams(collective_id=1, has_side_effects=True),
    )(x, bias, *shards)


def project_kernel(core_ref, x_ref, w_ref, bias_ref, out_ref, turned_ref):
    turned_ref[...] = x_ref[...].T
    out_ref[...] = (dot(x_ref[...], w_ref[...]) + bias_ref[...]).astype(BF16)


def project(core_at, x, w, bias, block=256):
    n, d = x.shape
    f = w.shape[1] // 2
    return pl.pallas_call(
        project_kernel,
        grid_spec=pltpu.PrefetchScalarGridSpec(
            num_scalar_prefetch=1,
            grid=(n // block,),
            in_specs=[
                pl.BlockSpec((block, d), lambda i, at: (i, 0)),
                pl.BlockSpec((d, f), lambda i, at: (0, at[0]), pipeline_mode=pl.Buffered(1)),
                pl.BlockSpec((1, f), lambda i, at: (0, 0)),
            ],
            out_specs=[pl.BlockSpec((block, f), lambda i, at: (i, 0)), pl.BlockSpec((d, block), lambda i, at: (0, i))],
        ),
        out_shape=[sds((n, f)), sds((d, n))],
        compiler_params=pltpu.CompilerParams(dimension_semantics=("arbitrary",)),
        cost_estimate=pl.CostEstimate(flops=2 * n * d * f, bytes_accessed=4 * n * d + 2 * n * f, transcendentals=0),
    )(core_at, x, w, bias)


def finish_kernel(n_p, n_t, *refs):
    dx, x_turned, *grads, up_a, up_b, out_a, out_b, small = refs[:13]
    given, qkv_out, up_out, out_out, small_out = refs[13:18]
    keep2, send2, acc, recv2, pairs, slots1, last, last_slot, up_cur, up_slot, out_cur, out_slot = refs[18:30]
    out_next, out_last, small_cur, small_slot = refs[30:34]
    bits = [n_p >> (s + 1) for s in range(n_p.bit_length() - 1)]
    curs, slots = refs[34 : 34 + len(bits)], refs[34 + len(bits) : 34 + 2 * len(bits)]
    send_sems, recv_sems = refs[-2:]
    p, core, t = lax.axis_index("p"), lax.axis_index("core"), lax.axis_index("tensor")
    partner = {"core": 1 - core}
    column = [{"tensor": lax.rem(t + r, n_t)} for r in range(1, n_t)]
    column += [{"core": 1 - core, "tensor": lax.rem(t + r, n_t)} for r in range(n_t)]
    plane = [{"p": flip(p, bit)} for bit in bits]
    line = {bit: {"tensor": flip(t, bit)} for bit in (2, 1)}
    barrier = pltpu.get_barrier_semaphore()
    for peer in column + plane:
        pl.semaphore_signal(barrier, inc=1, device_id=peer, device_id_type=MESH_ID)
    pl.semaphore_wait(barrier, len(column + plane))

    used = [0]

    def send(source, target, peer):
        at = used[0]
        used[0] += 1
        copy = pltpu.make_async_remote_copy(
            src_ref=source, dst_ref=target, send_sem=send_sems.at[at], recv_sem=recv_sems.at[at],
            device_id=peer, device_id_type=MESH_ID,
        )
        return copy

    def go(source, target, peer):
        copy = send(source, target, peer)
        copy.start()
        return copy

    def plus(a, b):
        return (a.astype(F32) + b.astype(F32)).astype(BF16)

    u, odd = t // 2, t % 2
    for at in range(4):
        out_cur[at % 2, at // 2] = plus(out_a[at], out_b[at])
    out_move = go(out_cur.at[1 - odd], out_slot, line[1])
    for at in (0, 1):
        up_cur[at] = plus(up_a[at], up_b[at])
    up_move = go(up_cur.at[1 - u], up_slot, line[2])

    held = given.shape[1]
    stays = core == u
    rows_a = dx.at[pl.ds(pl.multiple_of(odd * held, held), held), :]
    rows_b = dx.at[pl.ds(pl.multiple_of((1 - odd) * held, held), held), :]
    give_a = send(rows_a, given.at[odd], {"core": u, "tensor": 2 * core + odd})
    pl.when(jnp.logical_not(stays))(give_a.start)
    give_b = go(rows_b, given.at[odd], {"core": u, "tensor": 2 * core + 1 - odd})

    @pl.when(stays)
    def _():
        given[odd] = dx[pl.ds(pl.multiple_of(odd * held, held), held), :]

    orders = [bits, bits[::-1]]

    def spot(part, j):
        return sum(n_p >> (s + 1) for s, bit in enumerate(orders[part]) if j // bit % 2)

    r = keep2.shape[2] // 6
    swaps = []
    for part in (0, 1):
        for which in range(3):
            acc[...] = dot(x_turned[...], grads[3 * part + which][...]).astype(BF16)
            for bit in (0, 1):

                @pl.when(core == bit)
                def _():
                    for j in range(n_p):
                        at, to = (2 * j + bit) * r, (2 * j + 1 - bit) * r
                        for cb in (0, 1):
                            place = pl.ds((2 * which + cb) * r, r)
                            keep2[part, spot(part, j), place, :] = acc[at : at + r, cb * 128 : cb * 128 + 128]
                            send2[part, spot(part, j), place, :] = acc[to : to + r, cb * 128 : cb * 128 + 128]
        swaps.append(go(send2.at[part], recv2.at[part], partner))
    small_cur[0] = small[...]
    per_row = dx.shape[1] // 128
    for part in (0, 1):
        for which in (0, 1):
            total = jnp.sum(grads[3 * part + 2 * which][...].astype(F32), axis=0, keepdims=True)
            for bit in (0, 1):

                @pl.when(core == bit)
                def _():
                    at = (6 + which) * per_row + bit * (per_row // 2) + part * (per_row // 4)
                    for cb in (0, 1):
                        small_cur[0, at + cb : at + cb + 1, :] = total[:, cb * 128 : cb * 128 + 128]

    peers = [partner] + plane
    for at, peer in enumerate(peers):
        copy = go(small_cur.at[at], small_slot.at[at], peer)
        copy.wait()
        small_cur[at + 1] = small_cur[at] + small_slot[at]

    sources = []
    for part in (0, 1):
        swaps[part].wait()
        sources.append([keep2.at[part], recv2.at[part]])
    for s in range(len(bits)):
        size = n_p >> (s + 1)
        copies = []
        for part in (0, 1):
            bit = orders[part][s]
            mine = (p // bit) % 2
            peer = {"p": flip(p, bit)}
            copies.append(
                [go(sources[part][j].at[pl.ds((1 - mine) * size, size)], slots[s].at[part, j], peer) for j in (0, 1)]
            )
        for part in (0, 1):
            mine = (p // orders[part][s]) % 2
            for j in (0, 1):
                copies[part][j].wait()
                if size == 1:
                    pairs[part, core if j == 0 else 1 - core] = plus(sources[part][j][mine], slots[s][part, j, 0])
                else:
                    for at in range(size):
                        curs[s][part, j, at] = plus(sources[part][j][mine * size + at], slots[s][part, j, at])
            sources[part] = [curs[s].at[part, 0], curs[s].at[part, 1]]
    pair_move = go(pairs.at[1 - odd], slots1, line[1])
    out_move.wait()
    for at in (0, 1):
        out_next[at] = plus(out_cur[odd, at], out_slot[at])
    out_move = go(out_next.at[1 - u], out_last, line[2])
    pair_move.wait()
    for at in (0, 1):
        last[at] = plus(pairs[odd, at], slots1[at])
    last_move = go(last.at[1 - u], last_slot, line[2])
    for bit in (1, 2):
        at = len(peers)
        copy = go(small_cur.at[at], small_slot.at[at], line[bit])
        copy.wait()
        peers.append(None)
        if bit == 2:
            small_out[...] = small_cur[at] + small_slot[at]
        else:
            small_cur[at + 1] = small_cur[at] + small_slot[at]
    up_move.wait()
    up_out[...] = up_cur[u].astype(F32) + up_slot[...].astype(F32)
    out_move.wait()
    out_out[...] = out_next[u].astype(F32) + out_last[...].astype(F32)
    last_move.wait()
    qkv_out[...] = last[u].astype(F32) + last_slot[...].astype(F32)
    pl.when(jnp.logical_not(stays))(give_a.wait)
    give_b.wait()


def finish(n_p, n_t, dx, x_turned, first, second, up_, out_, small):
    d, wide = x_turned.shape[0], first[0].shape[1]
    rows_ = 3 * wide * d // (2 * n_p) // 128
    bits = n_p.bit_length() - 1
    steps = 1 + bits + 2
    box = lambda *lead: pltpu.VMEM(lead + (rows_, 128), BF16)
    like = lambda lead, value: pltpu.VMEM(lead + value.shape[1:], BF16)
    halves = [box(2, 2, n_p >> (s + 1)) for s in range(bits)]
    vmem = pl.BlockSpec(memory_space=pltpu.VMEM)
    count = 9 + steps + 4 * bits
    return pl.pallas_call(
        functools.partial(finish_kernel, n_p, n_t),
        out_shape=[
            sds((2, dx.shape[0] // 2, dx.shape[1])), sds((rows_, 128), F32), sds(up_[0].shape[1:], F32),
            sds(out_[0].shape[1:], F32), sds(small.shape, F32),
        ],
        in_specs=[vmem] * 13,
        out_specs=[vmem] * 5,
        scratch_shapes=[
            box(2, n_p), box(2, n_p), pltpu.VMEM((d, wide), BF16), box(2, n_p), box(2, 2), box(2), box(2), box(),
            like((2,), up_[0]), like((), up_[0]), like((2, 2), out_[0]), like((2,), out_[0]), like((2,), out_[0]),
            like((), out_[0]), pltpu.VMEM((steps,) + small.shape, F32), pltpu.VMEM((steps,) + small.shape, F32),
            *halves, *halves,
            pltpu.SemaphoreType.DMA((count,)), pltpu.SemaphoreType.DMA((count,)),
        ],
        compiler_params=pltpu.CompilerParams(collective_id=0, has_side_effects=True),
        cost_estimate=pl.CostEstimate(flops=32 * d * d * 1024, bytes_accessed=64 * d * d, transcendentals=0),
    )(dx, x_turned, *first, *second, *up_, *out_, small)


def swap_cores(value):
    return lax.ppermute(value, "core", [(0, 1), (1, 0)])


def column_routes(tensor_size):
    first, second = [], []
    for core in range(2):
        for t in range(tensor_size):
            at = core * tensor_size + t
            first.append((at, (t >> 1) * tensor_size + 2 * core + (t & 1)))
            second.append((at, (t >> 1) * tensor_size + 2 * core + 1 - (t & 1)))
    return first, second


def back(route):
    return [(b, a) for a, b in route]


def by_core(core, mine, other, axis):
    return jnp.where(
        core == 0, jnp.concatenate([mine, other], axis=axis), jnp.concatenate([other, mine], axis=axis)
    )


def body(
    inputs, segment_ids, token_valid, qkv_weight, qv_bias, out_weight, norm_gains, row_biases,
    up_weight, up_bias, down_weight, out_grad,
):
    COL = ("core", "tensor")
    ALL = ("p", "core", "tensor")
    core, tensor = lax.axis_index("core"), lax.axis_index("tensor")
    n_p, n_t = lax.axis_size("p"), lax.axis_size("tensor")
    n_dp = 2 * n_p
    micro, held_rows, width = inputs.shape
    assert micro == 2 and n_t == 4
    odd = tensor & 1
    route_a, route_b = column_routes(n_t)

    def bring(value):
        a = lax.ppermute(value[odd], COL, route_a)
        b = lax.ppermute(value[1 - odd], COL, route_b)
        return jnp.where(odd == 0, jnp.concatenate([a, b]), jnp.concatenate([b, a]))

    def blocks(value):
        return [lax.dynamic_slice_in_dim(value, at * held_rows, held_rows) for at in (odd, 1 - odd)]

    def give(a, b):
        a, b = lax.ppermute(a, COL, back(route_a)), lax.ppermute(b, COL, back(route_b))
        return jnp.where(odd == 0, jnp.stack([a, b]), jnp.stack([b, a]))

    def gathered(weight):
        got = lax.all_gather(weight, ALL, axis=0, tiled=False)
        return got.reshape((n_dp, n_t) + weight.shape)

    labels = jnp.stack([segment_ids[:, 0], token_valid[:, 0]], axis=1)[odd]
    labels = jnp.where((tensor >> 1) == core, labels, swap_cores(labels))
    segment, valid = labels[0], labels[1]

    shards, kinds = [qkv_weight, up_weight], ["rows", "rows"]
    wide = out_weight.shape[1] % 128 == 0
    if wide:
        shards, kinds = [qkv_weight, out_weight, up_weight, down_weight], ["rows", "columns", "rows", "columns"]
    local_bias = jnp.concatenate([qv_bias.reshape(-1), up_bias]).reshape(-1, 128)
    x_full, bias_all, *fulls = start_gather(inputs, local_bias, shards, kinds, n_p, n_t)
    if wide:
        w_qkv, w_out, w_up, w_down = fulls
    else:
        w_qkv, w_up = fulls
        w_out = gathered(out_weight).transpose(1, 2, 0, 3).reshape(-1, width)
        w_down = gathered(down_weight).transpose(1, 2, 0, 3).reshape(-1, width)
    out_grad, x_full = lax.optimization_barrier((out_grad, x_full))
    rows = x_full.shape[0] // 2
    own = w_qkv.shape[1] // 6
    bias_all = bias_all.reshape(n_t, -1)
    n_qv = qv_bias.size
    up_bias_all = bias_all[:, n_qv:].reshape(1, -1)
    qv_own = lax.dynamic_slice_in_dim(bias_all[:, :n_qv], 2 * core, 2).reshape(2, 2, -1)
    bias = jnp.stack([qv_own[:, 0], jnp.zeros_like(qv_own[:, 0]), qv_own[:, 1]], axis=1).reshape(1, -1)
    core_at = jnp.reshape(core, (1,)).astype(jnp.int32)
    qkv, x_turned = project(core_at, x_full, w_qkv, bias)
    context, lse = attend_fwd(qkv, segment, valid, 512, 512)
    mine = lax.dynamic_slice_in_dim(context, core * rows, rows)
    other = lax.dynamic_slice_in_dim(context, (1 - core) * rows, rows)
    c_own = by_core(core, mine, swap_cores(other), 1)
    hl, hl_turned, normed, inverse = mix(core_at, x_full, c_own, w_out, row_biases, norm_gains)
    active, slope = up(hl, w_up, up_bias_all)
    grad_own = bring(out_grad)
    layer, dr, dz, sums_two = down(active, w_down, normed, grad_own, row_biases, norm_gains)

    p_bits = [1 << s for s in range(n_p.bit_length() - 1)]
    t_bits = [1, 2]

    class Total:
        def __init__(self, parts, downward):
            lead = [("p", n_p, bit) for bit in reversed(p_bits)] + [("tensor", n_t, bit) for bit in (2, 1)]
            self.rest = parts[0].shape[2:]
            self.dims = lead
            self.parts = [part.reshape((2,) * len(lead) + self.rest) for part in parts]
            order = list(reversed(p_bits)) if downward else p_bits
            self.groups = [order[:1], order[1:], t_bits[:1], t_bits[1:]]

        def sum_of(self, pick):
            total = pick(self.parts[0]).astype(F32)
            for part in self.parts[1:]:
                total = total + pick(part).astype(F32)
            return total

        def cut_one(self, axis, bit):
            at = [d[0] + str(d[2]) for d in self.dims].index(axis + str(bit))
            size = self.dims[at][1]
            self.dims = self.dims[:at] + self.dims[at + 1 :]
            mine = (lax.axis_index(axis) // bit) % 2
            side = lambda which: self.sum_of(lambda part: lax.dynamic_index_in_dim(part, which, at, keepdims=False)).astype(BF16)
            self.live = [side(mine), side(1 - mine)]
            self.route = (axis, [(i, i ^ bit) for i in range(size)])

        def move(self):
            self.parts = [self.live[0], lax.ppermute(self.live[1], *self.route)]
            return self

        def cut(self, group):
            axis = "p" if group < 2 else "tensor"
            for j, bit in enumerate(self.groups[group]):
                if j:
                    self.move()
                self.cut_one(axis, bit)
            return self

    def together(sums, *others):
        lives, others = lax.optimization_barrier(([s.live for s in sums], others))
        for s, live in zip(sums, lives):
            s.live = live
            s.move()
        return others

    du, up_sum = slope_pull(dz, w_down, slope)
    active, du = lax.optimization_barrier((active, du))
    down_keep, down_send = col_grad(active, dz, n_p, n_t)
    down_send, du = lax.optimization_barrier((down_send, du))
    down_recv = swap_cores(down_send)
    up_keep, up_send = row_grad(hl_turned, du, n_p, n_t)
    up_recv = swap_cores(up_send)
    down_sum = Total([down_keep, down_recv], False).cut(0)
    (du,) = together([down_sum], du)
    dm, da, sums_one = mix_pull(du, w_up, dr, normed, inverse, norm_gains)
    dc = dot(da, w_out, NT).astype(BF16)
    mine = lax.dynamic_slice_in_dim(dc, core * own, own, 1)
    other = lax.dynamic_slice_in_dim(dc, (1 - core) * own, own, 1)
    dc_recv = swap_cores(other)
    up_sums = Total([up_keep, up_recv], True).cut(0)
    out_keep, out_send = col_grad(c_own, da, n_p, n_t)
    out_recv = swap_cores(out_send)
    dc_full = by_core(core, mine, dc_recv, 0)
    dc_full, layer = together([up_sums], dc_full, blocks(layer))
    layer_out = give(*layer)

    first = attend_bwd(0, qkv, context, dc_full, lse, segment, valid, 512, 256)
    out_sum = Total([out_keep, out_recv], False)
    dc_full, layer_out = together([down_sum.cut(1), up_sums.cut(1), out_sum.cut(0)], dc_full, layer_out)
    second = attend_bwd(1, qkv, context, dc_full, lse, segment, valid, 512, 256)
    (second,) = together([down_sum.cut(2), up_sums.cut(2), out_sum.cut(1)], second)

    dx_other = swap_cores(input_pull(1 - core, core, (*first, *second), w_qkv))
    dx_mine = input_pull(core, core, (*first, *second), w_qkv, dm)
    dx = (dx_mine + dx_other.astype(F32)).astype(BF16)
    (dx,) = together([down_sum.cut(3)], dx)
    down_total = down_sum.sum_of(lambda part: part)
    small = jnp.concatenate(
        [
            jnp.stack([sums_one[0], sums_two[0], sums_one[1], sums_one[2], sums_two[1], sums_two[2]]).reshape(-1),
            jnp.zeros((2 * width,), F32),
            up_sum[0],
        ]
    )
    rows_of = lambda part, count: part.reshape(count, -1, part.shape[-1])
    given, qkv_total, up_total, out_total, small = finish(
        n_p, n_t, dx, x_turned, first, second, [rows_of(part, 2) for part in up_sums.parts],
        [rows_of(part, 4) for part in out_sum.parts], small.reshape(-1, 128),
    )
    input_grad = given.astype(F32)
    small = small.reshape(-1)
    up_total = up_total.reshape(up_sums.rest).transpose(1, 0, 2).reshape(up_weight.shape)
    qkv_total = qkv_total.reshape(3, own // 256, -1, 128).transpose(0, 2, 1, 3).reshape(qkv_weight.shape)
    gain_sum = small[: 2 * width].reshape(2, width)
    bias_sum = small[2 * width : 6 * width].reshape(4, width)
    qv_total = lax.dynamic_slice_in_dim(small[6 * width : 8 * width].reshape(2, width), tensor * qv_bias.shape[1], qv_bias.shape[1], 1)
    up_bias_total = lax.dynamic_slice_in_dim(small[8 * width :], tensor * up_bias.shape[0], up_bias.shape[0])
    return (
        layer_out, input_grad, qkv_total, qv_total, out_total, gain_sum, bias_sum, up_total, up_bias_total, down_total,
    )


def solution(mesh):
    dp, tensor = mesh.devices.shape
    split = jax.sharding.Mesh(mesh.devices.reshape(dp // 2, 2, tensor), ("p", "core", "tensor"))
    pc = ("p", "core")
    tokens = P(None, ("p", "core", "tensor"), None)
    return jax.shard_map(
        body,
        mesh=split,
        in_specs=(
            tokens, P(None, pc, None), P(None, pc, None), P(None, pc, "tensor"), P(None, "tensor"), P("tensor", pc),
            P(), P(), P(pc, "tensor"), P("tensor"), P("tensor", pc), tokens,
        ),
        out_specs=(
            tokens, tokens, P(None, pc, "tensor"), P(None, "tensor"), P("tensor", pc), P(), P(), P(pc, "tensor"),
            P("tensor"), P("tensor", pc),
        ),
        check_vma=False,
    )
```

```python
import functools
import math
import jax
import jax.numpy as jnp
from jax import lax
from jax.sharding import PartitionSpec as P
from jax.experimental import pallas as pl
from jax.experimental.pallas import tpu as pltpu

HEAD = 64
PAIR = 2 * HEAD
NEG_FILL = -1e30
F32 = jnp.float32
BF16 = jnp.bfloat16
NT = (((1,), (1,)), ((), ()))
NN = (((1,), (0,)), ((), ()))
TN = (((0,), (0,)), ((), ()))


def dot(a, b, dims=NN, precision=None):
    return lax.dot_general(a, b, dims, preferred_element_type=F32, precision=precision)


def head_lanes(rows, which):
    lane = lax.broadcasted_iota(jnp.int32, (rows, PAIR), 1)
    return (lane < HEAD) if which == 0 else (lane >= HEAD)


def attend_fwd_kernel(bk, lo_ref, hi_ref, pad_ref, q_ref, k_ref, v_ref, qcode_ref, kcode_ref, o_ref, lse_ref, v_turned):
    i = pl.program_id(1)
    bq = q_ref.shape[0]

    @pl.when(i == 0)
    def _():
        v_turned[...] = v_ref[...].T

    q = q_ref[...] * jnp.asarray(0.125, BF16)
    heads = [jnp.where(head_lanes(bq, w), q, jnp.zeros_like(q)) for w in (0, 1)]
    qcode = qcode_ref[...]
    first = i * bq

    def run(diagonal):
        def step(t, carry):
            at = pl.multiple_of(t * bk, bk)
            keys = pl.ds(at, bk)
            k = k_ref[keys, :]
            mask = jnp.tile(kcode_ref[keys, :], (1, bq // 128)) == qcode
            if diagonal:
                gap = lax.broadcasted_iota(jnp.int32, (bk, bq), 0) - lax.broadcasted_iota(jnp.int32, (bk, bq), 1)
                mask = mask | (gap == first - at)
            out = []
            for h in (0, 1):
                top, total, acc = carry[3 * h : 3 * h + 3]
                s = jnp.where(mask, dot(k, heads[h], NT), NEG_FILL)
                new = jnp.maximum(top, jnp.max(s, axis=0, keepdims=True))
                p = jnp.exp(s - new)
                old = jnp.exp(top - new)
                v = v_turned[h * HEAD : (h + 1) * HEAD, keys]
                out += [
                    new,
                    total * old + jnp.sum(p, axis=0, keepdims=True),
                    acc * old + dot(v, p.astype(BF16)),
                ]
            return tuple(out)

        one = (jnp.full((1, bq), NEG_FILL, F32), jnp.zeros((1, bq), F32), jnp.zeros((HEAD, bq), F32))
        ma, la, aa, mb, lb, ab = lax.fori_loop(lo_ref[i], hi_ref[i], step, one + one)
        o_ref[...] = jnp.concatenate([aa / la, ab / lb], axis=0).T.astype(BF16)
        lse_ref[0:1, :] = ma + jnp.log(la)
        lse_ref[1:2, :] = mb + jnp.log(lb)

    pl.when(pad_ref[i] > 0)(lambda: run(True))
    pl.when(pad_ref[i] == 0)(lambda: run(False))


def attend_bwd_kernel(
    bq, lo_ref, hi_ref, pad_ref, q_ref, k_ref, v_ref, c_ref, dc_ref, lse_ref, qcode_ref, kcode_ref,
    dq_ref, dk_ref, dv_ref, dq_acc, delta,
):
    i = pl.program_id(1)
    bk = k_ref.shape[0]
    first = i * bk

    @pl.when(i == 0)
    def _():
        dq_acc[...] = jnp.zeros_like(dq_acc)
        row = lax.broadcasted_iota(jnp.int32, (8, PAIR), 0)
        lane = lax.broadcasted_iota(jnp.int32, (8, PAIR), 1)
        pick = jnp.where(lane // HEAD == row, 1.0, 0.0).astype(F32)
        prod = dc_ref[...].astype(F32) * c_ref[...].astype(F32)
        delta[...] = dot(pick, prod, NT, lax.Precision.HIGHEST)

    k = k_ref[...] * jnp.asarray(0.125, BF16)
    v = v_ref[...]
    k_turned = k.T
    kh = [jnp.where(head_lanes(bk, w), k, jnp.zeros_like(k)) for w in (0, 1)]
    vh = [jnp.where(head_lanes(bk, w), v, jnp.zeros_like(v)) for w in (0, 1)]
    kcode = jnp.tile(kcode_ref[...], (1, bq // 128))

    def run(diagonal):
        def step(t, carry):
            dk, dv = carry
            at = pl.multiple_of(t * bq, bq)
            rows = pl.ds(at, bq)
            q = q_ref[rows, :]
            dc = dc_ref[rows, :]
            mask = kcode == qcode_ref[:, rows]
            if diagonal:
                gap = lax.broadcasted_iota(jnp.int32, (bk, bq), 1) - lax.broadcasted_iota(jnp.int32, (bk, bq), 0)
                mask = mask | (gap == first - at)
            for h in (0, 1):
                s = dot(kh[h], q, NT)
                p = jnp.exp(jnp.where(mask, s - lse_ref[h : h + 1, rows], NEG_FILL))
                dp = dot(vh[h], dc, NT)
                ds = (p * (dp - delta[h : h + 1, rows])).astype(BF16)
                own = head_lanes(bq, h)
                dv = dv + dot(p.astype(BF16), jnp.where(own, dc, jnp.zeros_like(dc)))
                dk = dk + dot(ds, jnp.where(own, q, jnp.zeros_like(q)))
                dq_acc[h * HEAD : (h + 1) * HEAD, rows] += dot(k_turned[h * HEAD : (h + 1) * HEAD, :], ds)
            return dk, dv

        zero = jnp.zeros((bk, PAIR), F32)
        dk, dv = lax.fori_loop(lo_ref[i], hi_ref[i], step, (zero, zero))
        dk_ref[...] = (dk * 0.125).astype(BF16)
        dv_ref[...] = dv.astype(BF16)

    pl.when(pad_ref[i] > 0)(lambda: run(True))
    pl.when(pad_ref[i] == 0)(lambda: run(False))

    @pl.when(i == pl.num_programs(1) - 1)
    def _():
        dq_ref[...] = dq_acc[...].T.astype(BF16)


def block_bounds(segment, valid, block, other):
    length = segment.shape[0]
    blocks = segment.reshape(length // block, block)
    lo = jnp.sum((segment[None, :] < blocks[:, :1]).astype(jnp.int32), axis=1) // other
    hi = (jnp.sum((segment[None, :] <= blocks[:, -1:]).astype(jnp.int32), axis=1) + other - 1) // other
    pad = jnp.sum((valid.reshape(length // block, block) == 0).astype(jnp.int32), axis=1)
    return lo, hi, pad


def attention_codes(segment, valid):
    kcode = jnp.where(valid > 0, segment, -1)
    qcode = segment
    wide = lambda a: jnp.broadcast_to(a[:, None], (a.shape[0], 128))
    return qcode, kcode, wide(qcode), wide(kcode)


def qkv_at(pair, which):
    return pair // 2 * 6 + which * 2 + pair % 2


def attend_fwd(qkv, segment, valid, bq=256, bk=256):
    length, width = qkv.shape
    pairs = width // 3 // PAIR
    lo, hi, pad = block_bounds(segment, valid, bq, bk)
    qcode, kcode, qwide, kwide = attention_codes(segment, valid)
    return pl.pallas_call(
        functools.partial(attend_fwd_kernel, bk),
        grid_spec=pltpu.PrefetchScalarGridSpec(
            num_scalar_prefetch=3,
            grid=(pairs, length // bq),
            in_specs=[
                pl.BlockSpec((bq, PAIR), lambda h, i, *_: (i, qkv_at(h, 0))),
                pl.BlockSpec((length, PAIR), lambda h, i, *_: (0, qkv_at(h, 1))),
                pl.BlockSpec((length, PAIR), lambda h, i, *_: (0, qkv_at(h, 2))),
                pl.BlockSpec((1, bq), lambda h, i, *_: (0, i)),
                pl.BlockSpec((length, 128), lambda h, i, *_: (0, 0)),
            ],
            out_specs=[
                pl.BlockSpec((bq, PAIR), lambda h, i, *_: (i, h)),
                pl.BlockSpec((8, bq), lambda h, i, *_: (h, i)),
            ],
            scratch_shapes=[pltpu.VMEM((PAIR, length), BF16)],
        ),
        out_shape=[
            jax.ShapeDtypeStruct((length, pairs * PAIR), BF16),
            jax.ShapeDtypeStruct((pairs * 8, length), F32),
        ],
        compiler_params=pltpu.CompilerParams(dimension_semantics=("arbitrary", "arbitrary")),
        cost_estimate=pl.CostEstimate(flops=8 * 2 * length * length * PAIR, bytes_accessed=8 * length * width, transcendentals=4 * length * length),
    )(lo, hi, pad, qkv, qkv, qkv, qcode[None, :], kwide)


def attend_bwd(part, qkv, context, context_grad, lse, segment, valid, bq=256, bk=256):
    length, width = qkv.shape
    pairs = width // 6 // PAIR
    base = part * pairs
    lo, hi, pad = block_bounds(segment, valid, bk, bq)
    qcode, kcode, qwide, kwide = attention_codes(segment, valid)
    whole = pl.BlockSpec((length, PAIR), lambda h, i, *_: (0, h))
    piece = pl.BlockSpec((bk, PAIR), lambda h, i, *_: (i, h))
    source = pl.BlockSpec((length, PAIR), lambda h, i, *_: (0, base + h))
    cols = lambda at: pl.BlockSpec((bk, PAIR), lambda h, i, *_: (i, qkv_at(base + h, at)))
    shape = jax.ShapeDtypeStruct((length, pairs * PAIR), BF16)
    return pl.pallas_call(
        functools.partial(attend_bwd_kernel, bq),
        grid_spec=pltpu.PrefetchScalarGridSpec(
            num_scalar_prefetch=3,
            grid=(pairs, length // bk),
            in_specs=[
                pl.BlockSpec((length, PAIR), lambda h, i, *_: (0, qkv_at(base + h, 0))), cols(1), cols(2), source, source,
                pl.BlockSpec((8, length), lambda h, i, *_: (base + h, 0)),
                pl.BlockSpec((1, length), lambda h, i, *_: (0, 0)),
                pl.BlockSpec((bk, 128), lambda h, i, *_: (i, 0)),
            ],
            out_specs=[whole, piece, piece],
            scratch_shapes=[pltpu.VMEM((PAIR, length), F32), pltpu.VMEM((8, length), F32)],
        ),
        out_shape=[shape, shape, shape],
        compiler_params=pltpu.CompilerParams(dimension_semantics=("arbitrary", "arbitrary")),
        cost_estimate=pl.CostEstimate(flops=20 * 2 * length * length * PAIR, bytes_accessed=16 * length * width, transcendentals=4 * length * length),
    )(lo, hi, pad, qkv, qkv, qkv, context, context_grad, lse, qcode[None, :], kwide)


def norm_stats(values):
    center = values - jnp.mean(values, axis=1, keepdims=True)
    inverse = lax.rsqrt(jnp.mean(center * center, axis=1, keepdims=True) + 1e-05)
    return center * inverse, inverse


def norm_pull(incoming, normed, inverse, gain):
    scaled = incoming * gain
    return inverse * (
        scaled - jnp.mean(scaled, axis=1, keepdims=True) - normed * jnp.mean(scaled * normed, axis=1, keepdims=True)
    )


def col_sum(values):
    return jnp.sum(values, axis=0, keepdims=True)


def add_sums(ref, parts):
    @pl.when(pl.program_id(0) == 0)
    def _():
        ref[...] = jnp.zeros_like(ref)

    for at, part in enumerate(parts):
        ref[at : at + 1, :] += col_sum(part)


def mix_kernel(at_ref, x_ref, c_ref, w_ref, bias_ref, gain_ref, hl_ref, turned_ref, n_ref, r_ref):
    mixed = x_ref[...].astype(F32) + dot(c_ref[...], w_ref[...]) + bias_ref[0:1, :]
    normed, inverse = norm_stats(mixed)
    hl = (normed * gain_ref[0:1, :] + bias_ref[1:2, :]).astype(BF16)
    hl_ref[...] = hl
    turned_ref[...] = hl.T
    n_ref[...] = normed
    r_ref[...] = jnp.broadcast_to(inverse, r_ref.shape)


def up_kernel(h_ref, w_ref, bias_ref, g_ref, slope_ref):
    u = dot(h_ref[...], w_ref[...]) + bias_ref[...]
    cdf = 0.5 + 0.5 * lax.erf(u * (1.0 / math.sqrt(2.0)))
    g_ref[...] = (u * cdf).astype(BF16)
    slope_ref[...] = (cdf + u * (jnp.exp(-0.5 * u * u) * (1.0 / math.sqrt(2.0 * math.pi)))).astype(BF16)


def assemble(w_ref, w_all, sem):
    for d in range(w_ref.shape[0]):
        for t in range(w_ref.shape[1]):
            rows_, cols = w_ref.shape[2:]
            pltpu.make_async_copy(
                w_ref.at[d, t], w_all.at[pl.ds(t * rows_, rows_), pl.ds(d * cols, cols)], sem
            ).start()
    pltpu.make_async_copy(w_all, w_all, sem).wait()


def down_kernel(g_ref, w_ref, n_ref, e_ref, bias_ref, gain_ref, out_ref, dr_ref, dz_ref, sum_ref, w_all, sem):
    pl.when(pl.program_id(0) == 0)(lambda: assemble(w_ref, w_all, sem))
    hidden = n_ref[...] * gain_ref[0:1, :] + bias_ref[1:2, :]
    normed, inverse = norm_stats(hidden + dot(g_ref[...], w_all[...]) + bias_ref[2:3, :])
    out_ref[...] = (normed * gain_ref[1:2, :] + bias_ref[3:4, :]).astype(BF16)
    e = e_ref[...].astype(F32)
    dr = norm_pull(e, normed, inverse, gain_ref[1:2, :])
    dr_ref[...] = dr
    dz_ref[...] = dr.astype(BF16)
    add_sums(sum_ref, (e * normed, dr, e))


def slope_kernel(dz_ref, w_ref, slope_ref, du_ref, sum_ref, w_all, sem):
    cols = slope_ref.shape[1]
    j = pl.program_id(0)
    pl.when(jnp.logical_and(j == 0, pl.program_id(1) == 0))(lambda: assemble(w_ref, w_all, sem))
    du = (dot(dz_ref[...], w_all[pl.ds(pl.multiple_of(j * cols, cols), cols), :], NT) * slope_ref[...].astype(F32)).astype(BF16)
    du_ref[...] = du

    @pl.when(pl.program_id(1) == 0)
    def _():
        sum_ref[...] = jnp.zeros_like(sum_ref)

    sum_ref[0:1, :] += col_sum(du.astype(F32))


def mix_pull_kernel(du_ref, w_ref, dr_ref, n_ref, r_ref, gain_ref, dm_ref, da_ref, sum_ref):
    dh = dr_ref[...] + dot(du_ref[...], w_ref[...], NT)
    normed = n_ref[...]
    dm = norm_pull(dh, normed, r_ref[:, 0:1], gain_ref[0:1, :])
    dm_ref[...] = dm
    da_ref[...] = dm.astype(BF16)
    add_sums(sum_ref, (dh * normed, dm, dh))


def call(kernel, grid, ins, outs, flops, nbytes, *args, scratch=()):
    return pl.pallas_call(
        kernel,
        grid=grid,
        in_specs=ins,
        out_specs=outs[0],
        out_shape=outs[1],
        scratch_shapes=list(scratch),
        compiler_params=pltpu.CompilerParams(dimension_semantics=("arbitrary",) * len(grid)),
        cost_estimate=pl.CostEstimate(flops=flops, bytes_accessed=nbytes, transcendentals=0),
    )(*args)


def rows(block, width):
    return pl.BlockSpec((block, width), lambda i: (i, 0))


def held(shape):
    return pl.BlockSpec(shape, lambda i: (0, 0))


def once(shape):
    return pl.BlockSpec(shape, lambda i: (0, 0), pipeline_mode=pl.Buffered(1))


def sds(shape, dtype=BF16):
    return jax.ShapeDtypeStruct(shape, dtype)


def mix(core_at, x, c, w, biases, gains, block=256):
    n, d = c.shape
    r = lambda width: pl.BlockSpec((block, width), lambda i, at: (i, 0))
    fixed = lambda value: pl.BlockSpec(value.shape, lambda i, at: (0, 0), pipeline_mode=pl.Buffered(1))
    steps = n // block
    return pl.pallas_call(
        mix_kernel,
        grid_spec=pltpu.PrefetchScalarGridSpec(
            num_scalar_prefetch=1,
            grid=(steps,),
            in_specs=[
                pl.BlockSpec((block, d), lambda i, at: (at[0] * steps + i, 0)), r(d), fixed(w), fixed(biases), fixed(gains),
            ],
            out_specs=[r(d), pl.BlockSpec((d, block), lambda i, at: (0, i)), r(d), r(128)],
        ),
        out_shape=[sds((n, d)), sds((d, n)), sds((n, d), F32), sds((n, 128), F32)],
        compiler_params=pltpu.CompilerParams(dimension_semantics=("arbitrary",)),
        cost_estimate=pl.CostEstimate(flops=2 * n * d * d, bytes_accessed=12 * n * d, transcendentals=0),
    )(core_at, x, c, w, biases, gains)


def up(h, w, bias, block=256, cols=1024):
    n, d = h.shape
    f = w.shape[1]
    cols = min(cols, f)
    tile = pl.BlockSpec((block, cols), lambda j, i: (i, j))
    return call(
        up_kernel, (f // cols, n // block),
        [pl.BlockSpec((block, d), lambda j, i: (i, 0)), pl.BlockSpec((d, cols), lambda j, i: (0, j)), pl.BlockSpec((1, cols), lambda j, i: (0, j))],
        ([tile, tile], [sds((n, f)), sds((n, f))]),
        2 * n * d * f, 4 * n * f + 2 * d * f, h, w, bias,
    )


def assembled(w):
    shape = (w.shape[1] * w.shape[2], w.shape[0] * w.shape[3])
    return shape, [pltpu.VMEM(shape, BF16), pltpu.SemaphoreType.DMA]


def down(g, w, normed, e, biases, gains, block=256):
    n, f = g.shape
    (_, d), scratch = assembled(w)
    r = functools.partial(rows, block)
    return call(
        down_kernel, (n // block,),
        [r(f), pl.BlockSpec(memory_space=pl.ANY), r(d), r(d), held(biases.shape), held(gains.shape)],
        ([r(d), r(d), r(d), held((8, d))], [sds((n, d)), sds((n, d), F32), sds((n, d)), sds((8, d), F32)]),
        2 * n * d * f, 2 * n * f + 2 * d * f, g, w, normed, e, biases, gains, scratch=scratch,
    )


def slope_pull(dz, w, slope, block=256, cols=1024):
    n, d = dz.shape
    (f, _), scratch = assembled(w)
    tile = pl.BlockSpec((block, cols), lambda j, i: (i, j))
    return call(
        slope_kernel, (f // cols, n // block),
        [pl.BlockSpec((block, d), lambda j, i: (i, 0)), pl.BlockSpec(memory_space=pl.ANY), tile],
        ([tile, pl.BlockSpec((8, cols), lambda j, i: (0, j))], [sds((n, f)), sds((8, f), F32)]),
        2 * n * d * f, 4 * n * f + 2 * d * f, dz, w, slope, scratch=scratch,
    )


def mix_pull(du, w, dr, normed, inverse, gains, block=256):
    n, f = du.shape
    d = w.shape[0]
    r = functools.partial(rows, block)
    return call(
        mix_pull_kernel, (n // block,),
        [r(f), once(w.shape), r(d), r(d), r(128), held(gains.shape)],
        ([r(d), r(d), held((8, d))], [sds((n, d), F32), sds((n, d)), sds((8, d), F32)]),
        2 * n * d * f, 2 * n * f + 2 * d * f, du, w, dr, normed, inverse, gains,
    )


def split_columns(acc, keep_ref, send_ref):
    n_p, c = keep_ref.shape[0], keep_ref.shape[3]
    for bit in (0, 1):

        @pl.when(lax.axis_index("core") == bit)
        def _():
            for p in range(n_p):
                at, to = (2 * p + bit) * c, (2 * p + 1 - bit) * c
                keep_ref[p, 0] = acc[:, at : at + c]
                send_ref[p, 0] = acc[:, to : to + c]


def split_rows(acc, place, keep_ref, send_ref):
    n_p, r = keep_ref.shape[0], keep_ref.shape[-2]
    for bit in (0, 1):

        @pl.when(lax.axis_index("core") == bit)
        def _():
            for p in range(n_p):
                at, to = (2 * p + bit) * r, (2 * p + 1 - bit) * r
                for cb in range(acc.shape[1] // 128):
                    keep_ref[(p, 0) + place + (cb,)] = acc[at : at + r, cb * 128 : cb * 128 + 128]
                    send_ref[(p, 0) + place + (cb,)] = acc[to : to + r, cb * 128 : cb * 128 + 128]


def col_grad_kernel(a_ref, b_ref, keep_ref, send_ref, acc):
    acc[...] = dot(a_ref[...], b_ref[...], TN).astype(BF16)
    split_columns(acc, keep_ref, send_ref)


def row_grad_kernel(a_ref, b_ref, keep_ref, send_ref, acc):
    acc[...] = dot(a_ref[...], b_ref[...]).astype(BF16)
    split_rows(acc, (), keep_ref, send_ref)


def grad_call(kernel, grid, ins, outs, scratch, flops, *args):
    return pl.pallas_call(
        kernel,
        grid=grid,
        in_specs=ins,
        out_specs=outs[0],
        out_shape=outs[1],
        scratch_shapes=scratch,
        compiler_params=pltpu.CompilerParams(dimension_semantics=("arbitrary",) * len(grid)),
        cost_estimate=pl.CostEstimate(flops=flops, bytes_accessed=flops // 512, transcendentals=0),
    )(*args)


def col_grad(a, b, n_p, n_t, block=512):
    n, f = a.shape
    d = b.shape[1]
    per_t, c = f // n_t, d // (2 * n_p)
    block = min(block, per_t)
    steps = per_t // block
    spec = pl.BlockSpec((n_p, 1, block, c), lambda i: (0, i // steps, i % steps, 0))
    shape = sds((n_p, n_t, per_t, c))
    return grad_call(
        col_grad_kernel, (f // block,),
        [pl.BlockSpec((n, block), lambda i: (0, i)), once((n, d))],
        ([spec, spec], [shape, shape]), [pltpu.VMEM((block, d), BF16)], 2 * n * f * d, a, b,
    )


def row_grad(a, b, n_p, n_t, block=512):
    d, n = a.shape
    f = b.shape[1]
    per_t, r = f // n_t, d // (2 * n_p)
    steps = per_t // block
    spec = pl.BlockSpec((n_p, 1, block // 128, r, 128), lambda i: (0, i // steps, i % steps, 0, 0))
    shape = sds((n_p, n_t, per_t // 128, r, 128))
    return grad_call(
        row_grad_kernel, (f // block,),
        [once((d, n)), pl.BlockSpec((n, block), lambda i: (0, i))],
        ([spec, spec], [shape, shape]), [pltpu.VMEM((d, block), BF16)], 2 * n * f * d, a, b,
    )


def input_pull_kernel(extra, at_ref, *refs):
    parts, w_ref = refs[:6], refs[6]
    c = w_ref.shape[1] // 6
    total = dot(parts[0][...], w_ref[:, :c], NT)
    for j in range(1, 6):
        total = total + dot(parts[j][...], w_ref[:, j * c : (j + 1) * c], NT)
    if extra:
        total = total + refs[7][...]
    refs[-1][...] = total.astype(refs[-1].dtype)


def input_pull(half, core, parts, w, dm=None, block=256):
    n, f = parts[0].shape
    d = w.shape[0]
    steps = n // 2 // block
    cols = pl.BlockSpec((block, f), lambda i, at: (at[0] * steps + i, 0))
    own = pl.BlockSpec((block, d), lambda i, at: (i, 0))
    extra = [] if dm is None else [dm]
    held_w = pl.BlockSpec((d, w.shape[1] // 2), lambda i, at: (0, at[1]), pipeline_mode=pl.Buffered(1))
    return pl.pallas_call(
        functools.partial(input_pull_kernel, len(extra)),
        grid_spec=pltpu.PrefetchScalarGridSpec(
            num_scalar_prefetch=1,
            grid=(steps,),
            in_specs=[cols] * 6 + [held_w] + [own] * len(extra),
            out_specs=own,
        ),
        out_shape=sds((n // 2, d), BF16 if dm is None else F32),
        compiler_params=pltpu.CompilerParams(dimension_semantics=("arbitrary",)),
        cost_estimate=pl.CostEstimate(flops=6 * n * f * d, bytes_accessed=8 * n * d, transcendentals=0),
    )(jnp.stack([half, core]).astype(jnp.int32), *parts, w, *extra)


MESH_ID = pl.DeviceIdType.MESH


def flip(value, bit):
    return value + bit - 2 * bit * ((value // bit) % 2)


def start_kernel(n_p, n_t, kinds, *refs):
    n = len(kinds)
    x_ref, bias_ref, *shards = refs[: n + 2]
    x_out, bias_out, *fulls = refs[n + 2 : 2 * n + 4]
    send_sems, recv_sems, own_sems = refs[2 * n + 4 :]
    p, core, t = lax.axis_index("p"), lax.axis_index("core"), lax.axis_index("tensor")
    me = 2 * p + core
    bits = [1 << s for s in range(n_p.bit_length() - 1)]
    column = [{"tensor": lax.rem(t + r, n_t)} for r in range(1, n_t)]
    across = [{"core": 1 - core, "tensor": lax.rem(t + r, n_t)} for r in range(n_t)]
    plane = [{"p": flip(p, bit)} for bit in bits]
    barrier = pltpu.get_barrier_semaphore()
    for peer in column + across + plane:
        pl.semaphore_signal(barrier, inc=1, device_id=peer, device_id_type=MESH_ID)
    pl.semaphore_wait(barrier, len(column + across + plane))

    used = [0, 0]

    def group():
        used[0] += 1
        return used[0] - 1

    def send(source, target, at, peer):
        pltpu.make_async_remote_copy(
            src_ref=source, dst_ref=target, send_sem=send_sems.at[at], recv_sem=recv_sems.at[at],
            device_id=peer, device_id_type=MESH_ID,
        ).start()

    def arrived(view, at):
        pltpu.make_async_copy(view, view, recv_sems.at[at]).wait()

    def left(view, at):
        pltpu.make_async_copy(view, view, send_sems.at[at]).wait()

    def keep(source, target):
        used[1] += 1
        copy = pltpu.make_async_copy(source, target, own_sems.at[used[1] - 1])
        copy.start()
        return copy

    def slab(i, d, half):
        full, kind = fulls[i], kinds[i]
        if kind == "rows":
            depth, wide = shards[i].shape[-2], full.shape[1] // 2
            return full.at[pl.ds(pl.multiple_of(d * depth, depth), depth), pl.ds(half * wide, wide)]
        depth, tall = shards[i].shape[-1], full.shape[0] // 2
        return full.at[pl.ds(half * tall, tall), pl.ds(pl.multiple_of(d * depth, depth), depth)]

    def slabs(i, count, half):
        full, kind = fulls[i], kinds[i]
        if kind == "rows":
            wide = full.shape[1] // 2
            return full.at[pl.ds(0, count * shards[i].shape[-2]), pl.ds(half * wide, wide)]
        tall = full.shape[0] // 2
        return full.at[pl.ds(half * tall, tall), pl.ds(0, count * shards[i].shape[-1])]

    def places(i, t):
        shard, full = shards[i], fulls[i]
        if kinds[i] == "columns":
            tall, depth = shard.shape
            return [(shard, full.at[pl.ds(pl.multiple_of(t * tall, tall), tall), pl.ds(pl.multiple_of(me * depth, depth), depth)])]
        depth, wide = shard.shape[-2:]
        rows_at = pl.ds(pl.multiple_of(me * depth, depth), depth)
        if len(shard.shape) == 2:
            return [(shard, full.at[rows_at, pl.ds(pl.multiple_of(t * wide, wide), wide)])]
        count = shard.shape[0]
        return [
            (shard.at[w], full.at[rows_at, pl.ds(pl.multiple_of((t * count + w) * wide, wide), wide)])
            for w in range(count)
        ]

    def shares(i, count):
        shard, full = shards[i], fulls[i]
        if kinds[i] == "columns":
            return full.at[pl.ds(0, count * shard.shape[0]), pl.ds(0, shard.shape[1])]
        wide = math.prod(shard.shape) // shard.shape[-2]
        return full.at[pl.ds(0, shard.shape[-2]), pl.ds(0, count * wide)]

    hops = n_t - 1
    own = [[keep(source, target) for source, target in places(i, t)] for i in range(n)]
    right, left_to = {"tensor": lax.rem(t + 1, n_t)}, {"tensor": lax.rem(t + n_t - 1, n_t)}
    line = [[(group(), group()) for _ in range(hops)] for _ in range(n)]

    def hop(i, s):
        to_right, to_left = line[i][s]

        @pl.when(jnp.logical_and(t + 1 < n_t, t >= s))
        def _():
            for source, target in places(i, t - s):
                send(source if s == 0 else target, target, to_right, right)

        @pl.when(jnp.logical_and(t >= 1, t + s < n_t))
        def _():
            for source, target in places(i, t + s):
                send(source if s == 0 else target, target, to_left, left_to)

    def hop_arrived(i, s):
        to_right, to_left = line[i][s]
        pl.when(t >= s + 1)(lambda: arrived(shares(i, 1), to_right))
        pl.when(t + s + 1 < n_t)(lambda: arrived(shares(i, 1), to_left))

    def hop_left(i, s):
        to_right, to_left = line[i][s]
        pl.when(jnp.logical_and(t + 1 < n_t, t >= s))(lambda: left(shares(i, 1), to_right))
        pl.when(jnp.logical_and(t >= 1, t + s < n_t))(lambda: left(shares(i, 1), to_left))

    for i in range(n):
        hop(i, 0)
    bias_at = group()
    bias_own = keep(bias_ref, bias_out.at[t])
    for peer in column:
        send(bias_ref, bias_out.at[t], bias_at, peer)

    held = x_ref.shape[1]
    odd = t % 2
    x_rows = x_out.at[pl.ds(pl.multiple_of(t * held, held), held), :]
    x_at = [group(), group()]
    stays = core == t // 2
    peer_a = {"core": t // 2, "tensor": 2 * core + odd}
    peer_b = {"core": t // 2, "tensor": 2 * core + 1 - odd}

    x_own = pltpu.make_async_copy(x_ref.at[odd], x_rows, own_sems.at[used[1]])
    used[1] += 1
    pl.when(stays)(x_own.start)

    def send_tokens():
        pl.when(jnp.logical_not(stays))(lambda: send(x_ref.at[odd], x_rows, x_at[0], peer_a))
        send(x_ref.at[1 - odd], x_rows, x_at[1], peer_b)

    partner = {"core": 1 - core}
    passes = []

    def forward(i, masks, half):
        at = group()
        guard = i == 0

        def go():
            for mask in masks:
                d = 2 * mask + core
                send(slab(i, d, half), slab(i, d, half), at, partner)

        if guard:
            pl.when(core == 1 - half)(go)
        else:
            go()
        passes.append((i, len(masks), half, at))

    states = {}

    def stage(i, s):
        if s == 0:
            hop_arrived(i, hops - 1)
            states[i] = {}
            for half in (0, 1):
                states[i][half] = ([p], None)
        else:
            for half in (0, 1):
                masks, at = states[i][half]
                arrived(slabs(i, len(masks), half), at)
                bit = bits[s - 1] if half == 0 else bits[-s]
                states[i][half] = (masks + [flip(m, bit) for m in masks], None)
        for half in (0, 1):
            masks, _ = states[i][half]
            if s < len(bits):
                at = group()
                bit = bits[s] if half == 0 else bits[-s - 1]
                for m in masks:
                    d = 2 * m + core
                    send(slab(i, d, half), slab(i, d, half), at, {"p": flip(p, bit)})
                states[i][half] = (masks, at)
                finish.append((i, len(masks), half, at))
            fresh = masks if s == 0 else masks[len(masks) // 2 :]
            forward(i, fresh, half)

    finish = []
    for step in range(n + hops - 1 + len(bits)):
        for i in range(n):
            at = step - i
            if 0 <= at < hops - 1:
                if at == 0:
                    for copy in own[i]:
                        copy.wait()
                hop_arrived(i, at)
                hop(i, at + 1)
                if i == n - 1 and at == hops - 2:
                    send_tokens()
            elif 0 <= at - (hops - 1) <= len(bits):
                stage(i, at - (hops - 1))

    pl.when(jnp.logical_not(stays))(lambda: arrived(x_rows, x_at[0]))
    pl.when(stays)(x_own.wait)
    arrived(x_rows, x_at[1])
    half_rows = x_out.at[pl.ds(pl.multiple_of(core * 2 * held, 2 * held), 2 * held), :]
    x_pass = group()
    send(half_rows, half_rows, x_pass, partner)
    bias_own.wait()
    arrived(bias_out.at[pl.ds(0, n_t - 1)], bias_at)
    for i, count, half, at in passes:
        if i == 0:
            pl.when(core == half)(functools.partial(arrived, slabs(i, count, half), at))
        else:
            arrived(slabs(i, count, half), at)
    arrived(half_rows, x_pass)
    left(half_rows, x_pass)
    for i, count, half, at in passes:
        if i == 0:
            pl.when(core == 1 - half)(functools.partial(left, slabs(i, count, half), at))
        else:
            left(slabs(i, count, half), at)
    for i, count, half, at in finish:
        left(slabs(i, count, half), at)
    for i in range(n):
        for s in range(hops):
            hop_left(i, s)
    left(bias_out.at[pl.ds(0, n_t - 1)], bias_at)
    pl.when(jnp.logical_not(stays))(lambda: left(x_rows, x_at[0]))
    left(x_rows, x_at[1])


def start_gather(x, bias, shards, kinds, n_p, n_t):
    n_dp = 2 * n_p
    fulls = []
    for shard, kind in zip(shards, kinds):
        if kind == "columns":
            fulls.append(sds((shard.shape[0] * n_t, shard.shape[1] * n_dp)))
        else:
            fulls.append(sds((shard.shape[-2] * n_dp, math.prod(shard.shape) // shard.shape[-2] * n_t)))
    bits = n_p.bit_length() - 1
    count = len(shards) * (2 * (n_t - 1) + 2 * bits + 2 * (bits + 1)) + 4
    vmem, away = pl.BlockSpec(memory_space=pltpu.VMEM), pl.BlockSpec(memory_space=pl.ANY)
    return pl.pallas_call(
        functools.partial(start_kernel, n_p, n_t, kinds),
        out_shape=[sds((n_t * x.shape[1], x.shape[2])), sds((n_t,) + bias.shape, F32)] + fulls,
        in_specs=[vmem] * (2 + len(shards)),
        out_specs=[away] * (2 + len(shards)),
        scratch_shapes=[
            pltpu.SemaphoreType.DMA((count,)), pltpu.SemaphoreType.DMA((count,)), pltpu.SemaphoreType.DMA((10,)),
        ],
        compiler_params=pltpu.CompilerParams(collective_id=1, has_side_effects=True),
    )(x, bias, *shards)


def project_kernel(core_ref, x_ref, w_ref, bias_ref, out_ref, turned_ref):
    turned_ref[...] = x_ref[...].T
    out_ref[...] = (dot(x_ref[...], w_ref[...]) + bias_ref[...]).astype(BF16)


def project(core_at, x, w, bias, block=256):
    n, d = x.shape
    f = w.shape[1] // 2
    return pl.pallas_call(
        project_kernel,
        grid_spec=pltpu.PrefetchScalarGridSpec(
            num_scalar_prefetch=1,
            grid=(n // block,),
            in_specs=[
                pl.BlockSpec((block, d), lambda i, at: (i, 0)),
                pl.BlockSpec((d, f), lambda i, at: (0, at[0]), pipeline_mode=pl.Buffered(1)),
                pl.BlockSpec((1, f), lambda i, at: (0, 0)),
            ],
            out_specs=[pl.BlockSpec((block, f), lambda i, at: (i, 0)), pl.BlockSpec((d, block), lambda i, at: (0, i))],
        ),
        out_shape=[sds((n, f)), sds((d, n))],
        compiler_params=pltpu.CompilerParams(dimension_semantics=("arbitrary",)),
        cost_estimate=pl.CostEstimate(flops=2 * n * d * f, bytes_accessed=4 * n * d + 2 * n * f, transcendentals=0),
    )(core_at, x, w, bias)


def finish_kernel(n_p, n_t, *refs):
    dx, x_turned, *grads, up_a, up_b, out_a, out_b, small = refs[:13]
    given, qkv_out, up_out, out_out, small_out = refs[13:18]
    keep2, send2, acc, recv2, pairs, slots1, last, last_slot, up_cur, up_slot, out_cur, out_slot = refs[18:30]
    out_next, out_last, small_cur, small_slot = refs[30:34]
    bits = [n_p >> (s + 1) for s in range(n_p.bit_length() - 1)]
    curs, slots = refs[34 : 34 + len(bits)], refs[34 + len(bits) : 34 + 2 * len(bits)]
    send_sems, recv_sems = refs[-2:]
    p, core, t = lax.axis_index("p"), lax.axis_index("core"), lax.axis_index("tensor")
    partner = {"core": 1 - core}
    column = [{"tensor": lax.rem(t + r, n_t)} for r in range(1, n_t)]
    column += [{"core": 1 - core, "tensor": lax.rem(t + r, n_t)} for r in range(n_t)]
    plane = [{"p": flip(p, bit)} for bit in bits]
    line = {bit: {"tensor": flip(t, bit)} for bit in (2, 1)}
    barrier = pltpu.get_barrier_semaphore()
    for peer in column + plane:
        pl.semaphore_signal(barrier, inc=1, device_id=peer, device_id_type=MESH_ID)
    pl.semaphore_wait(barrier, len(column + plane))

    used = [0]

    def send(source, target, peer):
        at = used[0]
        used[0] += 1
        copy = pltpu.make_async_remote_copy(
            src_ref=source, dst_ref=target, send_sem=send_sems.at[at], recv_sem=recv_sems.at[at],
            device_id=peer, device_id_type=MESH_ID,
        )
        return copy

    def go(source, target, peer):
        copy = send(source, target, peer)
        copy.start()
        return copy

    def plus(a, b):
        return (a.astype(F32) + b.astype(F32)).astype(BF16)

    u, odd = t // 2, t % 2
    for at in range(4):
        out_cur[at % 2, at // 2] = plus(out_a[at], out_b[at])
    out_move = go(out_cur.at[1 - odd], out_slot, line[1])
    for at in (0, 1):
        up_cur[at] = plus(up_a[at], up_b[at])
    up_move = go(up_cur.at[1 - u], up_slot, line[2])

    held = given.shape[1]
    stays = core == u
    rows_a = dx.at[pl.ds(pl.multiple_of(odd * held, held), held), :]
    rows_b = dx.at[pl.ds(pl.multiple_of((1 - odd) * held, held), held), :]
    give_a = send(rows_a, given.at[odd], {"core": u, "tensor": 2 * core + odd})
    pl.when(jnp.logical_not(stays))(give_a.start)
    give_b = go(rows_b, given.at[odd], {"core": u, "tensor": 2 * core + 1 - odd})

    @pl.when(stays)
    def _():
        given[odd] = dx[pl.ds(pl.multiple_of(odd * held, held), held), :]

    orders = [bits, bits[::-1]]

    def spot(part, j):
        return sum(n_p >> (s + 1) for s, bit in enumerate(orders[part]) if j // bit % 2)

    r = keep2.shape[2] // 6
    swaps = []
    for part in (0, 1):
        for which in range(3):
            acc[...] = dot(x_turned[...], grads[3 * part + which][...]).astype(BF16)
            for bit in (0, 1):

                @pl.when(core == bit)
                def _():
                    for j in range(n_p):
                        at, to = (2 * j + bit) * r, (2 * j + 1 - bit) * r
                        for cb in (0, 1):
                            place = pl.ds((2 * which + cb) * r, r)
                            keep2[part, spot(part, j), place, :] = acc[at : at + r, cb * 128 : cb * 128 + 128]
                            send2[part, spot(part, j), place, :] = acc[to : to + r, cb * 128 : cb * 128 + 128]
        swaps.append(go(send2.at[part], recv2.at[part], partner))
    small_cur[0] = small[...]
    per_row = dx.shape[1] // 128
    for part in (0, 1):
        for which in (0, 1):
            total = jnp.sum(grads[3 * part + 2 * which][...].astype(F32), axis=0, keepdims=True)
            for bit in (0, 1):

                @pl.when(core == bit)
                def _():
                    at = (6 + which) * per_row + bit * (per_row // 2) + part * (per_row // 4)
                    for cb in (0, 1):
                        small_cur[0, at + cb : at + cb + 1, :] = total[:, cb * 128 : cb * 128 + 128]

    peers = [partner] + plane
    for at, peer in enumerate(peers):
        copy = go(small_cur.at[at], small_slot.at[at], peer)
        copy.wait()
        small_cur[at + 1] = small_cur[at] + small_slot[at]

    sources = []
    for part in (0, 1):
        swaps[part].wait()
        sources.append([keep2.at[part], recv2.at[part]])
    for s in range(len(bits)):
        size = n_p >> (s + 1)
        copies = []
        for part in (0, 1):
            bit = orders[part][s]
            mine = (p // bit) % 2
            peer = {"p": flip(p, bit)}
            copies.append(
                [go(sources[part][j].at[pl.ds((1 - mine) * size, size)], slots[s].at[part, j], peer) for j in (0, 1)]
            )
        for part in (0, 1):
            mine = (p // orders[part][s]) % 2
            for j in (0, 1):
                copies[part][j].wait()
                if size == 1:
                    pairs[part, core if j == 0 else 1 - core] = plus(sources[part][j][mine], slots[s][part, j, 0])
                else:
                    for at in range(size):
                        curs[s][part, j, at] = plus(sources[part][j][mine * size + at], slots[s][part, j, at])
            sources[part] = [curs[s].at[part, 0], curs[s].at[part, 1]]
    pair_move = go(pairs.at[1 - odd], slots1, line[1])
    out_move.wait()
    for at in (0, 1):
        out_next[at] = plus(out_cur[odd, at], out_slot[at])
    out_move = go(out_next.at[1 - u], out_last, line[2])
    pair_move.wait()
    for at in (0, 1):
        last[at] = plus(pairs[odd, at], slots1[at])
    last_move = go(last.at[1 - u], last_slot, line[2])
    for bit in (1, 2):
        at = len(peers)
        copy = go(small_cur.at[at], small_slot.at[at], line[bit])
        copy.wait()
        peers.append(None)
        if bit == 2:
            small_out[...] = small_cur[at] + small_slot[at]
        else:
            small_cur[at + 1] = small_cur[at] + small_slot[at]
    up_move.wait()
    up_out[...] = up_cur[u].astype(F32) + up_slot[...].astype(F32)
    out_move.wait()
    out_out[...] = out_next[u].astype(F32) + out_last[...].astype(F32)
    last_move.wait()
    qkv_out[...] = last[u].astype(F32) + last_slot[...].astype(F32)
    pl.when(jnp.logical_not(stays))(give_a.wait)
    give_b.wait()


def finish(n_p, n_t, dx, x_turned, first, second, up_, out_, small):
    d, wide = x_turned.shape[0], first[0].shape[1]
    rows_ = 3 * wide * d // (2 * n_p) // 128
    bits = n_p.bit_length() - 1
    steps = 1 + bits + 2
    box = lambda *lead: pltpu.VMEM(lead + (rows_, 128), BF16)
    like = lambda lead, value: pltpu.VMEM(lead + value.shape[1:], BF16)
    halves = [box(2, 2, n_p >> (s + 1)) for s in range(bits)]
    vmem = pl.BlockSpec(memory_space=pltpu.VMEM)
    count = 9 + steps + 4 * bits
    return pl.pallas_call(
        functools.partial(finish_kernel, n_p, n_t),
        out_shape=[
            sds((2, dx.shape[0] // 2, dx.shape[1])), sds((rows_, 128), F32), sds(up_[0].shape[1:], F32),
            sds(out_[0].shape[1:], F32), sds(small.shape, F32),
        ],
        in_specs=[vmem] * 13,
        out_specs=[vmem] * 5,
        scratch_shapes=[
            box(2, n_p), box(2, n_p), pltpu.VMEM((d, wide), BF16), box(2, n_p), box(2, 2), box(2), box(2), box(),
            like((2,), up_[0]), like((), up_[0]), like((2, 2), out_[0]), like((2,), out_[0]), like((2,), out_[0]),
            like((), out_[0]), pltpu.VMEM((steps,) + small.shape, F32), pltpu.VMEM((steps,) + small.shape, F32),
            *halves, *halves,
            pltpu.SemaphoreType.DMA((count,)), pltpu.SemaphoreType.DMA((count,)),
        ],
        compiler_params=pltpu.CompilerParams(collective_id=0, has_side_effects=True),
        cost_estimate=pl.CostEstimate(flops=32 * d * d * 1024, bytes_accessed=64 * d * d, transcendentals=0),
    )(dx, x_turned, *first, *second, *up_, *out_, small)


def swap_cores(value):
    return lax.ppermute(value, "core", [(0, 1), (1, 0)])


def column_routes(tensor_size):
    first, second = [], []
    for core in range(2):
        for t in range(tensor_size):
            at = core * tensor_size + t
            first.append((at, (t >> 1) * tensor_size + 2 * core + (t & 1)))
            second.append((at, (t >> 1) * tensor_size + 2 * core + 1 - (t & 1)))
    return first, second


def back(route):
    return [(b, a) for a, b in route]


def by_core(core, mine, other, axis):
    return jnp.where(
        core == 0, jnp.concatenate([mine, other], axis=axis), jnp.concatenate([other, mine], axis=axis)
    )


def body(
    inputs, segment_ids, token_valid, qkv_weight, qv_bias, out_weight, norm_gains, row_biases,
    up_weight, up_bias, down_weight, out_grad,
):
    COL = ("core", "tensor")
    ALL = ("p", "core", "tensor")
    core, tensor = lax.axis_index("core"), lax.axis_index("tensor")
    n_p, n_t = lax.axis_size("p"), lax.axis_size("tensor")
    n_dp = 2 * n_p
    micro, held_rows, width = inputs.shape
    assert micro == 2 and n_t == 4
    odd = tensor & 1
    route_a, route_b = column_routes(n_t)

    def bring(value):
        a = lax.ppermute(value[odd], COL, route_a)
        b = lax.ppermute(value[1 - odd], COL, route_b)
        return jnp.where(odd == 0, jnp.concatenate([a, b]), jnp.concatenate([b, a]))

    def blocks(value):
        return [lax.dynamic_slice_in_dim(value, at * held_rows, held_rows) for at in (odd, 1 - odd)]

    def give(a, b):
        a, b = lax.ppermute(a, COL, back(route_a)), lax.ppermute(b, COL, back(route_b))
        return jnp.where(odd == 0, jnp.stack([a, b]), jnp.stack([b, a]))

    def gathered(weight):
        got = lax.all_gather(weight, ALL, axis=0, tiled=False)
        return got.reshape((n_dp, n_t) + weight.shape)

    labels = jnp.stack([segment_ids[:, 0], token_valid[:, 0]], axis=1)[odd]
    labels = jnp.where((tensor >> 1) == core, labels, swap_cores(labels))
    segment, valid = labels[0], labels[1]

    shards, kinds = [qkv_weight, up_weight], ["rows", "rows"]
    wide = out_weight.shape[1] % 128 == 0
    if wide:
        shards, kinds = [qkv_weight, out_weight, up_weight], ["rows", "columns", "rows"]
    local_bias = jnp.concatenate([qv_bias.reshape(-1), up_bias]).reshape(-1, 128)
    x_full, bias_all, *fulls = start_gather(inputs, local_bias, shards, kinds, n_p, n_t)
    out_grad, down_weight, x_full = lax.optimization_barrier((out_grad, down_weight, x_full))
    w_down = gathered(down_weight)
    if wide:
        w_qkv, w_out, w_up = fulls
    else:
        w_qkv, w_up = fulls
        w_out = gathered(out_weight).transpose(1, 2, 0, 3).reshape(-1, width)
        w_down = w_down.transpose(1, 2, 0, 3).reshape(1, 1, -1, width)
    rows = x_full.shape[0] // 2
    own = w_qkv.shape[1] // 6
    bias_all = bias_all.reshape(n_t, -1)
    n_qv = qv_bias.size
    up_bias_all = bias_all[:, n_qv:].reshape(1, -1)
    qv_own = lax.dynamic_slice_in_dim(bias_all[:, :n_qv], 2 * core, 2).reshape(2, 2, -1)
    bias = jnp.stack([qv_own[:, 0], jnp.zeros_like(qv_own[:, 0]), qv_own[:, 1]], axis=1).reshape(1, -1)
    core_at = jnp.reshape(core, (1,)).astype(jnp.int32)
    qkv, x_turned = project(core_at, x_full, w_qkv, bias)
    context, lse = attend_fwd(qkv, segment, valid, 512, 512)
    mine = lax.dynamic_slice_in_dim(context, core * rows, rows)
    other = lax.dynamic_slice_in_dim(context, (1 - core) * rows, rows)
    c_own = by_core(core, mine, swap_cores(other), 1)
    hl, hl_turned, normed, inverse = mix(core_at, x_full, c_own, w_out, row_biases, norm_gains)
    active, slope = up(hl, w_up, up_bias_all)
    grad_own = bring(out_grad)
    layer, dr, dz, sums_two = down(active, w_down, normed, grad_own, row_biases, norm_gains)

    p_bits = [1 << s for s in range(n_p.bit_length() - 1)]
    t_bits = [1, 2]

    class Total:
        def __init__(self, parts, downward):
            lead = [("p", n_p, bit) for bit in reversed(p_bits)] + [("tensor", n_t, bit) for bit in (2, 1)]
            self.rest = parts[0].shape[2:]
            self.dims = lead
            self.parts = [part.reshape((2,) * len(lead) + self.rest) for part in parts]
            order = list(reversed(p_bits)) if downward else p_bits
            self.groups = [order[:1], order[1:], t_bits[:1], t_bits[1:]]

        def sum_of(self, pick):
            total = pick(self.parts[0]).astype(F32)
            for part in self.parts[1:]:
                total = total + pick(part).astype(F32)
            return total

        def cut_one(self, axis, bit):
            at = [d[0] + str(d[2]) for d in self.dims].index(axis + str(bit))
            size = self.dims[at][1]
            self.dims = self.dims[:at] + self.dims[at + 1 :]
            mine = (lax.axis_index(axis) // bit) % 2
            side = lambda which: self.sum_of(lambda part: lax.dynamic_index_in_dim(part, which, at, keepdims=False)).astype(BF16)
            self.live = [side(mine), side(1 - mine)]
            self.route = (axis, [(i, i ^ bit) for i in range(size)])

        def move(self):
            self.parts = [self.live[0], lax.ppermute(self.live[1], *self.route)]
            return self

        def cut(self, group):
            axis = "p" if group < 2 else "tensor"
            for j, bit in enumerate(self.groups[group]):
                if j:
                    self.move()
                self.cut_one(axis, bit)
            return self

    def together(sums, *others):
        lives, others = lax.optimization_barrier(([s.live for s in sums], others))
        for s, live in zip(sums, lives):
            s.live = live
            s.move()
        return others

    du, up_sum = slope_pull(dz, w_down, slope)
    active, du = lax.optimization_barrier((active, du))
    down_keep, down_send = col_grad(active, dz, n_p, n_t)
    down_send, du = lax.optimization_barrier((down_send, du))
    down_recv = swap_cores(down_send)
    up_keep, up_send = row_grad(hl_turned, du, n_p, n_t)
    up_recv = swap_cores(up_send)
    down_sum = Total([down_keep, down_recv], False).cut(0)
    (du,) = together([down_sum], du)
    dm, da, sums_one = mix_pull(du, w_up, dr, normed, inverse, norm_gains)
    dc = dot(da, w_out, NT).astype(BF16)
    mine = lax.dynamic_slice_in_dim(dc, core * own, own, 1)
    other = lax.dynamic_slice_in_dim(dc, (1 - core) * own, own, 1)
    dc_recv = swap_cores(other)
    up_sums = Total([up_keep, up_recv], True).cut(0)
    out_keep, out_send = col_grad(c_own, da, n_p, n_t)
    out_recv = swap_cores(out_send)
    dc_full = by_core(core, mine, dc_recv, 0)
    dc_full, layer = together([up_sums], dc_full, blocks(layer))
    layer_out = give(*layer)

    first = attend_bwd(0, qkv, context, dc_full, lse, segment, valid, 512, 256)
    out_sum = Total([out_keep, out_recv], False)
    dc_full, layer_out = together([down_sum.cut(1), up_sums.cut(1), out_sum.cut(0)], dc_full, layer_out)
    second = attend_bwd(1, qkv, context, dc_full, lse, segment, valid, 512, 256)
    (second,) = together([down_sum.cut(2), up_sums.cut(2), out_sum.cut(1)], second)

    dx_other = swap_cores(input_pull(1 - core, core, (*first, *second), w_qkv))
    dx_mine = input_pull(core, core, (*first, *second), w_qkv, dm)
    dx = (dx_mine + dx_other.astype(F32)).astype(BF16)
    (dx,) = together([down_sum.cut(3)], dx)
    down_total = down_sum.sum_of(lambda part: part)
    small = jnp.concatenate(
        [
            jnp.stack([sums_one[0], sums_two[0], sums_one[1], sums_one[2], sums_two[1], sums_two[2]]).reshape(-1),
            jnp.zeros((2 * width,), F32),
            up_sum[0],
        ]
    )
    rows_of = lambda part, count: part.reshape(count, -1, part.shape[-1])
    given, qkv_total, up_total, out_total, small = finish(
        n_p, n_t, dx, x_turned, first, second, [rows_of(part, 2) for part in up_sums.parts],
        [rows_of(part, 4) for part in out_sum.parts], small.reshape(-1, 128),
    )
    input_grad = given.astype(F32)
    small = small.reshape(-1)
    up_total = up_total.reshape(up_sums.rest).transpose(1, 0, 2).reshape(up_weight.shape)
    qkv_total = qkv_total.reshape(3, own // 256, -1, 128).transpose(0, 2, 1, 3).reshape(qkv_weight.shape)
    gain_sum = small[: 2 * width].reshape(2, width)
    bias_sum = small[2 * width : 6 * width].reshape(4, width)
    qv_total = lax.dynamic_slice_in_dim(small[6 * width : 8 * width].reshape(2, width), tensor * qv_bias.shape[1], qv_bias.shape[1], 1)
    up_bias_total = lax.dynamic_slice_in_dim(small[8 * width :], tensor * up_bias.shape[0], up_bias.shape[0])
    return (
        layer_out, input_grad, qkv_total, qv_total, out_total, gain_sum, bias_sum, up_total, up_bias_total, down_total,
    )


def solution(mesh):
    dp, tensor = mesh.devices.shape
    split = jax.sharding.Mesh(mesh.devices.reshape(dp // 2, 2, tensor), ("p", "core", "tensor"))
    pc = ("p", "core")
    tokens = P(None, ("p", "core", "tensor"), None)
    return jax.shard_map(
        body,
        mesh=split,
        in_specs=(
            tokens, P(None, pc, None), P(None, pc, None), P(None, pc, "tensor"), P(None, "tensor"), P("tensor", pc),
            P(), P(), P(pc, "tensor"), P("tensor"), P("tensor", pc), tokens,
        ),
        out_specs=(
            tokens, tokens, P(None, pc, "tensor"), P(None, "tensor"), P("tensor", pc), P(), P(), P(pc, "tensor"),
            P("tensor"), P("tensor", pc),
        ),
        check_vma=False,
    )
```
